32 devices in a mesh: dp: 16 (over z, y, x), tensor: 2 (over core).
Axes of the slice: x: 2, y: 2, z: 4, core: 2. Of those that a mesh axis runs over, the one named last changes fastest.
Arguments:
- tokens: bfloat16 [2, 8192, 768], P(None, 'dp'), may hold values from -6 to 6
- seg_doc: int32 [2, 64], replicated, may hold values from 0 to 15, as said below
- doc_len: int32 [2, 16], replicated, may hold values from 1 to 1024, as said below
- w_qkv: bfloat16 [2, 3, 768, 768], P(None, None, None, 'tensor'), may hold values from -0.21875 to 0.21875
- b_qv: float32 [2, 2, 768], P(None, None, 'tensor'), may hold values from -3 to 3
- w_out: bfloat16 [2, 768, 768], P(None, 'tensor'), may hold values from -0.625 to 0.625
- w_up: bfloat16 [2, 768, 3072], P(None, None, 'tensor'), may hold values from -0.21875 to 0.21875
- b_up: float32 [2, 3072], P(None, 'tensor'), may hold values from -3 to 3
- w_down: bfloat16 [2, 3072, 768], P(None, 'tensor'), may hold values from -0.109375 to 0.109375
- norm_gain: float32 [2, 2, 768], replicated, may hold values from 0.25 to 1.75
- bias_terms: float32 [2, 4, 768], replicated, may hold values from -3 to 3
- seg_pos: float32 [8, 768], replicated, may hold values from -3 to 3
- cotangent: bfloat16 [2, 8192, 768], P(None, 'dp'), may hold values from -6 to 6
Outputs:
- encoded: bfloat16 [2, 8192, 768], P(None, 'dp')
- grad_tokens: float32 [2, 8192, 768], P(None, 'dp')
- grad_w_qkv: float32 [2, 3, 768, 768], P(None, None, 'dp', 'tensor')
- grad_b_qv: float32 [2, 2, 768], P(None, None, 'tensor')
- grad_w_out: float32 [2, 768, 768], P(None, 'tensor', 'dp')
- grad_w_up: float32 [2, 768, 3072], P(None, 'dp', 'tensor')
- grad_b_up: float32 [2, 3072], P(None, 'tensor')
- grad_w_down: float32 [2, 3072, 768], P(None, 'tensor', 'dp')
- grad_norm_gain: float32 [2, 2, 768], replicated
- grad_bias_terms: float32 [2, 4, 768], replicated
- grad_seg_pos: float32 [8, 768], replicated
The draws below stay inside these ranges and needn't reach their ends.
Inputs may be any that keep to these rules, and one draw needn't show every extreme that they name: `seg_doc`: segment ids never fall along a micro-batch; every document 0 to 15 covers 1 to 8 consecutive segments. `doc_len`: A document of n segments has more than 128 * (n - 1) and at most 128 * n tokens; in every micro-batch one document has exactly 1024.
All inputs are finite; a program needn't handle non-finite values.
Results may differ from the reference program's by a relative error of at most 0.024.
Values may be sent and summed in bfloat16 or wider, within the bound.
A program may use at most 192 MiB of HBM per device.

```python
import jax
import jax.numpy as jnp
from jax import lax

D = 768
HEADS = 12
HEAD_DIM = 64
FF = 3072
SEG = 128
MAXSEG = 8
MICRO = 2
SEGS = 64
DOCS = 16
TOKENS = 8192


def shuffle_one(order_seed):
    return jax.random.permutation(order_seed, DOCS)


def doc_plan(key):
    base_key = jax.random.fold_in(key, 7)
    delta_key, order_key, fill_key = jax.random.split(base_key, 3)
    pair_count = (DOCS - 4) // 2
    deltas = jax.random.randint(delta_key, (MICRO, pair_count), -3, 4)
    paired = jnp.stack([4 + deltas, 4 - deltas], axis=-1).reshape(MICRO, DOCS - 4)
    leading = jnp.broadcast_to(jnp.array([MAXSEG, 2, 3, 3], jnp.int32), (MICRO, 4))
    base_counts = jnp.concatenate([leading, paired.astype(jnp.int32)], axis=1)
    orders = jax.vmap(shuffle_one)(jax.random.split(order_key, MICRO))
    counts = jnp.take_along_axis(base_counts, orders, axis=1)
    last_fill = jax.random.randint(fill_key, (MICRO, DOCS), 1, SEG + 1)
    last_fill = jnp.where(counts == MAXSEG, SEG, last_fill)
    lengths = (counts - 1) * SEG + last_fill
    starts = jnp.cumsum(counts, axis=1) - counts
    seg_ids = jnp.arange(SEGS)
    seg_doc = jnp.sum((starts[:, None, :] <= seg_ids[None, :, None]).astype(jnp.int32), axis=2) - 1
    return (seg_doc.astype(jnp.int32), lengths.astype(jnp.int32))


def draw_seg_doc(key, part):
    return doc_plan(key)[0]


def draw_doc_len(key, part):
    return doc_plan(key)[1]


def block_scale(own_key, shape, cuts, least, largest):
    factor_of = 1.0
    for position, parts in cuts:
        draws = jax.random.uniform(jax.random.fold_in(jax.random.fold_in(own_key, 6), position), (parts,), jnp.float32, least / len(cuts), largest / len(cuts))
        factor_of = factor_of * jnp.repeat(jnp.exp(draws), shape[position] // parts).reshape((-1,) + (1,) * (len(shape) - 1 - position))
    return factor_of


def bell_draw(rng, extent, deviation, bound, shards=(), held_as=jnp.bfloat16):
    values = jax.random.normal(rng, extent, jnp.float32) * deviation
    if len(shards) > 0:
        values = block_scale(rng, extent, shards, -0.22, 0.18) * values
    return jnp.clip(values, min=-bound, max=bound).astype(held_as)


def setup_inputs(seed: int = 0) -> dict:
    keys = jax.random.split(jax.random.key(seed), 14)
    tokens = bell_draw(keys[0], (MICRO, TOKENS, D), 1.0, 6.0, ((1, 16),))
    seg_doc = draw_seg_doc(jax.random.fold_in(keys[13], 71), 0)
    doc_len = draw_doc_len(jax.random.fold_in(keys[13], 71), 0)
    w_qkv = bell_draw(keys[3], (2, 3, D, D), D ** -0.5, 0.21875, ((3, 2),))
    b_qv = bell_draw(keys[4], (2, 2, D), 0.5, 3.0, ((2, 2),), jnp.float32)
    w_out = bell_draw(keys[5], (2, D, D), (D // 8) ** -0.5, 0.625, ((1, 2),))
    w_up = bell_draw(keys[6], (2, D, FF), D ** -0.5, 0.21875, ((2, 2),))
    b_up = bell_draw(keys[7], (2, FF), 0.5, 3.0, ((1, 2),), jnp.float32)
    w_down = bell_draw(keys[8], (2, FF, D), FF ** -0.5, 0.109375, ((1, 2),))
    norm_gain = jnp.clip(1.0 + 0.15 * jax.random.normal(keys[9], (2, 2, D), jnp.float32), 0.25, 1.75)
    bias_terms = bell_draw(keys[10], (2, 4, D), 0.5, 3.0, (), jnp.float32)
    seg_pos = bell_draw(keys[11], (MAXSEG, D), 0.5, 3.0, (), jnp.float32)
    cotangent = bell_draw(keys[12], (MICRO, TOKENS, D), 1.0, 6.0, ((1, 16),))
    return {"tokens": tokens, "seg_doc": seg_doc, "doc_len": doc_len, "w_qkv": w_qkv, "b_qv": b_qv, "w_out": w_out, "w_up": w_up, "b_up": b_up, "w_down": w_down, "norm_gain": norm_gain, "bias_terms": bias_terms, "seg_pos": seg_pos, "cotangent": cotangent}


precise = lax.Precision.HIGHEST
norm_eps = 1e-05
masked_score = -1e+30

@jax.custom_vjp
def low(v):
    return lax.optimization_barrier(v.astype(jnp.bfloat16)).astype(jnp.float32)

@jax.custom_vjp
def low_back(v):
    return v

def low_keep(v):
    return (low(v), None)

def low_pass(kept, grad):
    return (grad,)

def back_keep(v):
    return (v, None)

def back_low(kept, grad):
    return (low(grad),)
low.defvjp(low_keep, low_pass)
low_back.defvjp(back_keep, back_low)

def both_round(values):
    return low(low_back(values))

def norm_rows(values, gain, shift):
    centre = values - lax.optimization_barrier(jnp.mean(values, axis=-1, keepdims=True))
    spread = lax.optimization_barrier(jnp.mean(centre * centre, axis=-1, keepdims=True))
    return centre * lax.rsqrt(spread + norm_eps) * gain + shift

def hat_layer(inputs, key_mask, weights):
    w_qkv, b_qv, w_out, w_up, b_up, w_down, norm_gain, bias_terms = weights
    groups, span = key_mask.shape
    row_count, width = inputs.shape
    split_shape = (groups, span, HEADS, HEAD_DIM)
    inputs_b = low(inputs)
    queries = both_round(jnp.dot(inputs_b, w_qkv[0], precision=precise) + b_qv[0])
    key_rows = both_round(jnp.dot(inputs_b, w_qkv[1], precision=precise))
    value_rows = both_round(jnp.dot(inputs_b, w_qkv[2], precision=precise) + b_qv[1])
    raw = jnp.einsum('glhd,gmhd->ghlm', queries.reshape(split_shape), key_rows.reshape(split_shape), precision=precise) * HEAD_DIM ** (-0.5)
    scores = low_back(jnp.where(key_mask[:, None, None, :], raw, masked_score))
    attn_probs = low(jax.nn.softmax(scores, axis=-1))
    head_out = both_round(jnp.einsum('ghlm,gmhd->glhd', attn_probs, value_rows.reshape(split_shape), precision=precise).reshape(row_count, width))
    attn_out = low_back(jnp.dot(head_out, w_out, precision=precise) + bias_terms[0])
    hidden = norm_rows(inputs + attn_out, norm_gain[0], bias_terms[2])
    pre_act = low_back(jnp.dot(low(hidden), w_up, precision=precise) + b_up)
    active = low(jax.nn.gelu(pre_act, approximate=False))
    mlp_out = low_back(jnp.dot(active, w_down, precision=precise) + bias_terms[1])
    return norm_rows(hidden + mlp_out, norm_gain[1], bias_terms[3])

def deal_map(doc_ids, total_docs):
    return jnp.where(doc_ids % 2 == 1, (doc_ids + total_docs // 2) % total_docs, doc_ids).astype(jnp.int32)

def layout(seg_order, doc_lengths):
    doc_ids = jnp.arange(DOCS, dtype=jnp.int32)
    deal_row = deal_map(doc_ids, DOCS)
    starts = lax.optimization_barrier(jnp.sum((seg_order[None, :] < doc_ids[:, None]).astype(jnp.int32), axis=1))
    counts = lax.optimization_barrier(jnp.sum((seg_order[None, :] == doc_ids[:, None]).astype(jnp.int32), axis=1))
    seg_ids = jnp.arange(SEGS, dtype=jnp.int32)
    within = seg_ids - starts[seg_order]
    valid_tokens = jnp.minimum(SEG, doc_lengths[seg_order] - within * SEG)
    tok_mask = jnp.arange(SEG, dtype=jnp.int32)[None, :] < valid_tokens[:, None]
    src_slot = deal_row[seg_order] * MAXSEG + within
    slot_index = jnp.arange(MAXSEG, dtype=jnp.int32)
    cross_mask = slot_index[None, :] < counts[deal_row][:, None]
    target = jnp.where(cross_mask, starts[deal_row][:, None] + slot_index[None, :], 0).astype(jnp.int32)
    return (tok_mask, cross_mask, target, src_slot)

def forward(inputs, weights, tables):
    tok_mask, cross_mask, target, src_slot = tables
    w_qkv, b_qv, w_out, w_up, b_up, w_down, norm_gain, bias_terms, seg_pos = weights

    def params(level):
        return (w_qkv[level], b_qv[level], w_out[level], w_up[level], b_up[level], w_down[level], norm_gain[level], bias_terms[level])
    per_block = min(SEGS, 32)
    block_count = SEGS // per_block

    def seg_block(paired):
        return hat_layer(paired[0], paired[1], params(0))
    seg_out = lax.map(jax.checkpoint(seg_block), (inputs.reshape(block_count, per_block * SEG, D), tok_mask.reshape(block_count, per_block, SEG)))
    seg_out = seg_out.reshape(SEGS, SEG, D)
    cls_rows = both_round(seg_out[:, 0])
    cross_in = jnp.where(cross_mask[:, :, None], cls_rows[target], 0.0) + seg_pos[None]
    cross_out = hat_layer(cross_in.reshape(DOCS * MAXSEG, D), cross_mask, params(1))
    returned = both_round(cross_out)[src_slot]
    return seg_out.at[:, 0].set(returned).reshape(SEGS * SEG, D)

def reference(tokens, seg_doc, doc_len, w_qkv, b_qv, w_out, w_up, b_up, w_down, norm_gain, bias_terms, seg_pos, cotangent):
    weights = tuple((item_array.astype(jnp.float32) for item_array in (w_qkv, b_qv, w_out, w_up, b_up, w_down, norm_gain, bias_terms, seg_pos)))
    encoded = []
    grad_rows = []
    gradients = []
    for batch_index in range(MICRO):
        tables = layout(seg_doc[batch_index], doc_len[batch_index])

        def forward_fn(inputs, *params_list):
            return forward(inputs, params_list, tables)
        result, pullback = jax.vjp(forward_fn, tokens[batch_index].astype(jnp.float32), *weights)
        pulled = pullback(cotangent[batch_index].astype(jnp.float32))
        encoded.append(result.astype(jnp.bfloat16))
        grad_rows.append(pulled[0])
        gradients.append(pulled[1:])
    totals = [sum_terms for sum_terms in gradients[0]]
    for later in gradients[1:]:
        totals = [left + right for left, right in zip(totals, later)]
    return (jnp.stack(encoded), jnp.stack(grad_rows), totals[0], totals[1], totals[2], totals[3], totals[4], totals[5], totals[6], totals[7], totals[8])
```

```python
from functools import partial, reduce

import jax
import jax.numpy as jnp
from jax import lax
from jax.experimental import pallas as pl
from jax.experimental.pallas import tpu as pltpu
from jax.sharding import PartitionSpec as P

HEAD_DIM = 64
SEG = 128
MAXSEG = 8


norm_eps = 1e-05
masked_score = -1e30


def norm_rows(values, gain, shift):
    centre = values - jnp.mean(values, axis=-1, keepdims=True)
    spread = jnp.mean(centre * centre, axis=-1, keepdims=True)
    return centre * lax.rsqrt(spread + norm_eps) * gain + shift


def exact_gelu(values):
    return jax.nn.gelu(values, approximate=False)


def my_rows(values):
    part_rows = values.shape[0] // lax.axis_size("tensor")
    return lax.dynamic_slice_in_dim(values, lax.axis_index("tensor") * part_rows, part_rows, 0)


def attn_scores(queries, key_rows, key_mask, split_shape):
    raw = jnp.einsum(
        "glhd,gmhd->ghlm",
        queries.reshape(split_shape),
        key_rows.reshape(split_shape),
        preferred_element_type=jnp.float32,
    ) * HEAD_DIM ** (-0.5)
    return jnp.where(key_mask[:, None, None, :], raw, masked_score)


def layer_forward(inputs, key_mask, weights):
    w_qkv, b_qv, w_out, w_up, b_up, w_down, norm_gain, bias_terms = weights
    groups, span = key_mask.shape
    row_count = inputs.shape[0]
    local_width = w_qkv.shape[2]
    split_shape = (groups, span, local_width // HEAD_DIM, HEAD_DIM)
    inputs_b = inputs.astype(jnp.bfloat16)
    projected = jnp.einsum("rd,cde->cre", inputs_b, w_qkv, preferred_element_type=jnp.float32)
    queries = (projected[0] + b_qv[0]).astype(jnp.bfloat16)
    key_rows = projected[1].astype(jnp.bfloat16)
    value_rows = (projected[2] + b_qv[1]).astype(jnp.bfloat16)
    scores = attn_scores(queries, key_rows, key_mask, split_shape)
    row_max = jnp.max(scores, axis=-1, keepdims=True)
    log_total = row_max + jnp.log(jnp.sum(jnp.exp(scores - row_max), axis=-1, keepdims=True))
    attn_probs = jnp.exp(scores - log_total).astype(jnp.bfloat16)
    head_out = jnp.einsum(
        "ghlm,gmhd->glhd",
        attn_probs,
        value_rows.reshape(split_shape),
        preferred_element_type=jnp.float32,
    )
    head_out = head_out.reshape(row_count, local_width).astype(jnp.bfloat16)
    attn_part = (
        lax.psum_scatter(
            jnp.dot(head_out, w_out, preferred_element_type=jnp.float32),
            "tensor",
            scatter_dimension=0,
            tiled=True,
        )
        + bias_terms[0]
    )
    resid_one = lax.all_gather(my_rows(inputs) + attn_part, "tensor", axis=0, tiled=True)
    hidden = norm_rows(resid_one, norm_gain[0], bias_terms[2])
    hidden_b = hidden.astype(jnp.bfloat16)
    pre_act = jnp.dot(hidden_b, w_up, preferred_element_type=jnp.float32) + b_up
    active_b = exact_gelu(pre_act).astype(jnp.bfloat16)
    mlp_part = (
        lax.psum_scatter(
            jnp.dot(active_b, w_down, preferred_element_type=jnp.float32),
            "tensor",
            scatter_dimension=0,
            tiled=True,
        )
        + bias_terms[1]
    )
    resid_two = lax.all_gather(my_rows(hidden) + mlp_part, "tensor", axis=0, tiled=True)
    stored = (
        inputs_b,
        queries,
        key_rows,
        value_rows,
        log_total,
        head_out,
        resid_one,
        hidden_b,
        pre_act,
        active_b,
        resid_two,
    )
    return (norm_rows(resid_two, norm_gain[1], bias_terms[3]), stored)


def layer_backward(grad_out, key_mask, weights, stored):
    w_qkv, b_qv, w_out, w_up, b_up, w_down, norm_gain, bias_terms = weights
    (
        inputs_b,
        queries,
        key_rows,
        value_rows,
        log_total,
        head_out,
        resid_one,
        hidden_b,
        pre_act,
        active_b,
        resid_two,
    ) = stored
    groups, span = key_mask.shape
    row_count, local_width = queries.shape
    split_shape = (groups, span, local_width // HEAD_DIM, HEAD_DIM)
    forward_two, norm_two = jax.vjp(norm_rows, resid_two, norm_gain[1], bias_terms[3])
    grad_two, gain_two, shift_two = norm_two(grad_out)
    grad_mlp = grad_two.astype(jnp.bfloat16)
    grad_wdown = jnp.dot(active_b.T, grad_mlp, preferred_element_type=jnp.float32)
    grad_act = jnp.dot(grad_mlp, w_down.T, preferred_element_type=jnp.float32)
    forward_gelu, gelu_back = jax.vjp(exact_gelu, pre_act)
    grad_pre = gelu_back(grad_act)[0].astype(jnp.bfloat16)
    grad_wup = jnp.dot(hidden_b.T, grad_pre, preferred_element_type=jnp.float32)
    up_part = lax.psum_scatter(
        jnp.dot(grad_pre, w_up.T, preferred_element_type=jnp.float32),
        "tensor",
        scatter_dimension=0,
        tiled=True,
    )
    grad_hidden = lax.all_gather(my_rows(grad_two) + up_part, "tensor", axis=0, tiled=True)
    forward_one, norm_one = jax.vjp(norm_rows, resid_one, norm_gain[0], bias_terms[2])
    grad_one, gain_one, shift_one = norm_one(grad_hidden)
    grad_attn = grad_one.astype(jnp.bfloat16)
    grad_wout = jnp.dot(head_out.T, grad_attn, preferred_element_type=jnp.float32)
    grad_heads = (
        jnp.dot(grad_attn, w_out.T, preferred_element_type=jnp.float32)
        .astype(jnp.bfloat16)
        .reshape(split_shape)
    )
    scores = attn_scores(queries, key_rows, key_mask, split_shape)
    attn_probs = jnp.exp(scores - log_total)
    grad_probs = jnp.einsum(
        "glhd,gmhd->ghlm",
        grad_heads,
        value_rows.reshape(split_shape),
        preferred_element_type=jnp.float32,
    )
    grad_values = jnp.einsum(
        "ghlm,glhd->gmhd",
        attn_probs.astype(jnp.bfloat16),
        grad_heads,
        preferred_element_type=jnp.float32,
    )
    grad_scores = (
        attn_probs * (grad_probs - jnp.sum(attn_probs * grad_probs, axis=-1, keepdims=True))
    ).astype(jnp.bfloat16)
    inv_root = HEAD_DIM ** (-0.5)
    grad_queries = (
        jnp.einsum(
            "ghlm,gmhd->glhd",
            grad_scores,
            key_rows.reshape(split_shape),
            preferred_element_type=jnp.float32,
        )
        * inv_root
    )
    grad_keys = (
        jnp.einsum(
            "ghlm,glhd->gmhd",
            grad_scores,
            queries.reshape(split_shape),
            preferred_element_type=jnp.float32,
        )
        * inv_root
    )
    grad_qkv = (
        jnp.stack([grad_queries, grad_keys, grad_values])
        .reshape(3, row_count, local_width)
        .astype(jnp.bfloat16)
    )
    grad_wqkv = jnp.einsum("rd,cre->cde", inputs_b, grad_qkv, preferred_element_type=jnp.float32)
    qkv_part = lax.psum_scatter(
        jnp.einsum("cre,cde->rd", grad_qkv, w_qkv, preferred_element_type=jnp.float32).astype(
            jnp.bfloat16
        ),
        "tensor",
        scatter_dimension=0,
        tiled=True,
    ).astype(jnp.float32)
    grad_inputs = lax.all_gather(
        (my_rows(grad_one) + qkv_part).astype(jnp.bfloat16), "tensor", axis=0, tiled=True
    ).astype(jnp.float32)
    grad_bqv = jnp.stack(
        [
            jnp.sum(grad_qkv[0].astype(jnp.float32), axis=0),
            jnp.sum(grad_qkv[2].astype(jnp.float32), axis=0),
        ]
    )
    grad_bup = jnp.sum(grad_pre.astype(jnp.float32), axis=0)
    grad_gain = jnp.stack([gain_one, gain_two])
    grad_shift = jnp.stack(
        [
            jnp.sum(grad_attn.astype(jnp.float32), axis=0),
            jnp.sum(grad_mlp.astype(jnp.float32), axis=0),
            shift_one,
            shift_two,
        ]
    )
    return (
        grad_inputs,
        (grad_wqkv, grad_bqv, grad_wout, grad_wup, grad_bup, grad_wdown, grad_gain, grad_shift),
    )


def deal_map(doc_ids, total_docs):
    return jnp.where(doc_ids % 2 == 1, (doc_ids + total_docs // 2) % total_docs, doc_ids)


def local_plan(seg_order, doc_lengths, seg_local, doc_local):
    total_docs = doc_lengths.shape[0]
    my_index = lax.axis_index("dp")
    doc_ids = jnp.arange(total_docs, dtype=jnp.int32)
    owner_pos = deal_map(doc_ids, total_docs)
    starts = jnp.sum((seg_order[None, :] < doc_ids[:, None]).astype(jnp.int32), axis=1)
    counts = jnp.sum((seg_order[None, :] == doc_ids[:, None]).astype(jnp.int32), axis=1)
    my_segments = my_index * seg_local + jnp.arange(seg_local, dtype=jnp.int32)
    seg_owner_doc = lax.dynamic_slice_in_dim(seg_order, my_index * seg_local, seg_local)
    seg_hot = seg_owner_doc[:, None] == doc_ids[None, :]
    my_start = jnp.sum(jnp.where(seg_hot, starts[None, :], 0), axis=1)
    my_length = jnp.sum(jnp.where(seg_hot, doc_lengths[None, :], 0), axis=1)
    my_owner = jnp.sum(jnp.where(seg_hot, owner_pos[None, :], 0), axis=1)
    within = my_segments - my_start
    valid_tokens = jnp.minimum(SEG, my_length - within * SEG)
    tok_mask = jnp.arange(SEG, dtype=jnp.int32)[None, :] < valid_tokens[:, None]
    src_slot = my_owner * MAXSEG + within
    my_deal = deal_map(my_index * doc_local + jnp.arange(doc_local, dtype=jnp.int32), total_docs)
    deal_hot = my_deal[:, None] == doc_ids[None, :]
    own_start = jnp.sum(jnp.where(deal_hot, starts[None, :], 0), axis=1)
    own_count = jnp.sum(jnp.where(deal_hot, counts[None, :], 0), axis=1)
    slot_index = jnp.arange(MAXSEG, dtype=jnp.int32)
    cross_mask = slot_index[None, :] < own_count[:, None]
    target = jnp.where(cross_mask, own_start[:, None] + slot_index[None, :], -1).reshape(-1)
    return (tok_mask, cross_mask, target, src_slot)


def picker(index_map, shard_rows):
    positions = jnp.arange(shard_rows.shape[0], dtype=jnp.int32)
    selector = (index_map[:, None] == positions[None, :]).astype(jnp.bfloat16)
    return jnp.dot(selector, shard_rows, preferred_element_type=jnp.float32)


def spreader(index_map, source_rows, row_span):
    positions = jnp.arange(row_span, dtype=jnp.int32)
    selector = (positions[:, None] == index_map[None, :]).astype(jnp.bfloat16)
    return jnp.dot(selector, source_rows, preferred_element_type=jnp.float32)


def add_terms(left, right):
    return jax.tree.map(jnp.add, left, right)


def local(
    tokens,
    seg_doc,
    doc_len,
    w_qkv,
    b_qv,
    w_out,
    w_up,
    b_up,
    w_down,
    norm_gain,
    bias_terms,
    seg_pos,
    cotangent,
):
    batches, local_rows, width = tokens.shape
    seg_local = local_rows // SEG
    doc_local = doc_len.shape[1] // lax.axis_size("dp")
    slot_rows = doc_local * MAXSEG

    def layer_weights(level):
        return (
            w_qkv[level],
            b_qv[level],
            w_out[level],
            w_up[level],
            b_up[level],
            w_down[level],
            norm_gain[level],
            bias_terms[level],
        )

    seg_weights = layer_weights(0)
    cross_weights = layer_weights(1)
    encoded = []
    grad_tokens = []
    seg_grads = []
    cross_grads = []
    pos_grads = []
    for batch_index in range(batches):
        tok_mask, cross_mask, target, src_slot = local_plan(
            seg_doc[batch_index], doc_len[batch_index], seg_local, doc_local
        )
        seg_out, seg_stored = layer_forward(
            tokens[batch_index].astype(jnp.float32), tok_mask, seg_weights
        )
        seg_cube = seg_out.reshape(seg_local, SEG, width)
        cls_rows = seg_cube[:, 0].astype(jnp.bfloat16)
        collected = picker(target, lax.all_gather(cls_rows, "dp", axis=0, tiled=True))
        cross_in = (collected.reshape(doc_local, MAXSEG, width) + seg_pos[None]).reshape(
            slot_rows, width
        )
        cross_out, cross_stored = layer_forward(cross_in, cross_mask, cross_weights)
        returned = picker(
            src_slot, lax.all_gather(cross_out.astype(jnp.bfloat16), "dp", axis=0, tiled=True)
        )
        encoded.append(
            seg_cube.at[:, 0].set(returned).reshape(local_rows, width).astype(jnp.bfloat16)
        )
        grad_cube = cotangent[batch_index].astype(jnp.float32).reshape(seg_local, SEG, width)
        grad_returned = grad_cube[:, 0].astype(jnp.bfloat16)
        grad_cross = lax.psum_scatter(
            spreader(src_slot, grad_returned, slot_rows * lax.axis_size("dp")),
            "dp",
            scatter_dimension=0,
            tiled=True,
        )
        grad_cross_in, cross_terms = layer_backward(
            grad_cross, cross_mask, cross_weights, cross_stored
        )
        pos_grads.append(jnp.sum(grad_cross_in.reshape(doc_local, MAXSEG, width), axis=0))
        grad_sent = grad_cross_in.astype(jnp.bfloat16)
        cross_grads.append(cross_terms)
        grad_cls = lax.psum_scatter(
            spreader(target, grad_sent, seg_local * lax.axis_size("dp")),
            "dp",
            scatter_dimension=0,
            tiled=True,
        )
        grad_seg = grad_cube.at[:, 0].set(grad_cls).reshape(local_rows, width)
        grad_inputs, seg_terms = layer_backward(grad_seg, tok_mask, seg_weights, seg_stored)
        grad_tokens.append(grad_inputs)
        seg_grads.append(seg_terms)
    seg_total = reduce(add_terms, seg_grads)
    cross_total = reduce(add_terms, cross_grads)
    pos_total = reduce(jnp.add, pos_grads)
    big_grads = (
        lax.psum_scatter(
            jnp.stack([seg_total[0], cross_total[0]]), "dp", scatter_dimension=2, tiled=True
        ),
        lax.psum_scatter(
            jnp.stack([seg_total[2], cross_total[2]]), "dp", scatter_dimension=2, tiled=True
        ),
        lax.psum_scatter(
            jnp.stack([seg_total[3], cross_total[3]]), "dp", scatter_dimension=1, tiled=True
        ),
        lax.psum_scatter(
            jnp.stack([seg_total[5], cross_total[5]]), "dp", scatter_dimension=2, tiled=True
        ),
    )
    small = lax.psum(
        (
            jnp.stack([seg_total[1], cross_total[1]]),
            jnp.stack([seg_total[4], cross_total[4]]),
            jnp.stack([seg_total[6], cross_total[6]]),
            jnp.stack([seg_total[7], cross_total[7]]),
            pos_total,
        ),
        "dp",
    )
    return (
        jnp.stack(encoded),
        jnp.stack(grad_tokens),
        big_grads[0],
        small[0],
        big_grads[1],
        big_grads[2],
        small[1],
        big_grads[3],
        small[2],
        small[3],
        small[4],
    )


BF = jnp.bfloat16
F32 = jnp.float32
D = 768
FF = 3072
HALF_FF = FF // 2
HALF_D = D // 2
CHUNK = 384
CHUNKS = 12
PAIRS = 6
MESH = pl.DeviceIdType.MESH
ROOT_HALF = 0.7071067811865476
PDF_SCALE = 0.3989422804014327


class Names:
    def __init__(self, **kw):
        self.__dict__.update(kw)


def mm(left, right):
    return jnp.dot(left, right, preferred_element_type=F32)


def mm_nt(left, right):
    return lax.dot_general(left, right, (((1,), (1,)), ((), ())), preferred_element_type=F32)


def span(index, size):
    return pl.ds(pl.multiple_of(index * size, size), size)


def row_norm(rows):
    centre = rows - jnp.mean(rows, axis=-1, keepdims=True)
    spread = jnp.mean(centre * centre, axis=-1, keepdims=True)
    scale = lax.rsqrt(spread + norm_eps)
    return centre * scale, scale


def stacked(pair, low_half):
    zero = jnp.zeros_like(pair)
    return jnp.concatenate(
        [jnp.where(low_half, pair, zero), jnp.where(low_half, zero, pair)], axis=0
    )


def soft_rows(scores):
    top = jnp.max(scores, axis=-1, keepdims=True)
    grown = jnp.exp(scores - top)
    return (grown * (1.0 / jnp.sum(grown, axis=-1, keepdims=True))).astype(BF)


def transpose_into(dest, source, rows):
    @pl.loop(0, rows // SEG)
    def _(s):
        dest[:, span(s, SEG)] = source[span(s, SEG), :].T


def core_forward(r, keep, ready, y_block):
    rows = r.xb.shape[0]
    ready("qkv")

    @pl.loop(0, 9)
    def _(i):
        c = lax.div(i, 3)
        cols = span(lax.rem(i, 3), 256)
        r.qkv[c, :, cols] = (mm(r.xb[...], r.wqkv[c, :, cols]) + r.b3[c, :, cols]).astype(BF)

    @pl.loop(0, rows // SEG)
    def _(s):
        at = span(s, SEG)
        live = keep(s)
        low_half = lax.broadcasted_iota(jnp.int32, (SEG, SEG), 1) < HEAD_DIM
        for p in range(PAIRS):
            cols = slice(p * SEG, p * SEG + SEG)
            keys = stacked(r.qkv[1, at, cols], low_half)
            vals = stacked(r.qkv[2, at, cols], low_half)
            raw = mm_nt(r.qkv[0, at, cols], keys) * HEAD_DIM ** (-0.5)
            one = soft_rows(jnp.where(live, raw[:, :SEG], masked_score))
            two = soft_rows(jnp.where(live, raw[:, SEG:], masked_score))
            both = jnp.concatenate([one, two], axis=1)
            r.p[s, p] = both
            r.o[at, cols] = mm(both, vals).astype(BF)

    ready("out")

    @pl.loop(0, 3)
    def _(n):
        cols = span(n, 256)
        r.xh1[:, cols] = mm(r.o[...], r.wout[:, cols]) + r.bt[0, :, cols]

    @pl.loop(0, rows // 64)
    def _(s):
        at = span(s, 64)
        hat, scale = row_norm(r.x_rows(at) + r.xh1[at, :])
        r.xh1[at, :] = hat
        r.rs1[at, :] = jnp.broadcast_to(scale, (64, SEG))
        hidden = hat * r.gain[0] + r.bt[2]
        r.h1[at, :] = hidden
        r.h1b[at, :] = hidden.astype(BF)

    ready("up")

    @pl.loop(0, 12)
    def _(j):
        cols = span(j, 256)
        for b in range(rows // SEG):
            at = slice(b * SEG, b * SEG + SEG)
            u = mm(r.h1b[at, :], r.wup[:, cols]) + r.bup[:, cols]
            cdf = 0.5 * (1.0 + lax.erf(u * ROOT_HALF))
            r.g[at, cols] = (u * cdf).astype(BF)
            r.gp[at, cols] = (cdf + u * (PDF_SCALE * jnp.exp(-0.5 * u * u))).astype(BF)

    transpose_into(r.h1t, r.h1b, rows)
    ready("down")

    @pl.loop(0, 3)
    def _(n):
        cols = span(n, 256)
        r.xh2[:, cols] = r.h1[:, cols] + mm(r.g[...], r.wdown[:, cols]) + r.bt[1, :, cols]

    @pl.loop(0, rows // 64)
    def _(s):
        at = span(s, 64)
        hat, scale = row_norm(r.xh2[at, :])
        r.xh2[at, :] = hat
        r.rs2[at, :] = jnp.broadcast_to(scale, (64, SEG))
        y_block(at, hat * r.gain[1] + r.bt[3])


def norm_back(grad, hat, scale, gain):
    d_hat = grad * gain
    first = jnp.mean(d_hat, axis=-1, keepdims=True)
    second = jnp.mean(d_hat * hat, axis=-1, keepdims=True)
    return (d_hat - first - hat * second) * scale


def norm_back_rows(r, rows, hat_ref, scale_ref, gain, grad_of):
    zero = jnp.zeros((1, D), F32)

    def step(s, sums):
        at = span(s, 64)
        grad = grad_of(s, at)
        hat = hat_ref[at, :]
        out = norm_back(grad, hat, scale_ref[at, 0:1], gain)
        low = out.astype(BF)
        r.dr[at, :] = out
        r.dm[at, :] = low
        return (
            sums[0] + jnp.sum(grad * hat, axis=0, keepdims=True),
            sums[1] + jnp.sum(grad, axis=0, keepdims=True),
            sums[2] + jnp.sum(low.astype(F32), axis=0, keepdims=True),
        )

    sums = lax.fori_loop(0, rows // 64, step, (zero, zero, zero))
    transpose_into(r.dmt, r.dm, rows)
    return sums


def core_backward(r, grad_of, ready, hooks):
    rows = r.dr.shape[0]
    ready("norm2")
    sums = norm_back_rows(r, rows, r.xh2, r.rs2, r.gain[1], grad_of)
    r.small_common[1], r.small_common[5], r.small_common[3] = sums
    ready("down")
    hooks("down")

    @pl.loop(0, 12)
    def _(j):
        cols = span(j, 256)
        total = jnp.zeros((1, 256), F32)
        for b in range(rows // SEG):
            at = slice(b * SEG, b * SEG + SEG)
            du = (mm_nt(r.dm[at, :], r.wdown[cols, :]) * r.gp[at, cols].astype(F32)).astype(BF)
            r.gp[at, cols] = du
            total = total + jnp.sum(du.astype(F32), axis=0, keepdims=True)
        r.bup_sum[:, cols] = total

    hooks("up")
    ready("up")

    @pl.loop(0, 3)
    def _(n):
        cols = span(n, 256)
        r.dr[:, cols] = r.dr[:, cols] + mm_nt(r.gp[...], r.wup[cols, :])

    ready("norm1")
    sums = norm_back_rows(r, rows, r.xh1, r.rs1, r.gain[0], lambda s, at: r.dr[at, :])
    r.small_common[0], r.small_common[4], r.small_common[2] = sums
    ready("out")
    hooks("out")

    @pl.loop(0, 3)
    def _(n):
        cols = span(n, 256)
        r.o[:, cols] = mm_nt(r.dm[...], r.wout[cols, :]).astype(BF)

    ready("attn")

    @pl.loop(0, rows // SEG)
    def _(s):
        at = span(s, SEG)
        low_half = lax.broadcasted_iota(jnp.int32, (SEG, SEG), 1) < HEAD_DIM
        scale = HEAD_DIM ** (-0.5)
        for p in range(PAIRS):
            cols = slice(p * SEG, p * SEG + SEG)
            query = r.qkv[0, at, cols]
            keys = stacked(r.qkv[1, at, cols], low_half)
            vals = stacked(r.qkv[2, at, cols], low_half)
            d_head = r.o[at, cols]
            probs = r.p[s, p]
            d_probs = mm_nt(d_head, vals)
            d_vals = mm(probs.T, d_head)
            wide = probs.astype(F32)
            prod = wide * d_probs
            parts = []
            for h in range(2):
                own = slice(h * SEG, h * SEG + SEG)
                parts.append(
                    prod[:, own]
                    - wide[:, own] * jnp.sum(prod[:, own], axis=-1, keepdims=True)
                )
            d_scores = jnp.concatenate(parts, axis=1).astype(BF)
            d_keys = mm(d_scores.T, query) * scale
            r.qkv[0, at, cols] = (mm(d_scores, keys) * scale).astype(BF)
            r.qkv[1, at, cols] = jnp.where(low_half, d_keys[:SEG], d_keys[SEG:]).astype(BF)
            r.qkv[2, at, cols] = jnp.where(low_half, d_vals[:SEG], d_vals[SEG:]).astype(BF)

    for c in (0, 2):
        r.qv_sum[c // 2] = jnp.sum(r.qkv[c].astype(F32), axis=0, keepdims=True)
    ready("qkv")
    hooks("qkv")

    @pl.loop(0, 3)
    def _(n):
        cols = span(n, 256)
        total = r.dr[:, cols]
        for c in range(3):
            total = total + mm_nt(r.qkv[c], r.wqkv[c, cols, :])
        r.dr[:, cols] = total


def chunk_operands(r, c):
    if c < 4:
        return r.dmt, (r.g, c * CHUNK, HALF_FF + c * CHUNK)
    if c < 8:
        return r.h1t, (r.gp, (c - 4) * CHUNK, HALF_FF + (c - 4) * CHUNK)
    if c == 8:
        return r.dmt, (r.o, 0, HALF_D)
    return r.xt, (r.qkv.at[c - 9], 0, HALF_D)


HOOK_CHUNKS = {"down": (0, 4), "up": (4, 8), "out": (8, 9), "qkv": (9, 12)}


class Copies:
    def __init__(self, sems):
        self.sems = sems
        self.used = 0

    def start(self, source, dest):
        copy = pltpu.make_async_copy(source, dest, self.sems.at[self.used])
        self.used += 1
        copy.start()
        return copy


def place():
    return lax.axis_index("dp"), lax.axis_index("tensor")


def remote(source, dest, send_sem, recv_sem, device):
    return pltpu.make_async_remote_copy(
        src_ref=source,
        dst_ref=dest,
        send_sem=send_sem,
        recv_sem=recv_sem,
        device_id=device,
        device_id_type=MESH,
    )


def greet(devices):
    barrier = pltpu.get_barrier_semaphore()
    for device in devices:
        pl.semaphore_signal(barrier, inc=1, device_id=device, device_id_type=MESH)
    return barrier


def load_half(copies, r, half, layer, wqkv, wout, wup, wdown, which):
    if which == "qkv":
        return copies.start(wqkv.at[layer], r.wqkv.at[:, :, half * HALF_D : (half + 1) * HALF_D])
    if which == "out":
        return copies.start(wout.at[layer], r.wout.at[half * HALF_D : (half + 1) * HALF_D, :])
    if which == "up":
        return copies.start(wup.at[layer], r.wup.at[:, half * HALF_FF : (half + 1) * HALF_FF])
    return copies.start(wdown.at[layer], r.wdown.at[half * HALF_FF : (half + 1) * HALF_FF, :])


def fill_bias(r, half, packed, layer):
    lanes = slice(half * HALF_D, (half + 1) * HALF_D)
    r.b3[0, :, lanes] = packed[layer, :, 0:HALF_D]
    r.b3[1, :, lanes] = jnp.zeros((1, HALF_D), F32)
    r.b3[2, :, lanes] = packed[layer, :, HALF_D : 2 * HALF_D]
    r.bup[:, half * HALF_FF : (half + 1) * HALF_FF] = packed[layer, :, 2 * HALF_D :]


WEIGHT_SCRATCH = dict(
    wqkv=((3, D, D), BF), wout=((D, D), BF), wup=((D, FF), BF), wdown=((FF, D), BF)
)
PACK = 2 * HALF_D + HALF_FF


def saved_shapes(rows):
    return dict(
        xt=((D, rows), BF),
        h1t=((D, rows), BF),
        qkv=((3, rows, D), BF),
        o=((rows, D), BF),
        p=((rows // SEG, PAIRS, SEG, 2 * SEG), BF),
        xh1=((rows, D), F32),
        rs1=((rows, SEG), F32),
        g=((rows, FF), BF),
        gp=((rows, FF), BF),
        xh2=((rows, D), F32),
        rs2=((rows, SEG), F32),
    )


def forward_shapes(rows):
    return dict(
        xb=((rows, D), BF),
        h1=((rows, D), F32),
        h1b=((rows, D), BF),
        b3=((3, 1, D), F32),
        bup=((1, FF), F32),
    )


def vmem(table):
    return [pltpu.VMEM(shape, kind) for shape, kind in table.values()]


def arrays(table):
    return [jax.ShapeDtypeStruct(shape, kind) for shape, kind in table.values()]


def first_kernel(dp, names, *refs):
    r = Names(**dict(zip(names, refs)))
    r.__dict__.update({k: getattr(r, "v_" + k) for k in saved_shapes(SEG)})
    d, t = place()
    sibling = (d, 1 - t)
    rows = r.xb.shape[0]
    segs = rows // SEG
    barrier = greet([sibling] + [(lax.rem(d + o, dp), t) for o in range(1, dp)])
    copies = Copies(r.local_sem)
    own = (r.a_wqkv, r.a_wout, r.a_wup, r.a_wdown)
    other = (r.x_wqkv, r.x_wout, r.x_wup, r.x_wdown)
    load_x = copies.start(r.tokens.at[t], r.xb)
    loads = {w: load_half(copies, r, 0, 0, *own, w) for w in ("qkv", "out", "up", "down")}
    firsts = [copies.start(r.cot.at[t, pl.ds(s * SEG, 16)], r.cot_first.at[s]) for s in range(segs)]
    pl.semaphore_wait(barrier, dp)
    swaps = {}

    def swap(layer, k):
        swaps[layer, k] = remote(
            own[k].at[layer], other[k].at[layer], r.w_send.at[layer, k], r.w_recv.at[layer, k], sibling
        )
        swaps[layer, k].start()

    swap(0, 0)
    swap_bias = remote(r.packed, r.x_packed, r.w_send.at[0, 4], r.w_recv.at[0, 4], sibling)
    swap_bias.start()
    swap(0, 1)
    for copy in firsts:
        copy.wait()

    def gather(own_rows, everyone, send, recv):
        everyone[d] = own_rows
        sends = []
        for o in range(1, dp):
            copy = remote(
                everyone.at[d], everyone.at[d], send.at[o], recv.at[d], (lax.rem(d + o, dp), t)
            )
            copy.start()
            sends.append(copy)
        return sends

    def arrived(everyone, send, recv):
        for o in range(1, dp):
            source = lax.rem(d + o, dp)
            remote(everyone.at[source], everyone.at[source], send.at[o], recv.at[source], (source, t)).wait_recv()

    cot_rows = jnp.concatenate([r.cot_first[s].astype(F32)[0:1] for s in range(segs)], axis=0)
    sends = gather(cot_rows.astype(BF), r.cot_all, r.cot_send, r.cot_recv)

    def ready(phase):
        if phase == "qkv":
            load_x.wait()
            transpose_into(r.xt, r.xb, rows)
            fill_bias(r, 0, r.packed, 0)
            loads["qkv"].wait()
            swaps[0, 0].wait_recv()
            more = load_half(copies, r, 1, 0, *other, "qkv")
            swap(0, 2)
            swap(0, 3)
            swap_bias.wait_recv()
            fill_bias(r, 1, r.x_packed, 0)
            more.wait()
        else:
            k = {"out": 1, "up": 2, "down": 3}[phase]
            swaps[0, k].wait_recv()
            more = load_half(copies, r, 1, 0, *other, phase)
            if phase == "out":
                for w in range(4):
                    swap(1, w)
            loads[phase].wait()
            more.wait()

    def keep(s):
        seg = d * segs + s
        doc = r.seg_doc[t, seg]
        within = jnp.int32(0)
        for back in range(1, MAXSEG):
            same = r.seg_doc[t, jnp.maximum(seg - back, 0)] == doc
            within = within + jnp.where(jnp.logical_and(seg >= back, same), 1, 0)
        valid = jnp.minimum(SEG, r.doc_len[t, doc] - SEG * within)
        return lax.broadcasted_iota(jnp.int32, (1, SEG), 1) < valid

    r.x_rows = lambda at: r.xb[at, :].astype(F32)

    def y_block(at, values):
        r.v_y1[at, :] = values.astype(BF)

    core_forward(r, keep, ready, y_block)
    cls = jnp.concatenate(
        [r.v_y1[s * SEG : s * SEG + 16, :].astype(F32)[0:1] for s in range(segs)], axis=0
    )
    sends += gather(cls.astype(BF), r.cls_all, r.cls_send, r.cls_recv)
    outs = [copies.start(getattr(r, "v_" + k), getattr(r, "o_" + k)) for k in list(saved_shapes(SEG)) + ["y1"]]
    outs.append(copies.start(r.x_packed, r.o_packed))
    arrived(r.cot_all, r.cot_send, r.cot_recv)
    outs.append(copies.start(r.cot_all, r.o_cot))
    arrived(r.cls_all, r.cls_send, r.cls_recv)
    outs.append(copies.start(r.cls_all, r.o_cls))
    for copy in sends:
        copy.wait_send()
    swap_bias.wait_send()
    for (layer, k), copy in swaps.items():
        copy.wait_send()
        if layer == 1:
            copy.wait_recv()
    for copy in outs:
        copy.wait()


def run_first(dp, rows, seg_doc, doc_len, tokens, cot, packed, gain, terms, wqkv, wout, wup, wdown):
    hbm = pl.BlockSpec(memory_space=pl.ANY)
    smem = pl.BlockSpec(memory_space=pltpu.SMEM)
    small = pl.BlockSpec(memory_space=pltpu.VMEM)
    segs = rows // SEG
    saved = saved_shapes(rows)
    outs = dict(
        x_wqkv=(wqkv.shape, BF),
        x_wout=(wout.shape, BF),
        x_wup=(wup.shape, BF),
        x_wdown=(wdown.shape, BF),
        o_packed=(packed.shape, F32),
        o_cls=((dp, segs, D), BF),
        o_cot=((dp, segs, D), BF),
        o_y1=((rows, D), BF),
    )
    outs.update({"o_" + k: v for k, v in saved.items()})
    scratch = {"v_" + k: v for k, v in saved.items()}
    scratch["v_y1"] = ((rows, D), BF)
    scratch.update(WEIGHT_SCRATCH)
    scratch.update(forward_shapes(rows))
    scratch.update(
        x_packed=(packed.shape, F32),
        cls_all=((dp, segs, D), BF),
        cot_all=((dp, segs, D), BF),
        cot_first=((segs, 16, D), BF),
    )
    sems = dict(
        local_sem=pltpu.SemaphoreType.DMA((40,)),
        w_send=pltpu.SemaphoreType.DMA((2, 5)),
        w_recv=pltpu.SemaphoreType.DMA((2, 5)),
        cot_send=pltpu.SemaphoreType.DMA((dp,)),
        cot_recv=pltpu.SemaphoreType.DMA((dp,)),
        cls_send=pltpu.SemaphoreType.DMA((dp,)),
        cls_recv=pltpu.SemaphoreType.DMA((dp,)),
    )
    ins = ["seg_doc", "doc_len", "tokens", "cot", "packed", "gain", "bt", "a_wqkv", "a_wout", "a_wup", "a_wdown"]
    names = ins + list(outs) + list(scratch) + list(sems)
    result = pl.pallas_call(
        partial(first_kernel, dp, names),
        out_shape=arrays(outs),
        in_specs=[smem, smem, hbm, hbm, small, small, small, hbm, hbm, hbm, hbm],
        out_specs=[hbm] * len(outs),
        scratch_shapes=vmem(scratch) + list(sems.values()),
        compiler_params=pltpu.CompilerParams(
            collective_id=0, has_side_effects=True, vmem_limit_bytes=60 << 20
        ),
        name="segment_forward",
    )(seg_doc, doc_len, tokens, cot, packed, gain, terms, wqkv, wout, wup, wdown)
    return dict(zip(outs, result))


def cross_kernel(segs, names, *refs):
    r = Names(**dict(zip(names, refs)))
    d, t = place()
    total_segs = r.cls.shape[0]
    slots = r.dr.shape[0]
    total_docs = slots // MAXSEG
    copies = Copies(r.local_sem)
    own = (r.a_wqkv, r.a_wout, r.a_wup, r.a_wdown)
    other = (r.x_wqkv, r.x_wout, r.x_wup, r.x_wdown)
    loads = {}
    for which in ("qkv", "out", "up", "down"):
        loads[which] = [
            load_half(copies, r, half, 1, *source, which) for half, source in enumerate((own, other))
        ]

    def ready(phase):
        for copy in loads.pop(phase, ()):
            copy.wait()

    fill_bias(r, 0, r.packed, 1)
    fill_bias(r, 1, r.x_packed, 1)

    doc_row = jnp.broadcast_to(r.seg_doc[t], (total_segs, total_segs))
    below = lax.broadcasted_iota(jnp.int32, (total_segs, total_segs), 0)
    across = lax.broadcasted_iota(jnp.int32, (total_segs, total_segs), 1)
    doc_col = jnp.sum(jnp.where(below == across, doc_row, 0).astype(F32), axis=1, keepdims=True)
    earlier = jnp.logical_and(doc_col == doc_row.astype(F32), below < across)
    within = jnp.sum(jnp.where(earlier, 1.0, 0.0), axis=0, keepdims=True).astype(jnp.int32)
    doc = r.seg_doc[t]
    moved = doc + total_docs // 2
    moved = jnp.where(moved >= total_docs, moved - total_docs, moved)
    slot_of = jnp.where((doc & 1) == 1, moved, doc) * MAXSEG + within
    slot_ids = lax.broadcasted_iota(jnp.int32, (slots, total_segs), 0)
    deal = jnp.where(slot_ids == slot_of, 1.0, 0.0).astype(BF)
    pick_row = lax.broadcasted_iota(jnp.int32, (8, total_segs), 0)
    pick_seg = lax.broadcasted_iota(jnp.int32, (8, total_segs), 1)
    pick = jnp.where(
        jnp.logical_and(pick_row < segs, pick_seg == d * segs + pick_row), 1.0, 0.0
    ).astype(BF)
    back = mm_nt(pick, deal).astype(BF)
    live = mm_nt(jnp.ones((8, total_segs), BF), deal)[0:1] > 0.5
    key_doc = lax.broadcasted_iota(jnp.int32, (SEG, SEG), 1) >> 3
    row_doc = lax.broadcasted_iota(jnp.int32, (SEG, SEG), 0) >> 3
    allowed = jnp.logical_and(key_doc == row_doc, live)

    r.x32[...] = mm(deal, r.cls[...]) + jnp.concatenate([r.pos[...]] * total_docs, axis=0)
    r.xb[...] = r.x32[...].astype(BF)
    r.dy[...] = mm(deal, r.cot[...])
    r.x_rows = lambda at: r.x32[at, :]
    transpose_into(r.xt, r.xb, slots)

    def y_block(at, values):
        r.yb[at, :] = values.astype(BF)

    core_forward(r, lambda s: allowed, ready, y_block)
    r.ret[...] = mm(back, r.yb[...])
    shard = D // r.dp

    def hooks(name):
        low, high = HOOK_CHUNKS[name]
        for c in range(low, high):
            left, (right, own_at, other_at) = chunk_operands(r, c)
            mine = left[pl.ds(pl.multiple_of(d * shard, 16), shard), :]
            r.shard[0, c] = mm(mine, right[:, own_at : own_at + CHUNK])
            r.shard[1, c] = mm(mine, right[:, other_at : other_at + CHUNK])

    r.small_common = r.small
    core_backward(r, lambda s, at: r.dy[at, :], ready, hooks)
    pack_halves(r)
    low = r.dr[...].astype(BF)
    r.dc[...] = mm(back, low)
    total = r.dr[0:MAXSEG, :]
    for j in range(1, total_docs):
        total = total + r.dr[j * MAXSEG : (j + 1) * MAXSEG, :]
    r.d_pos[...] = total


def pack_halves(r):
    for half in range(2):
        at = 6 + 3 * half
        lanes = slice(half * HALF_D, (half + 1) * HALF_D)
        r.small[at, :, 0:HALF_D] = r.qv_sum[0, :, lanes]
        r.small[at, :, HALF_D:] = r.qv_sum[1, :, lanes]
        base = half * HALF_FF
        r.small[at + 1] = r.bup_sum[:, base : base + D]
        r.small[at + 2] = r.bup_sum[:, base + D : base + 2 * D]


BACK_SCRATCH = dict(qv_sum=((2, 1, D), F32), bup_sum=((1, FF), F32))


def run_cross(dp, segs, slots, seg_doc, cls, cot, pos, packed, x_packed, gain, terms, own, other):
    hbm = pl.BlockSpec(memory_space=pl.ANY)
    small = pl.BlockSpec(memory_space=pltpu.VMEM)
    outs = dict(
        ret=((8, D), F32),
        dc=((8, D), F32),
        d_pos=((MAXSEG, D), F32),
        small=((12, 1, D), F32),
        shard=((2, CHUNKS, D // dp, CHUNK), F32),
    )
    scratch = dict(saved_shapes(slots))
    scratch.update(WEIGHT_SCRATCH)
    scratch.update(forward_shapes(slots))
    scratch.update(BACK_SCRATCH)
    scratch.update(
        x32=((slots, D), F32),
        dy=((slots, D), F32),
        yb=((slots, D), BF),
        dr=((slots, D), F32),
        dm=((slots, D), BF),
        dmt=((D, slots), BF),
    )
    ins = ["seg_doc", "cls", "cot", "pos", "packed", "x_packed", "gain", "bt"]
    ins += ["a_wqkv", "a_wout", "a_wup", "a_wdown", "x_wqkv", "x_wout", "x_wup", "x_wdown"]
    names = ins + list(outs) + list(scratch) + ["local_sem"]

    def kernel(*refs):
        cross_kernel_with(dp, segs, names, *refs)

    result = pl.pallas_call(
        kernel,
        out_shape=arrays(outs),
        in_specs=[small] * 8 + [hbm] * 8,
        out_specs=[small] * len(outs),
        scratch_shapes=vmem(scratch) + [pltpu.SemaphoreType.DMA((8,))],
        compiler_params=pltpu.CompilerParams(vmem_limit_bytes=60 << 20),
        name="document_layer",
    )(seg_doc, cls, cot, pos, packed, x_packed, gain, terms, *own, *other)
    return dict(zip(outs, result))


def cross_kernel_with(dp, segs, names, *refs):
    cross_kernel(segs, names + ["dp"], *refs, dp)


SLOTS = 4


def last_kernel(dp, names, *refs):
    r = Names(**dict(zip(names, refs)))
    d, t = place()
    x, y, z = lax.rem(d, 2), lax.rem(lax.div(d, 2), 2), lax.div(d, 4)
    zs = dp // 4
    sibling = (d, 1 - t)

    def chip(x_at, y_at, z_at):
        return (z_at * 4 + y_at * 2 + x_at, t)

    x_peer, y_peer = chip(1 - x, y, z), chip(x, 1 - y, z)
    z_peers = [chip(x, y, lax.rem(z + o, zs)) for o in range(1, zs)]
    barrier = greet([sibling, x_peer, y_peer] + z_peers)
    copies = Copies(r.local_sem)
    own = (r.a_wqkv, r.a_wout, r.a_wup, r.a_wdown)
    other = (r.x_wqkv, r.x_wout, r.x_wup, r.x_wdown)
    loads = {}

    def load(phase, *keys):
        loads.setdefault(phase, []).extend(
            copies.start(getattr(r, "i_" + k), getattr(r, k)) for k in keys
        )

    def load_weight(phase, which):
        for half, source in enumerate((own, other)):
            loads.setdefault(phase, []).append(load_half(copies, r, half, 0, *source, which))

    loads["norm2"] = [copies.start(r.i_cot.at[t], r.cot)]
    load("norm2", "xh2", "rs2")
    load("down", "g")
    load_weight("down", "down")
    load("down", "gp", "h1t")
    load_weight("up", "up")
    load("norm1", "xh1", "rs1")
    load("out", "o")
    load_weight("out", "out")
    load("attn", "qkv", "p")
    load("qkv", "xt")
    load_weight("qkv", "qkv")
    load("enc", "y1")
    load("shard", "shard1")

    def ready(phase):
        for copy in loads.pop(phase, ()):
            copy.wait()

    pl.semaphore_wait(barrier, zs + 2)
    shard_swap = remote(r.i_shard1.at[1], r.shard_in, r.misc_send.at[0], r.misc_recv.at[0], sibling)
    shard_swap.start()
    small1_swap = [
        remote(r.small1.at[0:6], r.small1_in.at[0:6], r.misc_send.at[1], r.misc_recv.at[1], sibling),
        remote(r.small1.at[9:20], r.small1_in.at[6:17], r.misc_send.at[2], r.misc_recv.at[2], sibling),
    ]
    for copy in small1_swap:
        copy.start()

    first_row = lax.broadcasted_iota(jnp.int32, (64, 1), 0)

    def with_first(values, s, table):
        row = first_row + 64 * lax.rem(s, 2)
        return jnp.where(row == 0, table[lax.div(s, 2)], values)

    def sib_copy(c):
        slot = lax.rem(c, SLOTS)
        return remote(
            r.sib_out.at[slot], r.sib_in.at[slot], r.sib_send.at[slot], r.sib_recv.at[slot], sibling
        )

    def stage_one(c, even):
        source = r.gbuf.at[c, :, :, 1 - x] if even else r.gbuf.at[c, :, 1 - y]
        return remote(source, r.one_in.at[c], r.one_send.at[c], r.one_recv.at[c], x_peer if even else y_peer)

    def stage_two(c, even):
        source = r.gbuf.at[c, :, 1 - y, x] if even else r.gbuf.at[c, :, y, 1 - x]
        return remote(source, r.two_in.at[c], r.two_send.at[c], r.two_recv.at[c], y_peer if even else x_peer)

    def stage_three(c, o):
        return remote(
            r.gbuf.at[c, lax.rem(z + o, zs), y, x],
            r.three_in.at[c, o - 1],
            r.three_send.at[c, o - 1],
            r.three_recv.at[c, o - 1],
            z_peers[o - 1],
        )

    def by_parity(c, act):
        @pl.when(lax.rem(c, 2) == 0)
        def _():
            act(True)

        @pl.when(lax.rem(c, 2) == 1)
        def _():
            act(False)

    def progress(c):
        sib_copy(c).wait_recv()
        slot = lax.rem(c, SLOTS)
        r.gbuf[c] = r.gbuf[c] + r.sib_in[slot].reshape(zs, 2, 2, D // dp, CHUNK)

        @pl.when(c < CHUNKS - SLOTS)
        def _():
            pl.semaphore_signal(r.credit, inc=1, device_id=sibling, device_id_type=MESH)

        by_parity(c, lambda even: stage_one(c, even).start())

    def emit(c, left, right, own_at, other_at):
        @pl.when(c >= SLOTS)
        def _():
            sib_copy(c).wait_send()
            pl.semaphore_wait(r.credit, 1)

        slot = lax.rem(c, SLOTS)
        r.sib_out[slot] = mm(left[...], right[:, pl.ds(other_at, CHUNK)]).astype(BF)
        sib_copy(c).start()
        mine = mm(left[...], right[:, pl.ds(own_at, CHUNK)]).astype(BF)
        r.gbuf[c] = mine.reshape(zs, 2, 2, D // dp, CHUNK)

        @pl.when(c >= 1)
        def _():
            progress(c - 1)

    def hooks(name):
        low, high = HOOK_CHUNKS[name]
        if name == "out":
            emit(jnp.int32(8), r.dmt, r.o, 0, HALF_D)
            return

        @pl.loop(low, high)
        def _(c):
            if name == "qkv":
                emit(c, r.xt, r.qkv.at[c - low], 0, HALF_D)
            else:
                base = pl.multiple_of((c - low) * CHUNK, 128)
                left, right = (r.dmt, r.g) if name == "down" else (r.h1t, r.gp)
                emit(c, left, right, base, pl.multiple_of(base + HALF_FF, 128))

    r.small_common = r.small
    core_backward(
        r, lambda s, at: with_first(r.cot[at, :].astype(F32), s, r.dc), ready, hooks
    )
    progress(jnp.int32(CHUNKS - 1))
    pack_halves(r)
    small_swap = [
        remote(r.small.at[0:6], r.small_in.at[0:6], r.misc_send.at[3], r.misc_recv.at[3], sibling),
        remote(r.small.at[9:12], r.small_in.at[6:9], r.misc_send.at[4], r.misc_recv.at[4], sibling),
    ]
    for copy in small_swap:
        copy.start()
    grad_swap = remote(r.dr, r.o_grad.at[t], r.misc_send.at[5], r.misc_recv.at[5], sibling)
    grad_swap.start()
    outs = [copies.start(r.dr, r.o_grad.at[t])]
    ready("enc")

    @pl.loop(0, r.y1.shape[0] // 64)
    def _(s):
        at = span(s, 64)
        r.y1[at, :] = with_first(r.y1[at, :].astype(F32), s, r.ret).astype(BF)

    enc_swap = remote(r.y1, r.o_enc.at[t], r.misc_send.at[6], r.misc_recv.at[6], sibling)
    enc_swap.start()
    outs.append(copies.start(r.y1, r.o_enc.at[t]))
    for copy in small_swap:
        copy.wait()
    r.total[...] = r.small[0:9] + r.small_in[...]
    x_small = remote(r.total, r.x_small, r.misc_send.at[7], r.misc_recv.at[7], x_peer)
    x_small.start()

    @pl.loop(0, CHUNKS)
    def _(c):
        def act(even):
            stage_one(c, even).wait_recv()
            if even:
                r.gbuf[c, :, :, x] = r.gbuf[c, :, :, x] + r.one_in[c]
            else:
                r.gbuf[c, :, y] = r.gbuf[c, :, y] + r.one_in[c]
            stage_two(c, even).start()

        by_parity(c, act)

    x_small.wait()
    r.total_x[...] = r.total[...] + r.x_small[...]
    y_small = remote(r.total_x, r.y_small, r.misc_send.at[8], r.misc_recv.at[8], y_peer)
    y_small.start()

    @pl.loop(0, CHUNKS)
    def _(c):
        by_parity(c, lambda even: stage_two(c, even).wait_recv())
        r.gbuf[c, :, y, x] = r.gbuf[c, :, y, x] + r.two_in[c]
        for o in range(1, zs):
            stage_three(c, o).start()

    y_small.wait()
    r.z_small[z] = r.total_x[...] + r.y_small[...]
    z_sends = []
    for o in range(1, zs):
        z_sends.append(
            remote(r.z_small.at[z], r.z_small.at[z], r.z_send.at[o], r.z_recv.at[z], z_peers[o - 1])
        )
        z_sends[-1].start()
    ready("shard")
    shard_swap.wait()
    for copy in small1_swap:
        copy.wait()
    r.o_shard[1] = r.shard1[0] + r.shard_in[...]
    r.o_small[9:26] = jnp.concatenate([r.small1[0:9], r.small1[12:20]], axis=0) + r.small1_in[...]

    @pl.loop(0, CHUNKS)
    def _(c):
        total = r.gbuf[c, z, y, x].astype(F32)
        for o in range(1, zs):
            stage_three(c, o).wait_recv()
            total = total + r.three_in[c, o - 1].astype(F32)
        r.o_shard[0, c] = total

    for o in range(1, zs):
        source = lax.rem(z + o, zs)
        remote(r.z_small.at[source], r.z_small.at[source], r.z_send.at[o], r.z_recv.at[source], z_peers[o - 1]).wait_recv()
    total = r.z_small[0]
    for k in range(1, zs):
        total = total + r.z_small[k]
    r.o_small[0:9] = total

    for copy in z_sends:
        copy.wait_send()

    @pl.loop(0, CHUNKS)
    def _(c):
        def act(even):
            stage_one(c, even).wait_send()
            stage_two(c, even).wait_send()

        by_parity(c, act)
        for o in range(1, zs):
            stage_three(c, o).wait_send()

    for c in range(CHUNKS - SLOTS, CHUNKS):
        sib_copy(jnp.int32(c)).wait_send()
    grad_swap.wait()
    enc_swap.wait()
    for copy in outs:
        copy.wait()


def run_last(dp, rows, batches, cot, gain, dc, ret, small1, shard1, y1, saved, own, other):
    hbm = pl.BlockSpec(memory_space=pl.ANY)
    small = pl.BlockSpec(memory_space=pltpu.VMEM)
    zs = dp // 4
    shard = D // dp
    outs = dict(
        o_grad=((batches, rows, D), F32),
        o_enc=((batches, rows, D), BF),
        o_shard=((2, CHUNKS, shard, CHUNK), F32),
        o_small=((26, 1, D), F32),
    )
    scratch = dict(saved_shapes(rows))
    scratch.update(WEIGHT_SCRATCH)
    scratch.update(BACK_SCRATCH)
    scratch.update(
        y1=((rows, D), BF),
        cot=((rows, D), BF),
        dr=((rows, D), F32),
        dm=((rows, D), BF),
        dmt=((D, rows), BF),
        small=((12, 1, D), F32),
        small_in=((9, 1, D), F32),
        small1_in=((17, 1, D), F32),
        total=((9, 1, D), F32),
        total_x=((9, 1, D), F32),
        x_small=((9, 1, D), F32),
        y_small=((9, 1, D), F32),
        z_small=((zs, 9, 1, D), F32),
        shard1=((2, CHUNKS, shard, CHUNK), F32),
        shard_in=((CHUNKS, shard, CHUNK), F32),
        gbuf=((CHUNKS, zs, 2, 2, shard, CHUNK), BF),
        sib_out=((SLOTS, D, CHUNK), BF),
        sib_in=((SLOTS, D, CHUNK), BF),
        one_in=((CHUNKS, zs, 2, shard, CHUNK), BF),
        two_in=((CHUNKS, zs, shard, CHUNK), BF),
        three_in=((CHUNKS, zs - 1, shard, CHUNK), BF),
    )
    dma = pltpu.SemaphoreType.DMA
    sems = dict(
        local_sem=dma((32,)),
        misc_send=dma((9,)),
        misc_recv=dma((9,)),
        sib_send=dma((SLOTS,)),
        sib_recv=dma((SLOTS,)),
        one_send=dma((CHUNKS,)),
        one_recv=dma((CHUNKS,)),
        two_send=dma((CHUNKS,)),
        two_recv=dma((CHUNKS,)),
        three_send=dma((CHUNKS, zs - 1)),
        three_recv=dma((CHUNKS, zs - 1)),
        z_send=dma((zs,)),
        z_recv=dma((zs,)),
        credit=pltpu.SemaphoreType.REGULAR,
    )
    keys = list(saved_shapes(rows))
    ins = ["i_cot", "gain", "dc", "ret", "small1", "i_shard1", "i_y1"] + ["i_" + k for k in keys]
    ins += ["a_wqkv", "a_wout", "a_wup", "a_wdown", "x_wqkv", "x_wout", "x_wup", "x_wdown"]
    names = ins + list(outs) + list(scratch) + list(sems)
    result = pl.pallas_call(
        partial(last_kernel, dp, names),
        out_shape=arrays(outs),
        in_specs=[hbm] + [small] * 4 + [hbm] * (2 + len(keys) + 8),
        out_specs=[hbm, hbm, small, small],
        scratch_shapes=vmem(scratch) + list(sems.values()),
        compiler_params=pltpu.CompilerParams(
            collective_id=1, has_side_effects=True, vmem_limit_bytes=63 << 20
        ),
        name="segment_backward",
    )(cot, gain, dc, ret, small1, shard1, y1, *[saved[k] for k in keys], *own, *other)
    return dict(zip(outs, result))


def fused(tokens, seg_doc, doc_len, w_qkv, b_qv, w_out, w_up, b_up, w_down, norm_gain, bias_terms, seg_pos, cotangent):
    batches, rows, width = tokens.shape
    dp = lax.axis_size("dp")
    segs = rows // SEG
    slots = doc_len.shape[1] * MAXSEG
    packed = jnp.concatenate([b_qv.reshape(2, 2 * HALF_D), b_up], axis=1).reshape(2, 1, PACK)
    gain = norm_gain.reshape(2, 2, 1, D)
    terms = bias_terms.reshape(2, 4, 1, D)
    own = (w_qkv, w_out, w_up, w_down)
    one = run_first(dp, rows, seg_doc, doc_len, tokens, cotangent, packed, gain[0], terms[0], *own)
    other = tuple(one[k] for k in ("x_wqkv", "x_wout", "x_wup", "x_wdown"))
    two = run_cross(
        dp, segs, slots, seg_doc.reshape(2, 1, -1), one["o_cls"].reshape(dp * segs, D),
        one["o_cot"].reshape(dp * segs, D), seg_pos, packed, one["o_packed"], gain[1], terms[1], own, other,
    )
    small1 = jnp.concatenate([two["small"], two["d_pos"].reshape(MAXSEG, 1, D)], axis=0)
    three = run_last(
        dp, rows, batches, cotangent, gain[0], two["dc"].reshape(8, 1, D), two["ret"].reshape(8, 1, D),
        small1, two["shard"], one["o_y1"], {k: one["o_" + k] for k in saved_shapes(rows)}, own, other,
    )
    shard = three["o_shard"]
    small = three["o_small"].reshape(26, D)
    both = small[:18].reshape(2, 9, D)
    shard_rows = D // dp
    return (
        three["o_enc"],
        three["o_grad"],
        shard[:, 9:12],
        both[:, 6].reshape(2, 2, HALF_D),
        shard[:, 8].transpose(0, 2, 1),
        shard[:, 4:8].transpose(0, 2, 1, 3).reshape(2, shard_rows, HALF_FF),
        both[:, 7:9].reshape(2, HALF_FF),
        shard[:, 0:4].transpose(0, 1, 3, 2).reshape(2, HALF_FF, shard_rows),
        both[:, 0:2],
        both[:, 2:6],
        small[18:26],
    )


def solution(mesh):
    in_specs = (
        P(None, "dp", None),
        P(),
        P(),
        P(None, None, None, "tensor"),
        P(None, None, "tensor"),
        P(None, "tensor", None),
        P(None, None, "tensor"),
        P(None, "tensor"),
        P(None, "tensor", None),
        P(),
        P(),
        P(),
        P(None, "dp", None),
    )
    out_specs = (
        P(None, "dp", None),
        P(None, "dp", None),
        P(None, None, "dp", "tensor"),
        P(None, None, "tensor"),
        P(None, "tensor", "dp"),
        P(None, "dp", "tensor"),
        P(None, "tensor"),
        P(None, "tensor", "dp"),
        P(),
        P(),
        P(),
    )
    body = fused if mesh.shape["dp"] == 16 and mesh.shape["tensor"] == 2 else local
    return jax.shard_map(body, mesh=mesh, in_specs=in_specs, out_specs=out_specs, check_vma=False)
```

```python
from functools import partial, reduce

import jax
import jax.numpy as jnp
from jax import lax
from jax.experimental import pallas as pl
from jax.experimental.pallas import tpu as pltpu
from jax.sharding import PartitionSpec as P

HEAD_DIM = 64
SEG = 128
MAXSEG = 8


norm_eps = 1e-05
masked_score = -1e30


def norm_rows(values, gain, shift):
    centre = values - jnp.mean(values, axis=-1, keepdims=True)
    spread = jnp.mean(centre * centre, axis=-1, keepdims=True)
    return centre * lax.rsqrt(spread + norm_eps) * gain + shift


def exact_gelu(values):
    return jax.nn.gelu(values, approximate=False)


def my_rows(values):
    part_rows = values.shape[0] // lax.axis_size("tensor")
    return lax.dynamic_slice_in_dim(values, lax.axis_index("tensor") * part_rows, part_rows, 0)


def attn_scores(queries, key_rows, key_mask, split_shape):
    raw = jnp.einsum(
        "glhd,gmhd->ghlm",
        queries.reshape(split_shape),
        key_rows.reshape(split_shape),
        preferred_element_type=jnp.float32,
    ) * HEAD_DIM ** (-0.5)
    return jnp.where(key_mask[:, None, None, :], raw, masked_score)


def layer_forward(inputs, key_mask, weights):
    w_qkv, b_qv, w_out, w_up, b_up, w_down, norm_gain, bias_terms = weights
    groups, span = key_mask.shape
    row_count = inputs.shape[0]
    local_width = w_qkv.shape[2]
    split_shape = (groups, span, local_width // HEAD_DIM, HEAD_DIM)
    inputs_b = inputs.astype(jnp.bfloat16)
    projected = jnp.einsum("rd,cde->cre", inputs_b, w_qkv, preferred_element_type=jnp.float32)
    queries = (projected[0] + b_qv[0]).astype(jnp.bfloat16)
    key_rows = projected[1].astype(jnp.bfloat16)
    value_rows = (projected[2] + b_qv[1]).astype(jnp.bfloat16)
    scores = attn_scores(queries, key_rows, key_mask, split_shape)
    row_max = jnp.max(scores, axis=-1, keepdims=True)
    log_total = row_max + jnp.log(jnp.sum(jnp.exp(scores - row_max), axis=-1, keepdims=True))
    attn_probs = jnp.exp(scores - log_total).astype(jnp.bfloat16)
    head_out = jnp.einsum(
        "ghlm,gmhd->glhd",
        attn_probs,
        value_rows.reshape(split_shape),
        preferred_element_type=jnp.float32,
    )
    head_out = head_out.reshape(row_count, local_width).astype(jnp.bfloat16)
    attn_part = (
        lax.psum_scatter(
            jnp.dot(head_out, w_out, preferred_element_type=jnp.float32),
            "tensor",
            scatter_dimension=0,
            tiled=True,
        )
        + bias_terms[0]
    )
    resid_one = lax.all_gather(my_rows(inputs) + attn_part, "tensor", axis=0, tiled=True)
    hidden = norm_rows(resid_one, norm_gain[0], bias_terms[2])
    hidden_b = hidden.astype(jnp.bfloat16)
    pre_act = jnp.dot(hidden_b, w_up, preferred_element_type=jnp.float32) + b_up
    active_b = exact_gelu(pre_act).astype(jnp.bfloat16)
    mlp_part = (
        lax.psum_scatter(
            jnp.dot(active_b, w_down, preferred_element_type=jnp.float32),
            "tensor",
            scatter_dimension=0,
            tiled=True,
        )
        + bias_terms[1]
    )
    resid_two = lax.all_gather(my_rows(hidden) + mlp_part, "tensor", axis=0, tiled=True)
    stored = (
        inputs_b,
        queries,
        key_rows,
        value_rows,
        log_total,
        head_out,
        resid_one,
        hidden_b,
        pre_act,
        active_b,
        resid_two,
    )
    return (norm_rows(resid_two, norm_gain[1], bias_terms[3]), stored)


def layer_backward(grad_out, key_mask, weights, stored):
    w_qkv, b_qv, w_out, w_up, b_up, w_down, norm_gain, bias_terms = weights
    (
        inputs_b,
        queries,
        key_rows,
        value_rows,
        log_total,
        head_out,
        resid_one,
        hidden_b,
        pre_act,
        active_b,
        resid_two,
    ) = stored
    groups, span = key_mask.shape
    row_count, local_width = queries.shape
    split_shape = (groups, span, local_width // HEAD_DIM, HEAD_DIM)
    forward_two, norm_two = jax.vjp(norm_rows, resid_two, norm_gain[1], bias_terms[3])
    grad_two, gain_two, shift_two = norm_two(grad_out)
    grad_mlp = grad_two.astype(jnp.bfloat16)
    grad_wdown = jnp.dot(active_b.T, grad_mlp, preferred_element_type=jnp.float32)
    grad_act = jnp.dot(grad_mlp, w_down.T, preferred_element_type=jnp.float32)
    forward_gelu, gelu_back = jax.vjp(exact_gelu, pre_act)
    grad_pre = gelu_back(grad_act)[0].astype(jnp.bfloat16)
    grad_wup = jnp.dot(hidden_b.T, grad_pre, preferred_element_type=jnp.float32)
    up_part = lax.psum_scatter(
        jnp.dot(grad_pre, w_up.T, preferred_element_type=jnp.float32),
        "tensor",
        scatter_dimension=0,
        tiled=True,
    )
    grad_hidden = lax.all_gather(my_rows(grad_two) + up_part, "tensor", axis=0, tiled=True)
    forward_one, norm_one = jax.vjp(norm_rows, resid_one, norm_gain[0], bias_terms[2])
    grad_one, gain_one, shift_one = norm_one(grad_hidden)
    grad_attn = grad_one.astype(jnp.bfloat16)
    grad_wout = jnp.dot(head_out.T, grad_attn, preferred_element_type=jnp.float32)
    grad_heads = (
        jnp.dot(grad_attn, w_out.T, preferred_element_type=jnp.float32)
        .astype(jnp.bfloat16)
        .reshape(split_shape)
    )
    scores = attn_scores(queries, key_rows, key_mask, split_shape)
    attn_probs = jnp.exp(scores - log_total)
    grad_probs = jnp.einsum(
        "glhd,gmhd->ghlm",
        grad_heads,
        value_rows.reshape(split_shape),
        preferred_element_type=jnp.float32,
    )
    grad_values = jnp.einsum(
        "ghlm,glhd->gmhd",
        attn_probs.astype(jnp.bfloat16),
        grad_heads,
        preferred_element_type=jnp.float32,
    )
    grad_scores = (
        attn_probs * (grad_probs - jnp.sum(attn_probs * grad_probs, axis=-1, keepdims=True))
    ).astype(jnp.bfloat16)
    inv_root = HEAD_DIM ** (-0.5)
    grad_queries = (
        jnp.einsum(
            "ghlm,gmhd->glhd",
            grad_scores,
            key_rows.reshape(split_shape),
            preferred_element_type=jnp.float32,
        )
        * inv_root
    )
    grad_keys = (
        jnp.einsum(
            "ghlm,glhd->gmhd",
            grad_scores,
            queries.reshape(split_shape),
            preferred_element_type=jnp.float32,
        )
        * inv_root
    )
    grad_qkv = (
        jnp.stack([grad_queries, grad_keys, grad_values])
        .reshape(3, row_count, local_width)
        .astype(jnp.bfloat16)
    )
    grad_wqkv = jnp.einsum("rd,cre->cde", inputs_b, grad_qkv, preferred_element_type=jnp.float32)
    qkv_part = lax.psum_scatter(
        jnp.einsum("cre,cde->rd", grad_qkv, w_qkv, preferred_element_type=jnp.float32).astype(
            jnp.bfloat16
        ),
        "tensor",
        scatter_dimension=0,
        tiled=True,
    ).astype(jnp.float32)
    grad_inputs = lax.all_gather(
        (my_rows(grad_one) + qkv_part).astype(jnp.bfloat16), "tensor", axis=0, tiled=True
    ).astype(jnp.float32)
    grad_bqv = jnp.stack(
        [
            jnp.sum(grad_qkv[0].astype(jnp.float32), axis=0),
            jnp.sum(grad_qkv[2].astype(jnp.float32), axis=0),
        ]
    )
    grad_bup = jnp.sum(grad_pre.astype(jnp.float32), axis=0)
    grad_gain = jnp.stack([gain_one, gain_two])
    grad_shift = jnp.stack(
        [
            jnp.sum(grad_attn.astype(jnp.float32), axis=0),
            jnp.sum(grad_mlp.astype(jnp.float32), axis=0),
            shift_one,
            shift_two,
        ]
    )
    return (
        grad_inputs,
        (grad_wqkv, grad_bqv, grad_wout, grad_wup, grad_bup, grad_wdown, grad_gain, grad_shift),
    )


def deal_map(doc_ids, total_docs):
    return jnp.where(doc_ids % 2 == 1, (doc_ids + total_docs // 2) % total_docs, doc_ids)


def local_plan(seg_order, doc_lengths, seg_local, doc_local):
    total_docs = doc_lengths.shape[0]
    my_index = lax.axis_index("dp")
    doc_ids = jnp.arange(total_docs, dtype=jnp.int32)
    owner_pos = deal_map(doc_ids, total_docs)
    starts = jnp.sum((seg_order[None, :] < doc_ids[:, None]).astype(jnp.int32), axis=1)
    counts = jnp.sum((seg_order[None, :] == doc_ids[:, None]).astype(jnp.int32), axis=1)
    my_segments = my_index * seg_local + jnp.arange(seg_local, dtype=jnp.int32)
    seg_owner_doc = lax.dynamic_slice_in_dim(seg_order, my_index * seg_local, seg_local)
    seg_hot = seg_owner_doc[:, None] == doc_ids[None, :]
    my_start = jnp.sum(jnp.where(seg_hot, starts[None, :], 0), axis=1)
    my_length = jnp.sum(jnp.where(seg_hot, doc_lengths[None, :], 0), axis=1)
    my_owner = jnp.sum(jnp.where(seg_hot, owner_pos[None, :], 0), axis=1)
    within = my_segments - my_start
    valid_tokens = jnp.minimum(SEG, my_length - within * SEG)
    tok_mask = jnp.arange(SEG, dtype=jnp.int32)[None, :] < valid_tokens[:, None]
    src_slot = my_owner * MAXSEG + within
    my_deal = deal_map(my_index * doc_local + jnp.arange(doc_local, dtype=jnp.int32), total_docs)
    deal_hot = my_deal[:, None] == doc_ids[None, :]
    own_start = jnp.sum(jnp.where(deal_hot, starts[None, :], 0), axis=1)
    own_count = jnp.sum(jnp.where(deal_hot, counts[None, :], 0), axis=1)
    slot_index = jnp.arange(MAXSEG, dtype=jnp.int32)
    cross_mask = slot_index[None, :] < own_count[:, None]
    target = jnp.where(cross_mask, own_start[:, None] + slot_index[None, :], -1).reshape(-1)
    return (tok_mask, cross_mask, target, src_slot)


def picker(index_map, shard_rows):
    positions = jnp.arange(shard_rows.shape[0], dtype=jnp.int32)
    selector = (index_map[:, None] == positions[None, :]).astype(jnp.bfloat16)
    return jnp.dot(selector, shard_rows, preferred_element_type=jnp.float32)


def spreader(index_map, source_rows, row_span):
    positions = jnp.arange(row_span, dtype=jnp.int32)
    selector = (positions[:, None] == index_map[None, :]).astype(jnp.bfloat16)
    return jnp.dot(selector, source_rows, preferred_element_type=jnp.float32)


def add_terms(left, right):
    return jax.tree.map(jnp.add, left, right)


def local(
    tokens,
    seg_doc,
    doc_len,
    w_qkv,
    b_qv,
    w_out,
    w_up,
    b_up,
    w_down,
    norm_gain,
    bias_terms,
    seg_pos,
    cotangent,
):
    batches, local_rows, width = tokens.shape
    seg_local = local_rows // SEG
    doc_local = doc_len.shape[1] // lax.axis_size("dp")
    slot_rows = doc_local * MAXSEG

    def layer_weights(level):
        return (
            w_qkv[level],
            b_qv[level],
            w_out[level],
            w_up[level],
            b_up[level],
            w_down[level],
            norm_gain[level],
            bias_terms[level],
        )

    seg_weights = layer_weights(0)
    cross_weights = layer_weights(1)
    encoded = []
    grad_tokens = []
    seg_grads = []
    cross_grads = []
    pos_grads = []
    for batch_index in range(batches):
        tok_mask, cross_mask, target, src_slot = local_plan(
            seg_doc[batch_index], doc_len[batch_index], seg_local, doc_local
        )
        seg_out, seg_stored = layer_forward(
            tokens[batch_index].astype(jnp.float32), tok_mask, seg_weights
        )
        seg_cube = seg_out.reshape(seg_local, SEG, width)
        cls_rows = seg_cube[:, 0].astype(jnp.bfloat16)
        collected = picker(target, lax.all_gather(cls_rows, "dp", axis=0, tiled=True))
        cross_in = (collected.reshape(doc_local, MAXSEG, width) + seg_pos[None]).reshape(
            slot_rows, width
        )
        cross_out, cross_stored = layer_forward(cross_in, cross_mask, cross_weights)
        returned = picker(
            src_slot, lax.all_gather(cross_out.astype(jnp.bfloat16), "dp", axis=0, tiled=True)
        )
        encoded.append(
            seg_cube.at[:, 0].set(returned).reshape(local_rows, width).astype(jnp.bfloat16)
        )
        grad_cube = cotangent[batch_index].astype(jnp.float32).reshape(seg_local, SEG, width)
        grad_returned = grad_cube[:, 0].astype(jnp.bfloat16)
        grad_cross = lax.psum_scatter(
            spreader(src_slot, grad_returned, slot_rows * lax.axis_size("dp")),
            "dp",
            scatter_dimension=0,
            tiled=True,
        )
        grad_cross_in, cross_terms = layer_backward(
            grad_cross, cross_mask, cross_weights, cross_stored
        )
        pos_grads.append(jnp.sum(grad_cross_in.reshape(doc_local, MAXSEG, width), axis=0))
        grad_sent = grad_cross_in.astype(jnp.bfloat16)
        cross_grads.append(cross_terms)
        grad_cls = lax.psum_scatter(
            spreader(target, grad_sent, seg_local * lax.axis_size("dp")),
            "dp",
            scatter_dimension=0,
            tiled=True,
        )
        grad_seg = grad_cube.at[:, 0].set(grad_cls).reshape(local_rows, width)
        grad_inputs, seg_terms = layer_backward(grad_seg, tok_mask, seg_weights, seg_stored)
        grad_tokens.append(grad_inputs)
        seg_grads.append(seg_terms)
    seg_total = reduce(add_terms, seg_grads)
    cross_total = reduce(add_terms, cross_grads)
    pos_total = reduce(jnp.add, pos_grads)
    big_grads = (
        lax.psum_scatter(
            jnp.stack([seg_total[0], cross_total[0]]), "dp", scatter_dimension=2, tiled=True
        ),
        lax.psum_scatter(
            jnp.stack([seg_total[2], cross_total[2]]), "dp", scatter_dimension=2, tiled=True
        ),
        lax.psum_scatter(
            jnp.stack([seg_total[3], cross_total[3]]), "dp", scatter_dimension=1, tiled=True
        ),
        lax.psum_scatter(
            jnp.stack([seg_total[5], cross_total[5]]), "dp", scatter_dimension=2, tiled=True
        ),
    )
    small = lax.psum(
        (
            jnp.stack([seg_total[1], cross_total[1]]),
            jnp.stack([seg_total[4], cross_total[4]]),
            jnp.stack([seg_total[6], cross_total[6]]),
            jnp.stack([seg_total[7], cross_total[7]]),
            pos_total,
        ),
        "dp",
    )
    return (
        jnp.stack(encoded),
        jnp.stack(grad_tokens),
        big_grads[0],
        small[0],
        big_grads[1],
        big_grads[2],
        small[1],
        big_grads[3],
        small[2],
        small[3],
        small[4],
    )


BF = jnp.bfloat16
F32 = jnp.float32
D = 768
FF = 3072
HALF_FF = FF // 2
HALF_D = D // 2
CHUNK = 384
CHUNKS = 12
PAIRS = 6
MESH = pl.DeviceIdType.MESH
ROOT_HALF = 0.7071067811865476
PDF_SCALE = 0.3989422804014327


class Names:
    def __init__(self, **kw):
        self.__dict__.update(kw)


def mm(left, right):
    return jnp.dot(left, right, preferred_element_type=F32)


def mm_nt(left, right):
    return lax.dot_general(left, right, (((1,), (1,)), ((), ())), preferred_element_type=F32)


def span(index, size):
    return pl.ds(pl.multiple_of(index * size, size), size)


def row_norm(rows):
    centre = rows - jnp.mean(rows, axis=-1, keepdims=True)
    spread = jnp.mean(centre * centre, axis=-1, keepdims=True)
    scale = lax.rsqrt(spread + norm_eps)
    return centre * scale, scale


def stacked(pair, low_half):
    zero = jnp.zeros_like(pair)
    return jnp.concatenate(
        [jnp.where(low_half, pair, zero), jnp.where(low_half, zero, pair)], axis=0
    )


def soft_rows(scores):
    top = jnp.max(scores, axis=-1, keepdims=True)
    grown = jnp.exp(scores - top)
    return (grown * (1.0 / jnp.sum(grown, axis=-1, keepdims=True))).astype(BF)


def transpose_into(dest, source, rows):
    @pl.loop(0, rows // SEG)
    def _(s):
        dest[:, span(s, SEG)] = source[span(s, SEG), :].T


def gelu_pair(u):
    cdf = 0.5 * (1.0 + lax.erf(u * ROOT_HALF))
    slope = cdf + u * (PDF_SCALE * jnp.exp(-0.5 * u * u))
    return (u * cdf).astype(BF), slope.astype(BF)


def project(r):
    @pl.loop(0, 9)
    def _(i):
        c = lax.div(i, 3)
        cols = span(lax.rem(i, 3), 256)
        r.qkv[c, :, cols] = (mm(r.xb[...], r.wqkv[c, :, cols]) + r.b3[c, :, cols]).astype(BF)


def attend(r, keep):
    @pl.loop(0, r.xb.shape[0] // SEG)
    def _(s):
        at = span(s, SEG)
        live = keep(s)
        low_half = lax.broadcasted_iota(jnp.int32, (SEG, SEG), 1) < HEAD_DIM
        for p in range(PAIRS):
            cols = slice(p * SEG, p * SEG + SEG)
            keys = stacked(r.qkv[1, at, cols], low_half)
            vals = stacked(r.qkv[2, at, cols], low_half)
            raw = mm_nt(r.qkv[0, at, cols], keys) * HEAD_DIM ** (-0.5)
            one = soft_rows(jnp.where(live, raw[:, :SEG], masked_score))
            two = soft_rows(jnp.where(live, raw[:, SEG:], masked_score))
            both = jnp.concatenate([one, two], axis=1)
            r.p[s, p] = both
            r.o[at, cols] = mm(both, vals).astype(BF)


def attn_out(r):
    @pl.loop(0, 3)
    def _(n):
        cols = span(n, 256)
        r.xh1[:, cols] = mm(r.o[...], r.wout[:, cols]) + r.bt[0, :, cols]


def norm_one(r):
    @pl.loop(0, r.xb.shape[0] // 64)
    def _(s):
        at = span(s, 64)
        hat, scale = row_norm(r.x_rows(at) + r.xh1[at, :])
        r.xh1[at, :] = hat
        r.rs1[at, :] = jnp.broadcast_to(scale, (64, SEG))
        hidden = hat * r.gain[0] + r.bt[2]
        r.h1[at, :] = hidden
        r.h1b[at, :] = hidden.astype(BF)


def mlp_up(r):
    @pl.loop(0, 12)
    def _(j):
        cols = span(j, 256)
        for b in range(r.xb.shape[0] // SEG):
            at = slice(b * SEG, b * SEG + SEG)
            u = mm(r.h1b[at, :], r.wup[:, cols]) + r.bup[:, cols]
            r.g[at, cols], r.gp[at, cols] = gelu_pair(u)


def mlp_down(r):
    @pl.loop(0, 3)
    def _(n):
        cols = span(n, 256)
        r.xh2[:, cols] = r.h1[:, cols] + mm(r.g[...], r.wdown[:, cols]) + r.bt[1, :, cols]


def norm_two(r, y_block):
    @pl.loop(0, r.xb.shape[0] // 64)
    def _(s):
        at = span(s, 64)
        hat, scale = row_norm(r.xh2[at, :])
        r.xh2[at, :] = hat
        r.rs2[at, :] = jnp.broadcast_to(scale, (64, SEG))
        y_block(at, hat * r.gain[1] + r.bt[3])


def core_forward(r, keep, ready, y_block):
    ready("qkv")
    project(r)
    attend(r, keep)
    ready("out")
    attn_out(r)
    norm_one(r)
    ready("up")
    mlp_up(r)
    transpose_into(r.h1t, r.h1b, r.xb.shape[0])
    ready("down")
    mlp_down(r)
    norm_two(r, y_block)


def norm_back(grad, hat, scale, gain):
    d_hat = grad * gain
    first = jnp.mean(d_hat, axis=-1, keepdims=True)
    second = jnp.mean(d_hat * hat, axis=-1, keepdims=True)
    return (d_hat - first - hat * second) * scale


def norm_back_rows(r, rows, hat_ref, scale_ref, gain, grad_of):
    zero = jnp.zeros((1, D), F32)

    def step(s, sums):
        at = span(s, 64)
        grad = grad_of(s, at)
        hat = hat_ref[at, :]
        out = norm_back(grad, hat, scale_ref[at, 0:1], gain)
        low = out.astype(BF)
        r.dr[at, :] = out
        r.dm[at, :] = low
        return (
            sums[0] + jnp.sum(grad * hat, axis=0, keepdims=True),
            sums[1] + jnp.sum(grad, axis=0, keepdims=True),
            sums[2] + jnp.sum(low.astype(F32), axis=0, keepdims=True),
        )

    sums = lax.fori_loop(0, rows // 64, step, (zero, zero, zero))
    transpose_into(r.dmt, r.dm, rows)
    return sums


def grad_hidden(r):
    @pl.loop(0, 12)
    def _(j):
        cols = span(j, 256)
        du = (mm_nt(r.dm[...], r.wdown[cols, :]) * r.gp[:, cols].astype(F32)).astype(BF)
        r.gp[:, cols] = du
        r.bup_sum[:, cols] = jnp.sum(du.astype(F32), axis=0, keepdims=True)


def grad_middle(r):
    @pl.loop(0, 3)
    def _(n):
        cols = span(n, 256)
        r.dr[:, cols] = r.dr[:, cols] + mm_nt(r.gp[...], r.wup[cols, :])


def grad_heads(r):
    @pl.loop(0, 3)
    def _(n):
        cols = span(n, 256)
        r.o[:, cols] = mm_nt(r.dm[...], r.wout[cols, :]).astype(BF)


def attend_back(r, between=None):
    segs = r.dr.shape[0] // SEG
    step = segs if between is None else 1
    for low in range(0, segs, step):
        attend_back_part(r, low, low + step)
        if between is not None:
            between(low)


def attend_back_part(r, low, high):
    @pl.loop(low, high)
    def _(s):
        at = span(s, SEG)
        low_half = lax.broadcasted_iota(jnp.int32, (SEG, SEG), 1) < HEAD_DIM
        scale = HEAD_DIM ** (-0.5)
        for p in range(PAIRS):
            cols = slice(p * SEG, p * SEG + SEG)
            query = r.qkv[0, at, cols]
            keys = stacked(r.qkv[1, at, cols], low_half)
            vals = stacked(r.qkv[2, at, cols], low_half)
            d_head = r.o[at, cols]
            probs = r.p[s, p]
            d_probs = mm_nt(d_head, vals)
            d_vals = mm(probs.T, d_head)
            wide = probs.astype(F32)
            prod = wide * d_probs
            parts = []
            for h in range(2):
                own = slice(h * SEG, h * SEG + SEG)
                parts.append(
                    prod[:, own]
                    - wide[:, own] * jnp.sum(prod[:, own], axis=-1, keepdims=True)
                )
            d_scores = jnp.concatenate(parts, axis=1).astype(BF)
            d_keys = mm(d_scores.T, query) * scale
            r.qkv[0, at, cols] = (mm(d_scores, keys) * scale).astype(BF)
            r.qkv[1, at, cols] = jnp.where(low_half, d_keys[:SEG], d_keys[SEG:]).astype(BF)
            r.qkv[2, at, cols] = jnp.where(low_half, d_vals[:SEG], d_vals[SEG:]).astype(BF)


def bias_heads(r):
    for c in (0, 2):
        r.qv_sum[c // 2] = jnp.sum(r.qkv[c].astype(F32), axis=0, keepdims=True)


def grad_input(r):
    @pl.loop(0, 3)
    def _(n):
        cols = span(n, 256)
        total = r.dr[:, cols]
        for c in range(3):
            total = total + mm_nt(r.qkv[c], r.wqkv[c, cols, :])
        r.dr[:, cols] = total


def back_norm_two(r, grad_of):
    sums = norm_back_rows(r, r.dr.shape[0], r.xh2, r.rs2, r.gain[1], grad_of)
    r.small_common[1], r.small_common[5], r.small_common[3] = sums


def back_norm_one(r):
    sums = norm_back_rows(r, r.dr.shape[0], r.xh1, r.rs1, r.gain[0], lambda s, at: r.dr[at, :])
    r.small_common[0], r.small_common[4], r.small_common[2] = sums


def chunk_operands(r, c):
    if c < 4:
        return r.dmt, (r.g, c * CHUNK, HALF_FF + c * CHUNK)
    if c < 8:
        return r.h1t, (r.gp, (c - 4) * CHUNK, HALF_FF + (c - 4) * CHUNK)
    if c == 8:
        return r.dmt, (r.o, 0, HALF_D)
    return r.xt, (r.qkv.at[c - 9], 0, HALF_D)


HOOK_CHUNKS = {"down": (0, 4), "up": (4, 8), "out": (8, 9), "qkv": (9, 12)}


class Copies:
    def __init__(self, sems):
        self.sems = sems
        self.used = 0

    def start(self, source, dest):
        copy = pltpu.make_async_copy(source, dest, self.sems.at[self.used])
        self.used += 1
        copy.start()
        return copy


def remote(source, dest, send_sem, recv_sem, device):
    return pltpu.make_async_remote_copy(
        src_ref=source,
        dst_ref=dest,
        send_sem=send_sem,
        recv_sem=recv_sem,
        device_id=device,
        device_id_type=MESH,
    )


class Gather:
    def __init__(self, dp, everyone, send, recv):
        self.dp, self.everyone, self.send, self.recv = dp, everyone, send, recv
        self.sends = []

    def start(self, block):
        d, t = lax.axis_index("dp"), lax.axis_index("tensor")
        everyone = self.everyone
        everyone[d] = block
        for o in range(1, self.dp):
            peer = (lax.rem(d + o, self.dp), t)
            copy = remote(everyone.at[d], everyone.at[d], self.send.at[o], self.recv.at[d], peer)
            copy.start()
            self.sends.append(copy)

    def arrived(self):
        d, t = lax.axis_index("dp"), lax.axis_index("tensor")
        for o in range(1, self.dp):
            source = lax.rem(d + o, self.dp)
            block = self.everyone.at[source]
            remote(block, block, self.send.at[o], self.recv.at[source], (source, t)).wait_recv()

    def rows_into(self, dest):
        segs = self.everyone.shape[1]
        pack = 8 // segs
        for i in range(self.dp // pack):
            blocks = [self.everyone[i * pack + k].astype(F32) for k in range(pack)]
            dest[i * 8 : i * 8 + 8, :] = jnp.concatenate(blocks, axis=0)


SLOTS = 3
RING = 8
WEIGHTS = ("wqkv", "wout", "wup", "wdown")


def half_of(ref, which, half):
    if which == "wqkv":
        return ref.at[:, :, half * HALF_D : (half + 1) * HALF_D]
    if which == "wout":
        return ref.at[half * HALF_D : (half + 1) * HALF_D, :]
    if which == "wup":
        return ref.at[:, half * HALF_FF : (half + 1) * HALF_FF]
    return ref.at[half * HALF_FF : (half + 1) * HALF_FF, :]


def fill_bias(b3, bup, half, layer, b_qv, b_up):
    lanes = slice(half * HALF_D, (half + 1) * HALF_D)
    b3[0, :, lanes] = b_qv[layer, 0:1, :]
    b3[1, :, lanes] = jnp.zeros((1, HALF_D), F32)
    b3[2, :, lanes] = b_qv[layer, 1:2, :]
    bup[:, half * HALF_FF : (half + 1) * HALF_FF] = b_up[layer : layer + 1, :]


def pack_halves(r):
    for half in range(2):
        at = 6 + 3 * half
        lanes = slice(half * HALF_D, (half + 1) * HALF_D)
        r.small[at, :, 0:HALF_D] = r.qv_sum[0, :, lanes]
        r.small[at, :, HALF_D:] = r.qv_sum[1, :, lanes]
        base = half * HALF_FF
        r.small[at + 1] = r.bup_sum[:, base : base + D]
        r.small[at + 2] = r.bup_sum[:, base + D : base + 2 * D]


def first_of_segments(ref, segs):
    return jnp.concatenate(
        [ref[s * SEG : s * SEG + 16, :].astype(F32)[0:1] for s in range(segs)], axis=0
    )


class Stream:
    COUNTS = {"qkv": 9, "out": 3, "up": 12, "down": 12}

    def __init__(self, r):
        self.r = r

    def parts(self, phase, j, act):
        r = self.r
        which = "w" + phase
        own, other = getattr(r, "a_" + which).at[1], getattr(r, "f_" + which)
        buffer, sems = (r.wide, r.wide_sem) if phase in ("qkv", "up") else (r.tall, r.tall_sem)
        slot = lax.rem(j, 3)
        half = (HALF_D if phase in ("qkv", "out") else HALF_FF) // SEG
        for k in range(2):
            if phase == "qkv":
                c, block = lax.div(j, 3), 2 * lax.rem(j, 3) + k
            else:
                c, block = None, 2 * j + k

            def source(ref, at):
                if phase == "qkv":
                    return ref.at[c, :, span(at, SEG)]
                return ref.at[:, span(at, SEG)] if phase == "up" else ref.at[span(at, SEG), :]

            lanes = slice(k * SEG, k * SEG + SEG)
            if phase in ("qkv", "up"):
                dest = buffer.at[slot, :, lanes]
            else:
                dest = buffer.at[slot, lanes, :]
            sem = sems.at[slot, k]
            if act == "wait":
                pltpu.make_async_copy(source(other, 0), dest, sem).wait()
                continue

            @pl.when(block < half)
            def _():
                pltpu.make_async_copy(source(own, block), dest, sem).start()

            @pl.when(block >= half)
            def _():
                pltpu.make_async_copy(source(other, block - half), dest, sem).start()

    def prime(self, phase):
        for j in range(3):
            self.parts(phase, jnp.int32(j), "start")

    def run(self, phase, body):
        buffer = self.r.wide if phase in ("qkv", "up") else self.r.tall
        count = self.COUNTS[phase]

        @pl.loop(0, count)
        def _(j):
            self.parts(phase, j, "wait")
            body(j, buffer.at[lax.rem(j, 3)])

            @pl.when(j + 3 < count)
            def _():
                self.parts(phase, j + 3, "start")


def cross_layer(r, q, stream, keep, pump, hooks):
    slots = q.xb.shape[0]

    def project_piece(j, w):
        c = lax.div(j, 3)
        cols = span(lax.rem(j, 3), 256)
        q.qkv[c, :, cols] = (mm(q.xb[...], w[...]) + q.b3[c, :, cols]).astype(BF)

    stream.run("qkv", project_piece)
    stream.prime("up")
    attend(q, keep)
    pump("attend")
    q.xh1[...] = jnp.broadcast_to(q.bt[0], (slots, D))

    def out_piece(j, w):
        q.xh1[...] = q.xh1[...] + mm(q.o[:, span(j, 256)], w[...])

    stream.run("out", out_piece)
    stream.prime("down")
    norm_one(q)
    transpose_into(q.h1t, q.h1b, slots)

    def up_piece(j, w):
        cols = span(j, 256)
        u = mm(q.h1b[...], w[...]) + q.bup[:, cols]
        act, slope = gelu_pair(u)
        q.g[:, cols] = act
        q.gp[:, cols] = slope

    stream.run("up", up_piece)
    stream.prime("up")
    pump("up")
    q.xh2[...] = q.h1[...] + q.bt[1]

    def down_piece(j, w):
        q.xh2[...] = q.xh2[...] + mm(q.g[:, span(j, 256)], w[...])

    stream.run("down", down_piece)
    stream.prime("down")

    def y_block(at, values):
        q.yb[at, :] = values.astype(BF)

    norm_two(q, y_block)
    pump("down")
    back_norm_two(q, lambda s, at: q.dy[at, :])
    hooks("down")

    def back_down_piece(j, w):
        cols = span(j, 256)
        du = (mm_nt(q.dm[...], w[...]) * q.gp[:, cols].astype(F32)).astype(BF)
        q.gp[:, cols] = du
        r.bup_sum[:, cols] = jnp.sum(du.astype(F32), axis=0, keepdims=True)

    stream.run("down", back_down_piece)
    stream.prime("out")
    pump("back_down")
    hooks("up")

    def back_up_piece(j, w):
        q.dr[...] = q.dr[...] + mm_nt(q.gp[:, span(j, 256)], w[...])

    stream.run("up", back_up_piece)
    stream.prime("qkv")
    pump("back_up")
    back_norm_one(q)
    hooks("out")

    def back_out_piece(j, w):
        q.o[:, span(j, 256)] = mm_nt(q.dm[...], w[...]).astype(BF)

    stream.run("out", back_out_piece)
    attend_back(q)
    bias_heads(q)
    pump("attend_back")
    hooks("qkv")

    def back_qkv_piece(j, w):
        q.dr[...] = q.dr[...] + mm_nt(q.qkv[lax.div(j, 3), :, span(lax.rem(j, 3), 256)], w[...])

    stream.run("qkv", back_qkv_piece)


def whole_kernel(dp, names, *refs):
    r = Names(**dict(zip(names, refs)))
    d, t = lax.axis_index("dp"), lax.axis_index("tensor")
    x, y, z = lax.rem(d, 2), lax.rem(lax.div(d, 2), 2), lax.div(d, 4)
    zs = dp // 4
    shard = D // dp
    rows = r.xb.shape[0]
    segs = rows // SEG
    sibling = (d, 1 - t)
    x_peer = (z * 4 + y * 2 + (1 - x), t)
    y_peer = (z * 4 + (1 - y) * 2 + x, t)
    z_peers = [(lax.rem(z + o, zs) * 4 + y * 2 + x, t) for o in range(1, zs)]
    r.dr, r.dm, r.y1 = r.h1, r.h1b, r.xb

    barrier = pltpu.get_barrier_semaphore()
    for device in [sibling] + [(lax.rem(d + o, dp), t) for o in range(1, dp)]:
        pl.semaphore_signal(barrier, inc=1, device_id=device, device_id_type=MESH)
    copies = Copies(r.local_sem)
    for layer, gain, terms in ((0, r.gain, r.bt), (1, r.gain_cross, r.bt_cross)):
        for k in range(2):
            gain[k] = r.norm_gain[layer, k : k + 1, :]
        for k in range(4):
            terms[k] = r.bias_terms[layer, k : k + 1, :]
    own = {w: getattr(r, "a_" + w) for w in WEIGHTS}
    full = {w: getattr(r, "f_" + w) for w in WEIGHTS}
    load_x = copies.start(r.tokens.at[t], r.xb)
    loads = {w: copies.start(own[w].at[0], half_of(getattr(r, w), w, 0)) for w in WEIGHTS}
    load_cot = copies.start(r.cotangent.at[t], r.cot)
    pl.semaphore_wait(barrier, dp)

    swaps = {}

    def swap(layer, w):
        k = WEIGHTS.index(w)
        dest = half_of(getattr(r, w), w, 1) if layer == 0 else full[w]
        swaps[layer, w] = remote(
            own[w].at[layer], dest, r.w_send.at[layer, k], r.w_recv.at[layer, k], sibling
        )
        swaps[layer, w].start()

    swap(0, "wqkv")
    swap_bias = [
        remote(r.b_qv, r.x_bqv, r.w_send.at[0, 4], r.w_recv.at[0, 4], sibling),
        remote(r.b_up, r.x_bup, r.w_send.at[1, 4], r.w_recv.at[1, 4], sibling),
    ]
    for copy in swap_bias:
        copy.start()
    swap(0, "wout")
    cot_gather = Gather(dp, r.cot_all, r.g_send.at[0], r.g_recv.at[0])
    cls_gather = Gather(dp, r.cls_all, r.g_send.at[1], r.g_recv.at[1])
    hat_gather = Gather(dp, r.hat_all, r.g_send.at[2], r.g_recv.at[2])
    act_gather = Gather(dp, r.act_all, r.g_send.at[3], r.g_recv.at[3])

    def ready(phase):
        if phase == "qkv":
            load_x.wait()
            transpose_into(r.xt, r.xb, rows)
            fill_bias(r.b3, r.bup, 0, 0, r.b_qv, r.b_up)
            fill_bias(r.b3_cross, r.bup_cross, 0, 1, r.b_qv, r.b_up)
            load_cot.wait()
            cot_gather.start(first_of_segments(r.cot, segs).astype(BF))
            loads["wqkv"].wait()
            swaps[0, "wqkv"].wait_recv()
            swap(0, "wup")
            swap(0, "wdown")
            for copy in swap_bias:
                copy.wait_recv()
            fill_bias(r.b3, r.bup, 1, 0, r.x_bqv, r.x_bup)
            fill_bias(r.b3_cross, r.bup_cross, 1, 1, r.x_bqv, r.x_bup)
        else:
            w = "w" + phase
            loads[w].wait()
            swaps[0, w].wait_recv()
            if phase == "out":
                swap(1, "wqkv")
                swap(1, "wout")
            elif phase == "up":
                swap(1, "wup")
                swap(1, "wdown")

    def keep(s):
        seg = d * segs + s
        doc = r.seg_doc[t, seg]
        within = jnp.int32(0)
        for back in range(1, MAXSEG):
            same = r.seg_doc[t, jnp.maximum(seg - back, 0)] == doc
            within = within + jnp.where(jnp.logical_and(seg >= back, same), 1, 0)
        valid = jnp.minimum(SEG, r.doc_len[t, doc] - SEG * within)
        return lax.broadcasted_iota(jnp.int32, (1, SEG), 1) < valid

    r.x_rows = lambda at: r.xb[at, :].astype(F32)

    def y_block(at, values):
        r.y1[at, :] = values.astype(BF)

    core_forward(r, keep, ready, y_block)
    cls_gather.start(first_of_segments(r.y1, segs).astype(BF))
    hats = first_of_segments(r.xh2, segs)
    hat_gather.start(jnp.concatenate([hats, first_of_segments(r.rs2, segs)], axis=1))
    act_gather.start(first_of_segments(r.g, segs).astype(BF))

    def sib_copy(c):
        slot = lax.rem(c, SLOTS)
        return remote(
            r.sib_out.at[slot], r.sib_in.at[slot], r.sib_send.at[slot], r.sib_recv.at[slot], sibling
        )

    def ring(c):
        return lax.rem(c, RING)

    def stage_one(c, even):
        g = r.gbuf.at[ring(c)]
        source = g.at[:, :, 1 - x] if even else g.at[:, 1 - y]
        return remote(source, r.one_in.at[ring(c)], r.one_send.at[c], r.one_recv.at[c], x_peer if even else y_peer)

    def stage_two(c, even):
        g = r.gbuf.at[ring(c)]
        source = g.at[:, 1 - y, x] if even else g.at[:, y, 1 - x]
        return remote(source, r.two_in.at[ring(c)], r.two_send.at[c], r.two_recv.at[c], y_peer if even else x_peer)

    def stage_three(c, o):
        return remote(
            r.gbuf.at[ring(c), lax.rem(z + o, zs), y, x],
            r.three_in.at[ring(c), o - 1],
            r.three_send.at[c, o - 1],
            r.three_recv.at[c, o - 1],
            z_peers[o - 1],
        )

    def by_parity(c, act):
        @pl.when(lax.rem(c, 2) == 0)
        def _():
            act(True)

        @pl.when(lax.rem(c, 2) == 1)
        def _():
            act(False)

    def progress(c):
        sib_copy(c).wait_recv()
        slot = lax.rem(c, SLOTS)
        r.gbuf[ring(c)] = r.gbuf[ring(c)] + r.sib_in[slot].reshape(zs, 2, 2, shard, CHUNK)

        @pl.when(c < CHUNKS - SLOTS)
        def _():
            pl.semaphore_signal(r.credit, inc=1, device_id=sibling, device_id_type=MESH)

        by_parity(c, lambda even: stage_one(c, even).start())

    def emit(c, left, right, own_at, other_at):
        @pl.when(c >= SLOTS)
        def _():
            sib_copy(c).wait_send()
            pl.semaphore_wait(r.credit, 1)

        slot = lax.rem(c, SLOTS)
        r.sib_out[slot] = mm(left[...], right[:, pl.ds(other_at, CHUNK)]).astype(BF)
        sib_copy(c).start()
        mine = mm(left[...], right[:, pl.ds(own_at, CHUNK)]).astype(BF)
        r.gbuf[ring(c)] = mine.reshape(zs, 2, 2, shard, CHUNK)

    def hooks(name):
        low, high = HOOK_CHUNKS[name]

        @pl.loop(low, high)
        def _(c):
            if name == "out":
                emit(c, r.dmt, r.o, 0, HALF_D)
            elif name == "qkv":
                emit(c, r.xt, r.qkv.at[c - low], 0, HALF_D)
            else:
                base = pl.multiple_of((c - low) * CHUNK, 128)
                left, right = (r.dmt, r.g) if name == "down" else (r.h1t, r.gp)
                emit(c, left, right, base, pl.multiple_of(base + HALF_FF, 128))

            @pl.when(c > low)
            def _():
                progress(c - 1)

    def second(*chunks):
        for c in chunks:
            even = c % 2 == 0
            c = jnp.int32(c)
            stage_one(c, even).wait_recv()
            if even:
                r.gbuf[ring(c), :, :, x] = r.gbuf[ring(c), :, :, x] + r.one_in[ring(c)]
            else:
                r.gbuf[ring(c), :, y] = r.gbuf[ring(c), :, y] + r.one_in[ring(c)]
            stage_two(c, even).start()

    def third(*chunks):
        for c in chunks:
            even = c % 2 == 0
            c = jnp.int32(c)
            stage_two(c, even).wait_recv()
            r.gbuf[ring(c), :, y, x] = r.gbuf[ring(c), :, y, x] + r.two_in[ring(c)]
            for o in range(1, zs):
                stage_three(c, o).start()

    def finish(*chunks):
        for c in chunks:
            even = c % 2 == 0
            at = jnp.int32(c)
            total = r.gbuf[ring(at), z, y, x].astype(F32)
            for o in range(1, zs):
                stage_three(at, o).wait_recv()
                total = total + r.three_in[ring(at), o - 1].astype(F32)
            r.mine[c] = r.mine[c] + total if c < 4 else total
            stage_one(at, even).wait_send()
            stage_two(at, even).wait_send()
            for o in range(1, zs):
                stage_three(at, o).wait_send()

    first_row = lax.broadcasted_iota(jnp.int32, (64, 1), 0)

    def without_first(s, at):
        row = first_row + 64 * lax.rem(s, segs * SEG // (segs * 64))
        return jnp.where(row == 0, 0.0, r.cot[at, :].astype(F32))

    r.small_common = r.small
    back_norm_two(r, without_first)
    hooks("down")

    q = Names(
        **{k: getattr(r, "q_" + k) for k in CROSS},
        g=r.g.at[0:SEG],
        gp=r.g.at[SEG : 2 * SEG],
        gain=r.gain_cross,
        bt=r.bt_cross,
        b3=r.b3_cross,
        bup=r.bup_cross,
        qv_sum=r.qv_sum,
    )
    q.dr, q.dm, q.small_common = q.h1, q.h1b, r.small1
    slots = q.xb.shape[0]
    total_docs = slots // MAXSEG
    total_segs = dp * segs
    for w in WEIGHTS:
        swaps[1, w].wait_recv()
    stream = Stream(r)
    stream.prime("qkv")
    stream.prime("out")

    doc = jnp.where(t == 0, r.seg_doc_v[0:1, :], r.seg_doc_v[1:2, :])
    below = lax.broadcasted_iota(jnp.int32, (total_segs, total_segs), 0)
    across = lax.broadcasted_iota(jnp.int32, (total_segs, total_segs), 1)

    def column(row):
        wide = jnp.broadcast_to(row, (total_segs, total_segs))
        return jnp.sum(jnp.where(below == across, wide, 0.0), axis=1, keepdims=True)

    doc_f = doc.astype(F32)
    earlier = jnp.logical_and(column(doc_f) == doc_f, below < across)
    within = jnp.sum(jnp.where(earlier, 1.0, 0.0), axis=0, keepdims=True).astype(jnp.int32)
    moved = doc + total_docs // 2
    moved = jnp.where(moved >= total_docs, moved - total_docs, moved)
    slot_of = (jnp.where((doc & 1) == 1, moved, doc) * MAXSEG + within).astype(F32)
    slot_ids = lax.broadcasted_iota(jnp.int32, (slots, total_segs), 0).astype(F32)
    deal = jnp.where(slot_ids == slot_of, 1.0, 0.0).astype(BF)
    slot_row = lax.broadcasted_iota(jnp.int32, (total_segs, slots), 1).astype(F32)
    r.undeal[...] = jnp.where(slot_row == column(slot_of), 1.0, 0.0).astype(BF)
    pick_row = lax.broadcasted_iota(jnp.int32, (8, total_segs), 0)
    pick_seg = lax.broadcasted_iota(jnp.int32, (8, total_segs), 1)
    picked = jnp.logical_and(pick_row < segs, pick_seg == d * segs + pick_row)
    r.back[...] = mm(jnp.where(picked, 1.0, 0.0).astype(BF), r.undeal[...]).astype(BF)
    live = mm_nt(jnp.ones((8, total_segs), BF), deal)[0:1] > 0.5
    key_doc = lax.broadcasted_iota(jnp.int32, (SEG, SEG), 1) >> 3
    row_doc = lax.broadcasted_iota(jnp.int32, (SEG, SEG), 0) >> 3
    r.allowed[...] = jnp.where(jnp.logical_and(key_doc == row_doc, live), 1.0, 0.0)

    cot_gather.arrived()
    cot_gather.rows_into(r.rows64)
    q.dy[...] = mm(deal, r.rows64[...].astype(BF))
    cls_gather.arrived()
    cls_gather.rows_into(r.rows64)
    q.x32[...] = mm(deal, r.rows64[...].astype(BF)) + jnp.concatenate(
        [r.seg_pos[...]] * total_docs, axis=0
    )
    q.xb[...] = q.x32[...].astype(BF)
    q.x_rows = lambda at: q.x32[at, :]
    transpose_into(q.xt, q.xb, slots)
    progress(jnp.int32(3))

    def cross_hooks(name):
        low, high = HOOK_CHUNKS[name]
        for c in range(low, high):
            left, (right, own_at, other_at) = chunk_operands(q, c)
            mine = left[pl.ds(pl.multiple_of(d * shard, 16), shard), :]
            r.shard1[c] = mm(mine, right[:, own_at : own_at + CHUNK])
            r.shard_out[c] = mm(mine, right[:, other_at : other_at + CHUNK]).astype(BF)

    def pump(point):
        if point == "up":
            second(0, 1)
        elif point == "back_down":
            second(2, 3)
        elif point == "attend_back":
            third(0, 1)

    cross_layer(r, q, stream, lambda s: r.allowed[...] > 0.5, pump, cross_hooks)
    r.small, keep_small = r.small1, r.small
    pack_halves(r)
    r.small = keep_small
    total = q.dr[0:MAXSEG, :]
    for j in range(1, total_docs):
        total = total + q.dr[j * MAXSEG : (j + 1) * MAXSEG, :]
    for k in range(MAXSEG):
        r.small1[12 + k] = total[k : k + 1, :]
    r.ret[...] = mm(r.back[...], q.yb[...])
    low = q.dr[...].astype(BF)
    r.dc[...] = mm(r.back[...], low)

    gain_sum = jnp.zeros((1, D), F32)
    shift_sum, low_sum = gain_sum, gain_sum
    top = lax.broadcasted_iota(jnp.int32, (16, 1), 0) == 0
    for s in range(segs):
        at = slice(s * SEG, s * SEG + 16)
        grad = jnp.where(top, r.dc[s : s + 1, :], 0.0)
        hat = r.xh2[at, :]
        out = jnp.where(top, norm_back(grad, hat, r.rs2[at, 0:1], r.gain[1]), 0.0)
        out_low = out.astype(BF)
        r.dr[at, :] = jnp.where(top, out, r.dr[at, :])
        r.dm[at, :] = jnp.where(top, out_low.astype(F32), r.dm[at, :].astype(F32)).astype(BF)
        gain_sum = gain_sum + jnp.sum(grad * hat, axis=0, keepdims=True)
        shift_sum = shift_sum + jnp.sum(grad, axis=0, keepdims=True)
        low_sum = low_sum + jnp.sum(out_low.astype(F32), axis=0, keepdims=True)
        r.y1[at, :] = jnp.where(top, r.ret[s : s + 1, :], r.y1[at, :].astype(F32)).astype(BF)
    r.small_common[1] = r.small_common[1] + gain_sum
    r.small_common[5] = r.small_common[5] + shift_sum
    r.small_common[3] = r.small_common[3] + low_sum
    outs = [copies.start(r.y1, r.o_enc.at[t])]
    enc_swap = remote(r.y1, r.o_enc.at[t], r.misc_send.at[0], r.misc_recv.at[0], sibling)
    enc_swap.start()

    hat_gather.arrived()
    hat_gather.rows_into(r.hat64)
    act_gather.arrived()
    act_gather.rows_into(r.act64)
    all_grads = mm(r.undeal[...], low)
    late = norm_back(all_grads, r.hat64[:, 0:D], r.hat64[:, D : D + 1], r.gain[1]).astype(BF)
    r.late[0:total_segs, :] = late
    r.late[total_segs:, :] = jnp.zeros((SEG - total_segs, D), BF)
    transpose_into(r.late_t, r.late, SEG)
    mine = r.late_t[pl.ds(pl.multiple_of(d * shard, 16), shard), 0:total_segs]
    for c in range(4):
        for half in range(2):
            cols = slice(half * HALF_FF + c * CHUNK, half * HALF_FF + (c + 1) * CHUNK)
            part = mm(mine, r.act64[:, cols].astype(BF))
            if half == 0:
                r.mine[c] = part
            else:
                r.shard_out[CHUNKS + c] = part.astype(BF)
    cross_swap = [
        remote(r.shard_out, r.shard_in, r.misc_send.at[1], r.misc_recv.at[1], sibling),
        remote(r.small1.at[0:6], r.small1_in.at[0:6], r.misc_send.at[2], r.misc_recv.at[2], sibling),
        remote(r.small1.at[9:20], r.small1_in.at[6:17], r.misc_send.at[3], r.misc_recv.at[3], sibling),
    ]
    for copy in cross_swap:
        copy.start()

    third(2, 3)
    grad_hidden(r)
    hooks("up")
    grad_middle(r)
    progress(jnp.int32(7))
    for copy in cross_swap:
        copy.wait()
    finish(0, 1, 2, 3)
    for c in range(CHUNKS):
        r.shard1[c] = r.shard1[c] + r.shard_in[c].astype(F32)
    for c in range(4):
        r.mine[c] = r.mine[c] + r.shard_in[CHUNKS + c].astype(F32)
    r.o_small[9:26] = (
        jnp.concatenate([r.small1[0:9], r.small1[12:20]], axis=0) + r.small1_in[...]
    )
    outs.append(copies.start(r.shard1, r.o_shard.at[1]))
    back_norm_one(r)
    second(4)
    hooks("out")
    grad_heads(r)
    progress(jnp.int32(8))

    def between(s):
        if s == 1:
            second(5)
        if s == 3:
            second(6, 7)

    attend_back(r, between)
    bias_heads(r)
    hooks("qkv")
    pack_halves(r)
    small_swap = [
        remote(r.small.at[0:6], r.small_in.at[0:6], r.misc_send.at[4], r.misc_recv.at[4], sibling),
        remote(r.small.at[9:12], r.small_in.at[6:9], r.misc_send.at[5], r.misc_recv.at[5], sibling),
    ]
    for copy in small_swap:
        copy.start()
    progress(jnp.int32(11))
    third(4, 5)
    grad_input(r)
    grad_swap = remote(r.dr, r.o_grad.at[t], r.misc_send.at[6], r.misc_recv.at[6], sibling)
    grad_swap.start()
    outs.append(copies.start(r.dr, r.o_grad.at[t]))
    for copy in small_swap:
        copy.wait()
    r.total[...] = r.small[0:9] + r.small_in[...]
    x_small = remote(r.total, r.x_small, r.misc_send.at[7], r.misc_recv.at[7], x_peer)
    x_small.start()
    third(6, 7)
    second(8)
    x_small.wait()
    r.total_x[...] = r.total[...] + r.x_small[...]
    y_small = remote(r.total_x, r.y_small, r.misc_send.at[8], r.misc_recv.at[8], y_peer)
    y_small.start()
    second(9)
    finish(4, 5, 6, 7)
    y_small.wait()
    r.z_small[z] = r.total_x[...] + r.y_small[...]
    z_sends = []
    for o in range(1, zs):
        z_sends.append(
            remote(r.z_small.at[z], r.z_small.at[z], r.z_send.at[o], r.z_recv.at[z], z_peers[o - 1])
        )
        z_sends[-1].start()
    second(10, 11)
    third(8, 9, 10, 11)
    for o in range(1, zs):
        source = lax.rem(z + o, zs)
        block = r.z_small.at[source]
        remote(block, block, r.z_send.at[o], r.z_recv.at[source], z_peers[o - 1]).wait_recv()
    total = r.z_small[0]
    for k in range(1, zs):
        total = total + r.z_small[k]
    r.o_small[0:9] = total
    finish(8, 9, 10, 11)
    outs.append(copies.start(r.mine, r.o_shard.at[0]))

    for copy in z_sends:
        copy.wait_send()
    for c in range(CHUNKS - SLOTS, CHUNKS):
        sib_copy(jnp.int32(c)).wait_send()
    for gathered in (cot_gather, cls_gather, hat_gather, act_gather):
        for copy in gathered.sends:
            copy.wait_send()
    for copy in swap_bias:
        copy.wait_send()
    for copy in swaps.values():
        copy.wait_send()
    grad_swap.wait()
    enc_swap.wait()
    for copy in outs:
        copy.wait()


CROSS = ("xb", "x32", "xt", "h1t", "h1b", "h1", "qkv", "o", "p", "xh1", "rs1", "xh2", "rs2", "yb", "dy", "dmt")
WEIGHT_SCRATCH = dict(
    wqkv=((3, D, D), BF), wout=((D, D), BF), wup=((D, FF), BF), wdown=((FF, D), BF)
)
BACK_SCRATCH = dict(qv_sum=((2, 1, D), F32), bup_sum=((1, FF), F32))


def saved_shapes(rows):
    return dict(
        xt=((D, rows), BF),
        h1t=((D, rows), BF),
        qkv=((3, rows, D), BF),
        o=((rows, D), BF),
        p=((rows // SEG, PAIRS, SEG, 2 * SEG), BF),
        xh1=((rows, D), F32),
        rs1=((rows, SEG), F32),
        g=((rows, FF), BF),
        gp=((rows, FF), BF),
        xh2=((rows, D), F32),
        rs2=((rows, SEG), F32),
    )


def forward_shapes(rows):
    return dict(
        xb=((rows, D), BF),
        h1=((rows, D), F32),
        h1b=((rows, D), BF),
        b3=((3, 1, D), F32),
        bup=((1, FF), F32),
    )


def vmem(table):
    return [pltpu.VMEM(shape, kind) for shape, kind in table.values()]


def arrays(table):
    return [jax.ShapeDtypeStruct(shape, kind) for shape, kind in table.values()]


def run_whole(dp, inputs):
    hbm = pl.BlockSpec(memory_space=pl.ANY)
    small = pl.BlockSpec(memory_space=pltpu.VMEM)
    smem = pl.BlockSpec(memory_space=pltpu.SMEM)
    batches, rows, _ = inputs["tokens"].shape
    slots = inputs["doc_len"].shape[1] * MAXSEG
    segs = rows // SEG
    total_segs = dp * segs
    zs = dp // 4
    shard = D // dp
    outs = dict(
        o_enc=((batches, rows, D), BF),
        o_grad=((batches, rows, D), F32),
        o_shard=((2, CHUNKS, shard, CHUNK), F32),
        o_small=((26, 1, D), F32),
    )
    outs.update({"f_" + w: (inputs["a_" + w].shape[1:], BF) for w in WEIGHTS})
    scratch = dict(saved_shapes(rows))
    scratch.update(WEIGHT_SCRATCH)
    scratch.update(forward_shapes(rows))
    scratch.update(BACK_SCRATCH)
    cross = dict(saved_shapes(slots))
    cross.update(forward_shapes(slots))
    cross.update(
        x32=((slots, D), F32), yb=((slots, D), BF), dy=((slots, D), F32), dmt=((D, slots), BF)
    )
    scratch.update({"q_" + k: cross[k] for k in CROSS})
    scratch.update(
        b3_cross=((3, 1, D), F32),
        bup_cross=((1, FF), F32),
        gain=((2, 1, D), F32),
        gain_cross=((2, 1, D), F32),
        bt=((4, 1, D), F32),
        bt_cross=((4, 1, D), F32),
        x_bqv=((2, 2, HALF_D), F32),
        x_bup=((2, HALF_FF), F32),
        cot=((rows, D), BF),
        dmt=((D, rows), BF),
        wide=((3, D, 256), BF),
        tall=((3, 256, D), BF),
        cot_all=((dp, segs, D), BF),
        cls_all=((dp, segs, D), BF),
        hat_all=((dp, segs, D + SEG), F32),
        act_all=((dp, segs, FF), BF),
        rows64=((total_segs, D), F32),
        hat64=((total_segs, D + SEG), F32),
        act64=((total_segs, FF), F32),
        undeal=((total_segs, slots), BF),
        back=((8, slots), BF),
        allowed=((SEG, SEG), F32),
        ret=((8, D), F32),
        dc=((8, D), F32),
        late=((SEG, D), BF),
        late_t=((D, SEG), BF),
        small=((12, 1, D), F32),
        small1=((20, 1, D), F32),
        small_in=((9, 1, D), F32),
        small1_in=((17, 1, D), F32),
        total=((9, 1, D), F32),
        total_x=((9, 1, D), F32),
        x_small=((9, 1, D), F32),
        y_small=((9, 1, D), F32),
        z_small=((zs, 9, 1, D), F32),
        shard1=((CHUNKS, shard, CHUNK), F32),
        shard_out=((CHUNKS + 4, shard, CHUNK), BF),
        shard_in=((CHUNKS + 4, shard, CHUNK), BF),
        mine=((CHUNKS, shard, CHUNK), F32),
        gbuf=((RING, zs, 2, 2, shard, CHUNK), BF),
        sib_out=((SLOTS, D, CHUNK), BF),
        sib_in=((SLOTS, D, CHUNK), BF),
        one_in=((RING, zs, 2, shard, CHUNK), BF),
        two_in=((RING, zs, shard, CHUNK), BF),
        three_in=((RING, zs - 1, shard, CHUNK), BF),
    )
    dma = pltpu.SemaphoreType.DMA
    sems = dict(
        local_sem=dma((20,)),
        w_send=dma((2, 5)),
        w_recv=dma((2, 5)),
        wide_sem=dma((3, 2)),
        tall_sem=dma((3, 2)),
        g_send=dma((4, dp)),
        g_recv=dma((4, dp)),
        misc_send=dma((9,)),
        misc_recv=dma((9,)),
        sib_send=dma((SLOTS,)),
        sib_recv=dma((SLOTS,)),
        one_send=dma((CHUNKS,)),
        one_recv=dma((CHUNKS,)),
        two_send=dma((CHUNKS,)),
        two_recv=dma((CHUNKS,)),
        three_send=dma((CHUNKS, zs - 1)),
        three_recv=dma((CHUNKS, zs - 1)),
        z_send=dma((zs,)),
        z_recv=dma((zs,)),
        credit=pltpu.SemaphoreType.REGULAR,
    )
    ins = dict(
        seg_doc=smem, doc_len=smem, seg_doc_v=small, tokens=hbm, cotangent=hbm, b_qv=small, b_up=small,
        norm_gain=small, bias_terms=small, seg_pos=small,
        a_wqkv=hbm, a_wout=hbm, a_wup=hbm, a_wdown=hbm,
    )
    names = list(ins) + list(outs) + list(scratch) + list(sems)
    result = pl.pallas_call(
        partial(whole_kernel, dp, names),
        out_shape=arrays(outs),
        in_specs=list(ins.values()),
        out_specs=[hbm, hbm, hbm, small] + [hbm] * 4,
        scratch_shapes=vmem(scratch) + list(sems.values()),
        compiler_params=pltpu.CompilerParams(
            collective_id=0, has_side_effects=True, vmem_limit_bytes=VMEM_LIMIT
        ),
        name="both_layers",
    )(*[inputs[k] for k in ins])
    return dict(zip(outs, result))


VMEM_LIMIT = 64 << 20


def finish_kernel(shard, small, g_qkv, g_bqv, g_out, g_up, g_bup, g_down, g_gain, g_terms, g_pos):
    for layer in range(2):
        at = 9 * layer
        for c in range(4):
            g_down[layer, :, c * CHUNK : (c + 1) * CHUNK] = shard[layer, c]
            g_up[layer, :, c * CHUNK : (c + 1) * CHUNK] = shard[layer, 4 + c]
        g_out[layer] = shard[layer, 8]
        for c in range(3):
            g_qkv[layer, c] = shard[layer, 9 + c]
        for k in range(2):
            g_gain[layer, k : k + 1, :] = small[at + k]
            g_bqv[layer, k : k + 1, :] = small[at + 6, :, k * HALF_D : (k + 1) * HALF_D]
            g_bup[layer : layer + 1, k * D : (k + 1) * D] = small[at + 7 + k]
        for k in range(4):
            g_terms[layer, k : k + 1, :] = small[at + 2 + k]
    for k in range(MAXSEG):
        g_pos[k : k + 1, :] = small[18 + k]


def fused(tokens, seg_doc, doc_len, w_qkv, b_qv, w_out, w_up, b_up, w_down, norm_gain, bias_terms, seg_pos, cotangent):
    dp = lax.axis_size("dp")
    whole = run_whole(
        dp,
        dict(
            seg_doc=seg_doc, doc_len=doc_len, seg_doc_v=seg_doc, tokens=tokens, cotangent=cotangent,
            b_qv=b_qv, b_up=b_up, norm_gain=norm_gain, bias_terms=bias_terms,
            seg_pos=seg_pos, a_wqkv=w_qkv, a_wout=w_out, a_wup=w_up, a_wdown=w_down,
        ),
    )
    rows = D // dp
    shapes = [
        (2, 3, rows, HALF_D), (2, 2, HALF_D), (2, rows, HALF_D), (2, rows, HALF_FF), (2, HALF_FF),
        (2, rows, HALF_FF), (2, 2, D), (2, 4, D), (MAXSEG, D),
    ]
    small = pl.BlockSpec(memory_space=pltpu.VMEM)
    grads = pl.pallas_call(
        finish_kernel,
        out_shape=[jax.ShapeDtypeStruct(shape, F32) for shape in shapes],
        in_specs=[small] * 2,
        out_specs=[small] * len(shapes),
        compiler_params=pltpu.CompilerParams(vmem_limit_bytes=32 << 20),
        name="lay_out",
    )(whole["o_shard"], whole["o_small"])
    g_qkv, g_bqv, g_out, g_up, g_bup, g_down, g_gain, g_terms, g_pos = grads
    return (
        whole["o_enc"], whole["o_grad"], g_qkv, g_bqv, g_out.transpose(0, 2, 1), g_up, g_bup,
        g_down.transpose(0, 2, 1), g_gain, g_terms, g_pos,
    )


def solution(mesh):
    in_specs = (
        P(None, "dp", None),
        P(),
        P(),
        P(None, None, None, "tensor"),
        P(None, None, "tensor"),
        P(None, "tensor", None),
        P(None, None, "tensor"),
        P(None, "tensor"),
        P(None, "tensor", None),
        P(),
        P(),
        P(),
        P(None, "dp", None),
    )
    out_specs = (
        P(None, "dp", None),
        P(None, "dp", None),
        P(None, None, "dp", "tensor"),
        P(None, None, "tensor"),
        P(None, "tensor", "dp"),
        P(None, "dp", "tensor"),
        P(None, "tensor"),
        P(None, "tensor", "dp"),
        P(),
        P(),
        P(),
    )
    body = fused if mesh.shape["dp"] == 16 and mesh.shape["tensor"] == 2 else local
    return jax.shard_map(body, mesh=mesh, in_specs=in_specs, out_specs=out_specs, check_vma=False)
```

```python
from functools import partial, reduce

import jax
import jax.numpy as jnp
from jax import lax
from jax.experimental import pallas as pl
from jax.experimental.pallas import tpu as pltpu
from jax.sharding import PartitionSpec as P

HEAD_DIM = 64
SEG = 128
MAXSEG = 8


norm_eps = 1e-05
masked_score = -1e30


def norm_rows(values, gain, shift):
    centre = values - jnp.mean(values, axis=-1, keepdims=True)
    spread = jnp.mean(centre * centre, axis=-1, keepdims=True)
    return centre * lax.rsqrt(spread + norm_eps) * gain + shift


def exact_gelu(values):
    return jax.nn.gelu(values, approximate=False)


def my_rows(values):
    part_rows = values.shape[0] // lax.axis_size("tensor")
    return lax.dynamic_slice_in_dim(values, lax.axis_index("tensor") * part_rows, part_rows, 0)


def attn_scores(queries, key_rows, key_mask, split_shape):
    raw = jnp.einsum(
        "glhd,gmhd->ghlm",
        queries.reshape(split_shape),
        key_rows.reshape(split_shape),
        preferred_element_type=jnp.float32,
    ) * HEAD_DIM ** (-0.5)
    return jnp.where(key_mask[:, None, None, :], raw, masked_score)


def layer_forward(inputs, key_mask, weights):
    w_qkv, b_qv, w_out, w_up, b_up, w_down, norm_gain, bias_terms = weights
    groups, span = key_mask.shape
    row_count = inputs.shape[0]
    local_width = w_qkv.shape[2]
    split_shape = (groups, span, local_width // HEAD_DIM, HEAD_DIM)
    inputs_b = inputs.astype(jnp.bfloat16)
    projected = jnp.einsum("rd,cde->cre", inputs_b, w_qkv, preferred_element_type=jnp.float32)
    queries = (projected[0] + b_qv[0]).astype(jnp.bfloat16)
    key_rows = projected[1].astype(jnp.bfloat16)
    value_rows = (projected[2] + b_qv[1]).astype(jnp.bfloat16)
    scores = attn_scores(queries, key_rows, key_mask, split_shape)
    row_max = jnp.max(scores, axis=-1, keepdims=True)
    log_total = row_max + jnp.log(jnp.sum(jnp.exp(scores - row_max), axis=-1, keepdims=True))
    attn_probs = jnp.exp(scores - log_total).astype(jnp.bfloat16)
    head_out = jnp.einsum(
        "ghlm,gmhd->glhd",
        attn_probs,
        value_rows.reshape(split_shape),
        preferred_element_type=jnp.float32,
    )
    head_out = head_out.reshape(row_count, local_width).astype(jnp.bfloat16)
    attn_part = (
        lax.psum_scatter(
            jnp.dot(head_out, w_out, preferred_element_type=jnp.float32),
            "tensor",
            scatter_dimension=0,
            tiled=True,
        )
        + bias_terms[0]
    )
    resid_one = lax.all_gather(my_rows(inputs) + attn_part, "tensor", axis=0, tiled=True)
    hidden = norm_rows(resid_one, norm_gain[0], bias_terms[2])
    hidden_b = hidden.astype(jnp.bfloat16)
    pre_act = jnp.dot(hidden_b, w_up, preferred_element_type=jnp.float32) + b_up
    active_b = exact_gelu(pre_act).astype(jnp.bfloat16)
    mlp_part = (
        lax.psum_scatter(
            jnp.dot(active_b, w_down, preferred_element_type=jnp.float32),
            "tensor",
            scatter_dimension=0,
            tiled=True,
        )
        + bias_terms[1]
    )
    resid_two = lax.all_gather(my_rows(hidden) + mlp_part, "tensor", axis=0, tiled=True)
    stored = (
        inputs_b,
        queries,
        key_rows,
        value_rows,
        log_total,
        head_out,
        resid_one,
        hidden_b,
        pre_act,
        active_b,
        resid_two,
    )
    return (norm_rows(resid_two, norm_gain[1], bias_terms[3]), stored)


def layer_backward(grad_out, key_mask, weights, stored):
    w_qkv, b_qv, w_out, w_up, b_up, w_down, norm_gain, bias_terms = weights
    (
        inputs_b,
        queries,
        key_rows,
        value_rows,
        log_total,
        head_out,
        resid_one,
        hidden_b,
        pre_act,
        active_b,
        resid_two,
    ) = stored
    groups, span = key_mask.shape
    row_count, local_width = queries.shape
    split_shape = (groups, span, local_width // HEAD_DIM, HEAD_DIM)
    forward_two, norm_two = jax.vjp(norm_rows, resid_two, norm_gain[1], bias_terms[3])
    grad_two, gain_two, shift_two = norm_two(grad_out)
    grad_mlp = grad_two.astype(jnp.bfloat16)
    grad_wdown = jnp.dot(active_b.T, grad_mlp, preferred_element_type=jnp.float32)
    grad_act = jnp.dot(grad_mlp, w_down.T, preferred_element_type=jnp.float32)
    forward_gelu, gelu_back = jax.vjp(exact_gelu, pre_act)
    grad_pre = gelu_back(grad_act)[0].astype(jnp.bfloat16)
    grad_wup = jnp.dot(hidden_b.T, grad_pre, preferred_element_type=jnp.float32)
    up_part = lax.psum_scatter(
        jnp.dot(grad_pre, w_up.T, preferred_element_type=jnp.float32),
        "tensor",
        scatter_dimension=0,
        tiled=True,
    )
    grad_hidden = lax.all_gather(my_rows(grad_two) + up_part, "tensor", axis=0, tiled=True)
    forward_one, norm_one = jax.vjp(norm_rows, resid_one, norm_gain[0], bias_terms[2])
    grad_one, gain_one, shift_one = norm_one(grad_hidden)
    grad_attn = grad_one.astype(jnp.bfloat16)
    grad_wout = jnp.dot(head_out.T, grad_attn, preferred_element_type=jnp.float32)
    grad_heads = (
        jnp.dot(grad_attn, w_out.T, preferred_element_type=jnp.float32)
        .astype(jnp.bfloat16)
        .reshape(split_shape)
    )
    scores = attn_scores(queries, key_rows, key_mask, split_shape)
    attn_probs = jnp.exp(scores - log_total)
    grad_probs = jnp.einsum(
        "glhd,gmhd->ghlm",
        grad_heads,
        value_rows.reshape(split_shape),
        preferred_element_type=jnp.float32,
    )
    grad_values = jnp.einsum(
        "ghlm,glhd->gmhd",
        attn_probs.astype(jnp.bfloat16),
        grad_heads,
        preferred_element_type=jnp.float32,
    )
    grad_scores = (
        attn_probs * (grad_probs - jnp.sum(attn_probs * grad_probs, axis=-1, keepdims=True))
    ).astype(jnp.bfloat16)
    inv_root = HEAD_DIM ** (-0.5)
    grad_queries = (
        jnp.einsum(
            "ghlm,gmhd->glhd",
            grad_scores,
            key_rows.reshape(split_shape),
            preferred_element_type=jnp.float32,
        )
        * inv_root
    )
    grad_keys = (
        jnp.einsum(
            "ghlm,glhd->gmhd",
            grad_scores,
            queries.reshape(split_shape),
            preferred_element_type=jnp.float32,
        )
        * inv_root
    )
    grad_qkv = (
        jnp.stack([grad_queries, grad_keys, grad_values])
        .reshape(3, row_count, local_width)
        .astype(jnp.bfloat16)
    )
    grad_wqkv = jnp.einsum("rd,cre->cde", inputs_b, grad_qkv, preferred_element_type=jnp.float32)
    qkv_part = lax.psum_scatter(
        jnp.einsum("cre,cde->rd", grad_qkv, w_qkv, preferred_element_type=jnp.float32).astype(
            jnp.bfloat16
        ),
        "tensor",
        scatter_dimension=0,
        tiled=True,
    ).astype(jnp.float32)
    grad_inputs = lax.all_gather(
        (my_rows(grad_one) + qkv_part).astype(jnp.bfloat16), "tensor", axis=0, tiled=True
    ).astype(jnp.float32)
    grad_bqv = jnp.stack(
        [
            jnp.sum(grad_qkv[0].astype(jnp.float32), axis=0),
            jnp.sum(grad_qkv[2].astype(jnp.float32), axis=0),
        ]
    )
    grad_bup = jnp.sum(grad_pre.astype(jnp.float32), axis=0)
    grad_gain = jnp.stack([gain_one, gain_two])
    grad_shift = jnp.stack(
        [
            jnp.sum(grad_attn.astype(jnp.float32), axis=0),
            jnp.sum(grad_mlp.astype(jnp.float32), axis=0),
            shift_one,
            shift_two,
        ]
    )
    return (
        grad_inputs,
        (grad_wqkv, grad_bqv, grad_wout, grad_wup, grad_bup, grad_wdown, grad_gain, grad_shift),
    )


def deal_map(doc_ids, total_docs):
    return jnp.where(doc_ids % 2 == 1, (doc_ids + total_docs // 2) % total_docs, doc_ids)


def local_plan(seg_order, doc_lengths, seg_local, doc_local):
    total_docs = doc_lengths.shape[0]
    my_index = lax.axis_index("dp")
    doc_ids = jnp.arange(total_docs, dtype=jnp.int32)
    owner_pos = deal_map(doc_ids, total_docs)
    starts = jnp.sum((seg_order[None, :] < doc_ids[:, None]).astype(jnp.int32), axis=1)
    counts = jnp.sum((seg_order[None, :] == doc_ids[:, None]).astype(jnp.int32), axis=1)
    my_segments = my_index * seg_local + jnp.arange(seg_local, dtype=jnp.int32)
    seg_owner_doc = lax.dynamic_slice_in_dim(seg_order, my_index * seg_local, seg_local)
    seg_hot = seg_owner_doc[:, None] == doc_ids[None, :]
    my_start = jnp.sum(jnp.where(seg_hot, starts[None, :], 0), axis=1)
    my_length = jnp.sum(jnp.where(seg_hot, doc_lengths[None, :], 0), axis=1)
    my_owner = jnp.sum(jnp.where(seg_hot, owner_pos[None, :], 0), axis=1)
    within = my_segments - my_start
    valid_tokens = jnp.minimum(SEG, my_length - within * SEG)
    tok_mask = jnp.arange(SEG, dtype=jnp.int32)[None, :] < valid_tokens[:, None]
    src_slot = my_owner * MAXSEG + within
    my_deal = deal_map(my_index * doc_local + jnp.arange(doc_local, dtype=jnp.int32), total_docs)
    deal_hot = my_deal[:, None] == doc_ids[None, :]
    own_start = jnp.sum(jnp.where(deal_hot, starts[None, :], 0), axis=1)
    own_count = jnp.sum(jnp.where(deal_hot, counts[None, :], 0), axis=1)
    slot_index = jnp.arange(MAXSEG, dtype=jnp.int32)
    cross_mask = slot_index[None, :] < own_count[:, None]
    target = jnp.where(cross_mask, own_start[:, None] + slot_index[None, :], -1).reshape(-1)
    return (tok_mask, cross_mask, target, src_slot)


def picker(index_map, shard_rows):
    positions = jnp.arange(shard_rows.shape[0], dtype=jnp.int32)
    selector = (index_map[:, None] == positions[None, :]).astype(jnp.bfloat16)
    return jnp.dot(selector, shard_rows, preferred_element_type=jnp.float32)


def spreader(index_map, source_rows, row_span):
    positions = jnp.arange(row_span, dtype=jnp.int32)
    selector = (positions[:, None] == index_map[None, :]).astype(jnp.bfloat16)
    return jnp.dot(selector, source_rows, preferred_element_type=jnp.float32)


def add_terms(left, right):
    return jax.tree.map(jnp.add, left, right)


def local(
    tokens,
    seg_doc,
    doc_len,
    w_qkv,
    b_qv,
    w_out,
    w_up,
    b_up,
    w_down,
    norm_gain,
    bias_terms,
    seg_pos,
    cotangent,
):
    batches, local_rows, width = tokens.shape
    seg_local = local_rows // SEG
    doc_local = doc_len.shape[1] // lax.axis_size("dp")
    slot_rows = doc_local * MAXSEG

    def layer_weights(level):
        return (
            w_qkv[level],
            b_qv[level],
            w_out[level],
            w_up[level],
            b_up[level],
            w_down[level],
            norm_gain[level],
            bias_terms[level],
        )

    seg_weights = layer_weights(0)
    cross_weights = layer_weights(1)
    encoded = []
    grad_tokens = []
    seg_grads = []
    cross_grads = []
    pos_grads = []
    for batch_index in range(batches):
        tok_mask, cross_mask, target, src_slot = local_plan(
            seg_doc[batch_index], doc_len[batch_index], seg_local, doc_local
        )
        seg_out, seg_stored = layer_forward(
            tokens[batch_index].astype(jnp.float32), tok_mask, seg_weights
        )
        seg_cube = seg_out.reshape(seg_local, SEG, width)
        cls_rows = seg_cube[:, 0].astype(jnp.bfloat16)
        collected = picker(target, lax.all_gather(cls_rows, "dp", axis=0, tiled=True))
        cross_in = (collected.reshape(doc_local, MAXSEG, width) + seg_pos[None]).reshape(
            slot_rows, width
        )
        cross_out, cross_stored = layer_forward(cross_in, cross_mask, cross_weights)
        returned = picker(
            src_slot, lax.all_gather(cross_out.astype(jnp.bfloat16), "dp", axis=0, tiled=True)
        )
        encoded.append(
            seg_cube.at[:, 0].set(returned).reshape(local_rows, width).astype(jnp.bfloat16)
        )
        grad_cube = cotangent[batch_index].astype(jnp.float32).reshape(seg_local, SEG, width)
        grad_returned = grad_cube[:, 0].astype(jnp.bfloat16)
        grad_cross = lax.psum_scatter(
            spreader(src_slot, grad_returned, slot_rows * lax.axis_size("dp")),
            "dp",
            scatter_dimension=0,
            tiled=True,
        )
        grad_cross_in, cross_terms = layer_backward(
            grad_cross, cross_mask, cross_weights, cross_stored
        )
        pos_grads.append(jnp.sum(grad_cross_in.reshape(doc_local, MAXSEG, width), axis=0))
        grad_sent = grad_cross_in.astype(jnp.bfloat16)
        cross_grads.append(cross_terms)
        grad_cls = lax.psum_scatter(
            spreader(target, grad_sent, seg_local * lax.axis_size("dp")),
            "dp",
            scatter_dimension=0,
            tiled=True,
        )
        grad_seg = grad_cube.at[:, 0].set(grad_cls).reshape(local_rows, width)
        grad_inputs, seg_terms = layer_backward(grad_seg, tok_mask, seg_weights, seg_stored)
        grad_tokens.append(grad_inputs)
        seg_grads.append(seg_terms)
    seg_total = reduce(add_terms, seg_grads)
    cross_total = reduce(add_terms, cross_grads)
    pos_total = reduce(jnp.add, pos_grads)
    big_grads = (
        lax.psum_scatter(
            jnp.stack([seg_total[0], cross_total[0]]), "dp", scatter_dimension=2, tiled=True
        ),
        lax.psum_scatter(
            jnp.stack([seg_total[2], cross_total[2]]), "dp", scatter_dimension=2, tiled=True
        ),
        lax.psum_scatter(
            jnp.stack([seg_total[3], cross_total[3]]), "dp", scatter_dimension=1, tiled=True
        ),
        lax.psum_scatter(
            jnp.stack([seg_total[5], cross_total[5]]), "dp", scatter_dimension=2, tiled=True
        ),
    )
    small = lax.psum(
        (
            jnp.stack([seg_total[1], cross_total[1]]),
            jnp.stack([seg_total[4], cross_total[4]]),
            jnp.stack([seg_total[6], cross_total[6]]),
            jnp.stack([seg_total[7], cross_total[7]]),
            pos_total,
        ),
        "dp",
    )
    return (
        jnp.stack(encoded),
        jnp.stack(grad_tokens),
        big_grads[0],
        small[0],
        big_grads[1],
        big_grads[2],
        small[1],
        big_grads[3],
        small[2],
        small[3],
        small[4],
    )


BF = jnp.bfloat16
F32 = jnp.float32
D = 768
FF = 3072
HALF_FF = FF // 2
HALF_D = D // 2
CHUNK = 384
CHUNKS = 12
PAIRS = 6
MESH = pl.DeviceIdType.MESH
ROOT_HALF = 0.7071067811865476
PDF_SCALE = 0.3989422804014327


class Names:
    def __init__(self, **kw):
        self.__dict__.update(kw)


def mm(left, right):
    return jnp.dot(left, right, preferred_element_type=F32)


def mm_nt(left, right):
    return lax.dot_general(left, right, (((1,), (1,)), ((), ())), preferred_element_type=F32)


def span(index, size):
    return pl.ds(pl.multiple_of(index * size, size), size)


def row_norm(rows):
    centre = rows - jnp.mean(rows, axis=-1, keepdims=True)
    spread = jnp.mean(centre * centre, axis=-1, keepdims=True)
    scale = lax.rsqrt(spread + norm_eps)
    return centre * scale, scale


def stacked(pair, low_half):
    zero = jnp.zeros_like(pair)
    return jnp.concatenate(
        [jnp.where(low_half, pair, zero), jnp.where(low_half, zero, pair)], axis=0
    )


def soft_rows(scores):
    top = jnp.max(scores, axis=-1, keepdims=True)
    grown = jnp.exp(scores - top)
    return (grown * (1.0 / jnp.sum(grown, axis=-1, keepdims=True))).astype(BF)


def transpose_into(dest, source, rows):
    @pl.loop(0, rows // SEG)
    def _(s):
        dest[:, span(s, SEG)] = source[span(s, SEG), :].T


def gelu_pair(u):
    cdf = 0.5 * (1.0 + lax.erf(u * ROOT_HALF))
    slope = cdf + u * (PDF_SCALE * jnp.exp(-0.5 * u * u))
    return (u * cdf).astype(BF), slope.astype(BF)


def project(r, half):
    lanes = slice(half * HALF_D, (half + 1) * HALF_D)
    for c in range(3):
        r.qkv[c, :, lanes] = (mm(r.xb[...], r.wqkv[c, :, lanes]) + r.b3[c, :, lanes]).astype(BF)


def low_lanes():
    return lax.broadcasted_iota(jnp.int32, (SEG, SEG), 1) < HEAD_DIM


def attend(r, keep, low, high):
    segs = r.xb.shape[0] // SEG
    root = jnp.asarray(HEAD_DIM ** (-0.5), BF)

    @pl.loop(0, segs, unroll=min(segs, 4))
    def _(s):
        at = span(s, SEG)
        live = keep(s)
        low_half = low_lanes()
        for p in range(low, high):
            cols = slice(p * SEG, p * SEG + SEG)
            keys = stacked(r.qkv[1, at, cols], low_half)
            vals = stacked(r.qkv[2, at, cols], low_half)
            raw = mm_nt(r.qkv[0, at, cols] * root, keys)
            one = soft_rows(jnp.where(live, raw[:, :SEG], masked_score))
            two = soft_rows(jnp.where(live, raw[:, SEG:], masked_score))
            both = jnp.concatenate([one, two], axis=1)
            r.p[s, p] = both
            r.o[at, cols] = mm(both, vals).astype(BF)


def attn_out(r):
    for n in range(3):
        cols = slice(n * 256, n * 256 + 256)
        r.xh1[:, cols] = mm(r.o[...], r.wout[:, cols]) + r.bt[0, :, cols]


def norm_one(r, x):
    rows = r.xh1.shape[0]
    hat, scale = row_norm(x + r.xh1[...])
    r.xh1[...] = hat
    r.rs1[...] = jnp.broadcast_to(scale, (rows, SEG))
    hidden = hat * r.gain[0] + r.bt[2]
    r.h1[...] = hidden
    r.h1b[...] = hidden.astype(BF)


def mlp_up(r, low, high):
    @pl.loop(low, high)
    def _(j):
        for k in range(3):
            cols = pl.ds(pl.multiple_of(j * D + k * 256, 256), 256)
            u = mm(r.h1b[...], r.wup[:, cols]) + r.bup[:, cols]
            r.g[:, cols], r.gp[:, cols] = gelu_pair(u)


def mlp_down(r, half):
    part = slice(half * HALF_FF, (half + 1) * HALF_FF)
    before = r.h1[...] + r.bt[1] if half == 0 else r.xh2[...]
    r.xh2[...] = before + mm(r.g[:, part], r.wdown[part, :])


def norm_two(r):
    hat, scale = row_norm(r.xh2[...])
    r.xh2[...] = hat
    r.rs2[...] = jnp.broadcast_to(scale, (r.xh2.shape[0], SEG))
    return hat * r.gain[1] + r.bt[3]


def norm_back(grad, hat, scale, gain):
    d_hat = grad * gain
    first = jnp.mean(d_hat, axis=-1, keepdims=True)
    second = jnp.mean(d_hat * hat, axis=-1, keepdims=True)
    return (d_hat - first - hat * second) * scale


def norm_back_rows(r, hat_ref, scale_ref, gain, grad_of):
    zero = jnp.zeros((1, D), F32)
    rows = r.dr.shape[0]
    block = min(rows, 256)

    def step(s, sums):
        at = span(s, block)
        grad = grad_of(s, at)
        hat = hat_ref[at, :]
        out = norm_back(grad, hat, scale_ref[at, 0:1], gain)
        low = out.astype(BF)
        r.dr[at, :] = out
        r.dm[at, :] = low
        return (
            sums[0] + jnp.sum(grad * hat, axis=0, keepdims=True),
            sums[1] + jnp.sum(grad, axis=0, keepdims=True),
            sums[2] + jnp.sum(low.astype(F32), axis=0, keepdims=True),
        )

    sums = lax.fori_loop(0, rows // block, step, (zero, zero, zero))
    transpose_into(r.dmt, r.dm, rows)
    return sums


def back_norm_two(r, grad_of):
    sums = norm_back_rows(r, r.xh2, r.rs2, r.gain[1], grad_of)
    r.small_common[1], r.small_common[5], r.small_common[3] = sums


def back_norm_one(r):
    sums = norm_back_rows(r, r.xh1, r.rs1, r.gain[0], lambda s, at: r.dr[at, :])
    r.small_common[0], r.small_common[4], r.small_common[2] = sums


def grad_hidden(r):
    @pl.loop(0, 3)
    def _(j):
        cols = span(j, 1024)
        du = (mm_nt(r.dm[...], r.wdown[cols, :]) * r.gp[:, cols].astype(F32)).astype(BF)
        r.gp[:, cols] = du
        r.bup_sum[:, cols] = jnp.sum(du.astype(F32), axis=0, keepdims=True)


def grad_middle(r):
    r.dr[...] = r.dr[...] + mm_nt(r.gp[...], r.wup[...])


def grad_heads(r):
    for n in range(3):
        cols = slice(n * 256, n * 256 + 256)
        r.dh[:, cols] = mm_nt(r.dm[...], r.wout[cols, :]).astype(BF)


def attend_back(r, low, high):
    root = jnp.asarray(HEAD_DIM ** (-0.5), BF)

    @pl.loop(low, high, unroll=min(high - low, 2))
    def _(s):
        at = span(s, SEG)
        low_half = low_lanes()
        head = lax.broadcasted_iota(jnp.int32, (SEG, 2 * SEG), 0) < HEAD_DIM
        side = lax.broadcasted_iota(jnp.int32, (SEG, 2 * SEG), 1) < SEG
        ones = jnp.where(head == side, 1.0, 0.0).astype(BF)
        for p in range(PAIRS):
            cols = slice(p * SEG, p * SEG + SEG)
            query = r.qkv[0, at, cols] * root
            keys = stacked(r.qkv[1, at, cols] * root, low_half)
            vals = stacked(r.qkv[2, at, cols], low_half)
            d_head = r.dh[at, cols]
            probs = r.p[s, p]
            d_probs = mm_nt(d_head, vals)
            inner = mm((d_head.astype(F32) * r.o[at, cols].astype(F32)).astype(BF), ones)
            d_scores = (probs.astype(F32) * (d_probs - inner)).astype(BF)
            d_keys = mm(d_scores.T, query)
            d_vals = mm(probs.T, d_head)
            for c, value in (
                (0, mm(d_scores, keys)),
                (1, jnp.where(low_half, d_keys[:SEG], d_keys[SEG:])),
                (2, jnp.where(low_half, d_vals[:SEG], d_vals[SEG:])),
            ):
                r.g[at, c * D + p * SEG : c * D + p * SEG + SEG] = value.astype(BF)


def bias_heads(r):
    for c in (0, 2):
        r.qv_sum[c // 2] = jnp.sum(
            r.g[:, c * D : (c + 1) * D].astype(F32), axis=0, keepdims=True
        )


def grad_input(r):
    for n in range(3):
        cols = slice(n * 256, n * 256 + 256)
        total = r.dr[:, cols]
        for c in range(3):
            total = total + mm_nt(r.g[:, c * D : (c + 1) * D], r.wqkv[c, cols, :])
        r.dr[:, cols] = total


def chunk_operands(r, c):
    if c < 4:
        return r.dmt, (r.g, c * CHUNK, HALF_FF + c * CHUNK)
    if c < 8:
        return r.h1t, (r.gp, (c - 4) * CHUNK, HALF_FF + (c - 4) * CHUNK)
    if c == 8:
        return r.dmt, (r.o, 0, HALF_D)
    return r.xt, (r.g, (c - 9) * D, (c - 9) * D + HALF_D)


HOOK_CHUNKS = {"down": (0, 4), "up": (4, 8), "out": (8, 9), "qkv": (9, 12)}


class Copies:
    def __init__(self, sems):
        self.sems = sems
        self.used = 0

    def start(self, source, dest):
        copy = pltpu.make_async_copy(source, dest, self.sems.at[self.used])
        self.used += 1
        copy.start()
        return copy


def remote(source, dest, send_sem, recv_sem, device):
    return pltpu.make_async_remote_copy(
        src_ref=source,
        dst_ref=dest,
        send_sem=send_sem,
        recv_sem=recv_sem,
        device_id=device,
        device_id_type=MESH,
    )


class Gather:
    def __init__(self, dp, everyone, send, recv):
        self.dp, self.everyone, self.send, self.recv = dp, everyone, send, recv
        self.sends = []

    def start(self, block):
        d, t = lax.axis_index("dp"), lax.axis_index("tensor")
        everyone = self.everyone
        everyone[d] = block
        for o in range(1, self.dp):
            peer = (lax.rem(d + o, self.dp), t)
            copy = remote(everyone.at[d], everyone.at[d], self.send.at[o], self.recv.at[d], peer)
            copy.start()
            self.sends.append(copy)

    def arrived(self):
        d, t = lax.axis_index("dp"), lax.axis_index("tensor")
        for o in range(1, self.dp):
            source = lax.rem(d + o, self.dp)
            block = self.everyone.at[source]
            remote(block, block, self.send.at[o], self.recv.at[source], (source, t)).wait_recv()

    def rows_into(self, dest):
        segs = self.everyone.shape[1]
        pack = 8 // segs
        for i in range(self.dp // pack):
            blocks = [self.everyone[i * pack + k].astype(F32) for k in range(pack)]
            dest[i * 8 : i * 8 + 8, :] = jnp.concatenate(blocks, axis=0)


SLOTS = 4
RING = 8
WEIGHTS = ("wqkv", "wout", "wup", "wdown")


def half_of(ref, which, half):
    if which == "wqkv":
        return ref.at[:, :, half * HALF_D : (half + 1) * HALF_D]
    if which == "wout":
        return ref.at[half * HALF_D : (half + 1) * HALF_D, :]
    if which == "wup_square":
        return ref.at[:, half * HALF_D : (half + 1) * HALF_D]
    if which == "wup":
        return ref.at[:, half * HALF_FF : (half + 1) * HALF_FF]
    return ref.at[half * HALF_FF : (half + 1) * HALF_FF, :]


def fill_bias(b3, bup, half, layer, b_qv, b_up):
    lanes = slice(half * HALF_D, (half + 1) * HALF_D)
    b3[0, :, lanes] = b_qv[layer, 0:1, :]
    b3[1, :, lanes] = jnp.zeros((1, HALF_D), F32)
    b3[2, :, lanes] = b_qv[layer, 1:2, :]
    bup[:, half * HALF_FF : (half + 1) * HALF_FF] = b_up[layer : layer + 1, :]


def pack_halves(r):
    for half in range(2):
        at = 6 + 3 * half
        lanes = slice(half * HALF_D, (half + 1) * HALF_D)
        r.small[at, :, 0:HALF_D] = r.qv_sum[0, :, lanes]
        r.small[at, :, HALF_D:] = r.qv_sum[1, :, lanes]
        base = half * HALF_FF
        r.small[at + 1] = r.bup_sum[:, base : base + D]
        r.small[at + 2] = r.bup_sum[:, base + D : base + 2 * D]


def first_of_segments(ref, segs):
    return jnp.concatenate(
        [ref[s * SEG : s * SEG + 16, :].astype(F32)[0:1] for s in range(segs)], axis=0
    )


class Stream:
    ORDER = (
        [("qkv", c) for c in range(3)] + [("out", 0)] + [("up", j) for j in range(4)]
        + [("down", j) for j in range(4)] * 2
        + [("up", j) for j in range(4)] + [("out", 0)] + [("qkv", c) for c in range(3)]
    )
    DEPTH = 4

    def __init__(self, r, arriving):
        self.r = r
        self.arriving = arriving
        self.next = 0
        self.pending = []

    def copies(self, n):
        r = self.r
        kind, index = self.ORDER[n]
        which = "w" + kind
        halves = (getattr(r, "a_" + which).at[1], getattr(r, "f_" + which))
        dest, sems = r.ring_w.at[n % self.DEPTH], r.ring_sem.at[n % self.DEPTH]
        if kind == "qkv":
            pairs = [(halves[h].at[index], half_of(dest, "wup_square", h)) for h in range(2)]
        elif kind == "out":
            pairs = [(halves[h], half_of(dest, "wout", h)) for h in range(2)]
        else:
            at = slice(index % 2 * D, index % 2 * D + D)
            source = halves[index // 2]
            pairs = [(source.at[:, at] if kind == "up" else source.at[at, :], dest)]
        return [pltpu.make_async_copy(a, b, sems.at[k]) for k, (a, b) in enumerate(pairs)]

    def start(self, n):
        if n < len(self.ORDER):
            kind, index = self.ORDER[n]
            if index >= 2 and kind in self.arriving:
                self.arriving.pop(kind).wait_recv()
            self.pending.append(self.copies(n))
            for copy in self.pending[-1]:
                copy.start()

    def take(self, body):
        for copy in self.pending.pop(0):
            copy.wait()
        kind, index = self.ORDER[self.next]
        body(index, self.r.ring_w.at[self.next % self.DEPTH])
        self.start(self.next + self.DEPTH)
        self.next += 1


def cross_layer(r, q, stream, keep, pump, hooks):
    def lanes(j):
        return slice(j * D, (j + 1) * D)

    def project_piece(c, w):
        q.qkv[c] = (mm(q.xb[...], w[...]) + q.b3[c]).astype(BF)

    for c in range(3):
        stream.take(project_piece)
    attend(q, keep, 0, PAIRS)
    pump("attend")

    def out_piece(j, w):
        q.xh1[...] = mm(q.o[...], w[...]) + q.bt[0]

    stream.take(out_piece)
    norm_one(q, q.x32[...])
    transpose_into(q.h1t, q.h1b, SEG)

    def up_piece(j, w):
        u = mm(q.h1b[...], w[...]) + q.bup[:, lanes(j)]
        q.g[:, lanes(j)], q.gp[:, lanes(j)] = gelu_pair(u)

    for j in range(4):
        stream.take(up_piece)
    pump("up")

    def down_piece(j, w):
        before = q.h1[...] + q.bt[1] if j == 0 else q.xh2[...]
        q.xh2[...] = before + mm(q.g[:, lanes(j)], w[...])

    for j in range(4):
        stream.take(down_piece)
    q.yb[...] = norm_two(q).astype(BF)
    pump("down")
    back_norm_two(q, lambda s, at: q.dy[at, :])
    hooks("down")

    def back_down_piece(j, w):
        du = (mm_nt(q.dm[...], w[...]) * q.gp[:, lanes(j)].astype(F32)).astype(BF)
        q.gp[:, lanes(j)] = du
        r.bup_sum[:, lanes(j)] = jnp.sum(du.astype(F32), axis=0, keepdims=True)

    for j in range(4):
        stream.take(back_down_piece)
    pump("back_down")
    hooks("up")

    def back_up_piece(j, w):
        q.dr[...] = q.dr[...] + mm_nt(q.gp[:, lanes(j)], w[...])

    for j in range(4):
        stream.take(back_up_piece)
    pump("back_up")
    back_norm_one(q)
    hooks("out")

    def back_out_piece(j, w):
        q.dh[...] = mm_nt(q.dm[...], w[...]).astype(BF)

    stream.take(back_out_piece)
    attend_back(q, 0, 1)
    bias_heads(q)
    pump("attend_back")
    hooks("qkv")

    def back_qkv_piece(c, w):
        q.dr[...] = q.dr[...] + mm_nt(q.g[:, lanes(c)], w[...])

    for c in range(3):
        stream.take(back_qkv_piece)


def whole_kernel(dp, names, *refs):
    r = Names(**dict(zip(names, refs)))
    d, t = lax.axis_index("dp"), lax.axis_index("tensor")
    x, y, z = lax.rem(d, 2), lax.rem(lax.div(d, 2), 2), lax.div(d, 4)
    zs = dp // 4
    shard = D // dp
    rows = r.xb.shape[0]
    segs = rows // SEG
    sibling = (d, 1 - t)
    x_peer = (z * 4 + y * 2 + (1 - x), t)
    y_peer = (z * 4 + (1 - y) * 2 + x, t)
    z_peers = [(lax.rem(z + o, zs) * 4 + y * 2 + x, t) for o in range(1, zs)]
    r.dr, r.dm, r.y1, r.dh = r.h1, r.h1b, r.xb, r.cot

    barrier = pltpu.get_barrier_semaphore()
    for device in [sibling] + [(lax.rem(d + o, dp), t) for o in range(1, dp)]:
        pl.semaphore_signal(barrier, inc=1, device_id=device, device_id_type=MESH)
    copies = Copies(r.local_sem)
    for layer, gain, terms in ((0, r.gain, r.bt), (1, r.gain_cross, r.bt_cross)):
        for k in range(2):
            gain[k] = r.norm_gain[layer, k : k + 1, :]
        for k in range(4):
            terms[k] = r.bias_terms[layer, k : k + 1, :]
    own = {w: getattr(r, "a_" + w) for w in WEIGHTS}
    full = {w: getattr(r, "f_" + w) for w in WEIGHTS}
    load_x = copies.start(r.tokens.at[t], r.xb)
    loads = {w: copies.start(own[w].at[0], half_of(getattr(r, w), w, 0)) for w in WEIGHTS}
    load_cot = copies.start(r.cotangent.at[t], r.cot)
    load_x.wait()
    transpose_into(r.xt, r.xb, rows)
    fill_bias(r.b3, r.bup, 0, 0, r.b_qv, r.b_up)
    fill_bias(r.b3_cross, r.bup_cross, 0, 1, r.b_qv, r.b_up)
    swaps = {}

    def swap(layer, w):
        k = WEIGHTS.index(w)
        dest = half_of(getattr(r, w), w, 1) if layer == 0 else full[w]
        swaps[layer, w] = remote(
            own[w].at[layer], dest, r.w_send.at[layer, k], r.w_recv.at[layer, k], sibling
        )
        swaps[layer, w].start()

    cot_gather = Gather(dp, r.cot_all, r.g_send.at[0], r.g_recv.at[0])
    cls_gather = Gather(dp, r.cls_all, r.g_send.at[1], r.g_recv.at[1])
    hat_gather = Gather(dp, r.hat_all, r.g_send.at[2], r.g_recv.at[2])
    act_gather = Gather(dp, r.act_all, r.g_send.at[3], r.g_recv.at[3])

    def keep(s):
        seg = d * segs + s
        doc = r.seg_doc[t, seg]
        within = jnp.int32(0)
        for back in range(1, MAXSEG):
            same = r.seg_doc[t, jnp.maximum(seg - back, 0)] == doc
            within = within + jnp.where(jnp.logical_and(seg >= back, same), 1, 0)
        valid = jnp.minimum(SEG, r.doc_len[t, doc] - SEG * within)
        return lax.broadcasted_iota(jnp.int32, (1, SEG), 1) < valid

    loads["wqkv"].wait()
    project(r, 0)
    pl.semaphore_wait(barrier, dp)
    swap(0, "wqkv")
    swap_bias = [
        remote(r.b_qv, r.x_bqv, r.w_send.at[0, 4], r.w_recv.at[0, 4], sibling),
        remote(r.b_up, r.x_bup, r.w_send.at[1, 4], r.w_recv.at[1, 4], sibling),
    ]
    for copy in swap_bias:
        copy.start()
    swap(0, "wout")
    attend(r, keep, 0, PAIRS // 2)
    swap(0, "wup")
    load_cot.wait()
    cot_gather.start(first_of_segments(r.cot, segs).astype(BF))
    for copy in swap_bias:
        copy.wait_recv()
    fill_bias(r.b3, r.bup, 1, 0, r.x_bqv, r.x_bup)
    fill_bias(r.b3_cross, r.bup_cross, 1, 1, r.x_bqv, r.x_bup)
    swaps[0, "wqkv"].wait_recv()
    project(r, 1)
    swap(0, "wdown")
    attend(r, keep, PAIRS // 2, PAIRS)
    loads["wout"].wait()
    swaps[0, "wout"].wait_recv()
    attn_out(r)
    norm_one(r, r.xb[...].astype(F32))
    loads["wup"].wait()
    mlp_up(r, 0, 2)
    swap(1, "wqkv")
    swap(1, "wout")
    transpose_into(r.h1t, r.h1b, rows)
    swaps[0, "wup"].wait_recv()
    mlp_up(r, 2, 4)
    loads["wdown"].wait()
    mlp_down(r, 0)
    swaps[0, "wdown"].wait_recv()
    mlp_down(r, 1)
    r.y1[...] = norm_two(r).astype(BF)
    cls_gather.start(first_of_segments(r.y1, segs).astype(BF))
    hats = first_of_segments(r.xh2, segs)
    hat_gather.start(jnp.concatenate([hats, first_of_segments(r.rs2, segs)], axis=1))

    def sib_copy(c):
        slot = lax.rem(c, SLOTS)
        return remote(
            r.sib_out.at[slot], r.sib_in.at[slot], r.sib_send.at[slot], r.sib_recv.at[slot], sibling
        )

    def ring(c):
        return lax.rem(c, RING)

    low_z, high_z = slice(0, zs // 2), slice(zs // 2, zs)

    def stage_one(c):
        g, into = r.gbuf.at[ring(c)], r.one_in.at[ring(c)]
        return (
            remote(g.at[low_z, :, 1 - x], into.at[0], r.one_send.at[c, 0], r.one_recv.at[c, 0], x_peer),
            remote(g.at[high_z, 1 - y], into.at[1], r.one_send.at[c, 1], r.one_recv.at[c, 1], y_peer),
        )

    def stage_two(c):
        g, into = r.gbuf.at[ring(c)], r.two_in.at[ring(c)]
        return (
            remote(g.at[low_z, 1 - y, x], into.at[0], r.two_send.at[c, 0], r.two_recv.at[c, 0], y_peer),
            remote(g.at[high_z, y, 1 - x], into.at[1], r.two_send.at[c, 1], r.two_recv.at[c, 1], x_peer),
        )

    def stage_three(c):
        g, into = r.gbuf.at[ring(c)], r.three_in.at[ring(c)]
        return [
            remote(
                g.at[lax.rem(z + o, zs), y, x],
                into.at[o - 1],
                r.three_send.at[c, o - 1],
                r.three_recv.at[c, o - 1],
                z_peers[o - 1],
            )
            for o in range(1, zs)
        ]

    def emit_other(c, left, right, at):
        @pl.when(c >= SLOTS)
        def _():
            sib_copy(c).wait_send()
            pl.semaphore_wait(r.credit, 1)

        r.sib_out[lax.rem(c, SLOTS)] = mm(left[...], right[:, pl.ds(at, CHUNK)]).astype(BF)
        sib_copy(c).start()

    def emit_own(c, left, right, at):
        mine = mm(left[...], right[:, pl.ds(at, CHUNK)])
        sib_copy(c).wait_recv()
        mine = (mine + r.sib_in[lax.rem(c, SLOTS)].astype(F32)).astype(BF)
        r.gbuf[ring(c)] = mine.reshape(zs, 2, 2, shard, CHUNK)

        @pl.when(c < CHUNKS - SLOTS)
        def _():
            pl.semaphore_signal(r.credit, inc=1, device_id=sibling, device_id_type=MESH)

        for copy in stage_one(c):
            copy.start()

    def hooks(name, which):
        low, high = HOOK_CHUNKS[name]
        left, (right, own_at, other_at) = chunk_operands(r, low)
        step = D if name == "qkv" else CHUNK

        def at(c, base):
            return pl.multiple_of((c - low) * step + base, SEG)

        if which == "other":

            @pl.loop(low, high)
            def _(c):
                emit_other(c, left, right, at(c, other_at))

        else:

            @pl.loop(low, high)
            def _(c):
                emit_own(c, left, right, at(c, own_at))

    def second(*chunks):
        for c in chunks:
            c = jnp.int32(c)
            g, into = r.gbuf.at[ring(c)], r.one_in.at[ring(c)]
            from_x, from_y = stage_one(c)
            to_y, to_x = stage_two(c)
            from_x.wait_recv()
            g[low_z, :, x] = g[low_z, :, x] + into[0]
            to_y.start()
            from_y.wait_recv()
            g[high_z, y] = g[high_z, y] + into[1]
            to_x.start()

    def third(*chunks):
        for c in chunks:
            c = jnp.int32(c)
            g, into = r.gbuf.at[ring(c)], r.two_in.at[ring(c)]
            for copy in stage_two(c):
                copy.wait_recv()
            g[low_z, y, x] = g[low_z, y, x] + into[0]
            g[high_z, y, x] = g[high_z, y, x] + into[1]
            for copy in stage_three(c):
                copy.start()

    def finish(*chunks):
        for c in chunks:
            at = jnp.int32(c)
            total = r.gbuf[ring(at), z, y, x].astype(F32)
            for o, copy in enumerate(stage_three(at)):
                copy.wait_recv()
                total = total + r.three_in[ring(at), o].astype(F32)
            r.mine[c] = r.mine[c] + total if c < 4 else total
            for copy in (*stage_one(at), *stage_two(at), *stage_three(at)):
                copy.wait_send()

    block_row = lax.broadcasted_iota(jnp.int32, (256, 1), 0)

    def without_first(s, at):
        return jnp.where(lax.rem(block_row, SEG) == 0, 0.0, r.cot[at, :].astype(F32))

    r.act_first[...] = first_of_segments(r.g, segs)
    r.small_common = r.small
    back_norm_two(r, without_first)
    hooks("down", "other")
    hooks("down", "own")
    act_gather.start(r.act_first[...].astype(BF))
    swap(1, "wup")
    swap(1, "wdown")

    q = Names(
        **{k: getattr(r, "q_" + k) for k in CROSS},
        g=r.g.at[0:SEG],
        gp=r.g.at[SEG : 2 * SEG],
        gain=r.gain_cross,
        bt=r.bt_cross,
        b3=r.b3_cross,
        bup=r.bup_cross,
        qv_sum=r.qv_sum,
    )
    q.dr, q.dm, q.small_common = q.h1, q.h1b, r.small1
    slots = q.xb.shape[0]
    total_docs = slots // MAXSEG
    total_segs = dp * segs
    stream = Stream(r, {"up": swaps[1, "wup"], "down": swaps[1, "wdown"]})
    for w in ("wqkv", "wout"):
        swaps[1, w].wait_recv()
    for n in range(stream.DEPTH):
        stream.start(n)

    doc = jnp.where(t == 0, r.seg_doc_v[0:1, :], r.seg_doc_v[1:2, :])
    below = lax.broadcasted_iota(jnp.int32, (total_segs, total_segs), 0)
    across = lax.broadcasted_iota(jnp.int32, (total_segs, total_segs), 1)

    def column(row):
        wide = jnp.broadcast_to(row, (total_segs, total_segs))
        return jnp.sum(jnp.where(below == across, wide, 0.0), axis=1, keepdims=True)

    doc_f = doc.astype(F32)
    earlier = jnp.logical_and(column(doc_f) == doc_f, below < across)
    within = jnp.sum(jnp.where(earlier, 1.0, 0.0), axis=0, keepdims=True).astype(jnp.int32)
    moved = doc + total_docs // 2
    moved = jnp.where(moved >= total_docs, moved - total_docs, moved)
    slot_of = (jnp.where((doc & 1) == 1, moved, doc) * MAXSEG + within).astype(F32)
    slot_ids = lax.broadcasted_iota(jnp.int32, (slots, total_segs), 0).astype(F32)
    deal = jnp.where(slot_ids == slot_of, 1.0, 0.0).astype(BF)
    slot_row = lax.broadcasted_iota(jnp.int32, (total_segs, slots), 1).astype(F32)
    r.undeal[...] = jnp.where(slot_row == column(slot_of), 1.0, 0.0).astype(BF)
    pick_row = lax.broadcasted_iota(jnp.int32, (8, total_segs), 0)
    pick_seg = lax.broadcasted_iota(jnp.int32, (8, total_segs), 1)
    picked = jnp.logical_and(pick_row < segs, pick_seg == d * segs + pick_row)
    r.back[...] = mm(jnp.where(picked, 1.0, 0.0).astype(BF), r.undeal[...]).astype(BF)
    live = mm_nt(jnp.ones((8, total_segs), BF), deal)[0:1] > 0.5
    key_doc = lax.broadcasted_iota(jnp.int32, (SEG, SEG), 1) >> 3
    row_doc = lax.broadcasted_iota(jnp.int32, (SEG, SEG), 0) >> 3
    r.allowed[...] = jnp.where(jnp.logical_and(key_doc == row_doc, live), 1.0, 0.0)

    cot_gather.arrived()
    cot_gather.rows_into(r.rows64)
    q.dy[...] = mm(deal, r.rows64[...].astype(BF))
    cls_gather.arrived()
    cls_gather.rows_into(r.rows64)
    q.x32[...] = mm(deal, r.rows64[...].astype(BF)) + jnp.concatenate(
        [r.seg_pos[...]] * total_docs, axis=0
    )
    q.xb[...] = q.x32[...].astype(BF)
    transpose_into(q.xt, q.xb, slots)

    def cross_hooks(name):
        low, high = HOOK_CHUNKS[name]
        for c in range(low, high):
            left, (right, own_at, other_at) = chunk_operands(q, c)
            mine = left[pl.ds(pl.multiple_of(d * shard, 16), shard), :]
            r.shard1[c] = mm(mine, right[:, own_at : own_at + CHUNK])
            r.shard_out[c] = mm(mine, right[:, other_at : other_at + CHUNK]).astype(BF)

    def pump(point):
        if point == "up":
            second(0, 1)
        elif point == "back_down":
            second(2, 3)
        elif point == "attend_back":
            third(0, 1)

    cross_layer(r, q, stream, lambda s: r.allowed[...] > 0.5, pump, cross_hooks)
    r.small, keep_small = r.small1, r.small
    pack_halves(r)
    r.small = keep_small
    total = q.dr[0:MAXSEG, :]
    for j in range(1, total_docs):
        total = total + q.dr[j * MAXSEG : (j + 1) * MAXSEG, :]
    for k in range(MAXSEG):
        r.small1[12 + k] = total[k : k + 1, :]
    r.ret[...] = mm(r.back[...], q.yb[...])
    low = q.dr[...].astype(BF)
    r.dc[...] = mm(r.back[...], low)

    gain_sum = jnp.zeros((1, D), F32)
    shift_sum, low_sum = gain_sum, gain_sum
    top = lax.broadcasted_iota(jnp.int32, (16, 1), 0) == 0
    for s in range(segs):
        at = slice(s * SEG, s * SEG + 16)
        grad = jnp.where(top, r.dc[s : s + 1, :], 0.0)
        hat = r.xh2[at, :]
        out = jnp.where(top, norm_back(grad, hat, r.rs2[at, 0:1], r.gain[1]), 0.0)
        out_low = out.astype(BF)
        r.dr[at, :] = jnp.where(top, out, r.dr[at, :])
        r.dm[at, :] = jnp.where(top, out_low.astype(F32), r.dm[at, :].astype(F32)).astype(BF)
        gain_sum = gain_sum + jnp.sum(grad * hat, axis=0, keepdims=True)
        shift_sum = shift_sum + jnp.sum(grad, axis=0, keepdims=True)
        low_sum = low_sum + jnp.sum(out_low.astype(F32), axis=0, keepdims=True)
        r.y1[at, :] = jnp.where(top, r.ret[s : s + 1, :], r.y1[at, :].astype(F32)).astype(BF)
    r.small_common[1] = r.small_common[1] + gain_sum
    r.small_common[5] = r.small_common[5] + shift_sum
    r.small_common[3] = r.small_common[3] + low_sum
    outs = [copies.start(r.y1, r.o_enc.at[t])]
    enc_swap = remote(r.y1, r.o_enc.at[t], r.misc_send.at[0], r.misc_recv.at[0], sibling)
    enc_swap.start()

    hat_gather.arrived()
    hat_gather.rows_into(r.hat64)
    act_gather.arrived()
    act_gather.rows_into(r.act64)
    all_grads = mm(r.undeal[...], low)
    late = norm_back(all_grads, r.hat64[:, 0:D], r.hat64[:, D : D + 1], r.gain[1]).astype(BF)
    r.late[0:total_segs, :] = late
    r.late[total_segs:, :] = jnp.zeros((SEG - total_segs, D), BF)
    transpose_into(r.late_t, r.late, SEG)
    mine = r.late_t[pl.ds(pl.multiple_of(d * shard, 16), shard), 0:total_segs]
    for c in range(4):
        for half in range(2):
            cols = slice(half * HALF_FF + c * CHUNK, half * HALF_FF + (c + 1) * CHUNK)
            part = mm(mine, r.act64[:, cols].astype(BF))
            if half == 0:
                r.mine[c] = part
            else:
                r.shard_out[CHUNKS + c] = part.astype(BF)
    cross_swap = [
        remote(r.shard_out, r.shard_in, r.misc_send.at[1], r.misc_recv.at[1], sibling),
        remote(r.small1.at[0:6], r.small1_in.at[0:6], r.misc_send.at[2], r.misc_recv.at[2], sibling),
        remote(r.small1.at[9:20], r.small1_in.at[6:17], r.misc_send.at[3], r.misc_recv.at[3], sibling),
    ]
    for copy in cross_swap:
        copy.start()

    third(2, 3)
    grad_hidden(r)
    hooks("up", "other")
    hooks("up", "own")
    grad_middle(r)
    for copy in cross_swap:
        copy.wait()
    finish(0, 1, 2, 3)
    for c in range(CHUNKS):
        r.shard1[c] = r.shard1[c] + r.shard_in[c].astype(F32)
    for c in range(4):
        r.mine[c] = r.mine[c] + r.shard_in[CHUNKS + c].astype(F32)
    r.o_small[9:26] = (
        jnp.concatenate([r.small1[0:9], r.small1[12:20]], axis=0) + r.small1_in[...]
    )
    outs.append(copies.start(r.shard1, r.o_shard.at[1]))
    back_norm_one(r)
    second(4)
    hooks("out", "other")
    grad_heads(r)
    hooks("out", "own")

    attend_back(r, 0, 2)
    second(5)
    attend_back(r, 2, segs)
    second(6, 7)
    bias_heads(r)
    hooks("qkv", "other")
    hooks("qkv", "own")
    pack_halves(r)
    small_swap = [
        remote(r.small.at[0:6], r.small_in.at[0:6], r.misc_send.at[4], r.misc_recv.at[4], sibling),
        remote(r.small.at[9:12], r.small_in.at[6:9], r.misc_send.at[5], r.misc_recv.at[5], sibling),
    ]
    for copy in small_swap:
        copy.start()
    third(4, 5)
    grad_input(r)
    grad_swap = remote(r.dr, r.o_grad.at[t], r.misc_send.at[6], r.misc_recv.at[6], sibling)
    grad_swap.start()
    outs.append(copies.start(r.dr, r.o_grad.at[t]))
    for copy in small_swap:
        copy.wait()
    r.total[...] = r.small[0:9] + r.small_in[...]
    x_small = remote(r.total, r.x_small, r.misc_send.at[7], r.misc_recv.at[7], x_peer)
    x_small.start()
    third(6, 7)
    second(8)
    x_small.wait()
    r.total_x[...] = r.total[...] + r.x_small[...]
    y_small = remote(r.total_x, r.y_small, r.misc_send.at[8], r.misc_recv.at[8], y_peer)
    y_small.start()
    second(9)
    finish(4, 5, 6, 7)
    y_small.wait()
    r.z_small[z] = r.total_x[...] + r.y_small[...]
    z_sends = []
    for o in range(1, zs):
        z_sends.append(
            remote(r.z_small.at[z], r.z_small.at[z], r.z_send.at[o], r.z_recv.at[z], z_peers[o - 1])
        )
        z_sends[-1].start()
    second(10, 11)
    third(8, 9, 10, 11)
    for o in range(1, zs):
        source = lax.rem(z + o, zs)
        block = r.z_small.at[source]
        remote(block, block, r.z_send.at[o], r.z_recv.at[source], z_peers[o - 1]).wait_recv()
    total = r.z_small[0]
    for k in range(1, zs):
        total = total + r.z_small[k]
    r.o_small[0:9] = total
    finish(8, 9, 10, 11)
    outs.append(copies.start(r.mine, r.o_shard.at[0]))

    for copy in z_sends:
        copy.wait_send()
    for c in range(CHUNKS - SLOTS, CHUNKS):
        sib_copy(jnp.int32(c)).wait_send()
    for gathered in (cot_gather, cls_gather, hat_gather, act_gather):
        for copy in gathered.sends:
            copy.wait_send()
    for copy in swap_bias:
        copy.wait_send()
    for copy in swaps.values():
        copy.wait_send()
    grad_swap.wait()
    enc_swap.wait()
    for copy in outs:
        copy.wait()


CROSS = ("xb", "x32", "xt", "h1t", "h1b", "h1", "qkv", "o", "p", "xh1", "rs1", "xh2", "rs2", "yb", "dy", "dmt", "dh")
WEIGHT_SCRATCH = dict(
    wqkv=((3, D, D), BF), wout=((D, D), BF), wup=((D, FF), BF), wdown=((FF, D), BF)
)
BACK_SCRATCH = dict(qv_sum=((2, 1, D), F32), bup_sum=((1, FF), F32))


def saved_shapes(rows):
    return dict(
        xt=((D, rows), BF),
        h1t=((D, rows), BF),
        qkv=((3, rows, D), BF),
        o=((rows, D), BF),
        p=((rows // SEG, PAIRS, SEG, 2 * SEG), BF),
        xh1=((rows, D), F32),
        rs1=((rows, SEG), F32),
        g=((rows, FF), BF),
        gp=((rows, FF), BF),
        xh2=((rows, D), F32),
        rs2=((rows, SEG), F32),
    )


def forward_shapes(rows):
    return dict(
        xb=((rows, D), BF),
        h1=((rows, D), F32),
        h1b=((rows, D), BF),
        b3=((3, 1, D), F32),
        bup=((1, FF), F32),
    )


def vmem(table):
    return [pltpu.VMEM(shape, kind) for shape, kind in table.values()]


def arrays(table):
    return [jax.ShapeDtypeStruct(shape, kind) for shape, kind in table.values()]


def run_whole(dp, inputs):
    hbm = pl.BlockSpec(memory_space=pl.ANY)
    small = pl.BlockSpec(memory_space=pltpu.VMEM)
    smem = pl.BlockSpec(memory_space=pltpu.SMEM)
    batches, rows, _ = inputs["tokens"].shape
    slots = inputs["doc_len"].shape[1] * MAXSEG
    segs = rows // SEG
    total_segs = dp * segs
    zs = dp // 4
    shard = D // dp
    outs = dict(
        o_enc=((batches, rows, D), BF),
        o_grad=((batches, rows, D), F32),
        o_shard=((2, CHUNKS, shard, CHUNK), F32),
        o_small=((26, 1, D), F32),
    )
    outs.update({"f_" + w: (inputs["a_" + w].shape[1:], BF) for w in WEIGHTS})
    scratch = dict(saved_shapes(rows))
    scratch.update(WEIGHT_SCRATCH)
    scratch.update(forward_shapes(rows))
    scratch.update(BACK_SCRATCH)
    cross = dict(saved_shapes(slots))
    cross.update(forward_shapes(slots))
    cross.update(
        x32=((slots, D), F32), yb=((slots, D), BF), dy=((slots, D), F32), dmt=((D, slots), BF),
        dh=((slots, D), BF),
    )
    scratch.update({"q_" + k: cross[k] for k in CROSS})
    scratch.update(
        b3_cross=((3, 1, D), F32),
        bup_cross=((1, FF), F32),
        gain=((2, 1, D), F32),
        gain_cross=((2, 1, D), F32),
        bt=((4, 1, D), F32),
        bt_cross=((4, 1, D), F32),
        x_bqv=((2, 2, HALF_D), F32),
        x_bup=((2, HALF_FF), F32),
        cot=((rows, D), BF),
        dmt=((D, rows), BF),
        ring_w=((4, D, D), BF),
        act_first=((segs, FF), F32),
        cot_all=((dp, segs, D), BF),
        cls_all=((dp, segs, D), BF),
        hat_all=((dp, segs, D + SEG), F32),
        act_all=((dp, segs, FF), BF),
        rows64=((total_segs, D), F32),
        hat64=((total_segs, D + SEG), F32),
        act64=((total_segs, FF), F32),
        undeal=((total_segs, slots), BF),
        back=((8, slots), BF),
        allowed=((SEG, SEG), F32),
        ret=((8, D), F32),
        dc=((8, D), F32),
        late=((SEG, D), BF),
        late_t=((D, SEG), BF),
        small=((12, 1, D), F32),
        small1=((20, 1, D), F32),
        small_in=((9, 1, D), F32),
        small1_in=((17, 1, D), F32),
        total=((9, 1, D), F32),
        total_x=((9, 1, D), F32),
        x_small=((9, 1, D), F32),
        y_small=((9, 1, D), F32),
        z_small=((zs, 9, 1, D), F32),
        shard1=((CHUNKS, shard, CHUNK), F32),
        shard_out=((CHUNKS + 4, shard, CHUNK), BF),
        shard_in=((CHUNKS + 4, shard, CHUNK), BF),
        mine=((CHUNKS, shard, CHUNK), F32),
        gbuf=((RING, zs, 2, 2, shard, CHUNK), BF),
        sib_out=((SLOTS, D, CHUNK), BF),
        sib_in=((SLOTS, D, CHUNK), BF),
        one_in=((RING, 2, zs // 2, 2, shard, CHUNK), BF),
        two_in=((RING, 2, zs // 2, shard, CHUNK), BF),
        three_in=((RING, zs - 1, shard, CHUNK), BF),
    )
    dma = pltpu.SemaphoreType.DMA
    sems = dict(
        local_sem=dma((20,)),
        w_send=dma((2, 5)),
        w_recv=dma((2, 5)),
        ring_sem=dma((4, 2)),
        g_send=dma((4, dp)),
        g_recv=dma((4, dp)),
        misc_send=dma((9,)),
        misc_recv=dma((9,)),
        sib_send=dma((SLOTS,)),
        sib_recv=dma((SLOTS,)),
        one_send=dma((CHUNKS, 2)),
        one_recv=dma((CHUNKS, 2)),
        two_send=dma((CHUNKS, 2)),
        two_recv=dma((CHUNKS, 2)),
        three_send=dma((CHUNKS, zs - 1)),
        three_recv=dma((CHUNKS, zs - 1)),
        z_send=dma((zs,)),
        z_recv=dma((zs,)),
        credit=pltpu.SemaphoreType.REGULAR,
    )
    ins = dict(
        seg_doc=smem, doc_len=smem, seg_doc_v=small, tokens=hbm, cotangent=hbm, b_qv=small, b_up=small,
        norm_gain=small, bias_terms=small, seg_pos=small,
        a_wqkv=hbm, a_wout=hbm, a_wup=hbm, a_wdown=hbm,
    )
    names = list(ins) + list(outs) + list(scratch) + list(sems)
    result = pl.pallas_call(
        partial(whole_kernel, dp, names),
        out_shape=arrays(outs),
        in_specs=list(ins.values()),
        out_specs=[hbm, hbm, hbm, small] + [hbm] * 4,
        scratch_shapes=vmem(scratch) + list(sems.values()),
        compiler_params=pltpu.CompilerParams(
            collective_id=0, has_side_effects=True, vmem_limit_bytes=VMEM_LIMIT
        ),
        name="both_layers",
    )(*[inputs[k] for k in ins])
    return dict(zip(outs, result))


VMEM_LIMIT = 64 << 20


def finish_kernel(
    enc, grad, shard, small, o_enc, o_grad, g_qkv, g_out, g_up, g_down, g_bqv, g_bup, g_gain, g_terms, g_pos,
    enc_v, grad_v, shard_v, sems,
):
    copies = Copies(sems)
    loads = [copies.start(grad.at[b], grad_v.at[b]) for b in range(grad.shape[0])]
    load_shard = copies.start(shard, shard_v)
    loads_enc = [copies.start(enc.at[b], enc_v.at[b]) for b in range(enc.shape[0])]
    outs = []
    for b, load in enumerate(loads):
        load.wait()
        outs.append(copies.start(grad_v.at[b], o_grad.at[b]))
    load_shard.wait()
    for layer in range(2):
        for c in range(4):
            lanes = slice(c * CHUNK, (c + 1) * CHUNK)
            outs.append(copies.start(shard_v.at[layer, c], g_down.at[layer, :, lanes]))
            outs.append(copies.start(shard_v.at[layer, 4 + c], g_up.at[layer, :, lanes]))
        outs.append(copies.start(shard_v.at[layer, 8], g_out.at[layer]))
        outs.append(copies.start(shard_v.at[layer, 9:12], g_qkv.at[layer]))
    for b, load in enumerate(loads_enc):
        load.wait()
        outs.append(copies.start(enc_v.at[b], o_enc.at[b]))
    for layer in range(2):
        at = 9 * layer
        for k in range(2):
            g_gain[layer, k : k + 1, :] = small[at + k]
            g_bqv[layer, k : k + 1, :] = small[at + 6, :, k * HALF_D : (k + 1) * HALF_D]
            g_bup[layer : layer + 1, k * D : (k + 1) * D] = small[at + 7 + k]
        for k in range(4):
            g_terms[layer, k : k + 1, :] = small[at + 2 + k]
    for k in range(MAXSEG):
        g_pos[k : k + 1, :] = small[18 + k]
    for copy in outs:
        copy.wait()


def fused(tokens, seg_doc, doc_len, w_qkv, b_qv, w_out, w_up, b_up, w_down, norm_gain, bias_terms, seg_pos, cotangent):
    dp = lax.axis_size("dp")
    whole = run_whole(
        dp,
        dict(
            seg_doc=seg_doc, doc_len=doc_len, seg_doc_v=seg_doc, tokens=tokens, cotangent=cotangent,
            b_qv=b_qv, b_up=b_up, norm_gain=norm_gain, bias_terms=bias_terms,
            seg_pos=seg_pos, a_wqkv=w_qkv, a_wout=w_out, a_wup=w_up, a_wdown=w_down,
        ),
    )
    rows = D // dp
    shapes = [
        (2, 3, rows, HALF_D), (2, rows, HALF_D), (2, rows, HALF_FF), (2, rows, HALF_FF),
        (2, 2, HALF_D), (2, HALF_FF), (2, 2, D), (2, 4, D), (MAXSEG, D),
    ]
    hbm = pl.BlockSpec(memory_space=pl.ANY)
    small = pl.BlockSpec(memory_space=pltpu.VMEM)
    results = [whole[k] for k in ("o_enc", "o_grad", "o_shard", "o_small")]
    enc, grad, g_qkv, g_out, g_up, g_down, g_bqv, g_bup, g_gain, g_terms, g_pos = pl.pallas_call(
        finish_kernel,
        out_shape=[jax.ShapeDtypeStruct(a.shape, a.dtype) for a in results[:2]]
        + [jax.ShapeDtypeStruct(shape, F32) for shape in shapes],
        in_specs=[hbm] * 3 + [small],
        out_specs=[hbm] * 6 + [small] * 5,
        scratch_shapes=[pltpu.VMEM(a.shape, a.dtype) for a in results[:3]]
        + [pltpu.SemaphoreType.DMA((40,))],
        compiler_params=pltpu.CompilerParams(vmem_limit_bytes=VMEM_LIMIT),
        name="lay_out",
    )(*results)
    return (
        enc, grad, g_qkv, g_bqv, g_out.transpose(0, 2, 1), g_up, g_bup, g_down.transpose(0, 2, 1),
        g_gain, g_terms, g_pos,
    )


def solution(mesh):
    in_specs = (
        P(None, "dp", None),
        P(),
        P(),
        P(None, None, None, "tensor"),
        P(None, None, "tensor"),
        P(None, "tensor", None),
        P(None, None, "tensor"),
        P(None, "tensor"),
        P(None, "tensor", None),
        P(),
        P(),
        P(),
        P(None, "dp", None),
    )
    out_specs = (
        P(None, "dp", None),
        P(None, "dp", None),
        P(None, None, "dp", "tensor"),
        P(None, None, "tensor"),
        P(None, "tensor", "dp"),
        P(None, "dp", "tensor"),
        P(None, "tensor"),
        P(None, "tensor", "dp"),
        P(),
        P(),
        P(),
    )
    body = fused if mesh.shape["dp"] == 16 and mesh.shape["tensor"] == 2 else local
    return jax.shard_map(body, mesh=mesh, in_specs=in_specs, out_specs=out_specs, check_vma=False)
```

```python
from functools import partial, reduce

import jax
import jax.numpy as jnp
from jax import lax
from jax.experimental import pallas as pl
from jax.experimental.pallas import tpu as pltpu
from jax.sharding import PartitionSpec as P

HEAD_DIM = 64
SEG = 128
MAXSEG = 8


norm_eps = 1e-05
masked_score = -1e30


def norm_rows(values, gain, shift):
    centre = values - jnp.mean(values, axis=-1, keepdims=True)
    spread = jnp.mean(centre * centre, axis=-1, keepdims=True)
    return centre * lax.rsqrt(spread + norm_eps) * gain + shift


def exact_gelu(values):
    return jax.nn.gelu(values, approximate=False)


def my_rows(values):
    part_rows = values.shape[0] // lax.axis_size("tensor")
    return lax.dynamic_slice_in_dim(values, lax.axis_index("tensor") * part_rows, part_rows, 0)


def attn_scores(queries, key_rows, key_mask, split_shape):
    raw = jnp.einsum(
        "glhd,gmhd->ghlm",
        queries.reshape(split_shape),
        key_rows.reshape(split_shape),
        preferred_element_type=jnp.float32,
    ) * HEAD_DIM ** (-0.5)
    return jnp.where(key_mask[:, None, None, :], raw, masked_score)


def layer_forward(inputs, key_mask, weights):
    w_qkv, b_qv, w_out, w_up, b_up, w_down, norm_gain, bias_terms = weights
    groups, span = key_mask.shape
    row_count = inputs.shape[0]
    local_width = w_qkv.shape[2]
    split_shape = (groups, span, local_width // HEAD_DIM, HEAD_DIM)
    inputs_b = inputs.astype(jnp.bfloat16)
    projected = jnp.einsum("rd,cde->cre", inputs_b, w_qkv, preferred_element_type=jnp.float32)
    queries = (projected[0] + b_qv[0]).astype(jnp.bfloat16)
    key_rows = projected[1].astype(jnp.bfloat16)
    value_rows = (projected[2] + b_qv[1]).astype(jnp.bfloat16)
    scores = attn_scores(queries, key_rows, key_mask, split_shape)
    row_max = jnp.max(scores, axis=-1, keepdims=True)
    log_total = row_max + jnp.log(jnp.sum(jnp.exp(scores - row_max), axis=-1, keepdims=True))
    attn_probs = jnp.exp(scores - log_total).astype(jnp.bfloat16)
    head_out = jnp.einsum(
        "ghlm,gmhd->glhd",
        attn_probs,
        value_rows.reshape(split_shape),
        preferred_element_type=jnp.float32,
    )
    head_out = head_out.reshape(row_count, local_width).astype(jnp.bfloat16)
    attn_part = (
        lax.psum_scatter(
            jnp.dot(head_out, w_out, preferred_element_type=jnp.float32),
            "tensor",
            scatter_dimension=0,
            tiled=True,
        )
        + bias_terms[0]
    )
    resid_one = lax.all_gather(my_rows(inputs) + attn_part, "tensor", axis=0, tiled=True)
    hidden = norm_rows(resid_one, norm_gain[0], bias_terms[2])
    hidden_b = hidden.astype(jnp.bfloat16)
    pre_act = jnp.dot(hidden_b, w_up, preferred_element_type=jnp.float32) + b_up
    active_b = exact_gelu(pre_act).astype(jnp.bfloat16)
    mlp_part = (
        lax.psum_scatter(
            jnp.dot(active_b, w_down, preferred_element_type=jnp.float32),
            "tensor",
            scatter_dimension=0,
            tiled=True,
        )
        + bias_terms[1]
    )
    resid_two = lax.all_gather(my_rows(hidden) + mlp_part, "tensor", axis=0, tiled=True)
    stored = (
        inputs_b,
        queries,
        key_rows,
        value_rows,
        log_total,
        head_out,
        resid_one,
        hidden_b,
        pre_act,
        active_b,
        resid_two,
    )
    return (norm_rows(resid_two, norm_gain[1], bias_terms[3]), stored)


def layer_backward(grad_out, key_mask, weights, stored):
    w_qkv, b_qv, w_out, w_up, b_up, w_down, norm_gain, bias_terms = weights
    (
        inputs_b,
        queries,
        key_rows,
        value_rows,
        log_total,
        head_out,
        resid_one,
        hidden_b,
        pre_act,
        active_b,
        resid_two,
    ) = stored
    groups, span = key_mask.shape
    row_count, local_width = queries.shape
    split_shape = (groups, span, local_width // HEAD_DIM, HEAD_DIM)
    forward_two, norm_two = jax.vjp(norm_rows, resid_two, norm_gain[1], bias_terms[3])
    grad_two, gain_two, shift_two = norm_two(grad_out)
    grad_mlp = grad_two.astype(jnp.bfloat16)
    grad_wdown = jnp.dot(active_b.T, grad_mlp, preferred_element_type=jnp.float32)
    grad_act = jnp.dot(grad_mlp, w_down.T, preferred_element_type=jnp.float32)
    forward_gelu, gelu_back = jax.vjp(exact_gelu, pre_act)
    grad_pre = gelu_back(grad_act)[0].astype(jnp.bfloat16)
    grad_wup = jnp.dot(hidden_b.T, grad_pre, preferred_element_type=jnp.float32)
    up_part = lax.psum_scatter(
        jnp.dot(grad_pre, w_up.T, preferred_element_type=jnp.float32),
        "tensor",
        scatter_dimension=0,
        tiled=True,
    )
    grad_hidden = lax.all_gather(my_rows(grad_two) + up_part, "tensor", axis=0, tiled=True)
    forward_one, norm_one = jax.vjp(norm_rows, resid_one, norm_gain[0], bias_terms[2])
    grad_one, gain_one, shift_one = norm_one(grad_hidden)
    grad_attn = grad_one.astype(jnp.bfloat16)
    grad_wout = jnp.dot(head_out.T, grad_attn, preferred_element_type=jnp.float32)
    grad_heads = (
        jnp.dot(grad_attn, w_out.T, preferred_element_type=jnp.float32)
        .astype(jnp.bfloat16)
        .reshape(split_shape)
    )
    scores = attn_scores(queries, key_rows, key_mask, split_shape)
    attn_probs = jnp.exp(scores - log_total)
    grad_probs = jnp.einsum(
        "glhd,gmhd->ghlm",
        grad_heads,
        value_rows.reshape(split_shape),
        preferred_element_type=jnp.float32,
    )
    grad_values = jnp.einsum(
        "ghlm,glhd->gmhd",
        attn_probs.astype(jnp.bfloat16),
        grad_heads,
        preferred_element_type=jnp.float32,
    )
    grad_scores = (
        attn_probs * (grad_probs - jnp.sum(attn_probs * grad_probs, axis=-1, keepdims=True))
    ).astype(jnp.bfloat16)
    inv_root = HEAD_DIM ** (-0.5)
    grad_queries = (
        jnp.einsum(
            "ghlm,gmhd->glhd",
            grad_scores,
            key_rows.reshape(split_shape),
            preferred_element_type=jnp.float32,
        )
        * inv_root
    )
    grad_keys = (
        jnp.einsum(
            "ghlm,glhd->gmhd",
            grad_scores,
            queries.reshape(split_shape),
            preferred_element_type=jnp.float32,
        )
        * inv_root
    )
    grad_qkv = (
        jnp.stack([grad_queries, grad_keys, grad_values])
        .reshape(3, row_count, local_width)
        .astype(jnp.bfloat16)
    )
    grad_wqkv = jnp.einsum("rd,cre->cde", inputs_b, grad_qkv, preferred_element_type=jnp.float32)
    qkv_part = lax.psum_scatter(
        jnp.einsum("cre,cde->rd", grad_qkv, w_qkv, preferred_element_type=jnp.float32).astype(
            jnp.bfloat16
        ),
        "tensor",
        scatter_dimension=0,
        tiled=True,
    ).astype(jnp.float32)
    grad_inputs = lax.all_gather(
        (my_rows(grad_one) + qkv_part).astype(jnp.bfloat16), "tensor", axis=0, tiled=True
    ).astype(jnp.float32)
    grad_bqv = jnp.stack(
        [
            jnp.sum(grad_qkv[0].astype(jnp.float32), axis=0),
            jnp.sum(grad_qkv[2].astype(jnp.float32), axis=0),
        ]
    )
    grad_bup = jnp.sum(grad_pre.astype(jnp.float32), axis=0)
    grad_gain = jnp.stack([gain_one, gain_two])
    grad_shift = jnp.stack(
        [
            jnp.sum(grad_attn.astype(jnp.float32), axis=0),
            jnp.sum(grad_mlp.astype(jnp.float32), axis=0),
            shift_one,
            shift_two,
        ]
    )
    return (
        grad_inputs,
        (grad_wqkv, grad_bqv, grad_wout, grad_wup, grad_bup, grad_wdown, grad_gain, grad_shift),
    )


def deal_map(doc_ids, total_docs):
    return jnp.where(doc_ids % 2 == 1, (doc_ids + total_docs // 2) % total_docs, doc_ids)


def local_plan(seg_order, doc_lengths, seg_local, doc_local):
    total_docs = doc_lengths.shape[0]
    my_index = lax.axis_index("dp")
    doc_ids = jnp.arange(total_docs, dtype=jnp.int32)
    owner_pos = deal_map(doc_ids, total_docs)
    starts = jnp.sum((seg_order[None, :] < doc_ids[:, None]).astype(jnp.int32), axis=1)
    counts = jnp.sum((seg_order[None, :] == doc_ids[:, None]).astype(jnp.int32), axis=1)
    my_segments = my_index * seg_local + jnp.arange(seg_local, dtype=jnp.int32)
    seg_owner_doc = lax.dynamic_slice_in_dim(seg_order, my_index * seg_local, seg_local)
    seg_hot = seg_owner_doc[:, None] == doc_ids[None, :]
    my_start = jnp.sum(jnp.where(seg_hot, starts[None, :], 0), axis=1)
    my_length = jnp.sum(jnp.where(seg_hot, doc_lengths[None, :], 0), axis=1)
    my_owner = jnp.sum(jnp.where(seg_hot, owner_pos[None, :], 0), axis=1)
    within = my_segments - my_start
    valid_tokens = jnp.minimum(SEG, my_length - within * SEG)
    tok_mask = jnp.arange(SEG, dtype=jnp.int32)[None, :] < valid_tokens[:, None]
    src_slot = my_owner * MAXSEG + within
    my_deal = deal_map(my_index * doc_local + jnp.arange(doc_local, dtype=jnp.int32), total_docs)
    deal_hot = my_deal[:, None] == doc_ids[None, :]
    own_start = jnp.sum(jnp.where(deal_hot, starts[None, :], 0), axis=1)
    own_count = jnp.sum(jnp.where(deal_hot, counts[None, :], 0), axis=1)
    slot_index = jnp.arange(MAXSEG, dtype=jnp.int32)
    cross_mask = slot_index[None, :] < own_count[:, None]
    target = jnp.where(cross_mask, own_start[:, None] + slot_index[None, :], -1).reshape(-1)
    return (tok_mask, cross_mask, target, src_slot)


def picker(index_map, shard_rows):
    positions = jnp.arange(shard_rows.shape[0], dtype=jnp.int32)
    selector = (index_map[:, None] == positions[None, :]).astype(jnp.bfloat16)
    return jnp.dot(selector, shard_rows, preferred_element_type=jnp.float32)


def spreader(index_map, source_rows, row_span):
    positions = jnp.arange(row_span, dtype=jnp.int32)
    selector = (positions[:, None] == index_map[None, :]).astype(jnp.bfloat16)
    return jnp.dot(selector, source_rows, preferred_element_type=jnp.float32)


def add_terms(left, right):
    return jax.tree.map(jnp.add, left, right)


def local(
    tokens,
    seg_doc,
    doc_len,
    w_qkv,
    b_qv,
    w_out,
    w_up,
    b_up,
    w_down,
    norm_gain,
    bias_terms,
    seg_pos,
    cotangent,
):
    batches, local_rows, width = tokens.shape
    seg_local = local_rows // SEG
    doc_local = doc_len.shape[1] // lax.axis_size("dp")
    slot_rows = doc_local * MAXSEG

    def layer_weights(level):
        return (
            w_qkv[level],
            b_qv[level],
            w_out[level],
            w_up[level],
            b_up[level],
            w_down[level],
            norm_gain[level],
            bias_terms[level],
        )

    seg_weights = layer_weights(0)
    cross_weights = layer_weights(1)
    encoded = []
    grad_tokens = []
    seg_grads = []
    cross_grads = []
    pos_grads = []
    for batch_index in range(batches):
        tok_mask, cross_mask, target, src_slot = local_plan(
            seg_doc[batch_index], doc_len[batch_index], seg_local, doc_local
        )
        seg_out, seg_stored = layer_forward(
            tokens[batch_index].astype(jnp.float32), tok_mask, seg_weights
        )
        seg_cube = seg_out.reshape(seg_local, SEG, width)
        cls_rows = seg_cube[:, 0].astype(jnp.bfloat16)
        collected = picker(target, lax.all_gather(cls_rows, "dp", axis=0, tiled=True))
        cross_in = (collected.reshape(doc_local, MAXSEG, width) + seg_pos[None]).reshape(
            slot_rows, width
        )
        cross_out, cross_stored = layer_forward(cross_in, cross_mask, cross_weights)
        returned = picker(
            src_slot, lax.all_gather(cross_out.astype(jnp.bfloat16), "dp", axis=0, tiled=True)
        )
        encoded.append(
            seg_cube.at[:, 0].set(returned).reshape(local_rows, width).astype(jnp.bfloat16)
        )
        grad_cube = cotangent[batch_index].astype(jnp.float32).reshape(seg_local, SEG, width)
        grad_returned = grad_cube[:, 0].astype(jnp.bfloat16)
        grad_cross = lax.psum_scatter(
            spreader(src_slot, grad_returned, slot_rows * lax.axis_size("dp")),
            "dp",
            scatter_dimension=0,
            tiled=True,
        )
        grad_cross_in, cross_terms = layer_backward(
            grad_cross, cross_mask, cross_weights, cross_stored
        )
        pos_grads.append(jnp.sum(grad_cross_in.reshape(doc_local, MAXSEG, width), axis=0))
        grad_sent = grad_cross_in.astype(jnp.bfloat16)
        cross_grads.append(cross_terms)
        grad_cls = lax.psum_scatter(
            spreader(target, grad_sent, seg_local * lax.axis_size("dp")),
            "dp",
            scatter_dimension=0,
            tiled=True,
        )
        grad_seg = grad_cube.at[:, 0].set(grad_cls).reshape(local_rows, width)
        grad_inputs, seg_terms = layer_backward(grad_seg, tok_mask, seg_weights, seg_stored)
        grad_tokens.append(grad_inputs)
        seg_grads.append(seg_terms)
    seg_total = reduce(add_terms, seg_grads)
    cross_total = reduce(add_terms, cross_grads)
    pos_total = reduce(jnp.add, pos_grads)
    big_grads = (
        lax.psum_scatter(
            jnp.stack([seg_total[0], cross_total[0]]), "dp", scatter_dimension=2, tiled=True
        ),
        lax.psum_scatter(
            jnp.stack([seg_total[2], cross_total[2]]), "dp", scatter_dimension=2, tiled=True
        ),
        lax.psum_scatter(
            jnp.stack([seg_total[3], cross_total[3]]), "dp", scatter_dimension=1, tiled=True
        ),
        lax.psum_scatter(
            jnp.stack([seg_total[5], cross_total[5]]), "dp", scatter_dimension=2, tiled=True
        ),
    )
    small = lax.psum(
        (
            jnp.stack([seg_total[1], cross_total[1]]),
            jnp.stack([seg_total[4], cross_total[4]]),
            jnp.stack([seg_total[6], cross_total[6]]),
            jnp.stack([seg_total[7], cross_total[7]]),
            pos_total,
        ),
        "dp",
    )
    return (
        jnp.stack(encoded),
        jnp.stack(grad_tokens),
        big_grads[0],
        small[0],
        big_grads[1],
        big_grads[2],
        small[1],
        big_grads[3],
        small[2],
        small[3],
        small[4],
    )


BF = jnp.bfloat16
F32 = jnp.float32
D = 768
FF = 3072
HALF_FF = FF // 2
HALF_D = D // 2
CHUNK = 384
CHUNKS = 12
PAIRS = 6
MESH = pl.DeviceIdType.MESH
ROOT_HALF = 0.7071067811865476
PDF_SCALE = 0.3989422804014327


class Names:
    def __init__(self, **kw):
        self.__dict__.update(kw)


def mm(left, right):
    return jnp.dot(left, right, preferred_element_type=F32)


def mm_nt(left, right):
    return lax.dot_general(left, right, (((1,), (1,)), ((), ())), preferred_element_type=F32)


def span(index, size):
    return pl.ds(pl.multiple_of(index * size, size), size)


def row_norm(rows):
    centre = rows - jnp.mean(rows, axis=-1, keepdims=True)
    spread = jnp.mean(centre * centre, axis=-1, keepdims=True)
    scale = lax.rsqrt(spread + norm_eps)
    return centre * scale, scale


def stacked(pair, low_half):
    zero = jnp.zeros_like(pair)
    return jnp.concatenate(
        [jnp.where(low_half, pair, zero), jnp.where(low_half, zero, pair)], axis=0
    )


def soft_rows(scores):
    top = jnp.max(scores, axis=-1, keepdims=True)
    grown = jnp.exp(scores - top)
    return (grown * (1.0 / jnp.sum(grown, axis=-1, keepdims=True))).astype(BF)


def transpose_into(dest, source, rows):
    @pl.loop(0, rows // SEG)
    def _(s):
        dest[:, span(s, SEG)] = source[span(s, SEG), :].T


def gelu_pair(u):
    cdf = 0.5 * (1.0 + lax.erf(u * ROOT_HALF))
    slope = cdf + u * (PDF_SCALE * jnp.exp(-0.5 * u * u))
    return (u * cdf).astype(BF), slope.astype(BF)


def project(r, half):
    lanes = span(half, HALF_D)
    for c in range(3):
        r.qkv[c, :, lanes] = (mm(r.xb[...], r.wqkv[c, :, lanes]) + r.b3[c, :, lanes]).astype(BF)


def low_lanes():
    return lax.broadcasted_iota(jnp.int32, (SEG, SEG), 1) < HEAD_DIM


def attend(r, keep, first, count):
    segs = r.xb.shape[0] // SEG
    root = jnp.asarray(HEAD_DIM ** (-0.5), BF)

    @pl.loop(0, segs, unroll=min(segs, 4))
    def _(s):
        at = span(s, SEG)
        live = keep(s)
        low_half = low_lanes()
        for k in range(count):
            p = first + k
            cols = span(p, SEG)
            keys = stacked(r.qkv[1, at, cols], low_half)
            vals = stacked(r.qkv[2, at, cols], low_half)
            raw = mm_nt(r.qkv[0, at, cols] * root, keys)
            one = soft_rows(jnp.where(live, raw[:, :SEG], masked_score))
            two = soft_rows(jnp.where(live, raw[:, SEG:], masked_score))
            both = jnp.concatenate([one, two], axis=1)
            r.p[s, p] = both
            r.o[at, cols] = mm(both, vals).astype(BF)


def attn_out(r):
    for n in range(3):
        cols = slice(n * 256, n * 256 + 256)
        r.xh1[:, cols] = mm(r.o[...], r.wout[:, cols]) + r.bt[0, :, cols]


def norm_one(r, x_ref):
    rows = r.xh1.shape[0]
    block = min(rows, 256)

    @pl.loop(0, rows // block)
    def _(s):
        at = span(s, block)
        hat, scale = row_norm(x_ref[at, :].astype(F32) + r.xh1[at, :])
        r.xh1[at, :] = hat
        r.rs1[at, :] = jnp.broadcast_to(scale, (block, SEG))
        hidden = hat * r.gain[0] + r.bt[2]
        r.h1[at, :] = hidden
        r.h1b[at, :] = hidden.astype(BF)
        r.xh2[at, :] = hidden + r.bt[1]


def mlp_up(r, before):
    @pl.loop(0, 4)
    def _(j):
        before(j)
        for k in range(3):
            cols = pl.ds(pl.multiple_of(j * D + k * 256, 256), 256)
            u = mm(r.h1b[...], r.wup[:, cols]) + r.bup[:, cols]
            r.g[:, cols], r.gp[:, cols] = gelu_pair(u)


def mlp_down(r, before):
    @pl.loop(0, 2)
    def _(half):
        before(half)
        part = span(half, HALF_FF)
        for n in range(3):
            cols = slice(n * 256, n * 256 + 256)
            r.xh2[:, cols] = r.xh2[:, cols] + mm(r.g[:, part], r.wdown[part, cols])


def norm_two(r, y_ref):
    rows = r.xh2.shape[0]
    block = min(rows, 256)

    @pl.loop(0, rows // block)
    def _(s):
        at = span(s, block)
        hat, scale = row_norm(r.xh2[at, :])
        r.xh2[at, :] = hat
        r.rs2[at, :] = jnp.broadcast_to(scale, (block, SEG))
        y_ref[at, :] = (hat * r.gain[1] + r.bt[3]).astype(BF)


def norm_back(grad, hat, scale, gain):
    d_hat = grad * gain
    first = jnp.mean(d_hat, axis=-1, keepdims=True)
    second = jnp.mean(d_hat * hat, axis=-1, keepdims=True)
    return (d_hat - first - hat * second) * scale


def norm_back_rows(r, hat_ref, scale_ref, gain, grad_of):
    zero = jnp.zeros((1, D), F32)
    rows = r.dr.shape[0]
    block = min(rows, 256)

    def step(s, sums):
        at = span(s, block)
        grad = grad_of(s, at)
        hat = hat_ref[at, :]
        out = norm_back(grad, hat, scale_ref[at, 0:1], gain)
        low = out.astype(BF)
        r.dr[at, :] = out
        r.dm[at, :] = low
        return (
            sums[0] + jnp.sum(grad * hat, axis=0, keepdims=True),
            sums[1] + jnp.sum(grad, axis=0, keepdims=True),
            sums[2] + jnp.sum(low.astype(F32), axis=0, keepdims=True),
        )

    sums = lax.fori_loop(0, rows // block, step, (zero, zero, zero))
    transpose_into(r.dmt, r.dm, rows)
    return sums


def back_norm_two(r, grad_of):
    sums = norm_back_rows(r, r.xh2, r.rs2, r.gain[1], grad_of)
    r.small_common[1], r.small_common[5], r.small_common[3] = sums


def back_norm_one(r):
    sums = norm_back_rows(r, r.xh1, r.rs1, r.gain[0], lambda s, at: r.dr[at, :])
    r.small_common[0], r.small_common[4], r.small_common[2] = sums


def grad_hidden(r):
    @pl.loop(0, 3)
    def _(j):
        cols = span(j, 1024)
        du = (mm_nt(r.dm[...], r.wdown[cols, :]) * r.gp[:, cols].astype(F32)).astype(BF)
        r.gp[:, cols] = du
        r.bup_sum[:, cols] = jnp.sum(du.astype(F32), axis=0, keepdims=True)


def grad_middle(r):
    @pl.loop(0, 2)
    def _(n):
        cols = span(n, CHUNK)
        r.dr[:, cols] = r.dr[:, cols] + mm_nt(r.gp[...], r.wup[cols, :])


def grad_heads(r):
    for n in range(3):
        cols = slice(n * 256, n * 256 + 256)
        r.dh[:, cols] = mm_nt(r.dm[...], r.wout[cols, :]).astype(BF)


def attend_back_values(r):
    segs = r.dh.shape[0] // SEG

    @pl.loop(0, segs, unroll=min(segs, 2))
    def _(s):
        at = span(s, SEG)
        low_half = low_lanes()
        for p in range(PAIRS):
            d_vals = mm(r.p[s, p].T, r.dh[at, p * SEG : p * SEG + SEG])
            cols = slice(2 * D + p * SEG, 2 * D + p * SEG + SEG)
            r.g[at, cols] = jnp.where(low_half, d_vals[:SEG], d_vals[SEG:]).astype(BF)


def attend_back(r, exact, before):
    root = jnp.asarray(HEAD_DIM ** (-0.5), BF)
    segs = r.dh.shape[0] // SEG
    together = min(segs, 2)

    def segment(s):
        at = span(s, SEG)
        low_half = low_lanes()
        head = lax.broadcasted_iota(jnp.int32, (SEG, 2 * SEG), 0) < HEAD_DIM
        side = lax.broadcasted_iota(jnp.int32, (SEG, 2 * SEG), 1) < SEG
        ones = jnp.where(head == side, 1.0, 0.0).astype(BF)
        for p in range(PAIRS):
            cols = slice(p * SEG, p * SEG + SEG)
            query = r.qkv[0, at, cols] * root
            keys = stacked(r.qkv[1, at, cols] * root, low_half)
            vals = stacked(r.qkv[2, at, cols], low_half)
            d_head = r.dh[at, cols]
            d_probs = mm_nt(d_head, vals)
            both = d_head.astype(F32) * r.o[at, cols].astype(F32)
            inner = mm(both.astype(BF), ones)
            if exact:
                inner = inner + mm((both - both.astype(BF).astype(F32)).astype(BF), ones)
            d_scores = (r.p[s, p].astype(F32) * (d_probs - inner)).astype(BF)
            d_keys = mm(d_scores.T, query)
            r.g[at, cols] = mm(d_scores, keys).astype(BF)
            cols = slice(D + p * SEG, D + p * SEG + SEG)
            r.g[at, cols] = jnp.where(low_half, d_keys[:SEG], d_keys[SEG:]).astype(BF)

    @pl.loop(0, segs // together)
    def _(i):
        before(i)
        for k in range(together):
            segment(i * together + k)


def bias_heads(r):
    for c in (0, 2):
        r.qv_sum[c // 2] = jnp.sum(
            r.g[:, c * D : (c + 1) * D].astype(F32), axis=0, keepdims=True
        )


def grad_input(r):
    for n in range(3):
        cols = slice(n * 256, n * 256 + 256)
        total = r.dr[:, cols]
        for c in range(3):
            total = total + mm_nt(r.g[:, c * D : (c + 1) * D], r.wqkv[c, cols, :])
        r.dr[:, cols] = total


def chunk_operands(r, c):
    if c < 4:
        return r.dmt, (r.g, c * CHUNK, HALF_FF + c * CHUNK)
    if c < 8:
        return r.h1t, (r.gp, (c - 4) * CHUNK, HALF_FF + (c - 4) * CHUNK)
    if c == 8:
        return r.dmt, (r.o, 0, HALF_D)
    at = QKV_OF[c - 9] * D
    return r.xt, (r.g, at, at + HALF_D)


QKV_OF = (2, 0, 1)
HOOK_CHUNKS = {"down": (0, 4), "up": (4, 8), "out": (8, 9), "qkv": (9, 12), "v": (9, 10), "qk": (10, 12)}


class Copies:
    def __init__(self, sems):
        self.sems = sems
        self.used = 0

    def start(self, source, dest):
        copy = pltpu.make_async_copy(source, dest, self.sems.at[self.used])
        self.used += 1
        copy.start()
        return copy


def remote(source, dest, send_sem, recv_sem, device):
    return pltpu.make_async_remote_copy(
        src_ref=source,
        dst_ref=dest,
        send_sem=send_sem,
        recv_sem=recv_sem,
        device_id=device,
        device_id_type=MESH,
    )


class Gather:
    def __init__(self, dp, everyone, send, recv):
        self.dp, self.everyone, self.send, self.recv = dp, everyone, send, recv

    def start(self, block):
        d, t = lax.axis_index("dp"), lax.axis_index("tensor")
        everyone = self.everyone
        everyone[d] = block
        for o in range(1, self.dp):
            peer = (lax.rem(d + o, self.dp), t)
            copy = remote(everyone.at[d], everyone.at[d], self.send.at[o], self.recv.at[d], peer)
            copy.start()

    def sent(self):
        d, t = lax.axis_index("dp"), lax.axis_index("tensor")
        block = self.everyone.at[d]
        for o in range(1, self.dp):
            peer = (lax.rem(d + o, self.dp), t)
            remote(block, block, self.send.at[o], self.recv.at[d], peer).wait_send()

    def arrived(self):
        d, t = lax.axis_index("dp"), lax.axis_index("tensor")
        for o in range(1, self.dp):
            source = lax.rem(d + o, self.dp)
            block = self.everyone.at[source]
            remote(block, block, self.send.at[o], self.recv.at[source], (source, t)).wait_recv()

    def rows_into(self, dest):
        segs = self.everyone.shape[1]
        pack = 8 // segs
        for i in range(self.dp // pack):
            blocks = [self.everyone[i * pack + k].astype(F32) for k in range(pack)]
            dest[i * 8 : i * 8 + 8, :] = jnp.concatenate(blocks, axis=0)


SLOTS = 4
RING = 9
WEIGHTS = ("wqkv", "wout", "wup", "wdown")


def half_of(ref, which, half):
    if which == "wqkv":
        return ref.at[:, :, half * HALF_D : (half + 1) * HALF_D]
    if which == "wout":
        return ref.at[half * HALF_D : (half + 1) * HALF_D, :]
    if which == "wup_square":
        return ref.at[:, half * HALF_D : (half + 1) * HALF_D]
    if which == "wup":
        return ref.at[:, half * HALF_FF : (half + 1) * HALF_FF]
    return ref.at[half * HALF_FF : (half + 1) * HALF_FF, :]


def fill_bias(b3, bup, half, layer, b_qv, b_up):
    lanes = slice(half * HALF_D, (half + 1) * HALF_D)
    b3[0, :, lanes] = b_qv[layer, 0:1, :]
    b3[1, :, lanes] = jnp.zeros((1, HALF_D), F32)
    b3[2, :, lanes] = b_qv[layer, 1:2, :]
    bup[:, half * HALF_FF : (half + 1) * HALF_FF] = b_up[layer : layer + 1, :]


def pack_halves(r):
    for half in range(2):
        at = 6 + 3 * half
        lanes = slice(half * HALF_D, (half + 1) * HALF_D)
        r.small[at, :, 0:HALF_D] = r.qv_sum[0, :, lanes]
        r.small[at, :, HALF_D:] = r.qv_sum[1, :, lanes]
        base = half * HALF_FF
        r.small[at + 1] = r.bup_sum[:, base : base + D]
        r.small[at + 2] = r.bup_sum[:, base + D : base + 2 * D]


def first_of_segments(ref, segs):
    return jnp.concatenate(
        [ref[s * SEG : s * SEG + 16, :].astype(F32)[0:1] for s in range(segs)], axis=0
    )


class Stream:
    ORDER = (
        [("qkv", c) for c in range(3)] + [("out", 0)] + [("up", j) for j in range(4)]
        + [("down", j) for j in range(4)] * 2
        + [("up", j) for j in range(4)] + [("out", 0)] + [("qkv", c) for c in range(3)]
    )
    DEPTH = 4

    def __init__(self, r, arriving):
        self.r = r
        self.arriving = arriving
        self.next = 0
        self.pending = []

    def copies(self, n):
        r = self.r
        kind, index = self.ORDER[n]
        which = "w" + kind
        halves = (getattr(r, "a_" + which).at[1], getattr(r, "f_" + which))
        dest, sems = r.ring_w.at[n % self.DEPTH], r.ring_sem.at[n % self.DEPTH]
        if kind == "qkv":
            pairs = [(halves[h].at[index], half_of(dest, "wup_square", h)) for h in range(2)]
        elif kind == "out":
            pairs = [(halves[h], half_of(dest, "wout", h)) for h in range(2)]
        else:
            at = slice(index % 2 * D, index % 2 * D + D)
            source = halves[index // 2]
            pairs = [(source.at[:, at] if kind == "up" else source.at[at, :], dest)]
        return [pltpu.make_async_copy(a, b, sems.at[k]) for k, (a, b) in enumerate(pairs)]

    def start(self, n):
        if n < len(self.ORDER):
            kind, index = self.ORDER[n]
            if index >= 2 and kind in self.arriving:
                self.arriving.pop(kind).wait_recv()
            self.pending.append(self.copies(n))
            for copy in self.pending[-1]:
                copy.start()

    def take(self, body):
        for copy in self.pending.pop(0):
            copy.wait()
        kind, index = self.ORDER[self.next]
        body(index, self.r.ring_w.at[self.next % self.DEPTH])
        self.start(self.next + self.DEPTH)
        self.next += 1


def cross_layer(r, q, stream, keep, pump, hooks):
    def lanes(j):
        return slice(j * D, (j + 1) * D)

    def project_piece(c, w):
        q.qkv[c] = (mm(q.xb[...], w[...]) + q.b3[c]).astype(BF)

    for c in range(3):
        stream.take(project_piece)
    attend(q, keep, 0, PAIRS)
    pump("attend")

    def out_piece(j, w):
        q.xh1[...] = mm(q.o[...], w[...]) + q.bt[0]

    stream.take(out_piece)
    norm_one(q, q.x32)
    transpose_into(q.h1t, q.h1b, SEG)

    def up_piece(j, w):
        u = mm(q.h1b[...], w[...]) + q.bup[:, lanes(j)]
        q.g[:, lanes(j)], q.gp[:, lanes(j)] = gelu_pair(u)

    for j in range(4):
        stream.take(up_piece)
    pump("up")

    def down_piece(j, w):
        q.xh2[...] = q.xh2[...] + mm(q.g[:, lanes(j)], w[...])

    for j in range(4):
        stream.take(down_piece)
    norm_two(q, q.yb)
    pump("down")
    back_norm_two(q, lambda s, at: q.dy[at, :])
    hooks("down")

    def back_down_piece(j, w):
        du = (mm_nt(q.dm[...], w[...]) * q.gp[:, lanes(j)].astype(F32)).astype(BF)
        q.gp[:, lanes(j)] = du
        r.bup_sum[:, lanes(j)] = jnp.sum(du.astype(F32), axis=0, keepdims=True)

    for j in range(4):
        stream.take(back_down_piece)
    pump("back_down")
    hooks("up")

    def back_up_piece(j, w):
        q.dr[...] = q.dr[...] + mm_nt(q.gp[:, lanes(j)], w[...])

    for j in range(4):
        stream.take(back_up_piece)
    pump("back_up")
    back_norm_one(q)
    hooks("out")

    def back_out_piece(j, w):
        q.dh[...] = mm_nt(q.dm[...], w[...]).astype(BF)

    stream.take(back_out_piece)
    attend_back_values(q)
    attend_back(q, True, lambda i: None)
    bias_heads(q)
    pump("attend_back")
    hooks("qkv")

    def back_qkv_piece(c, w):
        q.dr[...] = q.dr[...] + mm_nt(q.g[:, lanes(c)], w[...])

    for c in range(3):
        stream.take(back_qkv_piece)


def whole_kernel(dp, names, *refs):
    r = Names(**dict(zip(names, refs)))
    d, t = lax.axis_index("dp"), lax.axis_index("tensor")
    x, y, z = lax.rem(d, 2), lax.rem(lax.div(d, 2), 2), lax.div(d, 4)
    zs = dp // 4
    shard = D // dp
    rows = r.xb.shape[0]
    segs = rows // SEG
    sibling = (d, 1 - t)
    x_peer = (z * 4 + y * 2 + (1 - x), t)
    y_peer = (z * 4 + (1 - y) * 2 + x, t)
    z_peers = [(lax.rem(z + o, zs) * 4 + y * 2 + x, t) for o in range(1, zs)]
    r.dr, r.dm, r.y1, r.dh = r.h1, r.h1b, r.xb, r.cot

    barrier = pltpu.get_barrier_semaphore()
    for device in [sibling] + [(lax.rem(d + o, dp), t) for o in range(1, dp)]:
        pl.semaphore_signal(barrier, inc=1, device_id=device, device_id_type=MESH)
    copies = Copies(r.local_sem)
    for layer, gain, terms in ((0, r.gain, r.bt), (1, r.gain_cross, r.bt_cross)):
        for k in range(2):
            gain[k] = r.norm_gain[layer, k : k + 1, :]
        for k in range(4):
            terms[k] = r.bias_terms[layer, k : k + 1, :]
    own = {w: getattr(r, "a_" + w) for w in WEIGHTS}
    full = {w: getattr(r, "f_" + w) for w in WEIGHTS}
    load_x = copies.start(r.tokens.at[t], r.xb)
    loads = {w: copies.start(own[w].at[0], half_of(getattr(r, w), w, 0)) for w in WEIGHTS}
    load_cot = copies.start(r.cotangent.at[t], r.cot)
    load_x.wait()
    transpose_into(r.xt, r.xb, rows)
    fill_bias(r.b3, r.bup, 0, 0, r.b_qv, r.b_up)
    fill_bias(r.b3_cross, r.bup_cross, 0, 1, r.b_qv, r.b_up)
    swaps = {}

    def described(layer, w):
        k = WEIGHTS.index(w)
        dest = half_of(getattr(r, w), w, 1) if layer == 0 else full[w]
        return remote(own[w].at[layer], dest, r.w_send.at[layer, k], r.w_recv.at[layer, k], sibling)

    for layer in range(2):
        for w in WEIGHTS:
            swaps[layer, w] = described(layer, w)

    def swap(layer, w):
        swaps[layer, w].start()

    cot_gather = Gather(dp, r.cot_all, r.g_send.at[0], r.g_recv.at[0])
    cls_gather = Gather(dp, r.cls_all, r.g_send.at[1], r.g_recv.at[1])
    hat_gather = Gather(dp, r.hat_all, r.g_send.at[2], r.g_recv.at[2])
    act_gather = Gather(dp, r.act_all, r.g_send.at[3], r.g_recv.at[3])

    def keep(s):
        seg = d * segs + s
        doc = r.seg_doc[t, seg]
        within = jnp.int32(0)
        for back in range(1, MAXSEG):
            same = r.seg_doc[t, jnp.maximum(seg - back, 0)] == doc
            within = within + jnp.where(jnp.logical_and(seg >= back, same), 1, 0)
        valid = jnp.minimum(SEG, r.doc_len[t, doc] - SEG * within)
        return lax.broadcasted_iota(jnp.int32, (1, SEG), 1) < valid

    def start_swaps():
        pl.semaphore_wait(barrier, dp)
        swap(0, "wqkv")
        for copy in swap_bias:
            copy.start()
        swap(0, "wout")
        swap(0, "wup")
        load_cot.wait()
        cot_gather.start(first_of_segments(r.cot, segs).astype(BF))

    def take_other():
        for copy in swap_bias:
            copy.wait_recv()
        fill_bias(r.b3, r.bup, 1, 0, r.x_bqv, r.x_bup)
        fill_bias(r.b3_cross, r.bup_cross, 1, 1, r.x_bqv, r.x_bup)
        swaps[0, "wqkv"].wait_recv()

    swap_bias = [
        remote(r.b_qv, r.x_bqv, r.w_send.at[0, 4], r.w_recv.at[0, 4], sibling),
        remote(r.b_up, r.x_bup, r.w_send.at[1, 4], r.w_recv.at[1, 4], sibling),
    ]
    loads["wqkv"].wait()

    @pl.loop(0, 2)
    def _(half):
        pl.when(half == 1)(take_other)
        project(r, half)
        pl.when(half == 0)(start_swaps)
        attend(r, keep, half * (PAIRS // 2), PAIRS // 2)

    swap(0, "wdown")
    loads["wout"].wait()
    swaps[0, "wout"].wait_recv()
    attn_out(r)
    norm_one(r, r.xb)
    loads["wup"].wait()
    mlp_up(r, lambda j: pl.when(j == 2)(swaps[0, "wup"].wait_recv))
    transpose_into(r.h1t, r.h1b, rows)
    loads["wdown"].wait()
    mlp_down(r, lambda half: pl.when(half == 1)(swaps[0, "wdown"].wait_recv))
    swap(1, "wqkv")
    swap(1, "wout")
    norm_two(r, r.y1)
    cls_gather.start(first_of_segments(r.y1, segs).astype(BF))
    hats = first_of_segments(r.xh2, segs)
    hat_gather.start(jnp.concatenate([hats, first_of_segments(r.rs2, segs)], axis=1))

    def sib_copy(c):
        slot = lax.rem(c, SLOTS)
        return remote(
            r.sib_out.at[slot], r.sib_in.at[slot], r.sib_send.at[slot], r.sib_recv.at[slot], sibling
        )

    def ring(c):
        return lax.rem(c, RING)

    low_z, high_z = slice(0, zs // 2), slice(zs // 2, zs)

    def stage_one(c):
        g, into = r.gbuf.at[ring(c)], r.one_in.at[ring(c)]
        return (
            remote(g.at[low_z, :, 1 - x], into.at[0], r.one_send.at[c, 0], r.one_recv.at[c, 0], x_peer),
            remote(g.at[high_z, 1 - y], into.at[1], r.one_send.at[c, 1], r.one_recv.at[c, 1], y_peer),
        )

    def stage_two(c):
        g, into = r.gbuf.at[ring(c)], r.two_in.at[ring(c)]
        return (
            remote(g.at[low_z, 1 - y, x], into.at[0], r.two_send.at[c, 0], r.two_recv.at[c, 0], y_peer),
            remote(g.at[high_z, y, 1 - x], into.at[1], r.two_send.at[c, 1], r.two_recv.at[c, 1], x_peer),
        )

    def stage_three(c):
        g, into = r.gbuf.at[ring(c)], r.three_in.at[ring(c)]
        return [
            remote(
                g.at[lax.rem(z + o, zs), y, x],
                into.at[o - 1],
                r.three_send.at[c, o - 1],
                r.three_recv.at[c, o - 1],
                z_peers[o - 1],
            )
            for o in range(1, zs)
        ]

    def emit_other(c, left, right, at):
        @pl.when(c >= SLOTS)
        def _():
            sib_copy(c).wait_send()
            pl.semaphore_wait(r.credit, 1)

        r.sib_out[lax.rem(c, SLOTS)] = mm(left[...], right[:, pl.ds(at, CHUNK)]).astype(BF)
        sib_copy(c).start()

    def emit_own(c, left, right, at):
        mine = mm(left[...], right[:, pl.ds(at, CHUNK)])
        sib_copy(c).wait_recv()
        mine = (mine + r.sib_in[lax.rem(c, SLOTS)].astype(F32)).astype(BF)
        r.gbuf[ring(c)] = mine.reshape(zs, 2, 2, shard, CHUNK)

        @pl.when(c < CHUNKS - SLOTS)
        def _():
            pl.semaphore_signal(r.credit, inc=1, device_id=sibling, device_id_type=MESH)

    def launch(*chunks):
        for c in chunks:
            for copy in stage_one(jnp.int32(c)):
                copy.start()

    def hooks(name, which, part=None):
        low, high = HOOK_CHUNKS[name]
        left, (right, own_at, other_at) = chunk_operands(r, low)
        step = D if name == "qk" else CHUNK

        def at(c, base):
            return pl.multiple_of((c - low) * step + base, SEG)

        if which == "other":

            @pl.loop(low, high)
            def _(c):
                emit_other(c, left, right, at(c, other_at))

        else:

            @pl.loop(*(part or (low, high)))
            def _(c):
                emit_own(c, left, right, at(c, own_at))
                if which == "launch":
                    for copy in stage_one(c):
                        copy.start()

    def second(*chunks):
        for c in chunks:
            c = jnp.int32(c)
            g, into = r.gbuf.at[ring(c)], r.one_in.at[ring(c)]
            from_x, from_y = stage_one(c)
            to_y, to_x = stage_two(c)
            from_x.wait_recv()
            g[low_z, :, x] = g[low_z, :, x] + into[0]
            to_y.start()
            from_y.wait_recv()
            g[high_z, y] = g[high_z, y] + into[1]
            to_x.start()

    def third(*chunks):
        for c in chunks:
            c = jnp.int32(c)
            g, into = r.gbuf.at[ring(c)], r.two_in.at[ring(c)]
            for copy in stage_two(c):
                copy.wait_recv()
            g[low_z, y, x] = g[low_z, y, x] + into[0]
            g[high_z, y, x] = g[high_z, y, x] + into[1]
            for copy in stage_three(c):
                copy.start()

    def finish(*chunks):
        for c in chunks:
            at = jnp.int32(c)
            total = r.gbuf[ring(at), z, y, x].astype(F32)
            for o, copy in enumerate(stage_three(at)):
                copy.wait_recv()
                total = total + r.three_in[ring(at), o].astype(F32)
            r.mine[c] = r.mine[c] + total if c < 4 else total
            for copy in (*stage_one(at), *stage_two(at), *stage_three(at)):
                copy.wait_send()

    block_row = lax.broadcasted_iota(jnp.int32, (256, 1), 0)

    def without_first(s, at):
        return jnp.where(lax.rem(block_row, SEG) == 0, 0.0, r.cot[at, :].astype(F32))

    r.act_first[...] = first_of_segments(r.g, segs)
    r.small_common = r.small
    back_norm_two(r, without_first)
    hooks("down", "other")
    swap(1, "wup")
    hooks("down", "launch")
    swap(1, "wdown")
    act_gather.start(r.act_first[...].astype(BF))

    q = Names(
        **{k: getattr(r, "q_" + k) for k in CROSS},
        g=r.g.at[0:SEG],
        gp=r.g.at[SEG : 2 * SEG],
        gain=r.gain_cross,
        bt=r.bt_cross,
        b3=r.b3_cross,
        bup=r.bup_cross,
        qv_sum=r.qv_sum,
    )
    q.dr, q.dm, q.small_common = q.h1, q.h1b, r.small1
    slots = q.xb.shape[0]
    total_docs = slots // MAXSEG
    total_segs = dp * segs
    stream = Stream(r, {"up": swaps[1, "wup"], "down": swaps[1, "wdown"]})
    for w in ("wqkv", "wout"):
        swaps[1, w].wait_recv()
    for n in range(stream.DEPTH):
        stream.start(n)

    doc = jnp.where(t == 0, r.seg_doc_v[0:1, :], r.seg_doc_v[1:2, :])
    below = lax.broadcasted_iota(jnp.int32, (total_segs, total_segs), 0)
    across = lax.broadcasted_iota(jnp.int32, (total_segs, total_segs), 1)

    def column(row):
        wide = jnp.broadcast_to(row, (total_segs, total_segs))
        return jnp.sum(jnp.where(below == across, wide, 0.0), axis=1, keepdims=True)

    doc_f = doc.astype(F32)
    earlier = jnp.logical_and(column(doc_f) == doc_f, below < across)
    within = jnp.sum(jnp.where(earlier, 1.0, 0.0), axis=0, keepdims=True).astype(jnp.int32)
    moved = doc + total_docs // 2
    moved = jnp.where(moved >= total_docs, moved - total_docs, moved)
    slot_of = (jnp.where((doc & 1) == 1, moved, doc) * MAXSEG + within).astype(F32)
    slot_ids = lax.broadcasted_iota(jnp.int32, (slots, total_segs), 0).astype(F32)
    deal = jnp.where(slot_ids == slot_of, 1.0, 0.0).astype(BF)
    slot_row = lax.broadcasted_iota(jnp.int32, (total_segs, slots), 1).astype(F32)
    r.undeal[...] = jnp.where(slot_row == column(slot_of), 1.0, 0.0).astype(BF)
    pick_row = lax.broadcasted_iota(jnp.int32, (8, total_segs), 0)
    pick_seg = lax.broadcasted_iota(jnp.int32, (8, total_segs), 1)
    picked = jnp.logical_and(pick_row < segs, pick_seg == d * segs + pick_row)
    r.back[...] = mm(jnp.where(picked, 1.0, 0.0).astype(BF), r.undeal[...]).astype(BF)
    live = mm_nt(jnp.ones((8, total_segs), BF), deal)[0:1] > 0.5
    key_doc = lax.broadcasted_iota(jnp.int32, (SEG, SEG), 1) >> 3
    row_doc = lax.broadcasted_iota(jnp.int32, (SEG, SEG), 0) >> 3
    r.allowed[...] = jnp.where(jnp.logical_and(key_doc == row_doc, live), 1.0, 0.0)

    cot_gather.arrived()
    cot_gather.rows_into(r.rows64)
    q.dy[...] = mm(deal, r.rows64[...].astype(BF))
    cls_gather.arrived()
    cls_gather.rows_into(r.rows64)
    q.x32[...] = mm(deal, r.rows64[...].astype(BF)) + jnp.concatenate(
        [r.seg_pos[...]] * total_docs, axis=0
    )
    q.xb[...] = q.x32[...].astype(BF)
    transpose_into(q.xt, q.xb, slots)

    def cross_hooks(name):
        low, high = HOOK_CHUNKS[name]
        for c in range(low, high):
            left, (right, own_at, other_at) = chunk_operands(q, c)
            mine = left[pl.ds(pl.multiple_of(d * shard, 16), shard), :]
            r.shard1[c] = mm(mine, right[:, own_at : own_at + CHUNK])
            r.shard_out[c] = mm(mine, right[:, other_at : other_at + CHUNK]).astype(BF)

    def pump(point):
        if point == "back_up":
            second(0, 1)
        elif point == "attend_back":
            second(2, 3)

    cross_layer(r, q, stream, lambda s: r.allowed[...] > 0.5, pump, cross_hooks)
    r.small, keep_small = r.small1, r.small
    pack_halves(r)
    r.small = keep_small
    total = q.dr[0:MAXSEG, :]
    for j in range(1, total_docs):
        total = total + q.dr[j * MAXSEG : (j + 1) * MAXSEG, :]
    for k in range(MAXSEG):
        r.small1[12 + k] = total[k : k + 1, :]
    r.ret[...] = mm(r.back[...], q.yb[...])
    low = q.dr[...].astype(BF)
    r.dc[...] = mm(r.back[...], low)

    gain_sum = jnp.zeros((1, D), F32)
    shift_sum, low_sum = gain_sum, gain_sum
    top = lax.broadcasted_iota(jnp.int32, (16, 1), 0) == 0
    for s in range(segs):
        at = slice(s * SEG, s * SEG + 16)
        grad = jnp.where(top, r.dc[s : s + 1, :], 0.0)
        hat = r.xh2[at, :]
        out = jnp.where(top, norm_back(grad, hat, r.rs2[at, 0:1], r.gain[1]), 0.0)
        out_low = out.astype(BF)
        r.dr[at, :] = jnp.where(top, out, r.dr[at, :])
        r.dm[at, :] = jnp.where(top, out_low.astype(F32), r.dm[at, :].astype(F32)).astype(BF)
        gain_sum = gain_sum + jnp.sum(grad * hat, axis=0, keepdims=True)
        shift_sum = shift_sum + jnp.sum(grad, axis=0, keepdims=True)
        low_sum = low_sum + jnp.sum(out_low.astype(F32), axis=0, keepdims=True)
        r.y1[at, :] = jnp.where(top, r.ret[s : s + 1, :], r.y1[at, :].astype(F32)).astype(BF)
    r.small_common[1] = r.small_common[1] + gain_sum
    r.small_common[5] = r.small_common[5] + shift_sum
    r.small_common[3] = r.small_common[3] + low_sum
    outs = [copies.start(r.y1, r.o_enc.at[t])]
    enc_swap = remote(r.y1, r.o_enc.at[t], r.misc_send.at[0], r.misc_recv.at[0], sibling)
    enc_swap.start()

    hat_gather.arrived()
    hat_gather.rows_into(r.hat64)
    act_gather.arrived()
    act_gather.rows_into(r.act64)
    all_grads = mm(r.undeal[...], low)
    late = norm_back(all_grads, r.hat64[:, 0:D], r.hat64[:, D : D + 1], r.gain[1]).astype(BF)
    r.late[0:total_segs, :] = late
    r.late[total_segs:, :] = jnp.zeros((SEG - total_segs, D), BF)
    transpose_into(r.late_t, r.late, SEG)
    mine = r.late_t[pl.ds(pl.multiple_of(d * shard, 16), shard), 0:total_segs]
    for c in range(4):
        for half in range(2):
            cols = slice(half * HALF_FF + c * CHUNK, half * HALF_FF + (c + 1) * CHUNK)
            part = mm(mine, r.act64[:, cols].astype(BF))
            if half == 0:
                r.mine[c] = part
            else:
                r.shard_out[CHUNKS + c] = part.astype(BF)
    cross_swap = [
        remote(r.shard_out, r.shard_in, r.misc_send.at[1], r.misc_recv.at[1], sibling),
        remote(r.small1.at[0:6], r.small1_in.at[0:6], r.misc_send.at[2], r.misc_recv.at[2], sibling),
        remote(r.small1.at[9:20], r.small1_in.at[6:17], r.misc_send.at[3], r.misc_recv.at[3], sibling),
    ]
    for copy in cross_swap:
        copy.start()

    third(0, 1)
    grad_hidden(r)
    third(2, 3)
    hooks("up", "other")
    hooks("up", "own")
    launch(4, 5)
    grad_middle(r)
    for copy in cross_swap:
        copy.wait()
    for c in range(CHUNKS):
        r.shard1[c] = r.shard1[c] + r.shard_in[c].astype(F32)
    r.o_small[9:26] = (
        jnp.concatenate([r.small1[0:9], r.small1[12:20]], axis=0) + r.small1_in[...]
    )
    outs.append(copies.start(r.shard1, r.o_shard.at[1]))
    back_norm_one(r)
    second(4)
    launch(6)
    hooks("out", "other")
    grad_heads(r)
    hooks("out", "own")
    second(5)
    launch(7)
    attend_back_values(r)
    hooks("v", "other")
    finish(0, 1, 2, 3)
    for c in range(4):
        r.mine[c] = r.mine[c] + r.shard_in[CHUNKS + c].astype(F32)

    def halfway():
        second(6)
        third(4)
        hooks("v", "own")
        launch(8, 9)

    attend_back(r, False, lambda i: pl.when(i == 1)(halfway))
    bias_heads(r)
    pack_halves(r)
    small_swap = [
        remote(r.small.at[0:6], r.small_in.at[0:6], r.misc_send.at[4], r.misc_recv.at[4], sibling),
        remote(r.small.at[9:12], r.small_in.at[6:9], r.misc_send.at[5], r.misc_recv.at[5], sibling),
    ]
    for copy in small_swap:
        copy.start()
    hooks("qk", "other")
    second(7)
    third(5)
    for copy in small_swap:
        copy.wait()
    r.total[...] = r.small[0:9] + r.small_in[...]
    x_small = remote(r.total, r.x_small, r.misc_send.at[7], r.misc_recv.at[7], x_peer)
    x_small.start()
    hooks("qk", "own")
    launch(10, 11)
    x_small.wait()
    r.total_x[...] = r.total[...] + r.x_small[...]
    y_small = remote(r.total_x, r.y_small, r.misc_send.at[8], r.misc_recv.at[8], y_peer)
    y_small.start()
    third(6)
    second(8)
    grad_input(r)
    grad_swap = remote(r.dr, r.o_grad.at[t], r.misc_send.at[6], r.misc_recv.at[6], sibling)
    grad_swap.start()
    outs.append(copies.start(r.dr, r.o_grad.at[t]))
    third(7)
    y_small.wait()
    r.z_small[z] = r.total_x[...] + r.y_small[...]
    z_sends = []
    for o in range(1, zs):
        z_sends.append(
            remote(r.z_small.at[z], r.z_small.at[z], r.z_send.at[o], r.z_recv.at[z], z_peers[o - 1])
        )
        z_sends[-1].start()
    second(9)
    finish(4)
    third(8)
    second(10)
    finish(5)
    third(9)
    second(11)
    finish(6, 7)
    third(10)
    for o in range(1, zs):
        source = lax.rem(z + o, zs)
        block = r.z_small.at[source]
        remote(block, block, r.z_send.at[o], r.z_recv.at[source], z_peers[o - 1]).wait_recv()
    total = r.z_small[0]
    for k in range(1, zs):
        total = total + r.z_small[k]
    r.o_small[0:9] = total
    third(11)
    finish(8, 9, 10, 11)
    outs.append(copies.start(r.mine, r.o_shard.at[0]))

    for copy in z_sends:
        copy.wait_send()
    for c in range(CHUNKS - SLOTS, CHUNKS):
        sib_copy(jnp.int32(c)).wait_send()
    for gathered in (cot_gather, cls_gather, hat_gather, act_gather):
        gathered.sent()
    for copy in swap_bias:
        copy.wait_send()
    for copy in swaps.values():
        copy.wait_send()
    grad_swap.wait()
    enc_swap.wait()
    for copy in outs:
        copy.wait()


CROSS = ("xb", "x32", "xt", "h1t", "h1b", "h1", "qkv", "o", "p", "xh1", "rs1", "xh2", "rs2", "yb", "dy", "dmt", "dh")
WEIGHT_SCRATCH = dict(
    wqkv=((3, D, D), BF), wout=((D, D), BF), wup=((D, FF), BF), wdown=((FF, D), BF)
)
BACK_SCRATCH = dict(qv_sum=((2, 1, D), F32), bup_sum=((1, FF), F32))


def saved_shapes(rows):
    return dict(
        xt=((D, rows), BF),
        h1t=((D, rows), BF),
        qkv=((3, rows, D), BF),
        o=((rows, D), BF),
        p=((rows // SEG, PAIRS, SEG, 2 * SEG), BF),
        xh1=((rows, D), F32),
        rs1=((rows, SEG), F32),
        g=((rows, FF), BF),
        gp=((rows, FF), BF),
        xh2=((rows, D), F32),
        rs2=((rows, SEG), F32),
    )


def forward_shapes(rows):
    return dict(
        xb=((rows, D), BF),
        h1=((rows, D), F32),
        h1b=((rows, D), BF),
        b3=((3, 1, D), F32),
        bup=((1, FF), F32),
    )


def vmem(table):
    return [pltpu.VMEM(shape, kind) for shape, kind in table.values()]


def arrays(table):
    return [jax.ShapeDtypeStruct(shape, kind) for shape, kind in table.values()]


def run_whole(dp, inputs):
    hbm = pl.BlockSpec(memory_space=pl.ANY)
    small = pl.BlockSpec(memory_space=pltpu.VMEM)
    smem = pl.BlockSpec(memory_space=pltpu.SMEM)
    batches, rows, _ = inputs["tokens"].shape
    slots = inputs["doc_len"].shape[1] * MAXSEG
    segs = rows // SEG
    total_segs = dp * segs
    zs = dp // 4
    shard = D // dp
    outs = dict(
        o_enc=((batches, rows, D), BF),
        o_grad=((batches, rows, D), F32),
        o_shard=((2, CHUNKS, shard, CHUNK), F32),
        o_small=((26, 1, D), F32),
    )
    outs.update({"f_" + w: (inputs["a_" + w].shape[1:], BF) for w in WEIGHTS})
    scratch = dict(saved_shapes(rows))
    scratch.update(WEIGHT_SCRATCH)
    scratch.update(forward_shapes(rows))
    scratch.update(BACK_SCRATCH)
    cross = dict(saved_shapes(slots))
    cross.update(forward_shapes(slots))
    cross.update(
        x32=((slots, D), F32), yb=((slots, D), BF), dy=((slots, D), F32), dmt=((D, slots), BF),
        dh=((slots, D), BF),
    )
    scratch.update({"q_" + k: cross[k] for k in CROSS})
    scratch.update(
        b3_cross=((3, 1, D), F32),
        bup_cross=((1, FF), F32),
        gain=((2, 1, D), F32),
        gain_cross=((2, 1, D), F32),
        bt=((4, 1, D), F32),
        bt_cross=((4, 1, D), F32),
        x_bqv=((2, 2, HALF_D), F32),
        x_bup=((2, HALF_FF), F32),
        cot=((rows, D), BF),
        dmt=((D, rows), BF),
        ring_w=((4, D, D), BF),
        act_first=((segs, FF), F32),
        cot_all=((dp, segs, D), BF),
        cls_all=((dp, segs, D), BF),
        hat_all=((dp, segs, D + SEG), F32),
        act_all=((dp, segs, FF), BF),
        rows64=((total_segs, D), F32),
        hat64=((total_segs, D + SEG), F32),
        act64=((total_segs, FF), F32),
        undeal=((total_segs, slots), BF),
        back=((8, slots), BF),
        allowed=((SEG, SEG), F32),
        ret=((8, D), F32),
        dc=((8, D), F32),
        late=((SEG, D), BF),
        late_t=((D, SEG), BF),
        small=((12, 1, D), F32),
        small1=((20, 1, D), F32),
        small_in=((9, 1, D), F32),
        small1_in=((17, 1, D), F32),
        total=((9, 1, D), F32),
        total_x=((9, 1, D), F32),
        x_small=((9, 1, D), F32),
        y_small=((9, 1, D), F32),
        z_small=((zs, 9, 1, D), F32),
        shard1=((CHUNKS, shard, CHUNK), F32),
        shard_out=((CHUNKS + 4, shard, CHUNK), BF),
        shard_in=((CHUNKS + 4, shard, CHUNK), BF),
        mine=((CHUNKS, shard, CHUNK), F32),
        gbuf=((RING, zs, 2, 2, shard, CHUNK), BF),
        sib_out=((SLOTS, D, CHUNK), BF),
        sib_in=((SLOTS, D, CHUNK), BF),
        one_in=((RING, 2, zs // 2, 2, shard, CHUNK), BF),
        two_in=((RING, 2, zs // 2, shard, CHUNK), BF),
        three_in=((RING, zs - 1, shard, CHUNK), BF),
    )
    dma = pltpu.SemaphoreType.DMA
    sems = dict(
        local_sem=dma((20,)),
        w_send=dma((2, 5)),
        w_recv=dma((2, 5)),
        ring_sem=dma((4, 2)),
        g_send=dma((4, dp)),
        g_recv=dma((4, dp)),
        misc_send=dma((9,)),
        misc_recv=dma((9,)),
        sib_send=dma((SLOTS,)),
        sib_recv=dma((SLOTS,)),
        one_send=dma((CHUNKS, 2)),
        one_recv=dma((CHUNKS, 2)),
        two_send=dma((CHUNKS, 2)),
        two_recv=dma((CHUNKS, 2)),
        three_send=dma((CHUNKS, zs - 1)),
        three_recv=dma((CHUNKS, zs - 1)),
        z_send=dma((zs,)),
        z_recv=dma((zs,)),
        credit=pltpu.SemaphoreType.REGULAR,
    )
    ins = dict(
        seg_doc=smem, doc_len=smem, seg_doc_v=small, tokens=hbm, cotangent=hbm, b_qv=small, b_up=small,
        norm_gain=small, bias_terms=small, seg_pos=small,
        a_wqkv=hbm, a_wout=hbm, a_wup=hbm, a_wdown=hbm,
    )
    names = list(ins) + list(outs) + list(scratch) + list(sems)
    result = pl.pallas_call(
        partial(whole_kernel, dp, names),
        out_shape=arrays(outs),
        in_specs=list(ins.values()),
        out_specs=[hbm, hbm, hbm, small] + [hbm] * 4,
        scratch_shapes=vmem(scratch) + list(sems.values()),
        compiler_params=pltpu.CompilerParams(
            collective_id=0, has_side_effects=True, vmem_limit_bytes=VMEM_LIMIT
        ),
        name="both_layers",
    )(*[inputs[k] for k in ins])
    return dict(zip(outs, result))


VMEM_LIMIT = 64 << 20


def finish_kernel(
    enc, grad, shard, small, o_enc, o_grad, g_qkv, g_out, g_up, g_down, g_bqv, g_bup, g_gain, g_terms, g_pos,
    enc_v, grad_v, shard_v, sems,
):
    copies = Copies(sems)
    loads = [copies.start(grad.at[b], grad_v.at[b]) for b in range(grad.shape[0])]
    load_shard = copies.start(shard, shard_v)
    loads_enc = [copies.start(enc.at[b], enc_v.at[b]) for b in range(enc.shape[0])]
    outs = []
    for b, load in enumerate(loads):
        load.wait()
        outs.append(copies.start(grad_v.at[b], o_grad.at[b]))
    load_shard.wait()
    for layer in range(2):
        for c in range(4):
            lanes = slice(c * CHUNK, (c + 1) * CHUNK)
            outs.append(copies.start(shard_v.at[layer, c], g_down.at[layer, :, lanes]))
            outs.append(copies.start(shard_v.at[layer, 4 + c], g_up.at[layer, :, lanes]))
        outs.append(copies.start(shard_v.at[layer, 8], g_out.at[layer]))
        for k in range(3):
            outs.append(copies.start(shard_v.at[layer, 9 + k], g_qkv.at[layer, QKV_OF[k]]))
    for b, load in enumerate(loads_enc):
        load.wait()
        outs.append(copies.start(enc_v.at[b], o_enc.at[b]))
    for layer in range(2):
        at = 9 * layer
        for k in range(2):
            g_gain[layer, k : k + 1, :] = small[at + k]
            g_bqv[layer, k : k + 1, :] = small[at + 6, :, k * HALF_D : (k + 1) * HALF_D]
            g_bup[layer : layer + 1, k * D : (k + 1) * D] = small[at + 7 + k]
        for k in range(4):
            g_terms[layer, k : k + 1, :] = small[at + 2 + k]
    for k in range(MAXSEG):
        g_pos[k : k + 1, :] = small[18 + k]
    for copy in outs:
        copy.wait()


def fused(tokens, seg_doc, doc_len, w_qkv, b_qv, w_out, w_up, b_up, w_down, norm_gain, bias_terms, seg_pos, cotangent):
    dp = lax.axis_size("dp")
    whole = run_whole(
        dp,
        dict(
            seg_doc=seg_doc, doc_len=doc_len, seg_doc_v=seg_doc, tokens=tokens, cotangent=cotangent,
            b_qv=b_qv, b_up=b_up, norm_gain=norm_gain, bias_terms=bias_terms,
            seg_pos=seg_pos, a_wqkv=w_qkv, a_wout=w_out, a_wup=w_up, a_wdown=w_down,
        ),
    )
    rows = D // dp
    shapes = [
        (2, 3, rows, HALF_D), (2, rows, HALF_D), (2, rows, HALF_FF), (2, rows, HALF_FF),
        (2, 2, HALF_D), (2, HALF_FF), (2, 2, D), (2, 4, D), (MAXSEG, D),
    ]
    hbm = pl.BlockSpec(memory_space=pl.ANY)
    small = pl.BlockSpec(memory_space=pltpu.VMEM)
    results = [whole[k] for k in ("o_enc", "o_grad", "o_shard", "o_small")]
    enc, grad, g_qkv, g_out, g_up, g_down, g_bqv, g_bup, g_gain, g_terms, g_pos = pl.pallas_call(
        finish_kernel,
        out_shape=[jax.ShapeDtypeStruct(a.shape, a.dtype) for a in results[:2]]
        + [jax.ShapeDtypeStruct(shape, F32) for shape in shapes],
        in_specs=[hbm] * 3 + [small],
        out_specs=[hbm] * 6 + [small] * 5,
        scratch_shapes=[pltpu.VMEM(a.shape, a.dtype) for a in results[:3]]
        + [pltpu.SemaphoreType.DMA((40,))],
        compiler_params=pltpu.CompilerParams(vmem_limit_bytes=VMEM_LIMIT),
        name="lay_out",
    )(*results)
    return (
        enc, grad, g_qkv, g_bqv, g_out.transpose(0, 2, 1), g_up, g_bup, g_down.transpose(0, 2, 1),
        g_gain, g_terms, g_pos,
    )


def solution(mesh):
    in_specs = (
        P(None, "dp", None),
        P(),
        P(),
        P(None, None, None, "tensor"),
        P(None, None, "tensor"),
        P(None, "tensor", None),
        P(None, None, "tensor"),
        P(None, "tensor"),
        P(None, "tensor", None),
        P(),
        P(),
        P(),
        P(None, "dp", None),
    )
    out_specs = (
        P(None, "dp", None),
        P(None, "dp", None),
        P(None, None, "dp", "tensor"),
        P(None, None, "tensor"),
        P(None, "tensor", "dp"),
        P(None, "dp", "tensor"),
        P(None, "tensor"),
        P(None, "tensor", "dp"),
        P(),
        P(),
        P(),
    )
    body = fused if mesh.shape["dp"] == 16 and mesh.shape["tensor"] == 2 else local
    return jax.shard_map(body, mesh=mesh, in_specs=in_specs, out_specs=out_specs, check_vma=False)
```

```python
from functools import partial, reduce

import jax
import jax.numpy as jnp
from jax import lax
from jax.experimental import pallas as pl
from jax.experimental.pallas import tpu as pltpu
from jax.sharding import PartitionSpec as P

HEAD_DIM = 64
SEG = 128
MAXSEG = 8


norm_eps = 1e-05
masked_score = -1e30


def norm_rows(values, gain, shift):
    centre = values - jnp.mean(values, axis=-1, keepdims=True)
    spread = jnp.mean(centre * centre, axis=-1, keepdims=True)
    return centre * lax.rsqrt(spread + norm_eps) * gain + shift


def exact_gelu(values):
    return jax.nn.gelu(values, approximate=False)


def my_rows(values):
    part_rows = values.shape[0] // lax.axis_size("tensor")
    return lax.dynamic_slice_in_dim(values, lax.axis_index("tensor") * part_rows, part_rows, 0)


def attn_scores(queries, key_rows, key_mask, split_shape):
    raw = jnp.einsum(
        "glhd,gmhd->ghlm",
        queries.reshape(split_shape),
        key_rows.reshape(split_shape),
        preferred_element_type=jnp.float32,
    ) * HEAD_DIM ** (-0.5)
    return jnp.where(key_mask[:, None, None, :], raw, masked_score)


def layer_forward(inputs, key_mask, weights):
    w_qkv, b_qv, w_out, w_up, b_up, w_down, norm_gain, bias_terms = weights
    groups, span = key_mask.shape
    row_count = inputs.shape[0]
    local_width = w_qkv.shape[2]
    split_shape = (groups, span, local_width // HEAD_DIM, HEAD_DIM)
    inputs_b = inputs.astype(jnp.bfloat16)
    projected = jnp.einsum("rd,cde->cre", inputs_b, w_qkv, preferred_element_type=jnp.float32)
    queries = (projected[0] + b_qv[0]).astype(jnp.bfloat16)
    key_rows = projected[1].astype(jnp.bfloat16)
    value_rows = (projected[2] + b_qv[1]).astype(jnp.bfloat16)
    scores = attn_scores(queries, key_rows, key_mask, split_shape)
    row_max = jnp.max(scores, axis=-1, keepdims=True)
    log_total = row_max + jnp.log(jnp.sum(jnp.exp(scores - row_max), axis=-1, keepdims=True))
    attn_probs = jnp.exp(scores - log_total).astype(jnp.bfloat16)
    head_out = jnp.einsum(
        "ghlm,gmhd->glhd",
        attn_probs,
        value_rows.reshape(split_shape),
        preferred_element_type=jnp.float32,
    )
    head_out = head_out.reshape(row_count, local_width).astype(jnp.bfloat16)
    attn_part = (
        lax.psum_scatter(
            jnp.dot(head_out, w_out, preferred_element_type=jnp.float32),
            "tensor",
            scatter_dimension=0,
            tiled=True,
        )
        + bias_terms[0]
    )
    resid_one = lax.all_gather(my_rows(inputs) + attn_part, "tensor", axis=0, tiled=True)
    hidden = norm_rows(resid_one, norm_gain[0], bias_terms[2])
    hidden_b = hidden.astype(jnp.bfloat16)
    pre_act = jnp.dot(hidden_b, w_up, preferred_element_type=jnp.float32) + b_up
    active_b = exact_gelu(pre_act).astype(jnp.bfloat16)
    mlp_part = (
        lax.psum_scatter(
            jnp.dot(active_b, w_down, preferred_element_type=jnp.float32),
            "tensor",
            scatter_dimension=0,
            tiled=True,
        )
        + bias_terms[1]
    )
    resid_two = lax.all_gather(my_rows(hidden) + mlp_part, "tensor", axis=0, tiled=True)
    stored = (
        inputs_b,
        queries,
        key_rows,
        value_rows,
        log_total,
        head_out,
        resid_one,
        hidden_b,
        pre_act,
        active_b,
        resid_two,
    )
    return (norm_rows(resid_two, norm_gain[1], bias_terms[3]), stored)


def layer_backward(grad_out, key_mask, weights, stored):
    w_qkv, b_qv, w_out, w_up, b_up, w_down, norm_gain, bias_terms = weights
    (
        inputs_b,
        queries,
        key_rows,
        value_rows,
        log_total,
        head_out,
        resid_one,
        hidden_b,
        pre_act,
        active_b,
        resid_two,
    ) = stored
    groups, span = key_mask.shape
    row_count, local_width = queries.shape
    split_shape = (groups, span, local_width // HEAD_DIM, HEAD_DIM)
    forward_two, norm_two = jax.vjp(norm_rows, resid_two, norm_gain[1], bias_terms[3])
    grad_two, gain_two, shift_two = norm_two(grad_out)
    grad_mlp = grad_two.astype(jnp.bfloat16)
    grad_wdown = jnp.dot(active_b.T, grad_mlp, preferred_element_type=jnp.float32)
    grad_act = jnp.dot(grad_mlp, w_down.T, preferred_element_type=jnp.float32)
    forward_gelu, gelu_back = jax.vjp(exact_gelu, pre_act)
    grad_pre = gelu_back(grad_act)[0].astype(jnp.bfloat16)
    grad_wup = jnp.dot(hidden_b.T, grad_pre, preferred_element_type=jnp.float32)
    up_part = lax.psum_scatter(
        jnp.dot(grad_pre, w_up.T, preferred_element_type=jnp.float32),
        "tensor",
        scatter_dimension=0,
        tiled=True,
    )
    grad_hidden = lax.all_gather(my_rows(grad_two) + up_part, "tensor", axis=0, tiled=True)
    forward_one, norm_one = jax.vjp(norm_rows, resid_one, norm_gain[0], bias_terms[2])
    grad_one, gain_one, shift_one = norm_one(grad_hidden)
    grad_attn = grad_one.astype(jnp.bfloat16)
    grad_wout = jnp.dot(head_out.T, grad_attn, preferred_element_type=jnp.float32)
    grad_heads = (
        jnp.dot(grad_attn, w_out.T, preferred_element_type=jnp.float32)
        .astype(jnp.bfloat16)
        .reshape(split_shape)
    )
    scores = attn_scores(queries, key_rows, key_mask, split_shape)
    attn_probs = jnp.exp(scores - log_total)
    grad_probs = jnp.einsum(
        "glhd,gmhd->ghlm",
        grad_heads,
        value_rows.reshape(split_shape),
        preferred_element_type=jnp.float32,
    )
    grad_values = jnp.einsum(
        "ghlm,glhd->gmhd",
        attn_probs.astype(jnp.bfloat16),
        grad_heads,
        preferred_element_type=jnp.float32,
    )
    grad_scores = (
        attn_probs * (grad_probs - jnp.sum(attn_probs * grad_probs, axis=-1, keepdims=True))
    ).astype(jnp.bfloat16)
    inv_root = HEAD_DIM ** (-0.5)
    grad_queries = (
        jnp.einsum(
            "ghlm,gmhd->glhd",
            grad_scores,
            key_rows.reshape(split_shape),
            preferred_element_type=jnp.float32,
        )
        * inv_root
    )
    grad_keys = (
        jnp.einsum(
            "ghlm,glhd->gmhd",
            grad_scores,
            queries.reshape(split_shape),
            preferred_element_type=jnp.float32,
        )
        * inv_root
    )
    grad_qkv = (
        jnp.stack([grad_queries, grad_keys, grad_values])
        .reshape(3, row_count, local_width)
        .astype(jnp.bfloat16)
    )
    grad_wqkv = jnp.einsum("rd,cre->cde", inputs_b, grad_qkv, preferred_element_type=jnp.float32)
    qkv_part = lax.psum_scatter(
        jnp.einsum("cre,cde->rd", grad_qkv, w_qkv, preferred_element_type=jnp.float32).astype(
            jnp.bfloat16
        ),
        "tensor",
        scatter_dimension=0,
        tiled=True,
    ).astype(jnp.float32)
    grad_inputs = lax.all_gather(
        (my_rows(grad_one) + qkv_part).astype(jnp.bfloat16), "tensor", axis=0, tiled=True
    ).astype(jnp.float32)
    grad_bqv = jnp.stack(
        [
            jnp.sum(grad_qkv[0].astype(jnp.float32), axis=0),
            jnp.sum(grad_qkv[2].astype(jnp.float32), axis=0),
        ]
    )
    grad_bup = jnp.sum(grad_pre.astype(jnp.float32), axis=0)
    grad_gain = jnp.stack([gain_one, gain_two])
    grad_shift = jnp.stack(
        [
            jnp.sum(grad_attn.astype(jnp.float32), axis=0),
            jnp.sum(grad_mlp.astype(jnp.float32), axis=0),
            shift_one,
            shift_two,
        ]
    )
    return (
        grad_inputs,
        (grad_wqkv, grad_bqv, grad_wout, grad_wup, grad_bup, grad_wdown, grad_gain, grad_shift),
    )


def deal_map(doc_ids, total_docs):
    return jnp.where(doc_ids % 2 == 1, (doc_ids + total_docs // 2) % total_docs, doc_ids)


def local_plan(seg_order, doc_lengths, seg_local, doc_local):
    total_docs = doc_lengths.shape[0]
    my_index = lax.axis_index("dp")
    doc_ids = jnp.arange(total_docs, dtype=jnp.int32)
    owner_pos = deal_map(doc_ids, total_docs)
    starts = jnp.sum((seg_order[None, :] < doc_ids[:, None]).astype(jnp.int32), axis=1)
    counts = jnp.sum((seg_order[None, :] == doc_ids[:, None]).astype(jnp.int32), axis=1)
    my_segments = my_index * seg_local + jnp.arange(seg_local, dtype=jnp.int32)
    seg_owner_doc = lax.dynamic_slice_in_dim(seg_order, my_index * seg_local, seg_local)
    seg_hot = seg_owner_doc[:, None] == doc_ids[None, :]
    my_start = jnp.sum(jnp.where(seg_hot, starts[None, :], 0), axis=1)
    my_length = jnp.sum(jnp.where(seg_hot, doc_lengths[None, :], 0), axis=1)
    my_owner = jnp.sum(jnp.where(seg_hot, owner_pos[None, :], 0), axis=1)
    within = my_segments - my_start
    valid_tokens = jnp.minimum(SEG, my_length - within * SEG)
    tok_mask = jnp.arange(SEG, dtype=jnp.int32)[None, :] < valid_tokens[:, None]
    src_slot = my_owner * MAXSEG + within
    my_deal = deal_map(my_index * doc_local + jnp.arange(doc_local, dtype=jnp.int32), total_docs)
    deal_hot = my_deal[:, None] == doc_ids[None, :]
    own_start = jnp.sum(jnp.where(deal_hot, starts[None, :], 0), axis=1)
    own_count = jnp.sum(jnp.where(deal_hot, counts[None, :], 0), axis=1)
    slot_index = jnp.arange(MAXSEG, dtype=jnp.int32)
    cross_mask = slot_index[None, :] < own_count[:, None]
    target = jnp.where(cross_mask, own_start[:, None] + slot_index[None, :], -1).reshape(-1)
    return (tok_mask, cross_mask, target, src_slot)


def picker(index_map, shard_rows):
    positions = jnp.arange(shard_rows.shape[0], dtype=jnp.int32)
    selector = (index_map[:, None] == positions[None, :]).astype(jnp.bfloat16)
    return jnp.dot(selector, shard_rows, preferred_element_type=jnp.float32)


def spreader(index_map, source_rows, row_span):
    positions = jnp.arange(row_span, dtype=jnp.int32)
    selector = (positions[:, None] == index_map[None, :]).astype(jnp.bfloat16)
    return jnp.dot(selector, source_rows, preferred_element_type=jnp.float32)


def add_terms(left, right):
    return jax.tree.map(jnp.add, left, right)


def local(
    tokens,
    seg_doc,
    doc_len,
    w_qkv,
    b_qv,
    w_out,
    w_up,
    b_up,
    w_down,
    norm_gain,
    bias_terms,
    seg_pos,
    cotangent,
):
    batches, local_rows, width = tokens.shape
    seg_local = local_rows // SEG
    doc_local = doc_len.shape[1] // lax.axis_size("dp")
    slot_rows = doc_local * MAXSEG

    def layer_weights(level):
        return (
            w_qkv[level],
            b_qv[level],
            w_out[level],
            w_up[level],
            b_up[level],
            w_down[level],
            norm_gain[level],
            bias_terms[level],
        )

    seg_weights = layer_weights(0)
    cross_weights = layer_weights(1)
    encoded = []
    grad_tokens = []
    seg_grads = []
    cross_grads = []
    pos_grads = []
    for batch_index in range(batches):
        tok_mask, cross_mask, target, src_slot = local_plan(
            seg_doc[batch_index], doc_len[batch_index], seg_local, doc_local
        )
        seg_out, seg_stored = layer_forward(
            tokens[batch_index].astype(jnp.float32), tok_mask, seg_weights
        )
        seg_cube = seg_out.reshape(seg_local, SEG, width)
        cls_rows = seg_cube[:, 0].astype(jnp.bfloat16)
        collected = picker(target, lax.all_gather(cls_rows, "dp", axis=0, tiled=True))
        cross_in = (collected.reshape(doc_local, MAXSEG, width) + seg_pos[None]).reshape(
            slot_rows, width
        )
        cross_out, cross_stored = layer_forward(cross_in, cross_mask, cross_weights)
        returned = picker(
            src_slot, lax.all_gather(cross_out.astype(jnp.bfloat16), "dp", axis=0, tiled=True)
        )
        encoded.append(
            seg_cube.at[:, 0].set(returned).reshape(local_rows, width).astype(jnp.bfloat16)
        )
        grad_cube = cotangent[batch_index].astype(jnp.float32).reshape(seg_local, SEG, width)
        grad_returned = grad_cube[:, 0].astype(jnp.bfloat16)
        grad_cross = lax.psum_scatter(
            spreader(src_slot, grad_returned, slot_rows * lax.axis_size("dp")),
            "dp",
            scatter_dimension=0,
            tiled=True,
        )
        grad_cross_in, cross_terms = layer_backward(
            grad_cross, cross_mask, cross_weights, cross_stored
        )
        pos_grads.append(jnp.sum(grad_cross_in.reshape(doc_local, MAXSEG, width), axis=0))
        grad_sent = grad_cross_in.astype(jnp.bfloat16)
        cross_grads.append(cross_terms)
        grad_cls = lax.psum_scatter(
            spreader(target, grad_sent, seg_local * lax.axis_size("dp")),
            "dp",
            scatter_dimension=0,
            tiled=True,
        )
        grad_seg = grad_cube.at[:, 0].set(grad_cls).reshape(local_rows, width)
        grad_inputs, seg_terms = layer_backward(grad_seg, tok_mask, seg_weights, seg_stored)
        grad_tokens.append(grad_inputs)
        seg_grads.append(seg_terms)
    seg_total = reduce(add_terms, seg_grads)
    cross_total = reduce(add_terms, cross_grads)
    pos_total = reduce(jnp.add, pos_grads)
    big_grads = (
        lax.psum_scatter(
            jnp.stack([seg_total[0], cross_total[0]]), "dp", scatter_dimension=2, tiled=True
        ),
        lax.psum_scatter(
            jnp.stack([seg_total[2], cross_total[2]]), "dp", scatter_dimension=2, tiled=True
        ),
        lax.psum_scatter(
            jnp.stack([seg_total[3], cross_total[3]]), "dp", scatter_dimension=1, tiled=True
        ),
        lax.psum_scatter(
            jnp.stack([seg_total[5], cross_total[5]]), "dp", scatter_dimension=2, tiled=True
        ),
    )
    small = lax.psum(
        (
            jnp.stack([seg_total[1], cross_total[1]]),
            jnp.stack([seg_total[4], cross_total[4]]),
            jnp.stack([seg_total[6], cross_total[6]]),
            jnp.stack([seg_total[7], cross_total[7]]),
            pos_total,
        ),
        "dp",
    )
    return (
        jnp.stack(encoded),
        jnp.stack(grad_tokens),
        big_grads[0],
        small[0],
        big_grads[1],
        big_grads[2],
        small[1],
        big_grads[3],
        small[2],
        small[3],
        small[4],
    )


BF = jnp.bfloat16
F32 = jnp.float32
D = 768
FF = 3072
HALF_FF = FF // 2
HALF_D = D // 2
CHUNK = 384
CHUNKS = 12
PAIRS = 6
MESH = pl.DeviceIdType.MESH
ROOT_HALF = 0.7071067811865476
PDF_SCALE = 0.3989422804014327


class Names:
    def __init__(self, **kw):
        self.__dict__.update(kw)


def mm(left, right):
    return jnp.dot(left, right, preferred_element_type=F32)


def mm_nt(left, right):
    return lax.dot_general(left, right, (((1,), (1,)), ((), ())), preferred_element_type=F32)


def span(index, size):
    return pl.ds(pl.multiple_of(index * size, size), size)


def row_norm(rows):
    centre = rows - jnp.mean(rows, axis=-1, keepdims=True)
    spread = jnp.mean(centre * centre, axis=-1, keepdims=True)
    scale = lax.rsqrt(spread + norm_eps)
    return centre * scale, scale


def stacked(pair, low_half):
    zero = jnp.zeros_like(pair)
    return jnp.concatenate(
        [jnp.where(low_half, pair, zero), jnp.where(low_half, zero, pair)], axis=0
    )


def soft_rows(scores):
    top = jnp.max(scores, axis=-1, keepdims=True)
    grown = jnp.exp(scores - top)
    return (grown * (1.0 / jnp.sum(grown, axis=-1, keepdims=True))).astype(BF)


def transpose_into(dest, source, rows):
    @pl.loop(0, rows // SEG)
    def _(s):
        dest[:, span(s, SEG)] = source[span(s, SEG), :].T


def gelu_pair(u):
    cdf = 0.5 * (1.0 + lax.erf(u * ROOT_HALF))
    slope = cdf + u * (PDF_SCALE * jnp.exp(-0.5 * u * u))
    return (u * cdf).astype(BF), slope.astype(BF)


def project(r, half):
    lanes = span(half, HALF_D)
    for c in range(3):
        r.qkv[c, :, lanes] = (mm(r.xb[...], r.wqkv[c, :, lanes]) + r.b3[c, :, lanes]).astype(BF)


def low_lanes():
    return lax.broadcasted_iota(jnp.int32, (SEG, SEG), 1) < HEAD_DIM


def attend(r, keep, first, count):
    segs = r.xb.shape[0] // SEG
    root = jnp.asarray(HEAD_DIM ** (-0.5), BF)

    @pl.loop(0, segs, unroll=min(segs, 4))
    def _(s):
        at = span(s, SEG)
        live = keep(s)
        low_half = low_lanes()
        for k in range(count):
            p = first + k
            cols = span(p, SEG)
            keys = stacked(r.qkv[1, at, cols], low_half)
            vals = stacked(r.qkv[2, at, cols], low_half)
            raw = mm_nt(r.qkv[0, at, cols] * root, keys)
            one = soft_rows(jnp.where(live, raw[:, :SEG], masked_score))
            two = soft_rows(jnp.where(live, raw[:, SEG:], masked_score))
            both = jnp.concatenate([one, two], axis=1)
            r.p[s, p] = both
            r.o[at, cols] = mm(both, vals).astype(BF)


def attn_out(r):
    for n in range(3):
        cols = slice(n * 256, n * 256 + 256)
        r.xh1[:, cols] = mm(r.o[...], r.wout[:, cols]) + r.bt[0, :, cols]


def norm_one(r, x_ref):
    rows = r.xh1.shape[0]
    block = min(rows, 256)

    @pl.loop(0, rows // block)
    def _(s):
        at = span(s, block)
        hat, scale = row_norm(x_ref[at, :].astype(F32) + r.xh1[at, :])
        r.xh1[at, :] = hat
        r.rs1[at, :] = jnp.broadcast_to(scale, (block, SEG))
        hidden = hat * r.gain[0] + r.bt[2]
        r.h1[at, :] = hidden
        r.h1b[at, :] = hidden.astype(BF)
        r.xh2[at, :] = hidden + r.bt[1]


def mlp_up(r, before):
    @pl.loop(0, 4)
    def _(j):
        before(j)
        for k in range(3):
            cols = pl.ds(pl.multiple_of(j * D + k * 256, 256), 256)
            u = mm(r.h1b[...], r.wup[:, cols]) + r.bup[:, cols]
            r.g[:, cols], r.gp[:, cols] = gelu_pair(u)


def mlp_down(r, before):
    @pl.loop(0, 2)
    def _(half):
        before(half)
        part = span(half, HALF_FF)
        for n in range(3):
            cols = slice(n * 256, n * 256 + 256)
            r.xh2[:, cols] = r.xh2[:, cols] + mm(r.g[:, part], r.wdown[part, cols])


def norm_two(r, y_ref):
    rows = r.xh2.shape[0]
    block = min(rows, 256)

    @pl.loop(0, rows // block)
    def _(s):
        at = span(s, block)
        hat, scale = row_norm(r.xh2[at, :])
        r.xh2[at, :] = hat
        r.rs2[at, :] = jnp.broadcast_to(scale, (block, SEG))
        y_ref[at, :] = (hat * r.gain[1] + r.bt[3]).astype(BF)


def norm_back(grad, hat, scale, gain):
    d_hat = grad * gain
    first = jnp.mean(d_hat, axis=-1, keepdims=True)
    second = jnp.mean(d_hat * hat, axis=-1, keepdims=True)
    return (d_hat - first - hat * second) * scale


def norm_back_rows(r, hat_ref, scale_ref, gain, grad_of):
    zero = jnp.zeros((1, D), F32)
    rows = r.dr.shape[0]
    block = min(rows, 256)

    def step(s, sums):
        at = span(s, block)
        grad = grad_of(s, at)
        hat = hat_ref[at, :]
        out = norm_back(grad, hat, scale_ref[at, 0:1], gain)
        low = out.astype(BF)
        r.dr[at, :] = out
        r.dm[at, :] = low
        return (
            sums[0] + jnp.sum(grad * hat, axis=0, keepdims=True),
            sums[1] + jnp.sum(grad, axis=0, keepdims=True),
            sums[2] + jnp.sum(low.astype(F32), axis=0, keepdims=True),
        )

    sums = lax.fori_loop(0, rows // block, step, (zero, zero, zero))
    transpose_into(r.dmt, r.dm, rows)
    return sums


def back_norm_two(r, grad_of):
    sums = norm_back_rows(r, r.xh2, r.rs2, r.gain[1], grad_of)
    r.small_common[1], r.small_common[5], r.small_common[3] = sums


def back_norm_one(r):
    sums = norm_back_rows(r, r.xh1, r.rs1, r.gain[0], lambda s, at: r.dr[at, :])
    r.small_common[0], r.small_common[4], r.small_common[2] = sums


def grad_hidden(r):
    @pl.loop(0, 3)
    def _(j):
        cols = span(j, 1024)
        du = (mm_nt(r.dm[...], r.wdown[cols, :]) * r.gp[:, cols].astype(F32)).astype(BF)
        r.gp[:, cols] = du
        r.bup_sum[:, cols] = jnp.sum(du.astype(F32), axis=0, keepdims=True)


def grad_middle(r):
    @pl.loop(0, 2)
    def _(n):
        cols = span(n, CHUNK)
        r.dr[:, cols] = r.dr[:, cols] + mm_nt(r.gp[...], r.wup[cols, :])


def grad_heads(r):
    for n in range(3):
        cols = slice(n * 256, n * 256 + 256)
        r.dh[:, cols] = mm_nt(r.dm[...], r.wout[cols, :]).astype(BF)


def attend_back_values(r):
    segs = r.dh.shape[0] // SEG

    @pl.loop(0, segs, unroll=min(segs, 2))
    def _(s):
        at = span(s, SEG)
        low_half = low_lanes()
        for p in range(PAIRS):
            d_vals = mm(r.p[s, p].T, r.dh[at, p * SEG : p * SEG + SEG])
            cols = slice(2 * D + p * SEG, 2 * D + p * SEG + SEG)
            r.g[at, cols] = jnp.where(low_half, d_vals[:SEG], d_vals[SEG:]).astype(BF)


def attend_back(r, exact, before):
    root = jnp.asarray(HEAD_DIM ** (-0.5), BF)
    segs = r.dh.shape[0] // SEG
    together = min(segs, 2)

    def segment(s):
        at = span(s, SEG)
        low_half = low_lanes()
        head = lax.broadcasted_iota(jnp.int32, (SEG, 2 * SEG), 0) < HEAD_DIM
        side = lax.broadcasted_iota(jnp.int32, (SEG, 2 * SEG), 1) < SEG
        ones = jnp.where(head == side, 1.0, 0.0).astype(BF)
        for p in range(PAIRS):
            cols = slice(p * SEG, p * SEG + SEG)
            query = r.qkv[0, at, cols] * root
            keys = stacked(r.qkv[1, at, cols] * root, low_half)
            vals = stacked(r.qkv[2, at, cols], low_half)
            d_head = r.dh[at, cols]
            d_probs = mm_nt(d_head, vals)
            both = d_head.astype(F32) * r.o[at, cols].astype(F32)
            inner = mm(both.astype(BF), ones)
            if exact:
                inner = inner + mm((both - both.astype(BF).astype(F32)).astype(BF), ones)
            d_scores = (r.p[s, p].astype(F32) * (d_probs - inner)).astype(BF)
            d_keys = mm(d_scores.T, query)
            r.g[at, cols] = mm(d_scores, keys).astype(BF)
            cols = slice(D + p * SEG, D + p * SEG + SEG)
            r.g[at, cols] = jnp.where(low_half, d_keys[:SEG], d_keys[SEG:]).astype(BF)

    @pl.loop(0, segs // together)
    def _(i):
        before(i)
        for k in range(together):
            segment(i * together + k)


def bias_heads(r):
    for c in (0, 2):
        r.qv_sum[c // 2] = jnp.sum(
            r.g[:, c * D : (c + 1) * D].astype(F32), axis=0, keepdims=True
        )


def grad_input(r):
    for n in range(3):
        cols = slice(n * 256, n * 256 + 256)
        total = r.dr[:, cols]
        for c in range(3):
            total = total + mm_nt(r.g[:, c * D : (c + 1) * D], r.wqkv[c, cols, :])
        r.dr[:, cols] = total


def chunk_operands(r, c):
    if c < 4:
        return r.dmt, (r.g, c * CHUNK, HALF_FF + c * CHUNK)
    if c < 8:
        return r.h1t, (r.gp, (c - 4) * CHUNK, HALF_FF + (c - 4) * CHUNK)
    if c == 8:
        return r.dmt, (r.o, 0, HALF_D)
    at = QKV_OF[c - 9] * D
    return r.xt, (r.g, at, at + HALF_D)


QKV_OF = (2, 0, 1)
HOOK_CHUNKS = {"down": (0, 4), "up": (4, 8), "out": (8, 9), "qkv": (9, 12), "v": (9, 10), "qk": (10, 12)}


class Copies:
    def __init__(self, sems):
        self.sems = sems
        self.used = 0

    def start(self, source, dest):
        copy = pltpu.make_async_copy(source, dest, self.sems.at[self.used])
        self.used += 1
        copy.start()
        return copy


def remote(source, dest, send_sem, recv_sem, device):
    return pltpu.make_async_remote_copy(
        src_ref=source,
        dst_ref=dest,
        send_sem=send_sem,
        recv_sem=recv_sem,
        device_id=device,
        device_id_type=MESH,
    )


class Gather:
    def __init__(self, dp, everyone, send, recv):
        self.dp, self.everyone, self.send, self.recv = dp, everyone, send, recv

    def start(self, block):
        d, t = lax.axis_index("dp"), lax.axis_index("tensor")
        everyone = self.everyone
        everyone[d] = block
        for o in range(1, self.dp):
            peer = (lax.rem(d + o, self.dp), t)
            copy = remote(everyone.at[d], everyone.at[d], self.send.at[o], self.recv.at[d], peer)
            copy.start()

    def sent(self):
        d, t = lax.axis_index("dp"), lax.axis_index("tensor")
        block = self.everyone.at[d]
        for o in range(1, self.dp):
            peer = (lax.rem(d + o, self.dp), t)
            remote(block, block, self.send.at[o], self.recv.at[d], peer).wait_send()

    def arrived(self):
        d, t = lax.axis_index("dp"), lax.axis_index("tensor")
        for o in range(1, self.dp):
            source = lax.rem(d + o, self.dp)
            block = self.everyone.at[source]
            remote(block, block, self.send.at[o], self.recv.at[source], (source, t)).wait_recv()

    def rows_into(self, dest):
        segs = self.everyone.shape[1]
        tall = 16 if dest.dtype == BF else 8
        pack = tall // segs
        for i in range(self.dp // pack):
            blocks = [self.everyone[i * pack + k].astype(F32) for k in range(pack)]
            dest[i * tall : i * tall + tall, :] = jnp.concatenate(blocks, axis=0).astype(dest.dtype)


SLOTS = 4
RING = 9
WEIGHTS = ("wqkv", "wout", "wup", "wdown")


def half_of(ref, which, half):
    if which == "wqkv":
        return ref.at[:, :, half * HALF_D : (half + 1) * HALF_D]
    if which == "wout":
        return ref.at[half * HALF_D : (half + 1) * HALF_D, :]
    if which == "wup_square":
        return ref.at[:, half * HALF_D : (half + 1) * HALF_D]
    if which == "wup":
        return ref.at[:, half * HALF_FF : (half + 1) * HALF_FF]
    return ref.at[half * HALF_FF : (half + 1) * HALF_FF, :]


def fill_bias(b3, bup, half, layer, b_qv, b_up):
    lanes = slice(half * HALF_D, (half + 1) * HALF_D)
    b3[0, :, lanes] = b_qv[layer, 0:1, :]
    b3[1, :, lanes] = jnp.zeros((1, HALF_D), F32)
    b3[2, :, lanes] = b_qv[layer, 1:2, :]
    bup[:, half * HALF_FF : (half + 1) * HALF_FF] = b_up[layer : layer + 1, :]


def pack_halves(r):
    for half in range(2):
        at = 6 + 3 * half
        lanes = slice(half * HALF_D, (half + 1) * HALF_D)
        r.small[at, :, 0:HALF_D] = r.qv_sum[0, :, lanes]
        r.small[at, :, HALF_D:] = r.qv_sum[1, :, lanes]
        base = half * HALF_FF
        r.small[at + 1] = r.bup_sum[:, base : base + D]
        r.small[at + 2] = r.bup_sum[:, base + D : base + 2 * D]


def first_of_segments(ref, segs):
    return jnp.concatenate(
        [ref[s * SEG : s * SEG + 16, :].astype(F32)[0:1] for s in range(segs)], axis=0
    )


class Stream:
    ORDER = (
        [("qkv", c) for c in range(3)] + [("out", 0)] + [("up", j) for j in range(4)]
        + [("down", j) for j in range(4)] * 2
        + [("up", j) for j in range(4)] + [("out", 0)] + [("qkv", c) for c in range(3)]
    )
    DEPTH = 3

    def __init__(self, r, arriving):
        self.r = r
        self.arriving = arriving
        self.next = 0
        self.pending = []

    def copies(self, n):
        r = self.r
        kind, index = self.ORDER[n]
        which = "w" + kind
        halves = (getattr(r, "a_" + which).at[1], getattr(r, "f_" + which))
        dest, sems = r.ring_w.at[n % self.DEPTH], r.ring_sem.at[n % self.DEPTH]
        if kind == "qkv":
            pairs = [(halves[h].at[index], half_of(dest, "wup_square", h)) for h in range(2)]
        elif kind == "out":
            pairs = [(halves[h], half_of(dest, "wout", h)) for h in range(2)]
        else:
            at = slice(index % 2 * D, index % 2 * D + D)
            source = halves[index // 2]
            pairs = [(source.at[:, at] if kind == "up" else source.at[at, :], dest)]
        return [pltpu.make_async_copy(a, b, sems.at[k]) for k, (a, b) in enumerate(pairs)]

    def start(self, n):
        if n < len(self.ORDER):
            kind, index = self.ORDER[n]
            if index >= 2 and kind in self.arriving:
                self.arriving.pop(kind).wait_recv()
            self.pending.append(self.copies(n))
            for copy in self.pending[-1]:
                copy.start()

    def take(self, body):
        for copy in self.pending.pop(0):
            copy.wait()
        kind, index = self.ORDER[self.next]
        body(index, self.r.ring_w.at[self.next % self.DEPTH])
        self.start(self.next + self.DEPTH)
        self.next += 1


def cross_layer(r, q, stream, keep, pump, hooks):
    def lanes(j):
        return slice(j * D, (j + 1) * D)

    def project_piece(c, w):
        q.qkv[c] = (mm(q.xb[...], w[...]) + q.b3[c]).astype(BF)

    for c in range(3):
        stream.take(project_piece)
    attend(q, keep, 0, PAIRS)
    pump("attend")

    def out_piece(j, w):
        q.xh1[...] = mm(q.o[...], w[...]) + q.bt[0]

    stream.take(out_piece)
    norm_one(q, q.x32)
    transpose_into(q.h1t, q.h1b, SEG)

    def up_piece(j, w):
        u = mm(q.h1b[...], w[...]) + q.bup[:, lanes(j)]
        q.g[:, lanes(j)], q.gp[:, lanes(j)] = gelu_pair(u)

    for j in range(4):
        stream.take(up_piece)
    pump("up")

    def down_piece(j, w):
        q.xh2[...] = q.xh2[...] + mm(q.g[:, lanes(j)], w[...])

    for j in range(4):
        stream.take(down_piece)
    norm_two(q, q.yb)
    pump("down")
    back_norm_two(q, lambda s, at: q.dy[at, :])
    hooks("down")

    def back_down_piece(j, w):
        du = (mm_nt(q.dm[...], w[...]) * q.gp[:, lanes(j)].astype(F32)).astype(BF)
        q.gp[:, lanes(j)] = du
        q.bup_sum[:, lanes(j)] = jnp.sum(du.astype(F32), axis=0, keepdims=True)

    for j in range(4):
        stream.take(back_down_piece)
    pump("back_down")
    hooks("up")

    def back_up_piece(j, w):
        q.dr[...] = q.dr[...] + mm_nt(q.gp[:, lanes(j)], w[...])

    for j in range(4):
        stream.take(back_up_piece)
    pump("back_up")
    back_norm_one(q)
    hooks("out")

    def back_out_piece(j, w):
        q.dh[...] = mm_nt(q.dm[...], w[...]).astype(BF)

    stream.take(back_out_piece)
    attend_back_values(q)
    attend_back(q, True, lambda i: None)
    bias_heads(q)
    pump("attend_back")
    hooks("qkv")

    def back_qkv_piece(c, w):
        q.dr[...] = q.dr[...] + mm_nt(q.g[:, lanes(c)], w[...])

    for c in range(3):
        stream.take(back_qkv_piece)


def whole_kernel(dp, names, *refs):
    r = Names(**dict(zip(names, refs)))
    d, t = lax.axis_index("dp"), lax.axis_index("tensor")
    x, y, z = lax.rem(d, 2), lax.rem(lax.div(d, 2), 2), lax.div(d, 4)
    zs = dp // 4
    shard = D // dp
    rows = r.xb.shape[0]
    segs = rows // SEG
    sibling = (d, 1 - t)
    x_peer = (z * 4 + y * 2 + (1 - x), t)
    y_peer = (z * 4 + (1 - y) * 2 + x, t)
    z_peers = [(lax.rem(z + o, zs) * 4 + y * 2 + x, t) for o in range(1, zs)]
    r.dr, r.dm, r.y1, r.dh = r.h1, r.h1b, r.xb, r.cot

    barrier = pltpu.get_barrier_semaphore()
    for device in [sibling] + [(lax.rem(d + o, dp), t) for o in range(1, dp)]:
        pl.semaphore_signal(barrier, inc=1, device_id=device, device_id_type=MESH)
    copies = Copies(r.local_sem)
    for layer, gain, terms in ((0, r.gain, r.bt), (1, r.gain_cross, r.bt_cross)):
        for k in range(2):
            gain[k] = r.norm_gain[layer, k : k + 1, :]
        for k in range(4):
            terms[k] = r.bias_terms[layer, k : k + 1, :]
    own = {w: getattr(r, "a_" + w) for w in WEIGHTS}
    full = {w: getattr(r, "f_" + w) for w in WEIGHTS}
    load_x = copies.start(r.tokens.at[t], r.xb)
    loads = {w: copies.start(own[w].at[0], half_of(getattr(r, w), w, 0)) for w in WEIGHTS}
    load_cot = copies.start(r.cotangent.at[t], r.cot)
    load_x.wait()
    transpose_into(r.xt, r.xb, rows)
    fill_bias(r.b3, r.bup, 0, 0, r.b_qv, r.b_up)
    fill_bias(r.b3_cross, r.bup_cross, 0, 1, r.b_qv, r.b_up)
    swaps = {}

    def described(layer, w):
        k = WEIGHTS.index(w)
        dest = half_of(getattr(r, w), w, 1) if layer == 0 else full[w]
        return remote(own[w].at[layer], dest, r.w_send.at[layer, k], r.w_recv.at[layer, k], sibling)

    for layer in range(2):
        for w in WEIGHTS:
            swaps[layer, w] = described(layer, w)

    def swap(layer, w):
        swaps[layer, w].start()

    cot_gather = Gather(dp, r.cot_all, r.g_send.at[0], r.g_recv.at[0])
    cls_gather = Gather(dp, r.cls_all, r.g_send.at[1], r.g_recv.at[1])
    hat_gather = Gather(dp, r.hat_all, r.g_send.at[2], r.g_recv.at[2])
    act_gather = Gather(dp, r.act_all, r.g_send.at[3], r.g_recv.at[3])

    def keep(s):
        seg = d * segs + s
        doc = r.seg_doc[t, seg]
        within = jnp.int32(0)
        for back in range(1, MAXSEG):
            same = r.seg_doc[t, jnp.maximum(seg - back, 0)] == doc
            within = within + jnp.where(jnp.logical_and(seg >= back, same), 1, 0)
        valid = jnp.minimum(SEG, r.doc_len[t, doc] - SEG * within)
        return lax.broadcasted_iota(jnp.int32, (1, SEG), 1) < valid

    def start_swaps():
        pl.semaphore_wait(barrier, dp)
        swap(0, "wqkv")
        for copy in swap_bias:
            copy.start()
        swap(0, "wout")
        swap(0, "wup")
        load_cot.wait()
        cot_gather.start(first_of_segments(r.cot, segs).astype(BF))

    def take_other():
        for copy in swap_bias:
            copy.wait_recv()
        fill_bias(r.b3, r.bup, 1, 0, r.x_bqv, r.x_bup)
        fill_bias(r.b3_cross, r.bup_cross, 1, 1, r.x_bqv, r.x_bup)
        swaps[0, "wqkv"].wait_recv()

    swap_bias = [
        remote(r.b_qv, r.x_bqv, r.w_send.at[0, 4], r.w_recv.at[0, 4], sibling),
        remote(r.b_up, r.x_bup, r.w_send.at[1, 4], r.w_recv.at[1, 4], sibling),
    ]
    loads["wqkv"].wait()

    @pl.loop(0, 2)
    def _(half):
        pl.when(half == 1)(take_other)
        project(r, half)
        pl.when(half == 0)(start_swaps)
        attend(r, keep, half * (PAIRS // 2), PAIRS // 2)

    swap(0, "wdown")
    loads["wout"].wait()
    swaps[0, "wout"].wait_recv()
    attn_out(r)
    swap(1, "wqkv")
    swap(1, "wout")
    norm_one(r, r.xb)
    loads["wup"].wait()
    mlp_up(r, lambda j: pl.when(j == 2)(swaps[0, "wup"].wait_recv))
    swap(1, "wup")
    transpose_into(r.h1t, r.h1b, rows)
    loads["wdown"].wait()
    mlp_down(r, lambda half: pl.when(half == 1)(swaps[0, "wdown"].wait_recv))
    norm_two(r, r.y1)
    cls_gather.start(first_of_segments(r.y1, segs).astype(BF))
    hats = first_of_segments(r.xh2, segs)
    hat_gather.start(jnp.concatenate([hats, first_of_segments(r.rs2, segs)], axis=1))

    def sib_copy(c):
        slot = lax.rem(c, SLOTS)
        return remote(
            r.sib_out.at[slot], r.sib_in.at[slot], r.sib_send.at[slot], r.sib_recv.at[slot], sibling
        )

    def ring(c):
        return lax.rem(c, RING)

    low_z, high_z = slice(0, zs // 2), slice(zs // 2, zs)

    def stage_one(c):
        g, into = r.gbuf.at[ring(c)], r.one_in.at[ring(c)]
        return (
            remote(g.at[low_z, :, 1 - x], into.at[0], r.one_send.at[c, 0], r.one_recv.at[c, 0], x_peer),
            remote(g.at[high_z, 1 - y], into.at[1], r.one_send.at[c, 1], r.one_recv.at[c, 1], y_peer),
        )

    def stage_two(c):
        g, into = r.gbuf.at[ring(c)], r.two_in.at[ring(c)]
        return (
            remote(g.at[low_z, 1 - y, x], into.at[0], r.two_send.at[c, 0], r.two_recv.at[c, 0], y_peer),
            remote(g.at[high_z, y, 1 - x], into.at[1], r.two_send.at[c, 1], r.two_recv.at[c, 1], x_peer),
        )

    def stage_three(c):
        g, into = r.gbuf.at[ring(c)], r.three_in.at[ring(c)]
        return [
            remote(
                g.at[lax.rem(z + o, zs), y, x],
                into.at[o - 1],
                r.three_send.at[c, o - 1],
                r.three_recv.at[c, o - 1],
                z_peers[o - 1],
            )
            for o in range(1, zs)
        ]

    def emit_other(c, left, right, at):
        @pl.when(c >= SLOTS)
        def _():
            sib_copy(c).wait_send()
            pl.semaphore_wait(r.credit, 1)

        r.sib_out[lax.rem(c, SLOTS)] = mm(left[...], right[:, pl.ds(at, CHUNK)]).astype(BF)
        sib_copy(c).start()

    def emit_own(c, left, right, at):
        mine = mm(left[...], right[:, pl.ds(at, CHUNK)])
        sib_copy(c).wait_recv()
        mine = (mine + r.sib_in[lax.rem(c, SLOTS)].astype(F32)).astype(BF)
        r.gbuf[ring(c)] = mine.reshape(zs, 2, 2, shard, CHUNK)

        @pl.when(c < CHUNKS - SLOTS)
        def _():
            pl.semaphore_signal(r.credit, inc=1, device_id=sibling, device_id_type=MESH)

    def launch(*chunks):
        for c in chunks:
            for copy in stage_one(jnp.int32(c)):
                copy.start()

    def hooks(name, which, part=None):
        low, high = HOOK_CHUNKS[name]
        left, (right, own_at, other_at) = chunk_operands(r, low)
        step = D if name == "qk" else CHUNK

        def at(c, base):
            return pl.multiple_of((c - low) * step + base, SEG)

        if which == "other":

            @pl.loop(low, high)
            def _(c):
                emit_other(c, left, right, at(c, other_at))

        else:

            @pl.loop(*(part or (low, high)))
            def _(c):
                emit_own(c, left, right, at(c, own_at))
                if which == "launch":
                    for copy in stage_one(c):
                        copy.start()

    def second(*chunks):
        for c in chunks:
            c = jnp.int32(c)
            g, into = r.gbuf.at[ring(c)], r.one_in.at[ring(c)]
            from_x, from_y = stage_one(c)
            to_y, to_x = stage_two(c)
            from_x.wait_recv()
            g[low_z, :, x] = g[low_z, :, x] + into[0]
            to_y.start()
            from_y.wait_recv()
            g[high_z, y] = g[high_z, y] + into[1]
            to_x.start()

    def third(*chunks):
        for c in chunks:
            c = jnp.int32(c)
            g, into = r.gbuf.at[ring(c)], r.two_in.at[ring(c)]
            for copy in stage_two(c):
                copy.wait_recv()
            g[low_z, y, x] = g[low_z, y, x] + into[0]
            g[high_z, y, x] = g[high_z, y, x] + into[1]
            for copy in stage_three(c):
                copy.start()

    def finish(*chunks):
        for c in chunks:
            at = jnp.int32(c)
            total = r.gbuf[ring(at), z, y, x].astype(F32)
            for o, copy in enumerate(stage_three(at)):
                copy.wait_recv()
                total = total + r.three_in[ring(at), o].astype(F32)
            r.mine[c] = r.mine[c] + total if c < 8 else total
            for copy in (*stage_one(at), *stage_two(at), *stage_three(at)):
                copy.wait_send()

    block_row = lax.broadcasted_iota(jnp.int32, (256, 1), 0)

    def without_first(s, at):
        return jnp.where(lax.rem(block_row, SEG) == 0, 0.0, r.cot[at, :].astype(F32))

    r.act_first[:, 0:FF] = first_of_segments(r.g, segs)
    r.act_first[:, FF : 2 * FF] = first_of_segments(r.gp, segs)
    r.act_first[:, 2 * FF :] = first_of_segments(r.h1b, segs)
    r.small_common = r.small
    back_norm_two(r, without_first)
    hooks("down", "other")
    hooks("down", "launch")
    swap(1, "wdown")
    act_gather.start(r.act_first[...].astype(BF))
    grad_hidden(r)
    hooks("up", "other")
    hooks("up", "own")
    launch(4, 5)

    q = Names(
        **{k: getattr(r, "q_" + k) for k in CROSS},
        g=r.g.at[0:SEG],
        gp=r.g.at[SEG : 2 * SEG],
        gain=r.gain_cross,
        bt=r.bt_cross,
        b3=r.b3_cross,
        bup=r.bup_cross,
        qv_sum=r.qv_sum,
        bup_sum=r.bup_sum_cross,
        small=r.small1,
    )
    q.dr, q.dm, q.small_common = q.h1, q.h1b, r.small1
    slots = q.xb.shape[0]
    total_docs = slots // MAXSEG
    total_segs = dp * segs
    stream = Stream(r, {"up": swaps[1, "wup"], "down": swaps[1, "wdown"]})
    for w in ("wqkv", "wout"):
        swaps[1, w].wait_recv()
    for n in range(stream.DEPTH):
        stream.start(n)

    doc = jnp.where(t == 0, r.seg_doc_v[0:1, :], r.seg_doc_v[1:2, :])
    below = lax.broadcasted_iota(jnp.int32, (total_segs, total_segs), 0)
    across = lax.broadcasted_iota(jnp.int32, (total_segs, total_segs), 1)

    def column(row):
        wide = jnp.broadcast_to(row, (total_segs, total_segs))
        return jnp.sum(jnp.where(below == across, wide, 0.0), axis=1, keepdims=True)

    doc_f = doc.astype(F32)
    earlier = jnp.logical_and(column(doc_f) == doc_f, below < across)
    within = jnp.sum(jnp.where(earlier, 1.0, 0.0), axis=0, keepdims=True).astype(jnp.int32)
    moved = doc + total_docs // 2
    moved = jnp.where(moved >= total_docs, moved - total_docs, moved)
    slot_of = (jnp.where((doc & 1) == 1, moved, doc) * MAXSEG + within).astype(F32)
    slot_ids = lax.broadcasted_iota(jnp.int32, (slots, total_segs), 0).astype(F32)
    deal = jnp.where(slot_ids == slot_of, 1.0, 0.0).astype(BF)
    slot_row = lax.broadcasted_iota(jnp.int32, (total_segs, slots), 1).astype(F32)
    r.undeal[...] = jnp.where(slot_row == column(slot_of), 1.0, 0.0).astype(BF)
    pick_row = lax.broadcasted_iota(jnp.int32, (8, total_segs), 0)
    pick_seg = lax.broadcasted_iota(jnp.int32, (8, total_segs), 1)
    picked = jnp.logical_and(pick_row < segs, pick_seg == d * segs + pick_row)
    r.pick[...] = jnp.where(picked, 1.0, 0.0).astype(BF)
    r.back[...] = mm(r.pick[...], r.undeal[...]).astype(BF)
    live = mm_nt(jnp.ones((8, total_segs), BF), deal)[0:1] > 0.5
    key_doc = lax.broadcasted_iota(jnp.int32, (SEG, SEG), 1) >> 3
    row_doc = lax.broadcasted_iota(jnp.int32, (SEG, SEG), 0) >> 3
    r.allowed[...] = jnp.where(jnp.logical_and(key_doc == row_doc, live), 1.0, 0.0)

    cot_gather.arrived()
    cot_gather.rows_into(r.rows64)
    q.dy[...] = mm(deal, r.rows64[...].astype(BF))
    cls_gather.arrived()
    cls_gather.rows_into(r.rows64)
    q.x32[...] = mm(deal, r.rows64[...].astype(BF)) + jnp.concatenate(
        [r.seg_pos[...]] * total_docs, axis=0
    )
    q.xb[...] = q.x32[...].astype(BF)
    transpose_into(q.xt, q.xb, slots)

    def cross_hooks(name):
        low, high = HOOK_CHUNKS[name]
        for c in range(low, high):
            left, (right, own_at, other_at) = chunk_operands(q, c)
            mine = left[pl.ds(pl.multiple_of(d * shard, 16), shard), :]
            r.shard1[c] = mm(mine, right[:, own_at : own_at + CHUNK])
            r.shard_out[c] = mm(mine, right[:, other_at : other_at + CHUNK]).astype(BF)

    def pump(point):
        if point == "up":
            second(0, 1)
        elif point == "down":
            second(2, 3)
            launch(6, 7)
        elif point == "back_up":
            second(4, 5)
        elif point == "attend_back":
            third(0, 1)

    cross_layer(r, q, stream, lambda s: r.allowed[...] > 0.5, pump, cross_hooks)
    pack_halves(q)
    total = q.dr[0:MAXSEG, :]
    for j in range(1, total_docs):
        total = total + q.dr[j * MAXSEG : (j + 1) * MAXSEG, :]
    for k in range(MAXSEG):
        r.small1[12 + k] = total[k : k + 1, :]
    r.ret[...] = mm(r.back[...], q.yb[...])
    low = q.dr[...].astype(BF)
    r.dc[...] = mm(r.back[...], low)

    gain_sum = jnp.zeros((1, D), F32)
    shift_sum, low_sum = gain_sum, gain_sum
    top = lax.broadcasted_iota(jnp.int32, (16, 1), 0) == 0
    for s in range(segs):
        at = slice(s * SEG, s * SEG + 16)
        grad = jnp.where(top, r.dc[s : s + 1, :], 0.0)
        hat = r.xh2[at, :]
        out = jnp.where(top, norm_back(grad, hat, r.rs2[at, 0:1], r.gain[1]), 0.0)
        out_low = out.astype(BF)
        r.dr[at, :] = jnp.where(top, out, r.dr[at, :])
        gain_sum = gain_sum + jnp.sum(grad * hat, axis=0, keepdims=True)
        shift_sum = shift_sum + jnp.sum(grad, axis=0, keepdims=True)
        low_sum = low_sum + jnp.sum(out_low.astype(F32), axis=0, keepdims=True)
        r.y1[at, :] = jnp.where(top, r.ret[s : s + 1, :], r.y1[at, :].astype(F32)).astype(BF)
    r.small_common[1] = r.small_common[1] + gain_sum
    r.small_common[5] = r.small_common[5] + shift_sum
    r.small_common[3] = r.small_common[3] + low_sum
    outs = [copies.start(r.y1, r.o_enc.at[t])]
    enc_swap = remote(r.y1, r.o_enc.at[t], r.misc_send.at[0], r.misc_recv.at[0], sibling)
    enc_swap.start()

    hat_gather.arrived()
    hat_gather.rows_into(r.hat64)
    act_gather.arrived()
    act_gather.rows_into(r.act64)
    all_grads = mm(r.undeal[...], low)
    late = norm_back(all_grads, r.hat64[:, 0:D], r.hat64[:, D : D + 1], r.gain[1]).astype(BF)
    r.late[0:total_segs, :] = late
    r.late[total_segs:, :] = jnp.zeros((SEG - total_segs, D), BF)
    transpose_into(r.late_t, r.late, SEG)
    shard_rows = pl.ds(pl.multiple_of(d * shard, 16), shard)

    def late_chunks(low, base):
        mine = r.late_t[shard_rows, 0:total_segs]
        for c in range(4):
            for half in range(2):
                cols = slice(base + half * HALF_FF + c * CHUNK, base + half * HALF_FF + (c + 1) * CHUNK)
                part = mm(mine, r.act64[:, cols])
                if half == 0:
                    r.mine[low + c] = part
                else:
                    r.shard_out[CHUNKS + low + c] = part.astype(BF)

    late_chunks(0, 0)

    @pl.loop(0, 3)
    def _(j):
        cols = span(j, 1024)
        slopes = pl.ds(pl.multiple_of(FF + j * 1024, 1024), 1024)
        du = (mm_nt(r.late[0:total_segs, :], r.wdown[cols, :]) * r.act64[:, slopes].astype(F32)).astype(BF)
        r.act64[:, slopes] = du
        mine = mm(r.pick[...], du)
        r.bup_sum[:, cols] = r.bup_sum[:, cols] + jnp.sum(mine, axis=0, keepdims=True)
        for s in range(segs):
            at = slice(s * SEG, s * SEG + 16)
            r.gp[at, cols] = jnp.where(top, mine[s : s + 1, :], r.gp[at, cols].astype(F32)).astype(BF)

    r.late[0:total_segs, :] = r.act64[:, 2 * FF :]
    transpose_into(r.late_t, r.late, SEG)
    late_chunks(4, FF)
    cross_swap = [
        remote(r.shard_out, r.shard_in, r.misc_send.at[1], r.misc_recv.at[1], sibling),
        remote(r.small1.at[0:6], r.small1_in.at[0:6], r.misc_send.at[2], r.misc_recv.at[2], sibling),
        remote(r.small1.at[9:20], r.small1_in.at[6:17], r.misc_send.at[3], r.misc_recv.at[3], sibling),
    ]
    for copy in cross_swap:
        copy.start()

    third(2, 3)
    grad_middle(r)
    for copy in cross_swap:
        copy.wait()
    for c in range(CHUNKS):
        r.shard1[c] = r.shard1[c] + r.shard_in[c].astype(F32)
    r.o_small[9:26] = (
        jnp.concatenate([r.small1[0:9], r.small1[12:20]], axis=0) + r.small1_in[...]
    )
    outs.append(copies.start(r.shard1, r.o_shard.at[1]))
    back_norm_one(r)
    second(6, 7)
    hooks("out", "other")
    grad_heads(r)
    hooks("out", "own")
    launch(8)
    third(4, 5)
    attend_back_values(r)
    hooks("v", "other")
    finish(0, 1, 2, 3)
    for c in range(8):
        r.mine[c] = r.mine[c] + r.shard_in[CHUNKS + c].astype(F32)

    def halfway():
        hooks("v", "own")
        launch(9)
        third(6)

    attend_back(r, False, lambda i: pl.when(i == 1)(halfway))
    bias_heads(r)
    pack_halves(r)
    small_swap = [
        remote(r.small.at[0:6], r.small_in.at[0:6], r.misc_send.at[4], r.misc_recv.at[4], sibling),
        remote(r.small.at[9:12], r.small_in.at[6:9], r.misc_send.at[5], r.misc_recv.at[5], sibling),
    ]
    for copy in small_swap:
        copy.start()
    second(8)
    hooks("qk", "other")
    third(7)
    for copy in small_swap:
        copy.wait()
    r.total[...] = r.small[0:9] + r.small_in[...]
    x_small = remote(r.total, r.x_small, r.misc_send.at[7], r.misc_recv.at[7], x_peer)
    x_small.start()
    hooks("qk", "own", (10, 11))
    second(9)
    launch(10)
    hooks("qk", "own", (11, 12))
    launch(11)
    x_small.wait()
    r.total_x[...] = r.total[...] + r.x_small[...]
    y_small = remote(r.total_x, r.y_small, r.misc_send.at[8], r.misc_recv.at[8], y_peer)
    y_small.start()
    third(8)
    grad_input(r)
    grad_swap = remote(r.dr, r.o_grad.at[t], r.misc_send.at[6], r.misc_recv.at[6], sibling)
    grad_swap.start()
    outs.append(copies.start(r.dr, r.o_grad.at[t]))
    finish(4, 5, 6)
    third(9)
    second(10, 11)
    y_small.wait()
    r.z_small[z] = r.total_x[...] + r.y_small[...]
    z_sends = []
    for o in range(1, zs):
        z_sends.append(
            remote(r.z_small.at[z], r.z_small.at[z], r.z_send.at[o], r.z_recv.at[z], z_peers[o - 1])
        )
        z_sends[-1].start()
    finish(7)
    third(10)
    for o in range(1, zs):
        source = lax.rem(z + o, zs)
        block = r.z_small.at[source]
        remote(block, block, r.z_send.at[o], r.z_recv.at[source], z_peers[o - 1]).wait_recv()
    total = r.z_small[0]
    for k in range(1, zs):
        total = total + r.z_small[k]
    r.o_small[0:9] = total
    third(11)
    finish(8, 9, 10, 11)
    outs.append(copies.start(r.mine, r.o_shard.at[0]))

    for copy in z_sends:
        copy.wait_send()
    for c in range(CHUNKS - SLOTS, CHUNKS):
        sib_copy(jnp.int32(c)).wait_send()
    for gathered in (cot_gather, cls_gather, hat_gather, act_gather):
        gathered.sent()
    for copy in swap_bias:
        copy.wait_send()
    for copy in swaps.values():
        copy.wait_send()
    grad_swap.wait()
    enc_swap.wait()
    for copy in outs:
        copy.wait()


CROSS = ("xb", "x32", "xt", "h1t", "h1b", "h1", "qkv", "o", "p", "xh1", "rs1", "xh2", "rs2", "yb", "dy", "dmt", "dh")
WEIGHT_SCRATCH = dict(
    wqkv=((3, D, D), BF), wout=((D, D), BF), wup=((D, FF), BF), wdown=((FF, D), BF)
)
BACK_SCRATCH = dict(qv_sum=((2, 1, D), F32), bup_sum=((1, FF), F32))


def saved_shapes(rows):
    return dict(
        xt=((D, rows), BF),
        h1t=((D, rows), BF),
        qkv=((3, rows, D), BF),
        o=((rows, D), BF),
        p=((rows // SEG, PAIRS, SEG, 2 * SEG), BF),
        xh1=((rows, D), F32),
        rs1=((rows, SEG), F32),
        g=((rows, FF), BF),
        gp=((rows, FF), BF),
        xh2=((rows, D), F32),
        rs2=((rows, SEG), F32),
    )


def forward_shapes(rows):
    return dict(
        xb=((rows, D), BF),
        h1=((rows, D), F32),
        h1b=((rows, D), BF),
        b3=((3, 1, D), F32),
        bup=((1, FF), F32),
    )


def vmem(table):
    return [pltpu.VMEM(shape, kind) for shape, kind in table.values()]


def arrays(table):
    return [jax.ShapeDtypeStruct(shape, kind) for shape, kind in table.values()]


def run_whole(dp, inputs):
    hbm = pl.BlockSpec(memory_space=pl.ANY)
    small = pl.BlockSpec(memory_space=pltpu.VMEM)
    smem = pl.BlockSpec(memory_space=pltpu.SMEM)
    batches, rows, _ = inputs["tokens"].shape
    slots = inputs["doc_len"].shape[1] * MAXSEG
    segs = rows // SEG
    total_segs = dp * segs
    zs = dp // 4
    shard = D // dp
    outs = dict(
        o_enc=((batches, rows, D), BF),
        o_grad=((batches, rows, D), F32),
        o_shard=((2, CHUNKS, shard, CHUNK), F32),
        o_small=((26, 1, D), F32),
    )
    outs.update({"f_" + w: (inputs["a_" + w].shape[1:], BF) for w in WEIGHTS})
    scratch = dict(saved_shapes(rows))
    scratch.update(WEIGHT_SCRATCH)
    scratch.update(forward_shapes(rows))
    scratch.update(BACK_SCRATCH)
    cross = dict(saved_shapes(slots))
    cross.update(forward_shapes(slots))
    cross.update(
        x32=((slots, D), F32), yb=((slots, D), BF), dy=((slots, D), F32), dmt=((D, slots), BF),
        dh=((slots, D), BF),
    )
    scratch.update({"q_" + k: cross[k] for k in CROSS})
    scratch.update(
        b3_cross=((3, 1, D), F32),
        bup_cross=((1, FF), F32),
        gain=((2, 1, D), F32),
        gain_cross=((2, 1, D), F32),
        bt=((4, 1, D), F32),
        bt_cross=((4, 1, D), F32),
        x_bqv=((2, 2, HALF_D), F32),
        x_bup=((2, HALF_FF), F32),
        cot=((rows, D), BF),
        dmt=((D, rows), BF),
        ring_w=((3, D, D), BF),
        act_first=((segs, 2 * FF + D), F32),
        pick=((8, total_segs), BF),
        bup_sum_cross=((1, FF), F32),
        cot_all=((dp, segs, D), BF),
        cls_all=((dp, segs, D), BF),
        hat_all=((dp, segs, D + SEG), F32),
        act_all=((dp, segs, 2 * FF + D), BF),
        rows64=((total_segs, D), F32),
        hat64=((total_segs, D + SEG), F32),
        act64=((total_segs, 2 * FF + D), BF),
        undeal=((total_segs, slots), BF),
        back=((8, slots), BF),
        allowed=((SEG, SEG), F32),
        ret=((8, D), F32),
        dc=((8, D), F32),
        late=((SEG, D), BF),
        late_t=((D, SEG), BF),
        small=((12, 1, D), F32),
        small1=((20, 1, D), F32),
        small_in=((9, 1, D), F32),
        small1_in=((17, 1, D), F32),
        total=((9, 1, D), F32),
        total_x=((9, 1, D), F32),
        x_small=((9, 1, D), F32),
        y_small=((9, 1, D), F32),
        z_small=((zs, 9, 1, D), F32),
        shard1=((CHUNKS, shard, CHUNK), F32),
        shard_out=((CHUNKS + 8, shard, CHUNK), BF),
        shard_in=((CHUNKS + 8, shard, CHUNK), BF),
        mine=((CHUNKS, shard, CHUNK), F32),
        gbuf=((RING, zs, 2, 2, shard, CHUNK), BF),
        sib_out=((SLOTS, D, CHUNK), BF),
        sib_in=((SLOTS, D, CHUNK), BF),
        one_in=((RING, 2, zs // 2, 2, shard, CHUNK), BF),
        two_in=((RING, 2, zs // 2, shard, CHUNK), BF),
        three_in=((RING, zs - 1, shard, CHUNK), BF),
    )
    dma = pltpu.SemaphoreType.DMA
    sems = dict(
        local_sem=dma((20,)),
        w_send=dma((2, 5)),
        w_recv=dma((2, 5)),
        ring_sem=dma((3, 2)),
        g_send=dma((4, dp)),
        g_recv=dma((4, dp)),
        misc_send=dma((9,)),
        misc_recv=dma((9,)),
        sib_send=dma((SLOTS,)),
        sib_recv=dma((SLOTS,)),
        one_send=dma((CHUNKS, 2)),
        one_recv=dma((CHUNKS, 2)),
        two_send=dma((CHUNKS, 2)),
        two_recv=dma((CHUNKS, 2)),
        three_send=dma((CHUNKS, zs - 1)),
        three_recv=dma((CHUNKS, zs - 1)),
        z_send=dma((zs,)),
        z_recv=dma((zs,)),
        credit=pltpu.SemaphoreType.REGULAR,
    )
    ins = dict(
        seg_doc=smem, doc_len=smem, seg_doc_v=small, tokens=hbm, cotangent=hbm, b_qv=small, b_up=small,
        norm_gain=small, bias_terms=small, seg_pos=small,
        a_wqkv=hbm, a_wout=hbm, a_wup=hbm, a_wdown=hbm,
    )
    names = list(ins) + list(outs) + list(scratch) + list(sems)
    result = pl.pallas_call(
        partial(whole_kernel, dp, names),
        out_shape=arrays(outs),
        in_specs=list(ins.values()),
        out_specs=[hbm, hbm, hbm, small] + [hbm] * 4,
        scratch_shapes=vmem(scratch) + list(sems.values()),
        compiler_params=pltpu.CompilerParams(
            collective_id=0, has_side_effects=True, vmem_limit_bytes=VMEM_LIMIT
        ),
        name="both_layers",
    )(*[inputs[k] for k in ins])
    return dict(zip(outs, result))


VMEM_LIMIT = 64 << 20


def finish_kernel(
    enc, grad, shard, small, o_enc, o_grad, g_qkv, g_out, g_up, g_down, g_bqv, g_bup, g_gain, g_terms, g_pos,
    enc_v, grad_v, shard_v, sems,
):
    copies = Copies(sems)
    loads = [copies.start(grad.at[b], grad_v.at[b]) for b in range(grad.shape[0])]
    load_shard = copies.start(shard, shard_v)
    loads_enc = [copies.start(enc.at[b], enc_v.at[b]) for b in range(enc.shape[0])]
    outs = []
    for b, load in enumerate(loads):
        load.wait()
        outs.append(copies.start(grad_v.at[b], o_grad.at[b]))
    load_shard.wait()
    for layer in range(2):
        for c in range(4):
            lanes = slice(c * CHUNK, (c + 1) * CHUNK)
            outs.append(copies.start(shard_v.at[layer, c], g_down.at[layer, :, lanes]))
            outs.append(copies.start(shard_v.at[layer, 4 + c], g_up.at[layer, :, lanes]))
        outs.append(copies.start(shard_v.at[layer, 8], g_out.at[layer]))
        for k in range(3):
            outs.append(copies.start(shard_v.at[layer, 9 + k], g_qkv.at[layer, QKV_OF[k]]))
    for b, load in enumerate(loads_enc):
        load.wait()
        outs.append(copies.start(enc_v.at[b], o_enc.at[b]))
    for layer in range(2):
        at = 9 * layer
        for k in range(2):
            g_gain[layer, k : k + 1, :] = small[at + k]
            g_bqv[layer, k : k + 1, :] = small[at + 6, :, k * HALF_D : (k + 1) * HALF_D]
            g_bup[layer : layer + 1, k * D : (k + 1) * D] = small[at + 7 + k]
        for k in range(4):
            g_terms[layer, k : k + 1, :] = small[at + 2 + k]
    for k in range(MAXSEG):
        g_pos[k : k + 1, :] = small[18 + k]
    for copy in outs:
        copy.wait()


def fused(tokens, seg_doc, doc_len, w_qkv, b_qv, w_out, w_up, b_up, w_down, norm_gain, bias_terms, seg_pos, cotangent):
    dp = lax.axis_size("dp")
    whole = run_whole(
        dp,
        dict(
            seg_doc=seg_doc, doc_len=doc_len, seg_doc_v=seg_doc, tokens=tokens, cotangent=cotangent,
            b_qv=b_qv, b_up=b_up, norm_gain=norm_gain, bias_terms=bias_terms,
            seg_pos=seg_pos, a_wqkv=w_qkv, a_wout=w_out, a_wup=w_up, a_wdown=w_down,
        ),
    )
    rows = D // dp
    shapes = [
        (2, 3, rows, HALF_D), (2, rows, HALF_D), (2, rows, HALF_FF), (2, rows, HALF_FF),
        (2, 2, HALF_D), (2, HALF_FF), (2, 2, D), (2, 4, D), (MAXSEG, D),
    ]
    hbm = pl.BlockSpec(memory_space=pl.ANY)
    small = pl.BlockSpec(memory_space=pltpu.VMEM)
    results = [whole[k] for k in ("o_enc", "o_grad", "o_shard", "o_small")]
    enc, grad, g_qkv, g_out, g_up, g_down, g_bqv, g_bup, g_gain, g_terms, g_pos = pl.pallas_call(
        finish_kernel,
        out_shape=[jax.ShapeDtypeStruct(a.shape, a.dtype) for a in results[:2]]
        + [jax.ShapeDtypeStruct(shape, F32) for shape in shapes],
        in_specs=[hbm] * 3 + [small],
        out_specs=[hbm] * 6 + [small] * 5,
        scratch_shapes=[pltpu.VMEM(a.shape, a.dtype) for a in results[:3]]
        + [pltpu.SemaphoreType.DMA((40,))],
        compiler_params=pltpu.CompilerParams(vmem_limit_bytes=VMEM_LIMIT),
        name="lay_out",
    )(*results)
    return (
        enc, grad, g_qkv, g_bqv, g_out.transpose(0, 2, 1), g_up, g_bup, g_down.transpose(0, 2, 1),
        g_gain, g_terms, g_pos,
    )


def solution(mesh):
    in_specs = (
        P(None, "dp", None),
        P(),
        P(),
        P(None, None, None, "tensor"),
        P(None, None, "tensor"),
        P(None, "tensor", None),
        P(None, None, "tensor"),
        P(None, "tensor"),
        P(None, "tensor", None),
        P(),
        P(),
        P(),
        P(None, "dp", None),
    )
    out_specs = (
        P(None, "dp", None),
        P(None, "dp", None),
        P(None, None, "dp", "tensor"),
        P(None, None, "tensor"),
        P(None, "tensor", "dp"),
        P(None, "dp", "tensor"),
        P(None, "tensor"),
        P(None, "tensor", "dp"),
        P(),
        P(),
        P(),
    )
    body = fused if mesh.shape["dp"] == 16 and mesh.shape["tensor"] == 2 else local
    return jax.shard_map(body, mesh=mesh, in_specs=in_specs, out_specs=out_specs, check_vma=False)
```

```python
from functools import partial, reduce

import jax
import jax.numpy as jnp
from jax import lax
from jax.experimental import pallas as pl
from jax.experimental.pallas import tpu as pltpu
from jax.sharding import PartitionSpec as P

HEAD_DIM = 64
SEG = 128
MAXSEG = 8


norm_eps = 1e-05
masked_score = -1e30


def norm_rows(values, gain, shift):
    centre = values - jnp.mean(values, axis=-1, keepdims=True)
    spread = jnp.mean(centre * centre, axis=-1, keepdims=True)
    return centre * lax.rsqrt(spread + norm_eps) * gain + shift


def exact_gelu(values):
    return jax.nn.gelu(values, approximate=False)


def my_rows(values):
    part_rows = values.shape[0] // lax.axis_size("tensor")
    return lax.dynamic_slice_in_dim(values, lax.axis_index("tensor") * part_rows, part_rows, 0)


def attn_scores(queries, key_rows, key_mask, split_shape):
    raw = jnp.einsum(
        "glhd,gmhd->ghlm",
        queries.reshape(split_shape),
        key_rows.reshape(split_shape),
        preferred_element_type=jnp.float32,
    ) * HEAD_DIM ** (-0.5)
    return jnp.where(key_mask[:, None, None, :], raw, masked_score)


def layer_forward(inputs, key_mask, weights):
    w_qkv, b_qv, w_out, w_up, b_up, w_down, norm_gain, bias_terms = weights
    groups, span = key_mask.shape
    row_count = inputs.shape[0]
    local_width = w_qkv.shape[2]
    split_shape = (groups, span, local_width // HEAD_DIM, HEAD_DIM)
    inputs_b = inputs.astype(jnp.bfloat16)
    projected = jnp.einsum("rd,cde->cre", inputs_b, w_qkv, preferred_element_type=jnp.float32)
    queries = (projected[0] + b_qv[0]).astype(jnp.bfloat16)
    key_rows = projected[1].astype(jnp.bfloat16)
    value_rows = (projected[2] + b_qv[1]).astype(jnp.bfloat16)
    scores = attn_scores(queries, key_rows, key_mask, split_shape)
    row_max = jnp.max(scores, axis=-1, keepdims=True)
    log_total = row_max + jnp.log(jnp.sum(jnp.exp(scores - row_max), axis=-1, keepdims=True))
    attn_probs = jnp.exp(scores - log_total).astype(jnp.bfloat16)
    head_out = jnp.einsum(
        "ghlm,gmhd->glhd",
        attn_probs,
        value_rows.reshape(split_shape),
        preferred_element_type=jnp.float32,
    )
    head_out = head_out.reshape(row_count, local_width).astype(jnp.bfloat16)
    attn_part = (
        lax.psum_scatter(
            jnp.dot(head_out, w_out, preferred_element_type=jnp.float32),
            "tensor",
            scatter_dimension=0,
            tiled=True,
        )
        + bias_terms[0]
    )
    resid_one = lax.all_gather(my_rows(inputs) + attn_part, "tensor", axis=0, tiled=True)
    hidden = norm_rows(resid_one, norm_gain[0], bias_terms[2])
    hidden_b = hidden.astype(jnp.bfloat16)
    pre_act = jnp.dot(hidden_b, w_up, preferred_element_type=jnp.float32) + b_up
    active_b = exact_gelu(pre_act).astype(jnp.bfloat16)
    mlp_part = (
        lax.psum_scatter(
            jnp.dot(active_b, w_down, preferred_element_type=jnp.float32),
            "tensor",
            scatter_dimension=0,
            tiled=True,
        )
        + bias_terms[1]
    )
    resid_two = lax.all_gather(my_rows(hidden) + mlp_part, "tensor", axis=0, tiled=True)
    stored = (
        inputs_b,
        queries,
        key_rows,
        value_rows,
        log_total,
        head_out,
        resid_one,
        hidden_b,
        pre_act,
        active_b,
        resid_two,
    )
    return (norm_rows(resid_two, norm_gain[1], bias_terms[3]), stored)


def layer_backward(grad_out, key_mask, weights, stored):
    w_qkv, b_qv, w_out, w_up, b_up, w_down, norm_gain, bias_terms = weights
    (
        inputs_b,
        queries,
        key_rows,
        value_rows,
        log_total,
        head_out,
        resid_one,
        hidden_b,
        pre_act,
        active_b,
        resid_two,
    ) = stored
    groups, span = key_mask.shape
    row_count, local_width = queries.shape
    split_shape = (groups, span, local_width // HEAD_DIM, HEAD_DIM)
    forward_two, norm_two = jax.vjp(norm_rows, resid_two, norm_gain[1], bias_terms[3])
    grad_two, gain_two, shift_two = norm_two(grad_out)
    grad_mlp = grad_two.astype(jnp.bfloat16)
    grad_wdown = jnp.dot(active_b.T, grad_mlp, preferred_element_type=jnp.float32)
    grad_act = jnp.dot(grad_mlp, w_down.T, preferred_element_type=jnp.float32)
    forward_gelu, gelu_back = jax.vjp(exact_gelu, pre_act)
    grad_pre = gelu_back(grad_act)[0].astype(jnp.bfloat16)
    grad_wup = jnp.dot(hidden_b.T, grad_pre, preferred_element_type=jnp.float32)
    up_part = lax.psum_scatter(
        jnp.dot(grad_pre, w_up.T, preferred_element_type=jnp.float32),
        "tensor",
        scatter_dimension=0,
        tiled=True,
    )
    grad_hidden = lax.all_gather(my_rows(grad_two) + up_part, "tensor", axis=0, tiled=True)
    forward_one, norm_one = jax.vjp(norm_rows, resid_one, norm_gain[0], bias_terms[2])
    grad_one, gain_one, shift_one = norm_one(grad_hidden)
    grad_attn = grad_one.astype(jnp.bfloat16)
    grad_wout = jnp.dot(head_out.T, grad_attn, preferred_element_type=jnp.float32)
    grad_heads = (
        jnp.dot(grad_attn, w_out.T, preferred_element_type=jnp.float32)
        .astype(jnp.bfloat16)
        .reshape(split_shape)
    )
    scores = attn_scores(queries, key_rows, key_mask, split_shape)
    attn_probs = jnp.exp(scores - log_total)
    grad_probs = jnp.einsum(
        "glhd,gmhd->ghlm",
        grad_heads,
        value_rows.reshape(split_shape),
        preferred_element_type=jnp.float32,
    )
    grad_values = jnp.einsum(
        "ghlm,glhd->gmhd",
        attn_probs.astype(jnp.bfloat16),
        grad_heads,
        preferred_element_type=jnp.float32,
    )
    grad_scores = (
        attn_probs * (grad_probs - jnp.sum(attn_probs * grad_probs, axis=-1, keepdims=True))
    ).astype(jnp.bfloat16)
    inv_root = HEAD_DIM ** (-0.5)
    grad_queries = (
        jnp.einsum(
            "ghlm,gmhd->glhd",
            grad_scores,
            key_rows.reshape(split_shape),
            preferred_element_type=jnp.float32,
        )
        * inv_root
    )
    grad_keys = (
        jnp.einsum(
            "ghlm,glhd->gmhd",
            grad_scores,
            queries.reshape(split_shape),
            preferred_element_type=jnp.float32,
        )
        * inv_root
    )
    grad_qkv = (
        jnp.stack([grad_queries, grad_keys, grad_values])
        .reshape(3, row_count, local_width)
        .astype(jnp.bfloat16)
    )
    grad_wqkv = jnp.einsum("rd,cre->cde", inputs_b, grad_qkv, preferred_element_type=jnp.float32)
    qkv_part = lax.psum_scatter(
        jnp.einsum("cre,cde->rd", grad_qkv, w_qkv, preferred_element_type=jnp.float32).astype(
            jnp.bfloat16
        ),
        "tensor",
        scatter_dimension=0,
        tiled=True,
    ).astype(jnp.float32)
    grad_inputs = lax.all_gather(
        (my_rows(grad_one) + qkv_part).astype(jnp.bfloat16), "tensor", axis=0, tiled=True
    ).astype(jnp.float32)
    grad_bqv = jnp.stack(
        [
            jnp.sum(grad_qkv[0].astype(jnp.float32), axis=0),
            jnp.sum(grad_qkv[2].astype(jnp.float32), axis=0),
        ]
    )
    grad_bup = jnp.sum(grad_pre.astype(jnp.float32), axis=0)
    grad_gain = jnp.stack([gain_one, gain_two])
    grad_shift = jnp.stack(
        [
            jnp.sum(grad_attn.astype(jnp.float32), axis=0),
            jnp.sum(grad_mlp.astype(jnp.float32), axis=0),
            shift_one,
            shift_two,
        ]
    )
    return (
        grad_inputs,
        (grad_wqkv, grad_bqv, grad_wout, grad_wup, grad_bup, grad_wdown, grad_gain, grad_shift),
    )


def deal_map(doc_ids, total_docs):
    return jnp.where(doc_ids % 2 == 1, (doc_ids + total_docs // 2) % total_docs, doc_ids)


def local_plan(seg_order, doc_lengths, seg_local, doc_local):
    total_docs = doc_lengths.shape[0]
    my_index = lax.axis_index("dp")
    doc_ids = jnp.arange(total_docs, dtype=jnp.int32)
    owner_pos = deal_map(doc_ids, total_docs)
    starts = jnp.sum((seg_order[None, :] < doc_ids[:, None]).astype(jnp.int32), axis=1)
    counts = jnp.sum((seg_order[None, :] == doc_ids[:, None]).astype(jnp.int32), axis=1)
    my_segments = my_index * seg_local + jnp.arange(seg_local, dtype=jnp.int32)
    seg_owner_doc = lax.dynamic_slice_in_dim(seg_order, my_index * seg_local, seg_local)
    seg_hot = seg_owner_doc[:, None] == doc_ids[None, :]
    my_start = jnp.sum(jnp.where(seg_hot, starts[None, :], 0), axis=1)
    my_length = jnp.sum(jnp.where(seg_hot, doc_lengths[None, :], 0), axis=1)
    my_owner = jnp.sum(jnp.where(seg_hot, owner_pos[None, :], 0), axis=1)
    within = my_segments - my_start
    valid_tokens = jnp.minimum(SEG, my_length - within * SEG)
    tok_mask = jnp.arange(SEG, dtype=jnp.int32)[None, :] < valid_tokens[:, None]
    src_slot = my_owner * MAXSEG + within
    my_deal = deal_map(my_index * doc_local + jnp.arange(doc_local, dtype=jnp.int32), total_docs)
    deal_hot = my_deal[:, None] == doc_ids[None, :]
    own_start = jnp.sum(jnp.where(deal_hot, starts[None, :], 0), axis=1)
    own_count = jnp.sum(jnp.where(deal_hot, counts[None, :], 0), axis=1)
    slot_index = jnp.arange(MAXSEG, dtype=jnp.int32)
    cross_mask = slot_index[None, :] < own_count[:, None]
    target = jnp.where(cross_mask, own_start[:, None] + slot_index[None, :], -1).reshape(-1)
    return (tok_mask, cross_mask, target, src_slot)


def picker(index_map, shard_rows):
    positions = jnp.arange(shard_rows.shape[0], dtype=jnp.int32)
    selector = (index_map[:, None] == positions[None, :]).astype(jnp.bfloat16)
    return jnp.dot(selector, shard_rows, preferred_element_type=jnp.float32)


def spreader(index_map, source_rows, row_span):
    positions = jnp.arange(row_span, dtype=jnp.int32)
    selector = (positions[:, None] == index_map[None, :]).astype(jnp.bfloat16)
    return jnp.dot(selector, source_rows, preferred_element_type=jnp.float32)


def add_terms(left, right):
    return jax.tree.map(jnp.add, left, right)


def local(
    tokens,
    seg_doc,
    doc_len,
    w_qkv,
    b_qv,
    w_out,
    w_up,
    b_up,
    w_down,
    norm_gain,
    bias_terms,
    seg_pos,
    cotangent,
):
    batches, local_rows, width = tokens.shape
    seg_local = local_rows // SEG
    doc_local = doc_len.shape[1] // lax.axis_size("dp")
    slot_rows = doc_local * MAXSEG

    def layer_weights(level):
        return (
            w_qkv[level],
            b_qv[level],
            w_out[level],
            w_up[level],
            b_up[level],
            w_down[level],
            norm_gain[level],
            bias_terms[level],
        )

    seg_weights = layer_weights(0)
    cross_weights = layer_weights(1)
    encoded = []
    grad_tokens = []
    seg_grads = []
    cross_grads = []
    pos_grads = []
    for batch_index in range(batches):
        tok_mask, cross_mask, target, src_slot = local_plan(
            seg_doc[batch_index], doc_len[batch_index], seg_local, doc_local
        )
        seg_out, seg_stored = layer_forward(
            tokens[batch_index].astype(jnp.float32), tok_mask, seg_weights
        )
        seg_cube = seg_out.reshape(seg_local, SEG, width)
        cls_rows = seg_cube[:, 0].astype(jnp.bfloat16)
        collected = picker(target, lax.all_gather(cls_rows, "dp", axis=0, tiled=True))
        cross_in = (collected.reshape(doc_local, MAXSEG, width) + seg_pos[None]).reshape(
            slot_rows, width
        )
        cross_out, cross_stored = layer_forward(cross_in, cross_mask, cross_weights)
        returned = picker(
            src_slot, lax.all_gather(cross_out.astype(jnp.bfloat16), "dp", axis=0, tiled=True)
        )
        encoded.append(
            seg_cube.at[:, 0].set(returned).reshape(local_rows, width).astype(jnp.bfloat16)
        )
        grad_cube = cotangent[batch_index].astype(jnp.float32).reshape(seg_local, SEG, width)
        grad_returned = grad_cube[:, 0].astype(jnp.bfloat16)
        grad_cross = lax.psum_scatter(
            spreader(src_slot, grad_returned, slot_rows * lax.axis_size("dp")),
            "dp",
            scatter_dimension=0,
            tiled=True,
        )
        grad_cross_in, cross_terms = layer_backward(
            grad_cross, cross_mask, cross_weights, cross_stored
        )
        pos_grads.append(jnp.sum(grad_cross_in.reshape(doc_local, MAXSEG, width), axis=0))
        grad_sent = grad_cross_in.astype(jnp.bfloat16)
        cross_grads.append(cross_terms)
        grad_cls = lax.psum_scatter(
            spreader(target, grad_sent, seg_local * lax.axis_size("dp")),
            "dp",
            scatter_dimension=0,
            tiled=True,
        )
        grad_seg = grad_cube.at[:, 0].set(grad_cls).reshape(local_rows, width)
        grad_inputs, seg_terms = layer_backward(grad_seg, tok_mask, seg_weights, seg_stored)
        grad_tokens.append(grad_inputs)
        seg_grads.append(seg_terms)
    seg_total = reduce(add_terms, seg_grads)
    cross_total = reduce(add_terms, cross_grads)
    pos_total = reduce(jnp.add, pos_grads)
    big_grads = (
        lax.psum_scatter(
            jnp.stack([seg_total[0], cross_total[0]]), "dp", scatter_dimension=2, tiled=True
        ),
        lax.psum_scatter(
            jnp.stack([seg_total[2], cross_total[2]]), "dp", scatter_dimension=2, tiled=True
        ),
        lax.psum_scatter(
            jnp.stack([seg_total[3], cross_total[3]]), "dp", scatter_dimension=1, tiled=True
        ),
        lax.psum_scatter(
            jnp.stack([seg_total[5], cross_total[5]]), "dp", scatter_dimension=2, tiled=True
        ),
    )
    small = lax.psum(
        (
            jnp.stack([seg_total[1], cross_total[1]]),
            jnp.stack([seg_total[4], cross_total[4]]),
            jnp.stack([seg_total[6], cross_total[6]]),
            jnp.stack([seg_total[7], cross_total[7]]),
            pos_total,
        ),
        "dp",
    )
    return (
        jnp.stack(encoded),
        jnp.stack(grad_tokens),
        big_grads[0],
        small[0],
        big_grads[1],
        big_grads[2],
        small[1],
        big_grads[3],
        small[2],
        small[3],
        small[4],
    )


BF = jnp.bfloat16
F32 = jnp.float32
D = 768
FF = 3072
HALF_FF = FF // 2
HALF_D = D // 2
CHUNK = 384
CHUNKS = 12
PAIRS = 6
MESH = pl.DeviceIdType.MESH
ROOT_HALF = 0.7071067811865476
PDF_SCALE = 0.3989422804014327


class Names:
    def __init__(self, **kw):
        self.__dict__.update(kw)


def mm(left, right):
    return jnp.dot(left, right, preferred_element_type=F32)


def mm_nt(left, right):
    return lax.dot_general(left, right, (((1,), (1,)), ((), ())), preferred_element_type=F32)


def span(index, size):
    return pl.ds(pl.multiple_of(index * size, size), size)


def row_norm(rows):
    centre = rows - jnp.mean(rows, axis=-1, keepdims=True)
    spread = jnp.mean(centre * centre, axis=-1, keepdims=True)
    scale = lax.rsqrt(spread + norm_eps)
    return centre * scale, scale


def stacked(pair, low_half):
    zero = jnp.zeros_like(pair)
    return jnp.concatenate(
        [jnp.where(low_half, pair, zero), jnp.where(low_half, zero, pair)], axis=0
    )


def soft_rows(scores):
    top = jnp.max(scores, axis=-1, keepdims=True)
    grown = jnp.exp(scores - top)
    return (grown * (1.0 / jnp.sum(grown, axis=-1, keepdims=True))).astype(BF)


def transpose_into(dest, source, rows):
    @pl.loop(0, rows // SEG)
    def _(s):
        dest[:, span(s, SEG)] = source[span(s, SEG), :].T


def gelu_pair(u):
    cdf = 0.5 * (1.0 + lax.erf(u * ROOT_HALF))
    slope = cdf + u * (PDF_SCALE * jnp.exp(-0.5 * u * u))
    return (u * cdf).astype(BF), slope.astype(BF)


def project(r, half):
    lanes = span(half, HALF_D)
    for c in range(3):
        r.qkv[c, :, lanes] = (mm(r.xb[...], r.wqkv[c, :, lanes]) + r.b3[c, :, lanes]).astype(BF)


def low_lanes():
    return lax.broadcasted_iota(jnp.int32, (SEG, SEG), 1) < HEAD_DIM


def attend(r, keep, first, count):
    segs = r.xb.shape[0] // SEG
    root = jnp.asarray(HEAD_DIM ** (-0.5), BF)

    @pl.loop(0, segs, unroll=min(segs, 4))
    def _(s):
        at = span(s, SEG)
        live = keep(s)
        low_half = low_lanes()
        for k in range(count):
            p = first + k
            cols = span(p, SEG)
            keys = stacked(r.qkv[1, at, cols], low_half)
            vals = stacked(r.qkv[2, at, cols], low_half)
            raw = mm_nt(r.qkv[0, at, cols] * root, keys)
            one = soft_rows(jnp.where(live, raw[:, :SEG], masked_score))
            two = soft_rows(jnp.where(live, raw[:, SEG:], masked_score))
            both = jnp.concatenate([one, two], axis=1)
            r.p[s, p] = both
            r.o[at, cols] = mm(both, vals).astype(BF)


def attn_out(r):
    for n in range(3):
        cols = slice(n * 256, n * 256 + 256)
        r.xh1[:, cols] = mm(r.o[...], r.wout[:, cols]) + r.bt[0, :, cols]


def norm_one(r, x_ref):
    rows = r.xh1.shape[0]
    block = min(rows, 256)

    @pl.loop(0, rows // block)
    def _(s):
        at = span(s, block)
        hat, scale = row_norm(x_ref[at, :].astype(F32) + r.xh1[at, :])
        r.xh1[at, :] = hat
        r.rs1[at, :] = jnp.broadcast_to(scale, (block, SEG))
        hidden = hat * r.gain[0] + r.bt[2]
        r.h1[at, :] = hidden
        r.h1b[at, :] = hidden.astype(BF)
        r.xh2[at, :] = hidden + r.bt[1]


def mlp_up(r, before):
    @pl.loop(0, 4)
    def _(j):
        before(j)
        for k in range(3):
            cols = pl.ds(pl.multiple_of(j * D + k * 256, 256), 256)
            u = mm(r.h1b[...], r.wup[:, cols]) + r.bup[:, cols]
            r.g[:, cols], r.gp[:, cols] = gelu_pair(u)


def mlp_down(r, before):
    @pl.loop(0, 2)
    def _(half):
        before(half)
        part = span(half, HALF_FF)
        for n in range(3):
            cols = slice(n * 256, n * 256 + 256)
            r.xh2[:, cols] = r.xh2[:, cols] + mm(r.g[:, part], r.wdown[part, cols])


def norm_two(r, y_ref):
    rows = r.xh2.shape[0]
    block = min(rows, 256)

    @pl.loop(0, rows // block)
    def _(s):
        at = span(s, block)
        hat, scale = row_norm(r.xh2[at, :])
        r.xh2[at, :] = hat
        r.rs2[at, :] = jnp.broadcast_to(scale, (block, SEG))
        y_ref[at, :] = (hat * r.gain[1] + r.bt[3]).astype(BF)


def norm_back(grad, hat, scale, gain):
    d_hat = grad * gain
    first = jnp.mean(d_hat, axis=-1, keepdims=True)
    second = jnp.mean(d_hat * hat, axis=-1, keepdims=True)
    return (d_hat - first - hat * second) * scale


def norm_back_rows(r, hat_ref, scale_ref, gain, grad_of):
    zero = jnp.zeros((1, D), F32)
    rows = r.dr.shape[0]
    block = min(rows, 256)

    def step(s, sums):
        at = span(s, block)
        grad = grad_of(s, at)
        hat = hat_ref[at, :]
        out = norm_back(grad, hat, scale_ref[at, 0:1], gain)
        low = out.astype(BF)
        r.dr[at, :] = out
        r.dm[at, :] = low
        return (
            sums[0] + jnp.sum(grad * hat, axis=0, keepdims=True),
            sums[1] + jnp.sum(grad, axis=0, keepdims=True),
            sums[2] + jnp.sum(low.astype(F32), axis=0, keepdims=True),
        )

    sums = lax.fori_loop(0, rows // block, step, (zero, zero, zero))
    transpose_into(r.dmt, r.dm, rows)
    return sums


def back_norm_two(r, grad_of):
    sums = norm_back_rows(r, r.xh2, r.rs2, r.gain[1], grad_of)
    r.small_common[1], r.small_common[5], r.small_common[3] = sums


def back_norm_one(r):
    sums = norm_back_rows(r, r.xh1, r.rs1, r.gain[0], lambda s, at: r.dr[at, :])
    r.small_common[0], r.small_common[4], r.small_common[2] = sums


def grad_hidden(r):
    @pl.loop(0, 3)
    def _(j):
        cols = span(j, 1024)
        du = (mm_nt(r.dm[...], r.wdown[cols, :]) * r.gp[:, cols].astype(F32)).astype(BF)
        r.gp[:, cols] = du
        r.bup_sum[:, cols] = jnp.sum(du.astype(F32), axis=0, keepdims=True)


def grad_middle(r):
    for n in range(3):
        cols = slice(n * 256, n * 256 + 256)
        r.dr[:, cols] = r.dr[:, cols] + mm_nt(r.gp[...], r.wup[cols, :])


def grad_heads(r):
    for n in range(3):
        cols = slice(n * 256, n * 256 + 256)
        r.dh[:, cols] = mm_nt(r.dm[...], r.wout[cols, :]).astype(BF)


def attend_back_values(r):
    segs = r.dh.shape[0] // SEG

    @pl.loop(0, segs, unroll=min(segs, 2))
    def _(s):
        at = span(s, SEG)
        low_half = low_lanes()
        for p in range(PAIRS):
            d_vals = mm(r.p[s, p].T, r.dh[at, p * SEG : p * SEG + SEG])
            cols = slice(2 * D + p * SEG, 2 * D + p * SEG + SEG)
            r.g[at, cols] = jnp.where(low_half, d_vals[:SEG], d_vals[SEG:]).astype(BF)


def attend_back(r, exact, before):
    root = jnp.asarray(HEAD_DIM ** (-0.5), BF)
    segs = r.dh.shape[0] // SEG
    together = min(segs, 2)

    def segment(s):
        at = span(s, SEG)
        low_half = low_lanes()
        head = lax.broadcasted_iota(jnp.int32, (SEG, 2 * SEG), 0) < HEAD_DIM
        side = lax.broadcasted_iota(jnp.int32, (SEG, 2 * SEG), 1) < SEG
        ones = jnp.where(head == side, 1.0, 0.0).astype(BF)
        for p in range(PAIRS):
            cols = slice(p * SEG, p * SEG + SEG)
            query = r.qkv[0, at, cols] * root
            keys = stacked(r.qkv[1, at, cols] * root, low_half)
            vals = stacked(r.qkv[2, at, cols], low_half)
            d_head = r.dh[at, cols]
            d_probs = mm_nt(d_head, vals)
            both = d_head.astype(F32) * r.o[at, cols].astype(F32)
            inner = mm(both.astype(BF), ones)
            if exact:
                inner = inner + mm((both - both.astype(BF).astype(F32)).astype(BF), ones)
            d_scores = (r.p[s, p].astype(F32) * (d_probs - inner)).astype(BF)
            d_keys = mm(d_scores.T, query)
            r.g[at, cols] = mm(d_scores, keys).astype(BF)
            cols = slice(D + p * SEG, D + p * SEG + SEG)
            r.g[at, cols] = jnp.where(low_half, d_keys[:SEG], d_keys[SEG:]).astype(BF)

    @pl.loop(0, segs // together)
    def _(i):
        before(i)
        for k in range(together):
            segment(i * together + k)


def bias_heads(r):
    for c in (0, 2):
        r.qv_sum[c // 2] = jnp.sum(
            r.g[:, c * D : (c + 1) * D].astype(F32), axis=0, keepdims=True
        )


def grad_input(r):
    for n in range(3):
        cols = slice(n * 256, n * 256 + 256)
        total = r.dr[:, cols]
        for c in range(3):
            total = total + mm_nt(r.g[:, c * D : (c + 1) * D], r.wqkv[c, cols, :])
        r.dr[:, cols] = total


def chunk_operands(r, c):
    if c < 4:
        return r.dmt, (r.g, c * CHUNK, HALF_FF + c * CHUNK)
    if c < 8:
        return r.h1t, (r.gp, (c - 4) * CHUNK, HALF_FF + (c - 4) * CHUNK)
    if c == 8:
        return r.dmt, (r.o, 0, HALF_D)
    at = QKV_OF[c - 9] * D
    return r.xt, (r.g, at, at + HALF_D)


QKV_OF = (2, 0, 1)
HOOK_CHUNKS = {"down": (0, 4), "up": (4, 8), "out": (8, 9), "qkv": (9, 12), "v": (9, 10), "qk": (10, 12)}


class Copies:
    def __init__(self, sems):
        self.sems = sems
        self.used = 0

    def start(self, source, dest):
        copy = pltpu.make_async_copy(source, dest, self.sems.at[self.used])
        self.used += 1
        copy.start()
        return copy


def remote(source, dest, send_sem, recv_sem, device):
    return pltpu.make_async_remote_copy(
        src_ref=source,
        dst_ref=dest,
        send_sem=send_sem,
        recv_sem=recv_sem,
        device_id=device,
        device_id_type=MESH,
    )


class Gather:
    def __init__(self, dp, everyone, send, recv):
        self.dp, self.everyone, self.send, self.recv = dp, everyone, send, recv

    def start(self, block):
        d, t = lax.axis_index("dp"), lax.axis_index("tensor")
        everyone = self.everyone
        everyone[d] = block
        for o in range(1, self.dp):
            peer = (lax.rem(d + o, self.dp), t)
            copy = remote(everyone.at[d], everyone.at[d], self.send.at[o], self.recv.at[d], peer)
            copy.start()

    def sent(self):
        d, t = lax.axis_index("dp"), lax.axis_index("tensor")
        block = self.everyone.at[d]
        for o in range(1, self.dp):
            peer = (lax.rem(d + o, self.dp), t)
            remote(block, block, self.send.at[o], self.recv.at[d], peer).wait_send()

    def arrived(self):
        d, t = lax.axis_index("dp"), lax.axis_index("tensor")
        for o in range(1, self.dp):
            source = lax.rem(d + o, self.dp)
            block = self.everyone.at[source]
            remote(block, block, self.send.at[o], self.recv.at[source], (source, t)).wait_recv()

    def rows_into(self, dest):
        segs = self.everyone.shape[1]
        tall = 16 if dest.dtype == BF else 8
        pack = tall // segs
        for i in range(self.dp // pack):
            blocks = [self.everyone[i * pack + k].astype(F32) for k in range(pack)]
            dest[i * tall : i * tall + tall, :] = jnp.concatenate(blocks, axis=0).astype(dest.dtype)


SLOTS = 4
RING = 9
WEIGHTS = ("wqkv", "wout", "wup", "wdown")


def half_of(ref, which, half):
    if which == "wqkv":
        return ref.at[:, :, half * HALF_D : (half + 1) * HALF_D]
    if which == "wout":
        return ref.at[half * HALF_D : (half + 1) * HALF_D, :]
    if which == "wup_square":
        return ref.at[:, half * HALF_D : (half + 1) * HALF_D]
    if which == "wup":
        return ref.at[:, half * HALF_FF : (half + 1) * HALF_FF]
    return ref.at[half * HALF_FF : (half + 1) * HALF_FF, :]


def fill_bias(b3, bup, half, layer, b_qv, b_up):
    lanes = slice(half * HALF_D, (half + 1) * HALF_D)
    b3[0, :, lanes] = b_qv[layer, 0:1, :]
    b3[1, :, lanes] = jnp.zeros((1, HALF_D), F32)
    b3[2, :, lanes] = b_qv[layer, 1:2, :]
    bup[:, half * HALF_FF : (half + 1) * HALF_FF] = b_up[layer : layer + 1, :]


def pack_halves(r):
    for half in range(2):
        at = 6 + 3 * half
        lanes = slice(half * HALF_D, (half + 1) * HALF_D)
        r.small[at, :, 0:HALF_D] = r.qv_sum[0, :, lanes]
        r.small[at, :, HALF_D:] = r.qv_sum[1, :, lanes]
        base = half * HALF_FF
        r.small[at + 1] = r.bup_sum[:, base : base + D]
        r.small[at + 2] = r.bup_sum[:, base + D : base + 2 * D]


def first_of_segments(ref, segs):
    return jnp.concatenate(
        [ref[s * SEG : s * SEG + 16, :].astype(F32)[0:1] for s in range(segs)], axis=0
    )


class Stream:
    ORDER = (
        [("qkv", c) for c in range(3)] + [("out", 0)] + [("up", j) for j in range(4)]
        + [("down", j) for j in range(4)] * 2
        + [("up", j) for j in range(4)] + [("out", 0)] + [("qkv", c) for c in range(3)]
    )
    DEPTH = 3

    def __init__(self, r, arriving):
        self.r = r
        self.arriving = arriving
        self.next = 0
        self.pending = []

    def copies(self, n):
        r = self.r
        kind, index = self.ORDER[n]
        which = "w" + kind
        halves = (getattr(r, "a_" + which).at[1], getattr(r, "f_" + which))
        dest, sems = r.ring_w.at[n % self.DEPTH], r.ring_sem.at[n % self.DEPTH]
        if kind == "qkv":
            pairs = [(halves[h].at[index], half_of(dest, "wup_square", h)) for h in range(2)]
        elif kind == "out":
            pairs = [(halves[h], half_of(dest, "wout", h)) for h in range(2)]
        else:
            at = slice(index % 2 * D, index % 2 * D + D)
            source = halves[index // 2]
            pairs = [(source.at[:, at] if kind == "up" else source.at[at, :], dest)]
        return [pltpu.make_async_copy(a, b, sems.at[k]) for k, (a, b) in enumerate(pairs)]

    def start(self, n):
        if n < len(self.ORDER):
            kind, index = self.ORDER[n]
            if index >= 2 and kind in self.arriving:
                self.arriving.pop(kind).wait_recv()
            self.pending.append(self.copies(n))
            for copy in self.pending[-1]:
                copy.start()

    def take(self, body):
        for copy in self.pending.pop(0):
            copy.wait()
        kind, index = self.ORDER[self.next]
        body(index, self.r.ring_w.at[self.next % self.DEPTH])
        self.start(self.next + self.DEPTH)
        self.next += 1


def cross_layer(r, q, stream, keep, pump, hooks):
    def lanes(j):
        return slice(j * D, (j + 1) * D)

    def project_piece(c, w):
        q.qkv[c] = (mm(q.xb[...], w[...]) + q.b3[c]).astype(BF)

    for c in range(3):
        stream.take(project_piece)
    attend(q, keep, 0, PAIRS)
    pump("attend")

    def out_piece(j, w):
        q.xh1[...] = mm(q.o[...], w[...]) + q.bt[0]

    stream.take(out_piece)
    norm_one(q, q.x32)
    transpose_into(q.h1t, q.h1b, SEG)

    def up_piece(j, w):
        u = mm(q.h1b[...], w[...]) + q.bup[:, lanes(j)]
        q.g[:, lanes(j)], q.gp[:, lanes(j)] = gelu_pair(u)

    for j in range(4):
        stream.take(up_piece)
    pump("up")

    def down_piece(j, w):
        q.xh2[...] = q.xh2[...] + mm(q.g[:, lanes(j)], w[...])

    for j in range(4):
        stream.take(down_piece)
    norm_two(q, q.yb)
    pump("down")
    back_norm_two(q, lambda s, at: q.dy[at, :])
    hooks("down")

    def back_down_piece(j, w):
        du = (mm_nt(q.dm[...], w[...]) * q.gp[:, lanes(j)].astype(F32)).astype(BF)
        q.gp[:, lanes(j)] = du
        q.bup_sum[:, lanes(j)] = jnp.sum(du.astype(F32), axis=0, keepdims=True)

    for j in range(4):
        stream.take(back_down_piece)
    pump("back_down")
    hooks("up")

    def back_up_piece(j, w):
        q.dr[...] = q.dr[...] + mm_nt(q.gp[:, lanes(j)], w[...])

    for j in range(4):
        stream.take(back_up_piece)
    pump("back_up")
    back_norm_one(q)
    hooks("out")

    def back_out_piece(j, w):
        q.dh[...] = mm_nt(q.dm[...], w[...]).astype(BF)

    stream.take(back_out_piece)
    attend_back_values(q)
    attend_back(q, True, lambda i: None)
    bias_heads(q)
    pump("attend_back")
    hooks("qkv")

    def back_qkv_piece(c, w):
        q.dr[...] = q.dr[...] + mm_nt(q.g[:, lanes(c)], w[...])

    for c in range(3):
        stream.take(back_qkv_piece)


def whole_kernel(dp, names, *refs):
    r = Names(**dict(zip(names, refs)))
    d, t = lax.axis_index("dp"), lax.axis_index("tensor")
    x, y, z = lax.rem(d, 2), lax.rem(lax.div(d, 2), 2), lax.div(d, 4)
    zs = dp // 4
    shard = D // dp
    rows = r.xb.shape[0]
    segs = rows // SEG
    sibling = (d, 1 - t)
    x_peer = (z * 4 + y * 2 + (1 - x), t)
    y_peer = (z * 4 + (1 - y) * 2 + x, t)
    z_peers = [(lax.rem(z + o, zs) * 4 + y * 2 + x, t) for o in range(1, zs)]
    r.dr, r.dm, r.y1, r.dh = r.h1, r.h1b, r.xb, r.cot

    barrier = pltpu.get_barrier_semaphore()
    for device in [sibling] + [(lax.rem(d + o, dp), t) for o in range(1, dp)]:
        pl.semaphore_signal(barrier, inc=1, device_id=device, device_id_type=MESH)
    copies = Copies(r.local_sem)
    for layer, gain, terms in ((0, r.gain, r.bt), (1, r.gain_cross, r.bt_cross)):
        for k in range(2):
            gain[k] = r.norm_gain[layer, k : k + 1, :]
        for k in range(4):
            terms[k] = r.bias_terms[layer, k : k + 1, :]
    own = {w: getattr(r, "a_" + w) for w in WEIGHTS}
    full = {w: getattr(r, "f_" + w) for w in WEIGHTS}
    load_x = copies.start(r.tokens.at[t], r.xb)
    loads = {w: copies.start(own[w].at[0], half_of(getattr(r, w), w, 0)) for w in WEIGHTS}
    load_cot = copies.start(r.cotangent.at[t], r.cot)
    load_x.wait()
    transpose_into(r.xt, r.xb, rows)
    fill_bias(r.b3, r.bup, 0, 0, r.b_qv, r.b_up)
    fill_bias(r.b3_cross, r.bup_cross, 0, 1, r.b_qv, r.b_up)
    swaps = {}

    def described(layer, w):
        k = WEIGHTS.index(w)
        dest = half_of(getattr(r, w), w, 1) if layer == 0 else full[w]
        return remote(own[w].at[layer], dest, r.w_send.at[layer, k], r.w_recv.at[layer, k], sibling)

    for layer in range(2):
        for w in WEIGHTS:
            swaps[layer, w] = described(layer, w)

    def swap(layer, w):
        swaps[layer, w].start()

    cot_gather = Gather(dp, r.cot_all, r.g_send.at[0], r.g_recv.at[0])
    cls_gather = Gather(dp, r.cls_all, r.g_send.at[1], r.g_recv.at[1])
    hat_gather = Gather(dp, r.hat_all, r.g_send.at[2], r.g_recv.at[2])
    act_gather = Gather(dp, r.act_all, r.g_send.at[3], r.g_recv.at[3])

    def keep(s):
        seg = d * segs + s
        doc = r.seg_doc[t, seg]
        within = jnp.int32(0)
        for back in range(1, MAXSEG):
            same = r.seg_doc[t, jnp.maximum(seg - back, 0)] == doc
            within = within + jnp.where(jnp.logical_and(seg >= back, same), 1, 0)
        valid = jnp.minimum(SEG, r.doc_len[t, doc] - SEG * within)
        return lax.broadcasted_iota(jnp.int32, (1, SEG), 1) < valid

    def start_swaps():
        pl.semaphore_wait(barrier, dp)
        swap(0, "wqkv")
        for copy in swap_bias:
            copy.start()
        swap(0, "wout")
        swap(0, "wup")
        load_cot.wait()
        cot_gather.start(first_of_segments(r.cot, segs).astype(BF))

    def take_other():
        for copy in swap_bias:
            copy.wait_recv()
        fill_bias(r.b3, r.bup, 1, 0, r.x_bqv, r.x_bup)
        fill_bias(r.b3_cross, r.bup_cross, 1, 1, r.x_bqv, r.x_bup)
        swaps[0, "wqkv"].wait_recv()

    swap_bias = [
        remote(r.b_qv, r.x_bqv, r.w_send.at[0, 4], r.w_recv.at[0, 4], sibling),
        remote(r.b_up, r.x_bup, r.w_send.at[1, 4], r.w_recv.at[1, 4], sibling),
    ]
    loads["wqkv"].wait()

    @pl.loop(0, 2)
    def _(half):
        pl.when(half == 1)(take_other)
        project(r, half)
        pl.when(half == 0)(start_swaps)
        attend(r, keep, half * (PAIRS // 2), PAIRS // 2)

    swap(0, "wdown")
    loads["wout"].wait()
    swaps[0, "wout"].wait_recv()
    attn_out(r)
    swap(1, "wqkv")
    swap(1, "wout")
    norm_one(r, r.xb)
    loads["wup"].wait()
    mlp_up(r, lambda j: pl.when(j == 2)(swaps[0, "wup"].wait_recv))
    swap(1, "wup")
    transpose_into(r.h1t, r.h1b, rows)
    loads["wdown"].wait()
    mlp_down(r, lambda half: pl.when(half == 1)(swaps[0, "wdown"].wait_recv))
    norm_two(r, r.y1)
    cls_gather.start(first_of_segments(r.y1, segs).astype(BF))
    hats = first_of_segments(r.xh2, segs)
    hat_gather.start(jnp.concatenate([hats, first_of_segments(r.rs2, segs)], axis=1))

    def sib_copy(c):
        slot = lax.rem(c, SLOTS)
        return remote(
            r.sib_out.at[slot], r.sib_in.at[slot], r.sib_send.at[slot], r.sib_recv.at[slot], sibling
        )

    def ring(c):
        return lax.rem(c, RING)

    low_z, high_z = slice(0, zs // 2), slice(zs // 2, zs)

    def stage_one(c):
        g, into = r.gbuf.at[ring(c)], r.one_in.at[ring(c)]
        return (
            remote(g.at[low_z, :, 1 - x], into.at[0], r.one_send.at[c, 0], r.one_recv.at[c, 0], x_peer),
            remote(g.at[high_z, 1 - y], into.at[1], r.one_send.at[c, 1], r.one_recv.at[c, 1], y_peer),
        )

    def stage_two(c):
        g, into = r.gbuf.at[ring(c)], r.two_in.at[ring(c)]
        return (
            remote(g.at[low_z, 1 - y, x], into.at[0], r.two_send.at[c, 0], r.two_recv.at[c, 0], y_peer),
            remote(g.at[high_z, y, 1 - x], into.at[1], r.two_send.at[c, 1], r.two_recv.at[c, 1], x_peer),
        )

    def stage_three(c):
        g, into = r.gbuf.at[ring(c)], r.three_in.at[ring(c)]
        return [
            remote(
                g.at[lax.rem(z + o, zs), y, x],
                into.at[o - 1],
                r.three_send.at[c, o - 1],
                r.three_recv.at[c, o - 1],
                z_peers[o - 1],
            )
            for o in range(1, zs)
        ]

    def emit_other(c, left, right, at):
        @pl.when(c >= SLOTS)
        def _():
            sib_copy(c).wait_send()
            pl.semaphore_wait(r.credit, 1)

        r.sib_out[lax.rem(c, SLOTS)] = mm(left[...], right[:, pl.ds(at, CHUNK)]).astype(BF)
        sib_copy(c).start()

    def emit_own(c, left, right, at):
        mine = mm(left[...], right[:, pl.ds(at, CHUNK)])
        sib_copy(c).wait_recv()
        mine = (mine + r.sib_in[lax.rem(c, SLOTS)].astype(F32)).astype(BF)
        r.gbuf[ring(c)] = mine.reshape(zs, 2, 2, shard, CHUNK)

        @pl.when(c < CHUNKS - SLOTS)
        def _():
            pl.semaphore_signal(r.credit, inc=1, device_id=sibling, device_id_type=MESH)

    def launch(*chunks):
        for c in chunks:
            for copy in stage_one(jnp.int32(c)):
                copy.start()

    def hooks(name, which, part=None):
        low, high = HOOK_CHUNKS[name]
        left, (right, own_at, other_at) = chunk_operands(r, low)
        step = D if name == "qk" else CHUNK

        def at(c, base):
            return pl.multiple_of((c - low) * step + base, SEG)

        if which == "other":

            @pl.loop(low, high)
            def _(c):
                emit_other(c, left, right, at(c, other_at))

        else:

            @pl.loop(*(part or (low, high)))
            def _(c):
                emit_own(c, left, right, at(c, own_at))
                if which == "launch":
                    for copy in stage_one(c):
                        copy.start()

    def second(*chunks):
        for c in chunks:
            c = jnp.int32(c)
            g, into = r.gbuf.at[ring(c)], r.one_in.at[ring(c)]
            from_x, from_y = stage_one(c)
            to_y, to_x = stage_two(c)
            from_x.wait_recv()
            g[low_z, :, x] = g[low_z, :, x] + into[0]
            to_y.start()
            from_y.wait_recv()
            g[high_z, y] = g[high_z, y] + into[1]
            to_x.start()

    def third(*chunks):
        for c in chunks:
            c = jnp.int32(c)
            g, into = r.gbuf.at[ring(c)], r.two_in.at[ring(c)]
            for copy in stage_two(c):
                copy.wait_recv()
            g[low_z, y, x] = g[low_z, y, x] + into[0]
            g[high_z, y, x] = g[high_z, y, x] + into[1]
            for copy in stage_three(c):
                copy.start()

    def finish(*chunks):
        for c in chunks:
            at = jnp.int32(c)
            total = r.gbuf[ring(at), z, y, x].astype(F32)
            for o, copy in enumerate(stage_three(at)):
                copy.wait_recv()
                total = total + r.three_in[ring(at), o].astype(F32)
            r.mine[c] = r.mine[c] + total if c < 8 else total
            for copy in (*stage_one(at), *stage_two(at), *stage_three(at)):
                copy.wait_send()

    block_row = lax.broadcasted_iota(jnp.int32, (256, 1), 0)

    def without_first(s, at):
        return jnp.where(lax.rem(block_row, SEG) == 0, 0.0, r.cot[at, :].astype(F32))

    r.act_first[:, 0:FF] = first_of_segments(r.g, segs)
    r.act_first[:, FF : 2 * FF] = first_of_segments(r.gp, segs)
    r.act_first[:, 2 * FF :] = first_of_segments(r.h1b, segs)
    r.small_common = r.small
    back_norm_two(r, without_first)
    hooks("down", "other")
    hooks("down", "launch")
    swap(1, "wdown")
    act_gather.start(r.act_first[...].astype(BF))
    grad_hidden(r)
    hooks("up", "other")
    hooks("up", "own")
    launch(4, 5)

    q = Names(
        **{k: getattr(r, "q_" + k) for k in CROSS},
        g=r.g.at[0:SEG],
        gp=r.g.at[SEG : 2 * SEG],
        gain=r.gain_cross,
        bt=r.bt_cross,
        b3=r.b3_cross,
        bup=r.bup_cross,
        qv_sum=r.qv_sum,
        bup_sum=r.bup_sum_cross,
        small=r.small1,
    )
    q.dr, q.dm, q.small_common = q.h1, q.h1b, r.small1
    slots = q.xb.shape[0]
    total_docs = slots // MAXSEG
    total_segs = dp * segs
    stream = Stream(r, {"up": swaps[1, "wup"], "down": swaps[1, "wdown"]})
    for w in ("wqkv", "wout"):
        swaps[1, w].wait_recv()
    for n in range(stream.DEPTH):
        stream.start(n)

    doc = jnp.where(t == 0, r.seg_doc_v[0:1, :], r.seg_doc_v[1:2, :])
    below = lax.broadcasted_iota(jnp.int32, (total_segs, total_segs), 0)
    across = lax.broadcasted_iota(jnp.int32, (total_segs, total_segs), 1)

    def column(row):
        wide = jnp.broadcast_to(row, (total_segs, total_segs))
        return jnp.sum(jnp.where(below == across, wide, 0.0), axis=1, keepdims=True)

    doc_f = doc.astype(F32)
    earlier = jnp.logical_and(column(doc_f) == doc_f, below < across)
    within = jnp.sum(jnp.where(earlier, 1.0, 0.0), axis=0, keepdims=True).astype(jnp.int32)
    moved = doc + total_docs // 2
    moved = jnp.where(moved >= total_docs, moved - total_docs, moved)
    slot_of = (jnp.where((doc & 1) == 1, moved, doc) * MAXSEG + within).astype(F32)
    slot_ids = lax.broadcasted_iota(jnp.int32, (slots, total_segs), 0).astype(F32)
    deal = jnp.where(slot_ids == slot_of, 1.0, 0.0).astype(BF)
    slot_row = lax.broadcasted_iota(jnp.int32, (total_segs, slots), 1).astype(F32)
    r.undeal[...] = jnp.where(slot_row == column(slot_of), 1.0, 0.0).astype(BF)
    pick_row = lax.broadcasted_iota(jnp.int32, (8, total_segs), 0)
    pick_seg = lax.broadcasted_iota(jnp.int32, (8, total_segs), 1)
    picked = jnp.logical_and(pick_row < segs, pick_seg == d * segs + pick_row)
    r.pick[...] = jnp.where(picked, 1.0, 0.0).astype(BF)
    r.back[...] = mm(r.pick[...], r.undeal[...]).astype(BF)
    live = mm_nt(jnp.ones((8, total_segs), BF), deal)[0:1] > 0.5
    key_doc = lax.broadcasted_iota(jnp.int32, (SEG, SEG), 1) >> 3
    row_doc = lax.broadcasted_iota(jnp.int32, (SEG, SEG), 0) >> 3
    r.allowed[...] = jnp.where(jnp.logical_and(key_doc == row_doc, live), 1.0, 0.0)

    cot_gather.arrived()
    cot_gather.rows_into(r.rows64)
    q.dy[...] = mm(deal, r.rows64[...].astype(BF))
    cls_gather.arrived()
    cls_gather.rows_into(r.rows64)
    q.x32[...] = mm(deal, r.rows64[...].astype(BF)) + jnp.concatenate(
        [r.seg_pos[...]] * total_docs, axis=0
    )
    q.xb[...] = q.x32[...].astype(BF)
    transpose_into(q.xt, q.xb, slots)

    def cross_hooks(name):
        low, high = HOOK_CHUNKS[name]
        for c in range(low, high):
            left, (right, own_at, other_at) = chunk_operands(q, c)
            mine = left[pl.ds(pl.multiple_of(d * shard, 16), shard), :]
            r.shard1[c] = mm(mine, right[:, own_at : own_at + CHUNK])
            r.shard_out[c] = mm(mine, right[:, other_at : other_at + CHUNK]).astype(BF)

    def pump(point):
        if point == "up":
            second(0, 1)
        elif point == "down":
            second(2, 3)
            launch(6, 7)
        elif point == "back_up":
            second(4, 5)
        elif point == "attend_back":
            third(0, 1)

    cross_layer(r, q, stream, lambda s: r.allowed[...] > 0.5, pump, cross_hooks)
    pack_halves(q)
    total = q.dr[0:MAXSEG, :]
    for j in range(1, total_docs):
        total = total + q.dr[j * MAXSEG : (j + 1) * MAXSEG, :]
    for k in range(MAXSEG):
        r.small1[12 + k] = total[k : k + 1, :]
    r.ret[...] = mm(r.back[...], q.yb[...])
    low = q.dr[...].astype(BF)
    r.dc[...] = mm(r.back[...], low)

    gain_sum = jnp.zeros((1, D), F32)
    shift_sum, low_sum = gain_sum, gain_sum
    top = lax.broadcasted_iota(jnp.int32, (16, 1), 0) == 0
    for s in range(segs):
        at = slice(s * SEG, s * SEG + 16)
        grad = jnp.where(top, r.dc[s : s + 1, :], 0.0)
        hat = r.xh2[at, :]
        out = jnp.where(top, norm_back(grad, hat, r.rs2[at, 0:1], r.gain[1]), 0.0)
        out_low = out.astype(BF)
        r.dr[at, :] = jnp.where(top, out, r.dr[at, :])
        gain_sum = gain_sum + jnp.sum(grad * hat, axis=0, keepdims=True)
        shift_sum = shift_sum + jnp.sum(grad, axis=0, keepdims=True)
        low_sum = low_sum + jnp.sum(out_low.astype(F32), axis=0, keepdims=True)
        r.y1[at, :] = jnp.where(top, r.ret[s : s + 1, :], r.y1[at, :].astype(F32)).astype(BF)
    r.small_common[1] = r.small_common[1] + gain_sum
    r.small_common[5] = r.small_common[5] + shift_sum
    r.small_common[3] = r.small_common[3] + low_sum
    outs = [copies.start(r.y1, r.o_enc.at[t])]
    enc_swap = remote(r.y1, r.o_enc.at[t], r.misc_send.at[0], r.misc_recv.at[0], sibling)
    enc_swap.start()

    hat_gather.arrived()
    hat_gather.rows_into(r.hat64)
    act_gather.arrived()
    act_gather.rows_into(r.act64)
    all_grads = mm(r.undeal[...], low)
    late = norm_back(all_grads, r.hat64[:, 0:D], r.hat64[:, D : D + 1], r.gain[1]).astype(BF)
    r.late[0:total_segs, :] = late
    r.late[total_segs:, :] = jnp.zeros((SEG - total_segs, D), BF)
    transpose_into(r.late_t, r.late, SEG)
    shard_rows = pl.ds(pl.multiple_of(d * shard, 16), shard)

    def late_chunks(low, base):
        mine = r.late_t[shard_rows, 0:total_segs]
        for c in range(4):
            for half in range(2):
                cols = slice(base + half * HALF_FF + c * CHUNK, base + half * HALF_FF + (c + 1) * CHUNK)
                part = mm(mine, r.act64[:, cols])
                if half == 0:
                    r.mine[low + c] = part
                else:
                    r.shard_out[CHUNKS + low + c] = part.astype(BF)

    late_chunks(0, 0)

    @pl.loop(0, 3)
    def _(j):
        cols = span(j, 1024)
        slopes = pl.ds(pl.multiple_of(FF + j * 1024, 1024), 1024)
        du = (mm_nt(r.late[0:total_segs, :], r.wdown[cols, :]) * r.act64[:, slopes].astype(F32)).astype(BF)
        r.act64[:, slopes] = du
        mine = mm(r.pick[...], du)
        r.bup_sum[:, cols] = r.bup_sum[:, cols] + jnp.sum(mine, axis=0, keepdims=True)
        for s in range(segs):
            at = slice(s * SEG, s * SEG + 16)
            r.gp[at, cols] = jnp.where(top, mine[s : s + 1, :], r.gp[at, cols].astype(F32)).astype(BF)

    r.late[0:total_segs, :] = r.act64[:, 2 * FF :]
    transpose_into(r.late_t, r.late, SEG)
    late_chunks(4, FF)
    cross_swap = [
        remote(r.shard_out, r.shard_in, r.misc_send.at[1], r.misc_recv.at[1], sibling),
        remote(r.small1.at[0:6], r.small1_in.at[0:6], r.misc_send.at[2], r.misc_recv.at[2], sibling),
        remote(r.small1.at[9:20], r.small1_in.at[6:17], r.misc_send.at[3], r.misc_recv.at[3], sibling),
    ]
    for copy in cross_swap:
        copy.start()

    third(2, 3)
    grad_middle(r)
    for copy in cross_swap:
        copy.wait()
    for c in range(CHUNKS):
        r.shard1[c] = r.shard1[c] + r.shard_in[c].astype(F32)
    r.o_small[9:26] = (
        jnp.concatenate([r.small1[0:9], r.small1[12:20]], axis=0) + r.small1_in[...]
    )
    outs.append(copies.start(r.shard1, r.o_shard.at[1]))
    back_norm_one(r)
    second(6, 7)
    hooks("out", "other")
    grad_heads(r)
    hooks("out", "own")
    launch(8)
    third(4, 5)
    attend_back_values(r)
    hooks("v", "other")
    finish(0, 1, 2, 3)
    for c in range(8):
        r.mine[c] = r.mine[c] + r.shard_in[CHUNKS + c].astype(F32)

    def halfway():
        hooks("v", "own")
        launch(9)
        third(6)

    attend_back(r, False, lambda i: pl.when(i == 1)(halfway))
    bias_heads(r)
    pack_halves(r)
    small_swap = [
        remote(r.small.at[0:6], r.small_in.at[0:6], r.misc_send.at[4], r.misc_recv.at[4], sibling),
        remote(r.small.at[9:12], r.small_in.at[6:9], r.misc_send.at[5], r.misc_recv.at[5], sibling),
    ]
    for copy in small_swap:
        copy.start()
    second(8)
    hooks("qk", "other")
    third(7)
    for copy in small_swap:
        copy.wait()
    r.total[...] = r.small[0:9] + r.small_in[...]
    x_small = remote(r.total, r.x_small, r.misc_send.at[7], r.misc_recv.at[7], x_peer)
    x_small.start()
    hooks("qk", "own", (10, 11))
    second(9)
    launch(10)
    hooks("qk", "own", (11, 12))
    launch(11)
    x_small.wait()
    r.total_x[...] = r.total[...] + r.x_small[...]
    y_small = remote(r.total_x, r.y_small, r.misc_send.at[8], r.misc_recv.at[8], y_peer)
    y_small.start()
    third(8)
    grad_input(r)
    grad_swap = remote(r.dr, r.o_grad.at[t], r.misc_send.at[6], r.misc_recv.at[6], sibling)
    grad_swap.start()
    outs.append(copies.start(r.dr, r.o_grad.at[t]))
    finish(4, 5, 6)
    third(9)
    second(10, 11)
    y_small.wait()
    r.z_small[z] = r.total_x[...] + r.y_small[...]
    z_sends = []
    for o in range(1, zs):
        z_sends.append(
            remote(r.z_small.at[z], r.z_small.at[z], r.z_send.at[o], r.z_recv.at[z], z_peers[o - 1])
        )
        z_sends[-1].start()
    finish(7)
    third(10)
    for o in range(1, zs):
        source = lax.rem(z + o, zs)
        block = r.z_small.at[source]
        remote(block, block, r.z_send.at[o], r.z_recv.at[source], z_peers[o - 1]).wait_recv()
    total = r.z_small[0]
    for k in range(1, zs):
        total = total + r.z_small[k]
    r.o_small[0:9] = total
    third(11)
    finish(8, 9, 10, 11)
    outs.append(copies.start(r.mine, r.o_shard.at[0]))

    for copy in z_sends:
        copy.wait_send()
    for c in range(CHUNKS - SLOTS, CHUNKS):
        sib_copy(jnp.int32(c)).wait_send()
    for gathered in (cot_gather, cls_gather, hat_gather, act_gather):
        gathered.sent()
    for copy in swap_bias:
        copy.wait_send()
    for copy in swaps.values():
        copy.wait_send()
    grad_swap.wait()
    enc_swap.wait()
    for copy in outs:
        copy.wait()


CROSS = ("xb", "x32", "xt", "h1t", "h1b", "h1", "qkv", "o", "p", "xh1", "rs1", "xh2", "rs2", "yb", "dy", "dmt", "dh")
WEIGHT_SCRATCH = dict(
    wqkv=((3, D, D), BF), wout=((D, D), BF), wup=((D, FF), BF), wdown=((FF, D), BF)
)
BACK_SCRATCH = dict(qv_sum=((2, 1, D), F32), bup_sum=((1, FF), F32))


def saved_shapes(rows):
    return dict(
        xt=((D, rows), BF),
        h1t=((D, rows), BF),
        qkv=((3, rows, D), BF),
        o=((rows, D), BF),
        p=((rows // SEG, PAIRS, SEG, 2 * SEG), BF),
        xh1=((rows, D), F32),
        rs1=((rows, SEG), F32),
        g=((rows, FF), BF),
        gp=((rows, FF), BF),
        xh2=((rows, D), F32),
        rs2=((rows, SEG), F32),
    )


def forward_shapes(rows):
    return dict(
        xb=((rows, D), BF),
        h1=((rows, D), F32),
        h1b=((rows, D), BF),
        b3=((3, 1, D), F32),
        bup=((1, FF), F32),
    )


def vmem(table):
    return [pltpu.VMEM(shape, kind) for shape, kind in table.values()]


def arrays(table):
    return [jax.ShapeDtypeStruct(shape, kind) for shape, kind in table.values()]


def run_whole(dp, inputs):
    hbm = pl.BlockSpec(memory_space=pl.ANY)
    small = pl.BlockSpec(memory_space=pltpu.VMEM)
    smem = pl.BlockSpec(memory_space=pltpu.SMEM)
    batches, rows, _ = inputs["tokens"].shape
    slots = inputs["doc_len"].shape[1] * MAXSEG
    segs = rows // SEG
    total_segs = dp * segs
    zs = dp // 4
    shard = D // dp
    outs = dict(
        o_enc=((batches, rows, D), BF),
        o_grad=((batches, rows, D), F32),
        o_shard=((2, CHUNKS, shard, CHUNK), F32),
        o_small=((26, 1, D), F32),
    )
    outs.update({"f_" + w: (inputs["a_" + w].shape[1:], BF) for w in WEIGHTS})
    scratch = dict(saved_shapes(rows))
    scratch.update(WEIGHT_SCRATCH)
    scratch.update(forward_shapes(rows))
    scratch.update(BACK_SCRATCH)
    cross = dict(saved_shapes(slots))
    cross.update(forward_shapes(slots))
    cross.update(
        x32=((slots, D), F32), yb=((slots, D), BF), dy=((slots, D), F32), dmt=((D, slots), BF),
        dh=((slots, D), BF),
    )
    scratch.update({"q_" + k: cross[k] for k in CROSS})
    scratch.update(
        b3_cross=((3, 1, D), F32),
        bup_cross=((1, FF), F32),
        gain=((2, 1, D), F32),
        gain_cross=((2, 1, D), F32),
        bt=((4, 1, D), F32),
        bt_cross=((4, 1, D), F32),
        x_bqv=((2, 2, HALF_D), F32),
        x_bup=((2, HALF_FF), F32),
        cot=((rows, D), BF),
        dmt=((D, rows), BF),
        ring_w=((3, D, D), BF),
        act_first=((segs, 2 * FF + D), F32),
        pick=((8, total_segs), BF),
        bup_sum_cross=((1, FF), F32),
        cot_all=((dp, segs, D), BF),
        cls_all=((dp, segs, D), BF),
        hat_all=((dp, segs, D + SEG), F32),
        act_all=((dp, segs, 2 * FF + D), BF),
        rows64=((total_segs, D), F32),
        hat64=((total_segs, D + SEG), F32),
        act64=((total_segs, 2 * FF + D), BF),
        undeal=((total_segs, slots), BF),
        back=((8, slots), BF),
        allowed=((SEG, SEG), F32),
        ret=((8, D), F32),
        dc=((8, D), F32),
        late=((SEG, D), BF),
        late_t=((D, SEG), BF),
        small=((12, 1, D), F32),
        small1=((20, 1, D), F32),
        small_in=((9, 1, D), F32),
        small1_in=((17, 1, D), F32),
        total=((9, 1, D), F32),
        total_x=((9, 1, D), F32),
        x_small=((9, 1, D), F32),
        y_small=((9, 1, D), F32),
        z_small=((zs, 9, 1, D), F32),
        shard1=((CHUNKS, shard, CHUNK), F32),
        shard_out=((CHUNKS + 8, shard, CHUNK), BF),
        shard_in=((CHUNKS + 8, shard, CHUNK), BF),
        mine=((CHUNKS, shard, CHUNK), F32),
        gbuf=((RING, zs, 2, 2, shard, CHUNK), BF),
        sib_out=((SLOTS, D, CHUNK), BF),
        sib_in=((SLOTS, D, CHUNK), BF),
        one_in=((RING, 2, zs // 2, 2, shard, CHUNK), BF),
        two_in=((RING, 2, zs // 2, shard, CHUNK), BF),
        three_in=((RING, zs - 1, shard, CHUNK), BF),
    )
    dma = pltpu.SemaphoreType.DMA
    sems = dict(
        local_sem=dma((20,)),
        w_send=dma((2, 5)),
        w_recv=dma((2, 5)),
        ring_sem=dma((3, 2)),
        g_send=dma((4, dp)),
        g_recv=dma((4, dp)),
        misc_send=dma((9,)),
        misc_recv=dma((9,)),
        sib_send=dma((SLOTS,)),
        sib_recv=dma((SLOTS,)),
        one_send=dma((CHUNKS, 2)),
        one_recv=dma((CHUNKS, 2)),
        two_send=dma((CHUNKS, 2)),
        two_recv=dma((CHUNKS, 2)),
        three_send=dma((CHUNKS, zs - 1)),
        three_recv=dma((CHUNKS, zs - 1)),
        z_send=dma((zs,)),
        z_recv=dma((zs,)),
        credit=pltpu.SemaphoreType.REGULAR,
    )
    ins = dict(
        seg_doc=smem, doc_len=smem, seg_doc_v=small, tokens=hbm, cotangent=hbm, b_qv=small, b_up=small,
        norm_gain=small, bias_terms=small, seg_pos=small,
        a_wqkv=hbm, a_wout=hbm, a_wup=hbm, a_wdown=hbm,
    )
    names = list(ins) + list(outs) + list(scratch) + list(sems)
    result = pl.pallas_call(
        partial(whole_kernel, dp, names),
        out_shape=arrays(outs),
        in_specs=list(ins.values()),
        out_specs=[hbm, hbm, hbm, small] + [hbm] * 4,
        scratch_shapes=vmem(scratch) + list(sems.values()),
        compiler_params=pltpu.CompilerParams(
            collective_id=0, has_side_effects=True, vmem_limit_bytes=VMEM_LIMIT
        ),
        name="both_layers",
    )(*[inputs[k] for k in ins])
    return dict(zip(outs, result))


VMEM_LIMIT = 64 << 20


def finish_kernel(
    enc, grad, shard, small, o_enc, o_grad, g_qkv, g_out, g_up, g_down, g_bqv, g_bup, g_gain, g_terms, g_pos,
    enc_v, grad_v, shard_v, sems,
):
    copies = Copies(sems)
    quarter = grad.shape[1] // 4
    pieces = [(b, slice(k * quarter, (k + 1) * quarter)) for b in range(grad.shape[0]) for k in range(4)]
    loads = [copies.start(grad.at[b, at], grad_v.at[b, at]) for b, at in pieces]
    load_shard = copies.start(shard, shard_v)
    loads_enc = [copies.start(enc.at[b], enc_v.at[b]) for b in range(enc.shape[0])]
    outs = []
    for (b, at), load in zip(pieces, loads):
        load.wait()
        outs.append(copies.start(grad_v.at[b, at], o_grad.at[b, at]))
    load_shard.wait()
    for layer in range(2):
        for c in range(4):
            lanes = slice(c * CHUNK, (c + 1) * CHUNK)
            outs.append(copies.start(shard_v.at[layer, c], g_down.at[layer, :, lanes]))
            outs.append(copies.start(shard_v.at[layer, 4 + c], g_up.at[layer, :, lanes]))
        outs.append(copies.start(shard_v.at[layer, 8], g_out.at[layer]))
        for k in range(3):
            outs.append(copies.start(shard_v.at[layer, 9 + k], g_qkv.at[layer, QKV_OF[k]]))
    for b, load in enumerate(loads_enc):
        load.wait()
        outs.append(copies.start(enc_v.at[b], o_enc.at[b]))
    for layer in range(2):
        at = 9 * layer
        for k in range(2):
            g_gain[layer, k : k + 1, :] = small[at + k]
            g_bqv[layer, k : k + 1, :] = small[at + 6, :, k * HALF_D : (k + 1) * HALF_D]
            g_bup[layer : layer + 1, k * D : (k + 1) * D] = small[at + 7 + k]
        for k in range(4):
            g_terms[layer, k : k + 1, :] = small[at + 2 + k]
    for k in range(MAXSEG):
        g_pos[k : k + 1, :] = small[18 + k]
    for copy in outs:
        copy.wait()


def fused(tokens, seg_doc, doc_len, w_qkv, b_qv, w_out, w_up, b_up, w_down, norm_gain, bias_terms, seg_pos, cotangent):
    dp = lax.axis_size("dp")
    whole = run_whole(
        dp,
        dict(
            seg_doc=seg_doc, doc_len=doc_len, seg_doc_v=seg_doc, tokens=tokens, cotangent=cotangent,
            b_qv=b_qv, b_up=b_up, norm_gain=norm_gain, bias_terms=bias_terms,
            seg_pos=seg_pos, a_wqkv=w_qkv, a_wout=w_out, a_wup=w_up, a_wdown=w_down,
        ),
    )
    rows = D // dp
    shapes = [
        (2, 3, rows, HALF_D), (2, rows, HALF_D), (2, rows, HALF_FF), (2, rows, HALF_FF),
        (2, 2, HALF_D), (2, HALF_FF), (2, 2, D), (2, 4, D), (MAXSEG, D),
    ]
    hbm = pl.BlockSpec(memory_space=pl.ANY)
    small = pl.BlockSpec(memory_space=pltpu.VMEM)
    results = [whole[k] for k in ("o_enc", "o_grad", "o_shard", "o_small")]
    enc, grad, g_qkv, g_out, g_up, g_down, g_bqv, g_bup, g_gain, g_terms, g_pos = pl.pallas_call(
        finish_kernel,
        out_shape=[jax.ShapeDtypeStruct(a.shape, a.dtype) for a in results[:2]]
        + [jax.ShapeDtypeStruct(shape, F32) for shape in shapes],
        in_specs=[hbm] * 3 + [small],
        out_specs=[hbm] * 6 + [small] * 5,
        scratch_shapes=[pltpu.VMEM(a.shape, a.dtype) for a in results[:3]]
        + [pltpu.SemaphoreType.DMA((56,))],
        compiler_params=pltpu.CompilerParams(vmem_limit_bytes=VMEM_LIMIT),
        name="lay_out",
    )(*results)
    return (
        enc, grad, g_qkv, g_bqv, g_out.transpose(0, 2, 1), g_up, g_bup, g_down.transpose(0, 2, 1),
        g_gain, g_terms, g_pos,
    )


def solution(mesh):
    in_specs = (
        P(None, "dp", None),
        P(),
        P(),
        P(None, None, None, "tensor"),
        P(None, None, "tensor"),
        P(None, "tensor", None),
        P(None, None, "tensor"),
        P(None, "tensor"),
        P(None, "tensor", None),
        P(),
        P(),
        P(),
        P(None, "dp", None),
    )
    out_specs = (
        P(None, "dp", None),
        P(None, "dp", None),
        P(None, None, "dp", "tensor"),
        P(None, None, "tensor"),
        P(None, "tensor", "dp"),
        P(None, "dp", "tensor"),
        P(None, "tensor"),
        P(None, "tensor", "dp"),
        P(),
        P(),
        P(),
    )
    body = fused if mesh.shape["dp"] == 16 and mesh.shape["tensor"] == 2 else local
    return jax.shard_map(body, mesh=mesh, in_specs=in_specs, out_specs=out_specs, check_vma=False)
```
